32 devices in a mesh: row: 4 (over y, x), col: 8 (over z, core).
Axes of the slice: x: 2, y: 2, z: 4, core: 2. Of those that a mesh axis runs over, the one named last changes fastest.
Arguments:
- stream_in: bfloat16 [12288, 2048], P('row', 'col'), may hold values from -50 to 50
- w_qkv: bfloat16 [3, 2048, 2048], P(None, 'col', 'row'), may hold values from -0.125 to 0.125
- w_out: bfloat16 [2048, 2048], P('row', 'col'), may hold values from -0.5 to 0.5
- w_gate_up: bfloat16 [2, 2048, 8192], P(None, 'col', 'row'), may hold values from -0.125 to 0.125
- w_down: bfloat16 [8192, 2048], P('row', 'col'), may hold values from -0.125 to 0.125
- gain_attn: float32 [2048], P('col'), may hold values from 0.5 to 1.5
- gain_ffn: float32 [2048], P('col'), may hold values from 0.5 to 1.5
- gate_logit: float32 [16], P('row'), may hold values from -2 to 2
- memory: float32 [8, 16, 128, 128], P('col', 'row'), may hold values from -1.2 to 1.2
- memory_norm: float32 [8, 16, 128], P('col', 'row'), may hold values from 0.05 to 0.2
- offsets: int32 [8, 4], P('col'), may hold values from 512 to 1024, as said below
- lengths: int32 [8, 4], P('col'), may hold values from 64 to 128, as said below
- cotangent: bfloat16 [12288, 2048], P('row', 'col'), may hold values from -6 to 6
Outputs:
- stream_out: bfloat16 [12288, 2048], P('row', 'col')
- stream_grad: float32 [12288, 2048], P('row', 'col')
- grad_qkv: float32 [3, 2048, 2048], P(None, 'col', 'row')
- grad_out: float32 [2048, 2048], P('row', 'col')
- grad_gate_up: float32 [2, 2048, 8192], P(None, 'col', 'row')
- grad_down: float32 [8192, 2048], P('row', 'col')
- grad_gain_attn: float32 [2048], P('col')
- grad_gain_ffn: float32 [2048], P('col')
- grad_gate_logit: float32 [16], P('row')
- memory_new: float32 [8, 16, 128, 128], P('col', 'row')
- memory_norm_new: float32 [8, 16, 128], P('col', 'row')
- rms_table: float32 [4, 12288], P(None, 'row')
The draws below stay inside these ranges and needn't reach their ends.
Inputs may be any that keep to these rules, and one draw needn't show every extreme that they name: `offsets`: every group has a continuation that sees all 1024 prompt tokens. `lengths`: positions of a continuation at or after its length are padding: no query attends to their keys. Every group has a full continuation.
All inputs are finite; a program needn't handle non-finite values.
Results may differ from the reference program's by a relative error of at most 0.019.
Values may be sent and summed in bfloat16 or wider, within the bound.
A program may use at most 320 MiB of HBM per device.

```python
import math
import jax
import jax.numpy as jnp
from jax import lax

D = 2048
HEADS = 16
HD = 128
FF = 8192
PROMPT = 1024
CONT = 4
CLEN = 128
GLEN = 1536
GROUPS = 8
TOKENS = 12288


def draw_stream_in(key, part):
    key_values, key_rows, key_cols = jax.random.split(key, 3)
    column_rise = 3.0 ** (jnp.arange(D, dtype=jnp.float32) / D)
    column_rough = jax.random.uniform(key_cols, (D,), jnp.float32, 0.7, 1.4)
    row_scale = 10.0 ** jax.random.uniform(key_rows, (TOKENS, 1), jnp.float32, -0.5, 0.5)
    sample = jnp.clip(jax.random.normal(key_values, (TOKENS, D), jnp.float32), -6.0, 6.0)
    return (sample * row_scale * (column_rise * column_rough)[None, :] / 1.8).astype(jnp.bfloat16)


def draw_offsets(key, part):
    key_here = jax.random.fold_in(key, 11)
    key_vals, key_chosen = jax.random.split(key_here)
    values = jax.random.randint(key_vals, (GROUPS, CONT), PROMPT // 2, PROMPT + 1)
    chosen = jax.random.randint(key_chosen, (GROUPS, 1), 0, CONT)
    return jnp.where(jnp.arange(CONT)[None, :] == chosen, PROMPT, values).astype(jnp.int32)


def draw_lengths(key, part):
    key_here = jax.random.fold_in(key, 23)
    key_vals, key_chosen = jax.random.split(key_here)
    values = jax.random.randint(key_vals, (GROUPS, CONT), CLEN // 2, CLEN + 1)
    chosen = jax.random.randint(key_chosen, (GROUPS, 1), 0, CONT)
    return jnp.where(jnp.arange(CONT)[None, :] == chosen, CLEN, values).astype(jnp.int32)


def block_scale(key, dims, cuts, low, high):
    gain, own = 1.0, jax.random.fold_in(key, 6)
    for dim, parts in cuts:
        heights = jnp.exp(jax.random.uniform(jax.random.fold_in(own, dim), (parts,), jnp.float32, low / len(cuts), high / len(cuts)))
        gain = gain * jnp.repeat(heights, dims[dim] // parts).reshape([-1 if axis == dim else 1 for axis in range(len(dims))])
    return gain


def normal_values(key, extent, spread, limit, pieces=(), kind=jnp.bfloat16):
    factor_of = block_scale(key, extent, pieces, -0.22, 0.18) if pieces else 1.0
    entries = jax.random.normal(key, extent, jnp.float32) * spread * factor_of
    return jnp.minimum(jnp.maximum(entries, -limit), limit).astype(kind)


def setup_inputs(seed: int = 0) -> dict:
    streams_of = jax.random.split(jax.random.key(seed), 14)
    return {
        "stream_in": draw_stream_in(jax.random.fold_in(streams_of[13], 71), 0),
        "w_qkv": normal_values(streams_of[1], (3, D, D), D ** -0.5, 0.125, ((1, 8), (2, 4))),
        "w_out": normal_values(streams_of[2], (D, D), HD ** -0.5, 0.5, ((0, 4), (1, 8))),
        "w_gate_up": normal_values(streams_of[3], (2, D, FF), D ** -0.5, 0.125, ((1, 8), (2, 4))),
        "w_down": normal_values(streams_of[4], (FF, D), (FF // 4) ** -0.5, 0.125, ((0, 4), (1, 8))),
        "gain_attn": jnp.clip(1.0 + 0.1 * jax.random.normal(streams_of[5], (D,), jnp.float32), 0.5, 1.5),
        "gain_ffn": jnp.clip(1.0 + 0.1 * jax.random.normal(streams_of[6], (D,), jnp.float32), 0.5, 1.5),
        "gate_logit": jnp.clip(jax.random.uniform(streams_of[7], (HEADS,), jnp.float32, -2.0, 2.0) * block_scale(streams_of[7], (HEADS,), ((0, 4),), -0.4, 0.0), -2.0, 2.0),
        "memory": normal_values(streams_of[8], (GROUPS, HEADS, HD, HD), 0.2, 1.2, ((0, 8), (1, 4)), jnp.float32),
        "memory_norm": jnp.clip(jnp.exp(math.log(0.2) - 1.3862944 * jax.random.uniform(streams_of[9], (GROUPS, HEADS, HD), jnp.float32) ** block_scale(streams_of[9], (GROUPS, HEADS, HD), ((0, 8), (1, 4)), -0.2, 0.2)), 0.05, 0.2),
        "offsets": draw_offsets(jax.random.fold_in(streams_of[13], 71), 0),
        "lengths": draw_lengths(jax.random.fold_in(streams_of[13], 71), 0),
        "cotangent": normal_values(streams_of[12], (TOKENS, D), 1.0, 6.0, ((0, 4), (1, 8))),
    }


EPSILON = 1e-06
MASKED_LOGIT = -1e+30
TOP_PRECISION = lax.Precision.HIGHEST

@jax.custom_vjp
def reduced_dtype(v):
    return lax.optimization_barrier(v.astype(jnp.bfloat16)).astype(jnp.float32)

@jax.custom_vjp
def reduced_backward_dtype(v):
    return v

def low_keep(v):
    return (reduced_dtype(v), None)

def low_pass(kept, grad):
    return (grad,)

def back_keep(v):
    return (v, None)

def back_low(kept, grad):
    return (reduced_dtype(grad),)
reduced_dtype.defvjp(low_keep, low_pass)
reduced_backward_dtype.defvjp(back_keep, back_low)

def feature_map(values):
    return jnp.where(values > 0, values + 1.0, jnp.exp(jnp.minimum(values, 0.0)))

def head_attention(queries, keys_in, values_in, memory_one, norm_one, gate_one, offsets, lengths):
    logit_scale_factor = HD ** (-0.5)
    pos_prompt = jnp.arange(PROMPT)
    pos_cont = jnp.arange(CLEN)
    query_prompt = queries[:PROMPT]
    prompt_key_rows = keys_in[:PROMPT]
    prompt_value_rows = values_in[:PROMPT]
    continuation_query = queries[PROMPT:].reshape(CONT, CLEN, HD)
    key_cont = keys_in[PROMPT:].reshape(CONT, CLEN, HD)
    continuation_value = values_in[PROMPT:].reshape(CONT, CLEN, HD)
    keep_prompt = pos_prompt[:, None] >= pos_prompt[None, :]
    cross_keep_mask = pos_prompt[None, None, :] < offsets[:, None, None]
    keep_self = (pos_cont[None, :, None] >= pos_cont[None, None, :]) & (pos_cont[None, None, :] < lengths[:, None, None])
    scores_prompt = jnp.where(keep_prompt, reduced_backward_dtype(jnp.dot(query_prompt, prompt_key_rows.T, precision=TOP_PRECISION) * logit_scale_factor), MASKED_LOGIT)
    cross_logit_table = jnp.where(cross_keep_mask, reduced_backward_dtype(jnp.einsum('uio,so->uis', continuation_query, prompt_key_rows, precision=TOP_PRECISION) * logit_scale_factor), MASKED_LOGIT)
    scores_self = jnp.where(keep_self, reduced_backward_dtype(jnp.einsum('cld,cmd->clm', continuation_query, key_cont, precision=TOP_PRECISION) * logit_scale_factor), MASKED_LOGIT)
    peak_prompt = lax.optimization_barrier(jnp.max(scores_prompt, axis=1, keepdims=True))
    expo_prompt = jnp.exp(scores_prompt - peak_prompt)
    probs_prompt = expo_prompt / lax.optimization_barrier(jnp.sum(expo_prompt, axis=1, keepdims=True))
    peak_cont = jnp.maximum(lax.optimization_barrier(jnp.max(cross_logit_table, axis=2, keepdims=True)), lax.optimization_barrier(jnp.max(scores_self, axis=2, keepdims=True)))
    expo_cross = jnp.exp(cross_logit_table - peak_cont)
    expo_self = jnp.exp(scores_self - peak_cont)
    total_cont = lax.optimization_barrier(jnp.sum(expo_cross, axis=2, keepdims=True)) + lax.optimization_barrier(jnp.sum(expo_self, axis=2, keepdims=True))
    cross_probability = expo_cross / total_cont
    self_probability = expo_self / total_cont
    dot_prompt = jnp.dot(reduced_dtype(probs_prompt), prompt_value_rows, precision=TOP_PRECISION)
    continuation_product = jnp.einsum('qjb,bi->qji', reduced_dtype(cross_probability), prompt_value_rows, precision=TOP_PRECISION) + jnp.einsum('yzj,yja->yza', reduced_dtype(self_probability), continuation_value, precision=TOP_PRECISION)
    dot_part = jnp.concatenate([dot_prompt, continuation_product.reshape(CONT * CLEN, HD)], axis=0)
    lifted = feature_map(queries)
    numerator = jnp.dot(lifted, memory_one, precision=TOP_PRECISION)
    denominator = jnp.dot(lifted, norm_one, precision=TOP_PRECISION)
    memory_part = numerator / denominator[:, None]
    mixed = gate_one * memory_part + (1.0 - gate_one) * dot_part
    lifted_keys = feature_map(prompt_key_rows)
    memory_new = memory_one + jnp.dot(lifted_keys.T, prompt_value_rows, precision=TOP_PRECISION) / PROMPT
    norm_new = norm_one + lax.optimization_barrier(jnp.mean(lifted_keys, axis=0))
    return (mixed, memory_new, norm_new)

def group_layer(stream, w_qkv, w_out, w_gate_up, w_down, gain_attn, gain_ffn, gate_logit, memory_rows, norm_rows, offset_rows, length_rows):
    inv_in = lax.rsqrt(lax.optimization_barrier(jnp.mean(stream * stream, axis=1, keepdims=True)) + EPSILON)
    normed_in = reduced_dtype(stream * inv_in * gain_attn[None, :])
    packed = reduced_backward_dtype(reduced_dtype(jnp.einsum('td,kdo->tko', normed_in, w_qkv, precision=TOP_PRECISION)))
    heads_all = packed.reshape(GLEN, 3, HEADS, HD).transpose(1, 2, 0, 3)
    gate_value = jax.nn.sigmoid(gate_logit)

    def one_head(items):
        return head_attention(items[0], items[1], items[2], items[3], items[4], items[5], offset_rows, length_rows)
    mixed, memory_new, norm_new = lax.map(jax.checkpoint(one_head), (heads_all[0], heads_all[1], heads_all[2], memory_rows, norm_rows, gate_value))
    attn = reduced_backward_dtype(reduced_dtype(mixed.transpose(1, 0, 2).reshape(GLEN, D)))
    branch = reduced_backward_dtype(jnp.dot(attn, w_out, precision=TOP_PRECISION))
    middle = stream + branch
    inv_mid = lax.rsqrt(lax.optimization_barrier(jnp.mean(middle * middle, axis=1, keepdims=True)) + EPSILON)
    normed_ffn = reduced_dtype(middle * inv_mid * gain_ffn[None, :])
    gate_up = jnp.einsum('td,kdo->tko', normed_ffn, w_gate_up, precision=TOP_PRECISION)
    gate_pre = reduced_backward_dtype(gate_up[:, 0])
    up_pre = reduced_backward_dtype(gate_up[:, 1])
    hidden = reduced_dtype(jax.nn.silu(gate_pre) * up_pre)
    ffn = reduced_backward_dtype(jnp.dot(hidden, w_down, precision=TOP_PRECISION))
    result = middle + ffn
    rms_rows = jnp.stack([jnp.sqrt(lax.optimization_barrier(jnp.mean(branch * branch, axis=1))), jnp.sqrt(lax.optimization_barrier(jnp.mean(middle * middle, axis=1))), jnp.sqrt(lax.optimization_barrier(jnp.mean(ffn * ffn, axis=1))), jnp.sqrt(lax.optimization_barrier(jnp.mean(result * result, axis=1)))])
    return (result, (rms_rows, memory_new, norm_new))

def reference(stream_in, w_qkv, w_out, w_gate_up, w_down, gain_attn, gain_ffn, gate_logit, memory, memory_norm, offsets, lengths, cotangent):
    weights = (w_qkv.astype(jnp.float32), w_out.astype(jnp.float32), w_gate_up.astype(jnp.float32), w_down.astype(jnp.float32), gain_attn, gain_ffn, gate_logit)
    streams = stream_in.astype(jnp.float32).reshape(GROUPS, GLEN, D)
    cotangents = cotangent.astype(jnp.float32).reshape(GROUPS, GLEN, D)

    def group_step(totals, items):
        stream, cot_rows, memory_rows, norm_rows, offset_rows, length_rows = items

        def forward(stream_rows, wq_all, wo_all, wgu_all, wd_all, gain_one, gain_two, logit_all):
            return group_layer(stream_rows, wq_all, wo_all, wgu_all, wd_all, gain_one, gain_two, logit_all, memory_rows, norm_rows, offset_rows, length_rows)
        result, pullback, extras = jax.vjp(forward, stream, weights[0], weights[1], weights[2], weights[3], weights[4], weights[5], weights[6], has_aux=True)
        gradients = pullback(cot_rows)
        totals = tuple((before + increment for before, increment in zip(totals, gradients[1:])))
        return (totals, (result.astype(jnp.bfloat16), gradients[0], extras[0], extras[1], extras[2]))
    zero_grads = tuple((jnp.zeros_like(weight_item) for weight_item in weights))
    totals, outputs = lax.scan(group_step, zero_grads, (streams, cotangents, memory, memory_norm, offsets, lengths))
    out_rows, grad_rows, rms_rows, memory_new, norm_new = outputs
    return (out_rows.reshape(TOKENS, D), grad_rows.reshape(TOKENS, D), totals[0], totals[1], totals[2], totals[3], totals[4], totals[5], totals[6], memory_new, norm_new, rms_rows.transpose(1, 0, 2).reshape(4, TOKENS))
```

```python
import jax
import jax.numpy as jnp
from jax import lax
from jax.sharding import PartitionSpec as P

D = 2048
HD = 128
PROMPT = 1024
CONT = 4
CLEN = 128
GLEN = 1536


EPSILON = 1e-06
MASKED_LOGIT = -1e30
TOP_PRECISION = lax.Precision.HIGHEST


def shortened(value):

    def short(part):
        return part.astype(jnp.bfloat16) if part.dtype == jnp.float32 else part

    return jax.tree.map(short, value)


def feature_map(values):
    return jnp.where(values > 0, values + 1.0, jnp.exp(jnp.minimum(values, 0.0)))


def feature_slope(values):
    return jnp.where(values > 0, 1.0, jnp.exp(jnp.minimum(values, 0.0)))


def tokens_contract(left, right):
    return lax.dot_general(
        left, right, (((0,), (0,)), ((), ())), preferred_element_type=jnp.float32
    )


def against_rows(left, right):
    return lax.dot_general(
        left, right, (((1,), (1,)), ((), ())), preferred_element_type=jnp.float32
    )


def to_tokens(block):
    row_size = lax.axis_size("row")
    features = block.shape[1]
    groups = block.shape[0] // GLEN
    piece = GLEN // row_size
    split = block.reshape(groups, row_size, piece, features)
    split = lax.all_to_all(split, "row", split_axis=1, concat_axis=0, tiled=True)
    split = split.reshape(row_size * groups, piece, features)
    whole = lax.all_to_all(split, "col", split_axis=0, concat_axis=2, tiled=True)
    return whole.reshape(piece, -1)


def from_tokens(whole):
    row_size = lax.axis_size("row")
    col_size = lax.axis_size("col")
    piece = whole.shape[0]
    split = lax.all_to_all(whole[None], "col", split_axis=2, concat_axis=0, tiled=True)
    groups = col_size // row_size
    split = split.reshape(row_size, groups, piece, -1)
    split = lax.all_to_all(split, "row", split_axis=0, concat_axis=2, tiled=True)
    return split.reshape(groups * GLEN, -1)


def collect(values):
    return lax.all_gather(values, "row", axis=0, tiled=True)


def land(partial):
    return lax.psum_scatter(
        partial.astype(jnp.bfloat16), "row", scatter_dimension=0, tiled=True
    ).astype(jnp.float32)


def score_blocks(queries, keys_in, offsets, lengths):
    head_count = queries.shape[0]
    logit_scale_factor = HD ** (-0.5)
    query_prompt = queries[:, :PROMPT]
    prompt_key_rows = keys_in[:, :PROMPT]
    continuation_query = queries[:, PROMPT:].reshape(head_count, CONT, CLEN, HD)
    key_cont = keys_in[:, PROMPT:].reshape(head_count, CONT, CLEN, HD)
    pos_prompt = jnp.arange(PROMPT)
    pos_cont = jnp.arange(CLEN)
    keep_prompt = pos_prompt[:, None] >= pos_prompt[None, :]
    cross_keep_mask = pos_prompt[None, None, :] < offsets[:, None, None]
    keep_self = (pos_cont[None, :, None] >= pos_cont[None, None, :]) & (
        pos_cont[None, None, :] < lengths[:, None, None]
    )
    scores_prompt = (
        jnp.einsum(
            "hqd,hkd->hqk", query_prompt, prompt_key_rows, preferred_element_type=jnp.float32
        )
        * logit_scale_factor
    )
    cross_logit_table = (
        jnp.einsum(
            "hcld,hkd->hclk",
            continuation_query,
            prompt_key_rows,
            preferred_element_type=jnp.float32,
        )
        * logit_scale_factor
    )
    scores_self = (
        jnp.einsum(
            "hcld,hcmd->hclm", continuation_query, key_cont, preferred_element_type=jnp.float32
        )
        * logit_scale_factor
    )
    return (
        jnp.where(keep_prompt[None], scores_prompt, MASKED_LOGIT),
        jnp.where(cross_keep_mask[None], cross_logit_table, MASKED_LOGIT),
        jnp.where(keep_self[None], scores_self, MASKED_LOGIT),
    )


def attend_group(queries, keys_in, values_in, memory_one, norm_one, offsets, lengths, gate_value):
    head_count = queries.shape[0]
    scores_prompt, cross_logit_table, scores_self = score_blocks(queries, keys_in, offsets, lengths)
    peak_prompt = jnp.max(scores_prompt, axis=2)
    logsum_prompt = peak_prompt + jnp.log(
        jnp.sum(jnp.exp(scores_prompt - peak_prompt[..., None]), axis=2)
    )
    peak_cont = jnp.maximum(jnp.max(cross_logit_table, axis=3), jnp.max(scores_self, axis=3))
    logsum_cont = peak_cont + jnp.log(
        jnp.sum(jnp.exp(cross_logit_table - peak_cont[..., None]), axis=3)
        + jnp.sum(jnp.exp(scores_self - peak_cont[..., None]), axis=3)
    )
    probs_prompt = jnp.exp(scores_prompt - logsum_prompt[..., None]).astype(jnp.bfloat16)
    cross_probability = jnp.exp(cross_logit_table - logsum_cont[..., None]).astype(jnp.bfloat16)
    self_probability = jnp.exp(scores_self - logsum_cont[..., None]).astype(jnp.bfloat16)
    prompt_value_rows = values_in[:, :PROMPT]
    continuation_value = values_in[:, PROMPT:].reshape(head_count, CONT, CLEN, HD)
    dot_prompt = jnp.einsum(
        "hqk,hkd->hqd", probs_prompt, prompt_value_rows, preferred_element_type=jnp.float32
    )
    continuation_product = jnp.einsum(
        "hclk,hkd->hcld", cross_probability, prompt_value_rows, preferred_element_type=jnp.float32
    ) + jnp.einsum(
        "hclm,hcmd->hcld", self_probability, continuation_value, preferred_element_type=jnp.float32
    )
    dot_part = jnp.concatenate(
        [dot_prompt, continuation_product.reshape(head_count, CONT * CLEN, HD)], axis=1
    )
    lifted = feature_map(queries.astype(jnp.float32))
    numerator = jnp.einsum("htd,hde->hte", lifted, memory_one, precision=TOP_PRECISION)
    denominator = jnp.einsum("htd,hd->ht", lifted, norm_one, precision=TOP_PRECISION)
    memory_part = numerator / denominator[..., None]
    mixing = gate_value[:, None, None]
    attended = mixing * memory_part + (1.0 - mixing) * dot_part
    lifted_keys = feature_map(keys_in[:, :PROMPT].astype(jnp.float32))
    memory_new = (
        memory_one
        + jnp.einsum(
            "hkd,hke->hde",
            lifted_keys,
            prompt_value_rows.astype(jnp.float32),
            precision=TOP_PRECISION,
        )
        / PROMPT
    )
    norm_new = norm_one + jnp.mean(lifted_keys, axis=1)
    return (attended, logsum_prompt, logsum_cont, memory_part, dot_part, memory_new, norm_new)


def attend_back(
    queries,
    keys_in,
    values_in,
    grad_attn,
    logsum_prompt,
    logsum_cont,
    memory_part,
    dot_part,
    memory_one,
    norm_one,
    offsets,
    lengths,
    gate_value,
):
    head_count = queries.shape[0]
    logit_scale_factor = HD ** (-0.5)
    scores_prompt, cross_logit_table, scores_self = score_blocks(queries, keys_in, offsets, lengths)
    probs_prompt = jnp.exp(scores_prompt - logsum_prompt[..., None])
    cross_probability = jnp.exp(cross_logit_table - logsum_cont[..., None])
    self_probability = jnp.exp(scores_self - logsum_cont[..., None])
    keep_dot = (1.0 - gate_value)[:, None, None]
    keep_four = keep_dot[..., None]
    grad_float = grad_attn.astype(jnp.float32)
    grad_gate = jnp.sum(grad_float * (memory_part - dot_part), axis=(1, 2))
    query_prompt = queries[:, :PROMPT]
    prompt_key_rows = keys_in[:, :PROMPT]
    prompt_value_rows = values_in[:, :PROMPT]
    continuation_query = queries[:, PROMPT:].reshape(head_count, CONT, CLEN, HD)
    key_cont = keys_in[:, PROMPT:].reshape(head_count, CONT, CLEN, HD)
    continuation_value = values_in[:, PROMPT:].reshape(head_count, CONT, CLEN, HD)
    grad_prompt = grad_attn[:, :PROMPT]
    grad_cont = grad_attn[:, PROMPT:].reshape(head_count, CONT, CLEN, HD)
    dprob_prompt = (
        jnp.einsum(
            "hqd,hkd->hqk", grad_prompt, prompt_value_rows, preferred_element_type=jnp.float32
        )
        * keep_dot
    )
    dscore_prompt = probs_prompt * (
        dprob_prompt - jnp.sum(probs_prompt * dprob_prompt, axis=2, keepdims=True)
    )
    dprob_cross = (
        jnp.einsum(
            "hcld,hkd->hclk", grad_cont, prompt_value_rows, preferred_element_type=jnp.float32
        )
        * keep_four
    )
    dprob_self = (
        jnp.einsum(
            "hcld,hcmd->hclm", grad_cont, continuation_value, preferred_element_type=jnp.float32
        )
        * keep_four
    )
    centre = jnp.sum(cross_probability * dprob_cross, axis=3, keepdims=True) + jnp.sum(
        self_probability * dprob_self, axis=3, keepdims=True
    )
    low_prompt = dscore_prompt.astype(jnp.bfloat16)
    low_cross = (cross_probability * (dprob_cross - centre)).astype(jnp.bfloat16)
    low_self = (self_probability * (dprob_self - centre)).astype(jnp.bfloat16)
    query_grad_prompt = (
        jnp.einsum("hqk,hkd->hqd", low_prompt, prompt_key_rows, preferred_element_type=jnp.float32)
        * logit_scale_factor
    )
    query_grad_cont = (
        jnp.einsum("hclk,hkd->hcld", low_cross, prompt_key_rows, preferred_element_type=jnp.float32)
        + jnp.einsum("hclm,hcmd->hcld", low_self, key_cont, preferred_element_type=jnp.float32)
    ) * logit_scale_factor
    key_grad_prompt = (
        jnp.einsum("hqk,hqd->hkd", low_prompt, query_prompt, preferred_element_type=jnp.float32)
        + jnp.einsum(
            "hclk,hcld->hkd", low_cross, continuation_query, preferred_element_type=jnp.float32
        )
    ) * logit_scale_factor
    key_grad_cont = (
        jnp.einsum(
            "hclm,hcld->hcmd", low_self, continuation_query, preferred_element_type=jnp.float32
        )
        * logit_scale_factor
    )
    prob_low_prompt = probs_prompt.astype(jnp.bfloat16)
    prob_low_cross = cross_probability.astype(jnp.bfloat16)
    prob_low_self = self_probability.astype(jnp.bfloat16)
    value_grad_prompt = (
        jnp.einsum("hqk,hqd->hkd", prob_low_prompt, grad_prompt, preferred_element_type=jnp.float32)
        + jnp.einsum(
            "hclk,hcld->hkd", prob_low_cross, grad_cont, preferred_element_type=jnp.float32
        )
    ) * keep_dot
    value_grad_cont = (
        jnp.einsum("hclm,hcld->hcmd", prob_low_self, grad_cont, preferred_element_type=jnp.float32)
        * keep_four
    )
    query_float = queries.astype(jnp.float32)
    lifted = feature_map(query_float)
    denominator = jnp.einsum("htd,hd->ht", lifted, norm_one, precision=TOP_PRECISION)
    grad_memory = gate_value[:, None, None] * grad_float
    grad_numerator = grad_memory / denominator[..., None]
    grad_denominator = -jnp.sum(grad_memory * memory_part, axis=2) / denominator
    grad_lifted = (
        jnp.einsum("hte,hde->htd", grad_numerator, memory_one, precision=TOP_PRECISION)
        + grad_denominator[..., None] * norm_one[:, None, :]
    )
    grad_queries = jnp.concatenate(
        [query_grad_prompt, query_grad_cont.reshape(head_count, CONT * CLEN, HD)], axis=1
    ) + grad_lifted * feature_slope(query_float)
    grad_keys = jnp.concatenate(
        [key_grad_prompt, key_grad_cont.reshape(head_count, CONT * CLEN, HD)], axis=1
    )
    grad_values = jnp.concatenate(
        [value_grad_prompt, value_grad_cont.reshape(head_count, CONT * CLEN, HD)], axis=1
    )
    return (grad_queries, grad_keys, grad_values, grad_gate)


def local(
    stream_in,
    w_qkv,
    w_out,
    w_gate_up,
    w_down,
    gain_attn,
    gain_ffn,
    gate_logit,
    memory,
    memory_norm,
    offsets,
    lengths,
    cotangent,
):
    head_here = memory.shape[1]
    row_size = lax.axis_size("row")
    col_size = lax.axis_size("col")
    row_index = lax.axis_index("row")
    col_index = lax.axis_index("col")
    gains = lax.all_gather(jnp.stack([gain_attn, gain_ffn]), "col", axis=1, tiled=True)
    gain_in, gain_mid = gains[0:1], gains[1:2]
    whole_qkv, whole_out, whole_gu, whole_down = (
        lax.all_gather(w_qkv, "col", axis=1, tiled=True),
        lax.all_gather(w_out, "col", axis=1, tiled=True),
        lax.all_gather(w_gate_up, "col", axis=1, tiled=True),
        lax.all_gather(w_down, "col", axis=1, tiled=True),
    )
    stream = to_tokens(stream_in).astype(jnp.float32)
    inv_in = lax.rsqrt(jnp.mean(stream * stream, axis=1, keepdims=True) + EPSILON)
    normed_in = (stream * inv_in * gain_in).astype(jnp.bfloat16)
    local_in = collect(normed_in)
    cot_tokens = to_tokens(cotangent)
    local_cot = collect(cot_tokens)
    packed = jnp.einsum("td,kdo->tko", local_in, whole_qkv, preferred_element_type=jnp.float32)
    heads_all = (
        packed.astype(jnp.bfloat16).reshape(GLEN, 3, head_here, HD).transpose(1, 2, 0, 3)
    )
    gate_value = jax.nn.sigmoid(gate_logit)
    attended, logsum_prompt, logsum_cont, memory_part, dot_part, memory_new, norm_new = attend_group(
        heads_all[0],
        heads_all[1],
        heads_all[2],
        memory[0],
        memory_norm[0],
        offsets[0],
        lengths[0],
        gate_value,
    )
    attn_low = attended.astype(jnp.bfloat16).transpose(1, 0, 2).reshape(GLEN, head_here * HD)
    branch = land(jnp.dot(attn_low, whole_out, preferred_element_type=jnp.float32))
    middle = stream + branch
    inv_mid = lax.rsqrt(jnp.mean(middle * middle, axis=1, keepdims=True) + EPSILON)
    normed_ffn = (middle * inv_mid * gain_mid).astype(jnp.bfloat16)
    local_ffn = collect(normed_ffn)
    gate_up = jnp.einsum("td,kdo->tko", local_ffn, whole_gu, preferred_element_type=jnp.float32)
    gate_pre = gate_up[:, 0]
    up_pre = gate_up[:, 1]
    sigmoid_gate = jax.nn.sigmoid(gate_pre)
    hidden_low = (gate_pre * sigmoid_gate * up_pre).astype(jnp.bfloat16)
    ffn = land(jnp.dot(hidden_low, whole_down, preferred_element_type=jnp.float32))
    result = middle + ffn
    stream_out = from_tokens(result.astype(jnp.bfloat16))
    grad_hidden = against_rows(local_cot, whole_down)
    part_down = tokens_contract(hidden_low, local_cot)
    grad_up = grad_hidden * gate_pre * sigmoid_gate
    grad_gate = grad_hidden * up_pre * sigmoid_gate * (1.0 + gate_pre * (1.0 - sigmoid_gate))
    grad_gu_low = jnp.stack([grad_gate, grad_up], axis=1).astype(jnp.bfloat16)
    grad_normed_ffn = land(
        jnp.einsum("tko,kdo->td", grad_gu_low, whole_gu, preferred_element_type=jnp.float32)
    )
    part_gu = jnp.einsum("td,tko->kdo", local_ffn, grad_gu_low, preferred_element_type=jnp.float32)
    scaled_mid = grad_normed_ffn * gain_mid
    inner_mid = jnp.mean(scaled_mid * middle, axis=1, keepdims=True)
    grad_middle = (
        cot_tokens.astype(jnp.float32) + inv_mid * scaled_mid - middle * inv_mid**3 * inner_mid
    )
    part_gain_ffn = jnp.sum(grad_normed_ffn * middle * inv_mid, axis=0)
    branch_low = grad_middle.astype(jnp.bfloat16)
    local_branch = collect(branch_low)
    grad_attn_rows = against_rows(local_branch, whole_out)
    part_out = tokens_contract(attn_low, local_branch)
    grad_heads = (
        grad_attn_rows.astype(jnp.bfloat16).reshape(GLEN, head_here, HD).transpose(1, 0, 2)
    )
    grad_queries, grad_keys, grad_values, grad_gates = attend_back(
        heads_all[0],
        heads_all[1],
        heads_all[2],
        grad_heads,
        logsum_prompt,
        logsum_cont,
        memory_part,
        dot_part,
        memory[0],
        memory_norm[0],
        offsets[0],
        lengths[0],
        gate_value,
    )
    logit_part = gate_value * (1.0 - gate_value) * grad_gates
    grad_packed = (
        jnp.stack([grad_queries, grad_keys, grad_values], axis=0)
        .transpose(2, 0, 1, 3)
        .reshape(GLEN, 3, head_here * HD)
        .astype(jnp.bfloat16)
    )
    grad_normed_in = land(
        jnp.einsum("tko,kdo->td", grad_packed, whole_qkv, preferred_element_type=jnp.float32)
    )
    part_qkv = jnp.einsum("td,tko->kdo", local_in, grad_packed, preferred_element_type=jnp.float32)
    grad_qkv, grad_out, grad_gate_up, grad_down = (
        lax.psum_scatter(
            part_qkv.astype(jnp.bfloat16), "col", scatter_dimension=1, tiled=True
        ).astype(jnp.float32),
        lax.psum_scatter(
            part_out.astype(jnp.bfloat16), "col", scatter_dimension=1, tiled=True
        ).astype(jnp.float32),
        lax.psum_scatter(
            part_gu.astype(jnp.bfloat16), "col", scatter_dimension=1, tiled=True
        ).astype(jnp.float32),
        lax.psum_scatter(
            part_down.astype(jnp.bfloat16), "col", scatter_dimension=1, tiled=True
        ).astype(jnp.float32),
    )
    scaled_in = grad_normed_in * gain_in
    inner_in = jnp.mean(scaled_in * stream, axis=1, keepdims=True)
    grad_stream = grad_middle + inv_in * scaled_in - stream * inv_in**3 * inner_in
    stream_grad = from_tokens(grad_stream.astype(jnp.bfloat16)).astype(jnp.float32)
    part_gain_attn = jnp.sum(grad_normed_in * stream * inv_in, axis=0)
    logit_slots = lax.dynamic_update_slice(
        jnp.zeros((row_size * head_here,), jnp.float32), logit_part, (row_index * head_here,)
    )
    small = lax.psum(
        jnp.concatenate([part_gain_attn, part_gain_ffn, logit_slots]), ("row", "col")
    )
    features_here = gain_attn.shape[0]
    grad_gain_attn = lax.dynamic_slice(small, (col_index * features_here,), (features_here,))
    grad_gain_ffn = lax.dynamic_slice(small, (D + col_index * features_here,), (features_here,))
    grad_gate_logit = lax.dynamic_slice(small, (2 * D + row_index * head_here,), (head_here,))
    rms_here = jnp.sqrt(
        jnp.stack([jnp.mean(part * part, axis=1) for part in (branch, middle, ffn, result)])
    )
    rms_all = lax.all_gather(rms_here, ("col", "row"), axis=1, tiled=True)
    rows_here = stream_in.shape[0]
    rms_table = lax.dynamic_slice(rms_all, (0, row_index * rows_here), (4, rows_here))
    return (
        stream_out,
        stream_grad,
        grad_qkv,
        grad_out,
        grad_gate_up,
        grad_down,
        grad_gain_attn,
        grad_gain_ffn,
        grad_gate_logit,
        memory_new[None],
        norm_new[None],
        rms_table,
    )


def solution(mesh):
    return jax.shard_map(
        local,
        mesh=mesh,
        in_specs=(
            P("row", "col"),
            P(None, "col", "row"),
            P("row", "col"),
            P(None, "col", "row"),
            P("row", "col"),
            P("col"),
            P("col"),
            P("row"),
            P("col", "row", None, None),
            P("col", "row", None),
            P("col", None),
            P("col", None),
            P("row", "col"),
        ),
        out_specs=(
            P("row", "col"),
            P("row", "col"),
            P(None, "col", "row"),
            P("row", "col"),
            P(None, "col", "row"),
            P("row", "col"),
            P("col"),
            P("col"),
            P("row"),
            P("col", "row", None, None),
            P("col", "row", None),
            P(None, "row"),
        ),
        check_vma=False,
    )
```

```python
import jax
import jax.numpy as jnp
from jax import lax
from jax.experimental import pallas as pl
from jax.experimental.pallas import tpu as pltpu
from jax.sharding import PartitionSpec as P

D = 2048
HD = 128
PROMPT = 1024
CONT = 4
CLEN = 128
GLEN = 1536


EPSILON = 1e-06
MASKED_LOGIT = -1e30
BIG_VMEM = 60 * 1024 * 1024


def feature_map(values):
    return jnp.where(values > 0, values + 1.0, jnp.exp(jnp.minimum(values, 0.0)))


def feature_slope(values):
    return jnp.where(values > 0, 1.0, jnp.exp(jnp.minimum(values, 0.0)))


def split_two(value):
    high = value.astype(jnp.bfloat16)
    return high, (value - high.astype(jnp.float32)).astype(jnp.bfloat16)


def wide_dot(left, right, dims):
    left_high, left_low = split_two(left)
    right_high, right_low = split_two(right)

    def one(a, b):
        return lax.dot_general(a, b, (dims, ((), ())), preferred_element_type=jnp.float32)

    return one(left_high, right_high) + one(left_high, right_low) + one(left_low, right_high)


def narrow_dot(left, right, dims):
    right_high, right_low = split_two(right)

    def one(b):
        return lax.dot_general(left, b, (dims, ((), ())), preferred_element_type=jnp.float32)

    return one(right_high) + one(right_low)


def plain_dot(left, right, dims):
    return lax.dot_general(left, right, (dims, ((), ())), preferred_element_type=jnp.float32)


NN = ((1,), (0,))
NT = ((1,), (1,))
TN = ((0,), (0,))
QT = 256
PROMPT_TILES = PROMPT // QT
TILES = GLEN // QT


def tile_scores(tile, q, k_ref, offsets_ref, lengths_ref):
    scale = HD ** (-0.5)
    row = lax.broadcasted_iota(jnp.int32, (QT, QT), 0)
    column = lax.broadcasted_iota(jnp.int32, (QT, QT), 1)
    seen = min(tile * QT, PROMPT)
    own = plain_dot(q, k_ref[tile * QT : (tile + 1) * QT], NT) * scale
    if tile < PROMPT_TILES:
        own = jnp.where(row >= column, own, MASKED_LOGIT)
        ahead = plain_dot(q, k_ref[:seen], NT) * scale if seen else None
        return ahead, own, seen
    first = (tile - PROMPT_TILES) * (QT // CLEN)
    upper = lax.broadcasted_iota(jnp.int32, (QT, 1), 0) >= CLEN
    limit = jnp.where(upper, offsets_ref[first + 1], offsets_ref[first])
    live = jnp.where(upper, lengths_ref[first + 1] + CLEN, lengths_ref[first])
    same = (row >= CLEN) == (column >= CLEN)
    own = jnp.where((row >= column) & same & (column < live), own, MASKED_LOGIT)
    ahead = plain_dot(q, k_ref[:seen], NT) * scale
    position = lax.broadcasted_iota(jnp.int32, (QT, PROMPT), 1)
    return jnp.where(position < limit, ahead, MASKED_LOGIT), own, seen


def attend_kernel(
    offsets_ref, lengths_ref, gate_ref, qkv_ref, memory_ref, norm_ref,
    attn_ref, dot_ref, part_ref, logsum_ref, memory_new_ref, norm_new_ref,
):
    head = pl.program_id(0)
    gate = gate_ref[head]
    q_ref, k_ref, v_ref = qkv_ref.at[0, 0], qkv_ref.at[1, 0], qkv_ref.at[2, 0]
    memory_one = memory_ref[0]
    norm_one = norm_ref[0]
    for tile in range(TILES):
        rows = slice(tile * QT, (tile + 1) * QT)
        q = q_ref[rows]
        ahead, own, seen = tile_scores(tile, q, k_ref, offsets_ref, lengths_ref)
        peak = jnp.max(own, axis=1, keepdims=True)
        if ahead is not None:
            peak = jnp.maximum(peak, jnp.max(ahead, axis=1, keepdims=True))
        own = jnp.exp(own - peak)
        total = jnp.sum(own, axis=1, keepdims=True)
        dot_part = plain_dot(own.astype(jnp.bfloat16), v_ref[rows], NN)
        if ahead is not None:
            ahead = jnp.exp(ahead - peak)
            total += jnp.sum(ahead, axis=1, keepdims=True)
            dot_part += plain_dot(ahead.astype(jnp.bfloat16), v_ref[:seen], NN)
        dot_part = dot_part / total
        lifted = feature_map(q.astype(jnp.float32))
        memory_part = wide_dot(lifted, memory_one, NN) / jnp.sum(
            lifted * norm_one, axis=1, keepdims=True
        )
        attn_ref[rows, :] = (gate * memory_part + (1.0 - gate) * dot_part).astype(jnp.bfloat16)
        dot_ref[0, rows, :] = dot_part
        part_ref[0, rows, :] = memory_part
        logsum_ref[0, rows, :] = peak + jnp.log(total)
    lifted_keys = feature_map(k_ref[:PROMPT].astype(jnp.float32))
    high, low = split_two(lifted_keys)
    v = v_ref[:PROMPT]
    memory_new_ref[0] = memory_one + (plain_dot(high, v, TN) + plain_dot(low, v, TN)) / PROMPT
    norm_new_ref[0] = norm_one + jnp.mean(lifted_keys, axis=0, keepdims=True)


def head_block(shape, lead=0):
    zeros = (0,) * (len(shape) - 1 - lead)
    return pl.BlockSpec(shape, lambda h: (0,) * lead + (h,) + zeros)


SMEM_SPEC = pl.BlockSpec(memory_space=pltpu.SMEM)


def attend(heads_all, memory_one, norm_one, offsets, lengths, gate_value):
    heads = heads_all.shape[1]
    f32 = jnp.float32
    row_block = head_block((1, GLEN, HD))
    column = pl.BlockSpec((GLEN, HD), lambda h: (0, h))
    return pl.pallas_call(
        attend_kernel,
        grid=(heads,),
        in_specs=[
            SMEM_SPEC, SMEM_SPEC, SMEM_SPEC,
            head_block((3, 1, GLEN, HD), 1), head_block((1, HD, HD)), head_block((1, 1, HD)),
        ],
        out_specs=[
            column, row_block, row_block, head_block((1, GLEN, 1)),
            head_block((1, HD, HD)), head_block((1, 1, HD)),
        ],
        out_shape=[
            jax.ShapeDtypeStruct((GLEN, heads * HD), jnp.bfloat16),
            jax.ShapeDtypeStruct((heads, GLEN, HD), f32),
            jax.ShapeDtypeStruct((heads, GLEN, HD), f32),
            jax.ShapeDtypeStruct((heads, GLEN, 1), f32),
            jax.ShapeDtypeStruct((heads, HD, HD), f32),
            jax.ShapeDtypeStruct((heads, 1, HD), f32),
        ],
        compiler_params=pltpu.CompilerParams(vmem_limit_bytes=BIG_VMEM),
        cost_estimate=pl.CostEstimate(
            flops=heads * 800_000_000, bytes_accessed=heads * 6_000_000, transcendentals=heads * 1_300_000
        ),
        name="attend",
    )(offsets, lengths, gate_value, heads_all, memory_one, norm_one[:, None, :])


def attend_back_kernel(
    offsets_ref, lengths_ref, gate_ref, qkv_ref, grad_ref, dot_ref, part_ref, logsum_ref,
    memory_ref, norm_ref, out_ref, gate_out_ref, key_sum, value_sum,
):
    head = pl.program_id(0)
    gate = gate_ref[head]
    keep = 1.0 - gate
    scale = HD ** (-0.5)
    q_ref, k_ref, v_ref = qkv_ref.at[0, 0], qkv_ref.at[1, 0], qkv_ref.at[2, 0]
    memory_one = memory_ref[0]
    norm_one = norm_ref[0]
    gate_row = jnp.zeros((1, HD), jnp.float32)
    key_sum[...] = jnp.zeros_like(key_sum)
    value_sum[...] = jnp.zeros_like(value_sum)
    for tile in range(TILES):
        rows = slice(tile * QT, (tile + 1) * QT)
        q = q_ref[rows]
        grad = grad_ref[0, rows, :]
        grad_float = grad.astype(jnp.float32)
        memory_part = part_ref[0, rows, :]
        dot_part = dot_ref[0, rows, :]
        against_dot = jnp.sum(grad_float * dot_part, axis=1, keepdims=True)
        gate_row += jnp.sum(grad_float * (memory_part - dot_part), axis=0, keepdims=True)
        logsum = logsum_ref[0, rows, :]
        ahead, own, seen = tile_scores(tile, q, k_ref, offsets_ref, lengths_ref)
        own = jnp.exp(own - logsum)
        value_sum[rows, :] += plain_dot(own.astype(jnp.bfloat16), grad, TN)
        own = (keep * own * (plain_dot(grad, v_ref[rows], NT) - against_dot)).astype(jnp.bfloat16)
        key_sum[rows, :] += plain_dot(own, q, TN)
        grad_q = plain_dot(own, k_ref[rows], NN)
        if ahead is not None:
            ahead = jnp.exp(ahead - logsum)
            value_sum[:seen, :] += plain_dot(ahead.astype(jnp.bfloat16), grad, TN)
            ahead = (keep * ahead * (plain_dot(grad, v_ref[:seen], NT) - against_dot)).astype(
                jnp.bfloat16
            )
            key_sum[:seen, :] += plain_dot(ahead, q, TN)
            grad_q += plain_dot(ahead, k_ref[:seen], NN)
        q_float = q.astype(jnp.float32)
        lifted = feature_map(q_float)
        inverse = gate / jnp.sum(lifted * norm_one, axis=1, keepdims=True)
        against_memory = jnp.sum(grad_float * memory_part, axis=1, keepdims=True)
        grad_lifted = inverse * (narrow_dot(grad, memory_one, NT) - against_memory * norm_one)
        out_ref[0, rows, :] = (grad_q * scale + grad_lifted * feature_slope(q_float)).astype(
            jnp.bfloat16
        )
    out_ref[1, :, :] = (key_sum[...] * scale).astype(jnp.bfloat16)
    out_ref[2, :, :] = (value_sum[...] * keep).astype(jnp.bfloat16)
    gate_out_ref[0] = gate_row


def attend_back(heads_all, grad_heads, dot_part, memory_part, logsum, memory_one, norm_one, offsets, lengths, gate_value):
    heads = heads_all.shape[1]
    f32 = jnp.float32
    row_block = head_block((1, GLEN, HD))
    return pl.pallas_call(
        attend_back_kernel,
        grid=(heads,),
        in_specs=[
            SMEM_SPEC, SMEM_SPEC, SMEM_SPEC,
            head_block((3, 1, GLEN, HD), 1), row_block, row_block, row_block,
            head_block((1, GLEN, 1)), head_block((1, HD, HD)), head_block((1, 1, HD)),
        ],
        out_specs=[
            pl.BlockSpec((3, GLEN, HD), lambda h: (0, 0, h)),
            head_block((1, 1, HD)),
        ],
        out_shape=[
            jax.ShapeDtypeStruct((3, GLEN, heads * HD), jnp.bfloat16),
            jax.ShapeDtypeStruct((heads, 1, HD), f32),
        ],
        scratch_shapes=[pltpu.VMEM((GLEN, HD), f32), pltpu.VMEM((GLEN, HD), f32)],
        compiler_params=pltpu.CompilerParams(vmem_limit_bytes=BIG_VMEM),
        cost_estimate=pl.CostEstimate(
            flops=heads * 2_000_000_000, bytes_accessed=heads * 6_000_000, transcendentals=heads * 1_300_000
        ),
        name="attend_back",
    )(
        offsets, lengths, gate_value, heads_all, grad_heads, dot_part, memory_part, logsum,
        memory_one, norm_one[:, None, :],
    )


ANY = pl.BlockSpec(memory_space=pl.ANY)
VMEM = pl.BlockSpec(memory_space=pltpu.VMEM)
MESH_ID = pl.DeviceIdType.MESH
HALF = D // 2
AG_CUTS = 4


def remote(source, target, send, receive, device):
    return pltpu.make_async_remote_copy(
        src_ref=source, dst_ref=target, send_sem=send, recv_sem=receive,
        device_id=device, device_id_type=MESH_ID,
    )


def greet(peers):
    barrier = pltpu.get_barrier_semaphore()
    for peer in peers:
        pl.semaphore_signal(barrier, inc=1, device_id=peer, device_id_type=MESH_ID)
    pl.semaphore_wait(barrier, len(peers))


def square(row):
    along_x = (row // 2) * 2 + (1 - lax.rem(row, 2))
    along_y = lax.rem(row + 2, 4)
    across = (along_y // 2) * 2 + (1 - lax.rem(along_y, 2))
    return along_x, along_y, across


class Gather:
    def __init__(self, size, source, land, send, receive, own):
        self.size, self.source, self.land = size, source, land
        self.send, self.receive, self.own = send, receive, own
        self.row, self.col = lax.axis_index("row"), lax.axis_index("col")
        self.piece = source.shape[0]

    @staticmethod
    def semaphores(size):
        return 3 * AG_CUTS if size == 4 else size - 1

    def at(self, cut):
        height = self.piece // AG_CUTS
        return pl.ds(cut * height, height)

    def start(self):
        row, col = self.row, self.col
        if self.size != 4:
            peers = [lax.rem(row + d, self.size) for d in range(1, self.size)]
            greet([(peer, col) for peer in peers])
            self.order = [lax.rem(row + self.size - d, self.size) for d in range(1, self.size)]
            self.copies = [
                remote(self.source, self.land.at[row], self.send.at[i], self.receive.at[i], (peer, col))
                for i, peer in enumerate(peers)
            ]
            for copy in self.copies:
                copy.start()
        else:
            rx, ry, rd = square(row)
            self.order = [rx, ry, rd]
            self.px, self.py = (rx, col), (ry, col)
            greet([self.px, self.py])
            self.to_x, self.to_y, self.onward = {}, {}, []
            for step in range(AG_CUTS):
                for table, peer, base, cut in (
                    (self.to_x, self.px, 0, step),
                    (self.to_y, self.py, AG_CUTS, (step + AG_CUTS // 2) % AG_CUTS),
                ):
                    table[cut] = remote(
                        self.source.at[self.at(cut)], self.land.at[row, self.at(cut)],
                        self.send.at[base + cut], self.receive.at[base + cut], peer,
                    )
                    table[cut].start()
        self.keep = pltpu.make_async_copy(self.source, self.land.at[row], self.own)
        self.keep.start()
        self.keep.wait()

    def forward(self):
        if self.size != 4:
            return
        rx, ry, _ = self.order
        for step in range(AG_CUTS // 2):
            for table, peer, owner, cut in (
                (self.to_x, self.py, rx, step),
                (self.to_y, self.px, ry, step + AG_CUTS // 2),
            ):
                table[cut].wait_recv()
                place = self.land.at[owner, self.at(cut)]
                copy = remote(
                    place, place, self.send.at[2 * AG_CUTS + cut], self.receive.at[2 * AG_CUTS + cut], peer
                )
                copy.start()
                self.onward.append(copy)

    def wait(self, step):
        if self.size != 4:
            self.copies[step].wait_recv()
        elif step == 0:
            for cut in range(AG_CUTS // 2, AG_CUTS):
                self.to_x[cut].wait_recv()
        elif step == 1:
            for cut in range(AG_CUTS // 2):
                self.to_y[cut].wait_recv()
        else:
            for copy in self.onward:
                copy.wait_recv()
        return self.order[step]

    def finish(self):
        if self.size != 4:
            for copy in self.copies:
                copy.wait_send()
            return
        for copy in [*self.to_x.values(), *self.to_y.values(), *self.onward]:
            copy.wait_send()


class Scatter:
    def __init__(self, size, stage, land, total, send, receive):
        self.size, self.stage, self.land, self.total = size, stage, land, total
        self.send, self.receive = send, receive
        self.row, self.col = lax.axis_index("row"), lax.axis_index("col")

    @staticmethod
    def semaphores(size):
        return 6 if size == 4 else size - 1

    @staticmethod
    def stage_shape(size, piece):
        return (3 if size == 4 else size - 1, 2, piece, HALF)

    @staticmethod
    def land_shape(size, piece):
        return (6, piece, HALF) if size == 4 else (size - 1, 2, piece, HALF)

    def copy(self, index, source, peer):
        return remote(source, self.land.at[index], self.send.at[index], self.receive.at[index], peer)

    def run(self, partial, between=None, late=None):
        row, col = self.row, self.col

        def into(slot):
            def store(half, columns, value):
                self.stage[slot, half, :, columns] = value.astype(jnp.bfloat16)

            return store

        def into_total(half, columns, value):
            self.total[half, :, columns] = value

        if self.size != 4:
            peers = [lax.rem(row + d, self.size) for d in range(1, self.size)]
            greet([(peer, col) for peer in peers])
            copies = []
            for slot, peer in enumerate(peers):
                partial(peer, into(slot))
                copies.append(self.copy(slot, self.stage.at[slot], (peer, col)))
                copies[-1].start()
            partial(row, into_total)
            if between is not None:
                between()
            if late is not None:
                late()
            for slot, copy in enumerate(copies):
                copy.wait_recv()
                self.add_total(0, self.land.at[slot, 0])
                self.add_total(1, self.land.at[slot, 1])
            for copy in copies:
                copy.wait_send()
            return
        rx, ry, rd = square(row)
        px, py = (rx, col), (ry, col)
        greet([px, py])
        partial(rd, into(0))
        first = [self.copy(0, self.stage.at[0, 0], px), self.copy(1, self.stage.at[0, 1], py)]
        for copy in first:
            copy.start()
        partial(rx, into(1))
        first.append(self.copy(2, self.stage.at[1, 0], px))
        first[2].start()
        partial(ry, into(2))
        first.append(self.copy(3, self.stage.at[2, 1], py))
        first[3].start()
        if between is not None:
            between()
        first[0].wait_recv()
        self.add_stage(2, 0, self.land.at[0])
        second = [self.copy(4, self.stage.at[2, 0], py)]
        second[0].start()
        first[1].wait_recv()
        self.add_stage(1, 1, self.land.at[1])
        second.append(self.copy(5, self.stage.at[1, 1], px))
        second[1].start()
        partial(row, into_total)
        if late is not None:
            late()
        first[2].wait_recv()
        self.add_total(0, self.land.at[2])
        first[3].wait_recv()
        self.add_total(1, self.land.at[3])
        second[0].wait_recv()
        self.add_total(0, self.land.at[4])
        second[1].wait_recv()
        self.add_total(1, self.land.at[5])
        for copy in first + second:
            copy.wait_send()

    def add_stage(self, slot, half, landed):
        @pl.loop(0, landed.shape[0] // STRIP)
        def _(i):
            rows = pl.ds(pl.multiple_of(i * STRIP, STRIP), STRIP)
            value = self.stage[slot, half, rows, :].astype(jnp.float32) + landed[rows, :].astype(jnp.float32)
            self.stage[slot, half, rows, :] = value.astype(jnp.bfloat16)

    def add_total(self, half, landed):
        @pl.loop(0, landed.shape[0] // STRIP)
        def _(i):
            rows = pl.ds(pl.multiple_of(i * STRIP, STRIP), STRIP)
            self.total[half, rows, :] += landed[rows, :].astype(jnp.float32)


STRIP = 32


def scatter_scratch(size, piece):
    count = Scatter.semaphores(size)
    return [
        pltpu.VMEM(Scatter.stage_shape(size, piece), jnp.bfloat16),
        pltpu.VMEM(Scatter.land_shape(size, piece), jnp.bfloat16),
        pltpu.VMEM((2, piece, HALF), jnp.float32),
        pltpu.SemaphoreType.DMA((count,)),
        pltpu.SemaphoreType.DMA((count,)),
    ]


def gather_scratch(size, piece):
    count = Gather.semaphores(size)
    return [
        pltpu.VMEM((size, piece, D), jnp.bfloat16),
        pltpu.SemaphoreType.DMA((count,)),
        pltpu.SemaphoreType.DMA((count,)),
        pltpu.SemaphoreType.DMA,
    ]


def fetches(pairs, semaphores):
    copies = [pltpu.make_async_copy(a, b, semaphores.at[i]) for i, (a, b) in enumerate(pairs)]
    for copy in copies:
        copy.start()
    return copies


def wait_all(copies):
    for copy in copies:
        copy.wait()


def tiles_of(width, tile):
    def run(body):
        @pl.loop(0, width // tile)
        def _(t):
            body(t, pl.ds(pl.multiple_of(t * tile, tile), tile))

    return run


def comm_params(identity):
    return pltpu.CompilerParams(
        collective_id=identity, has_side_effects=True, vmem_limit_bytes=BIG_VMEM
    )


def bf(*shape):
    return jax.ShapeDtypeStruct(shape, jnp.bfloat16)


def fl(*shape):
    return jax.ShapeDtypeStruct(shape, jnp.float32)


def project_heads(size, normed, w_all):
    piece = normed.shape[0]
    cols, _, depth, width = w_all.shape
    heads = width // HD

    def kernel(x_ref, w_ref, heads_ref, all_ref, land, send, receive, own, w, w_sem, all_sem):
        loads = fetches([(w_ref.at[c], w.at[:, pl.ds(c * depth, depth), :]) for c in range(cols)], w_sem)
        gather = Gather(size, x_ref, land, send, receive, own)
        gather.start()

        def compute(row, slot):
            store = pltpu.make_async_copy(land.at[row], all_ref.at[row], all_sem.at[slot])
            store.start()
            rows = pl.ds(pl.multiple_of(row * piece, piece), piece)

            @pl.loop(0, 3)
            def _(j):
                value = jnp.dot(land[row], w[j], preferred_element_type=jnp.float32).astype(jnp.bfloat16)
                for head in range(heads):
                    heads_ref[j, head, rows, :] = value[:, head * HD : (head + 1) * HD]

            return store

        wait_all(loads)
        stores = [compute(gather.row, 0)]
        gather.forward()
        for step in range(size - 1):
            stores.append(compute(gather.wait(step), step + 1))
        wait_all(stores)
        gather.finish()

    return pl.pallas_call(
        kernel,
        out_shape=[bf(3, heads, GLEN, HD), bf(size, piece, D)],
        in_specs=[ANY, ANY],
        out_specs=[VMEM, ANY],
        scratch_shapes=gather_scratch(size, piece)
        + [
            pltpu.VMEM((3, D, width), jnp.bfloat16),
            pltpu.SemaphoreType.DMA((cols,)),
            pltpu.SemaphoreType.DMA((size,)),
        ],
        compiler_params=comm_params(1),
        cost_estimate=pl.CostEstimate(flops=6 * GLEN * D * width, bytes_accessed=40_000_000, transcendentals=0),
        name="project_heads",
    )(normed, w_all)


def strip_loop(piece, body):
    @pl.loop(0, piece // STRIP)
    def _(i):
        body(pl.ds(pl.multiple_of(i * STRIP, STRIP), STRIP))


def row_mean(first, second):
    return (jnp.sum(first, axis=1, keepdims=True) + jnp.sum(second, axis=1, keepdims=True)) / D


def lanes(first, second):
    lane = lax.broadcasted_iota(jnp.int32, (STRIP, HD), 1)
    return jnp.where(lane == 0, first, jnp.where(lane == 1, second, 0.0))


LEFT, RIGHT = slice(0, HALF), slice(HALF, D)


def branch_out(size, attn, w_all, x, gain):
    piece = GLEN // size
    cols, width, depth = w_all.shape

    def kernel(attn_ref, w_ref, x_ref, gain_ref, middle_ref, normed_ref, stat_ref, stage, land, total, send, receive, w, w_sem):
        loads = fetches([(w_ref.at[c], w.at[:, pl.ds(c * depth, depth)]) for c in range(cols)], w_sem)
        scatter = Scatter(size, stage, land, total, send, receive)
        wait_all(loads)

        def partial(row, store):
            rows = pl.ds(pl.multiple_of(row * piece, piece), piece)
            left = attn_ref[rows, :]
            for half in range(2):
                for t in range(2):
                    columns = slice(half * HALF + t * HALF // 2, half * HALF + (t + 1) * HALF // 2)
                    store(
                        half, slice(t * HALF // 2, (t + 1) * HALF // 2),
                        jnp.dot(left, w[:, columns], preferred_element_type=jnp.float32),
                    )

        scatter.run(partial)

        def finish(rows):
            branch = (total[0, rows, :], total[1, rows, :])
            middle = (
                x_ref[rows, LEFT].astype(jnp.float32) + branch[0],
                x_ref[rows, RIGHT].astype(jnp.float32) + branch[1],
            )
            mean = row_mean(middle[0] * middle[0], middle[1] * middle[1])
            inverse = lax.rsqrt(mean + EPSILON)
            for part, columns in zip(middle, (LEFT, RIGHT)):
                middle_ref[rows, columns] = part
                normed_ref[rows, columns] = (part * inverse * gain_ref[:, columns]).astype(jnp.bfloat16)
            stat_ref[rows, :] = lanes(row_mean(branch[0] * branch[0], branch[1] * branch[1]), mean)

        strip_loop(piece, finish)

    return pl.pallas_call(
        kernel,
        out_shape=[fl(piece, D), bf(piece, D), fl(piece, HD)],
        in_specs=[VMEM, ANY, VMEM, VMEM],
        out_specs=[VMEM, VMEM, VMEM],
        scratch_shapes=scatter_scratch(size, piece)
        + [pltpu.VMEM((width, D), jnp.bfloat16), pltpu.SemaphoreType.DMA((cols,))],
        compiler_params=comm_params(2),
        cost_estimate=pl.CostEstimate(flops=2 * GLEN * D * width, bytes_accessed=40_000_000, transcendentals=0),
        name="branch_out",
    )(attn, w_all, x, gain)


def feed_forward(size, normed, w_gu, w_down, cot):
    piece = normed.shape[0]
    cols, _, depth, wide = w_gu.shape
    tile = min(wide, 512)

    def kernel(
        x_ref, gu_ref, down_ref, cot_ref, hidden_ref, grad_ref, all_ref,
        land, send, receive, own, gu, down, cot_all, back, stage, gu_sem, down_sem, cot_sem, out_sem, all_sem,
    ):
        down_loads = fetches(
            [(down_ref.at[c], down.at[:, pl.ds(c * depth, depth)]) for c in range(cols)], down_sem
        )
        cot_load = pltpu.make_async_copy(cot_ref, cot_all, cot_sem)
        cot_load.start()
        gu_loads = fetches([(gu_ref.at[c], gu.at[:, pl.ds(c * depth, depth), :]) for c in range(cols)], gu_sem)
        gather = Gather(size, x_ref, land, send, receive, own)
        gather.start()
        wait_all(down_loads)
        cot_load.wait()

        def backward(row):
            @tiles_of(wide, tile)
            def _(t, columns):
                back[row, :, columns] = plain_dot(cot_all[row], down[columns, :], NT).astype(jnp.bfloat16)

        def moves(row, slot, columns):
            rows = pl.ds(pl.multiple_of(row * piece, piece), piece)
            return [
                pltpu.make_async_copy(stage.at[slot, 0], hidden_ref.at[rows, columns], out_sem.at[slot, 0]),
                pltpu.make_async_copy(stage.at[slot, 1], grad_ref.at[0, rows, columns], out_sem.at[slot, 1]),
                pltpu.make_async_copy(stage.at[slot, 2], grad_ref.at[1, rows, columns], out_sem.at[slot, 2]),
            ]

        count = wide // tile

        def compute(row, first):
            pltpu.make_async_copy(land.at[row], all_ref.at[row], all_sem).start()

            @pl.loop(0, count)
            def _(t):
                columns = pl.ds(pl.multiple_of(t * tile, tile), tile)
                slot = lax.rem(t, 2)
                x = land[row]
                gate_pre = jnp.dot(x, gu[0, :, columns], preferred_element_type=jnp.float32)
                up_pre = jnp.dot(x, gu[1, :, columns], preferred_element_type=jnp.float32)
                sigmoid = jax.nn.sigmoid(gate_pre)
                silu = gate_pre * sigmoid
                grad_hidden = back[row, :, columns].astype(jnp.float32)

                @pl.when(t >= 2)
                def _():
                    wait_all(moves(row, slot, columns))

                stage[slot, 0] = (silu * up_pre).astype(jnp.bfloat16)
                stage[slot, 1] = (grad_hidden * up_pre * (sigmoid + silu * (1.0 - sigmoid))).astype(jnp.bfloat16)
                stage[slot, 2] = (grad_hidden * silu).astype(jnp.bfloat16)
                for move in moves(row, slot, columns):
                    move.start()

            for slot in range(min(2, count)):
                wait_all(moves(row, slot, pl.ds(slot * tile, tile)))
            pltpu.make_async_copy(land.at[row], all_ref.at[row], all_sem).wait()

        backward(gather.row)
        gather.forward()
        for step in range(size - 1):
            backward(gather.order[step])
        wait_all(gu_loads)
        compute(gather.row, True)
        for step in range(size - 1):
            compute(gather.wait(step), False)
        gather.finish()

    return pl.pallas_call(
        kernel,
        out_shape=[bf(GLEN, wide), bf(2, GLEN, wide), bf(size, piece, D)],
        in_specs=[ANY, ANY, ANY, ANY],
        out_specs=[ANY, ANY, ANY],
        scratch_shapes=gather_scratch(size, piece)
        + [
            pltpu.VMEM((2, D, wide), jnp.bfloat16),
            pltpu.VMEM((wide, D), jnp.bfloat16),
            pltpu.VMEM((size, piece, D), jnp.bfloat16),
            pltpu.VMEM((size, piece, wide), jnp.bfloat16),
            pltpu.VMEM((2, 3, piece, tile), jnp.bfloat16),
            pltpu.SemaphoreType.DMA((cols,)),
            pltpu.SemaphoreType.DMA((cols,)),
            pltpu.SemaphoreType.DMA,
            pltpu.SemaphoreType.DMA((2, 3)),
            pltpu.SemaphoreType.DMA,
        ],
        compiler_params=comm_params(3),
        cost_estimate=pl.CostEstimate(flops=6 * GLEN * D * wide, bytes_accessed=70_000_000, transcendentals=GLEN * wide),
        name="feed_forward",
    )(normed, w_gu, w_down, cot.reshape(size, piece, D))


def norm_back(rows, total, stream, inverse, gain_ref, base, store, gain_sum):
    u = [total[half, rows, :] * gain_ref[:, columns] for half, columns in enumerate((LEFT, RIGHT))]
    inner = row_mean(u[0] * stream[0], u[1] * stream[1]) * inverse * inverse * inverse
    for half, columns in enumerate((LEFT, RIGHT)):
        store(columns, base[half] + inverse * u[half] - stream[half] * inner)
        gain_sum[:, columns] += jnp.sum(total[half, rows, :] * stream[half] * inverse, axis=0, keepdims=True)


def middle_back(size, grads, w_gu, middle, cot, gain):
    piece = middle.shape[0]
    cols, _, depth, wide = w_gu.shape
    tile = 512

    def kernel(
        g_ref, gu_ref, middle_ref, cot_ref, gain_ref, grad_ref, low_ref, gain_sum,
        stage, land, total, send, receive, gu, g, gu_sem, g_sem,
    ):
        loads = fetches([(gu_ref.at[c], gu.at[:, pl.ds(c * depth, depth), :]) for c in range(cols)], gu_sem)
        scatter = Scatter(size, stage, land, total, send, receive)
        g_loads = fetches([(g_ref.at[j], g.at[j]) for j in range(2)], g_sem)
        wait_all(g_loads)
        wait_all(loads)
        gain_sum[...] = jnp.zeros_like(gain_sum)

        def partial(row, store):
            rows = pl.ds(pl.multiple_of(row * piece, piece), piece)
            for half in range(2):
                @pl.loop(0, HALF // tile)
                def _(t):
                    columns = pl.ds(pl.multiple_of(t * tile, tile), tile)
                    depth_rows = pl.ds(pl.multiple_of(half * HALF + t * tile, tile), tile)
                    value = plain_dot(g[0, rows, :], gu[0, depth_rows, :], NT)
                    value += plain_dot(g[1, rows, :], gu[1, depth_rows, :], NT)
                    store(half, columns, value)

        scatter.run(partial)

        def finish(rows):
            stream = [middle_ref[rows, columns] for columns in (LEFT, RIGHT)]
            base = [cot_ref[rows, columns].astype(jnp.float32) for columns in (LEFT, RIGHT)]
            inverse = lax.rsqrt(row_mean(stream[0] * stream[0], stream[1] * stream[1]) + EPSILON)

            def store(columns, value):
                grad_ref[rows, columns] = value
                low_ref[rows, columns] = value.astype(jnp.bfloat16)

            norm_back(rows, total, stream, inverse, gain_ref, base, store, gain_sum)

        strip_loop(piece, finish)

    return pl.pallas_call(
        kernel,
        out_shape=[fl(piece, D), bf(piece, D), fl(1, D)],
        in_specs=[ANY, ANY, VMEM, VMEM, VMEM],
        out_specs=[VMEM, VMEM, VMEM],
        scratch_shapes=scatter_scratch(size, piece)
        + [
            pltpu.VMEM((2, D, wide), jnp.bfloat16),
            pltpu.VMEM((2, GLEN, wide), jnp.bfloat16),
            pltpu.SemaphoreType.DMA((cols,)),
            pltpu.SemaphoreType.DMA((2,)),
        ],
        compiler_params=comm_params(4),
        cost_estimate=pl.CostEstimate(flops=4 * GLEN * D * wide, bytes_accessed=60_000_000, transcendentals=0),
        name="middle_back",
    )(grads, w_gu, middle, cot, gain)


def blocked_store(ref, rows, depth, columns, value):
    for i in range(value.shape[1] // depth):
        ref[columns.start // depth + i, rows, :] = value[:, i * depth : (i + 1) * depth]


def ffn_out(size, hidden, w_down, middle):
    piece = middle.shape[0]
    cols, wide, depth = w_down.shape
    tile = 512

    def kernel(h_ref, w_ref, middle_ref, out_ref, stat_ref, stage, land, total, send, receive, w, w_sem):
        loads = fetches([(w_ref.at[c], w.at[:, pl.ds(c * depth, depth)]) for c in range(cols)], w_sem)
        scatter = Scatter(size, stage, land, total, send, receive)
        wait_all(loads)

        def partial(row, store):
            rows = pl.ds(pl.multiple_of(row * piece, piece), piece)
            for half in range(2):
                @pl.loop(0, HALF // tile)
                def _(t):
                    columns = pl.ds(pl.multiple_of(t * tile, tile), tile)
                    whole = pl.ds(pl.multiple_of(half * HALF + t * tile, tile), tile)
                    store(half, columns, jnp.dot(h_ref[rows, :], w[:, whole], preferred_element_type=jnp.float32))

        scatter.run(partial)

        def finish(rows):
            ffn = [total[half, rows, :] for half in range(2)]
            result = [middle_ref[rows, columns] + ffn[half] for half, columns in enumerate((LEFT, RIGHT))]
            for half, columns in enumerate((LEFT, RIGHT)):
                blocked_store(out_ref, rows, depth, columns, result[half].astype(jnp.bfloat16))
            stat_ref[rows, :] = lanes(
                row_mean(ffn[0] * ffn[0], ffn[1] * ffn[1]),
                row_mean(result[0] * result[0], result[1] * result[1]),
            )

        strip_loop(piece, finish)

    return pl.pallas_call(
        kernel,
        out_shape=[bf(cols, piece, depth), fl(piece, HD)],
        in_specs=[VMEM, ANY, VMEM],
        out_specs=[VMEM, VMEM],
        scratch_shapes=scatter_scratch(size, piece)
        + [pltpu.VMEM((wide, D), jnp.bfloat16), pltpu.SemaphoreType.DMA((cols,))],
        compiler_params=comm_params(5),
        cost_estimate=pl.CostEstimate(flops=2 * GLEN * D * wide, bytes_accessed=50_000_000, transcendentals=0),
        name="ffn_out",
    )(hidden, w_down, middle)


def branch_back(size, low, w_all):
    piece = low.shape[0]
    cols, width, depth = w_all.shape
    heads = width // HD

    def kernel(x_ref, w_ref, heads_ref, all_ref, land, send, receive, own, w, w_sem, all_sem):
        loads = fetches([(w_ref.at[c], w.at[:, pl.ds(c * depth, depth)]) for c in range(cols)], w_sem)
        gather = Gather(size, x_ref, land, send, receive, own)
        gather.start()

        def compute(row, slot):
            store = pltpu.make_async_copy(land.at[row], all_ref.at[row], all_sem.at[slot])
            store.start()
            rows = pl.ds(pl.multiple_of(row * piece, piece), piece)
            value = plain_dot(land[row], w[...], NT).astype(jnp.bfloat16)
            for head in range(heads):
                heads_ref[head, rows, :] = value[:, head * HD : (head + 1) * HD]
            return store

        wait_all(loads)
        stores = [compute(gather.row, 0)]
        gather.forward()
        for step in range(size - 1):
            stores.append(compute(gather.wait(step), step + 1))
        wait_all(stores)
        gather.finish()

    return pl.pallas_call(
        kernel,
        out_shape=[bf(heads, GLEN, HD), bf(size, piece, D)],
        in_specs=[ANY, ANY],
        out_specs=[VMEM, ANY],
        scratch_shapes=gather_scratch(size, piece)
        + [
            pltpu.VMEM((width, D), jnp.bfloat16),
            pltpu.SemaphoreType.DMA((cols,)),
            pltpu.SemaphoreType.DMA((size,)),
        ],
        compiler_params=comm_params(6),
        cost_estimate=pl.CostEstimate(flops=2 * GLEN * D * width, bytes_accessed=40_000_000, transcendentals=0),
        name="branch_back",
    )(low, w_all)


def stream_back(size, grads, w_all, x, grad_middle, gain):
    piece = x.shape[0]
    cols, _, depth, width = w_all.shape
    tile = 512

    def kernel(
        g_ref, w_ref, x_ref, middle_ref, gain_ref, out_ref, gain_sum,
        stage, land, total, send, receive, w, w_sem,
    ):
        loads = fetches([(w_ref.at[c], w.at[:, pl.ds(c * depth, depth), :]) for c in range(cols)], w_sem)
        scatter = Scatter(size, stage, land, total, send, receive)
        wait_all(loads)
        gain_sum[...] = jnp.zeros_like(gain_sum)

        def partial(row, store):
            rows = pl.ds(pl.multiple_of(row * piece, piece), piece)
            for half in range(2):
                @pl.loop(0, HALF // tile)
                def _(t):
                    columns = pl.ds(pl.multiple_of(t * tile, tile), tile)
                    depth_rows = pl.ds(pl.multiple_of(half * HALF + t * tile, tile), tile)
                    value = plain_dot(g_ref[0, rows, :], w[0, depth_rows, :], NT)
                    for j in (1, 2):
                        value += plain_dot(g_ref[j, rows, :], w[j, depth_rows, :], NT)
                    store(half, columns, value)

        scatter.run(partial)

        def finish(rows):
            stream = [x_ref[rows, columns].astype(jnp.float32) for columns in (LEFT, RIGHT)]
            base = [middle_ref[rows, columns] for columns in (LEFT, RIGHT)]
            inverse = lax.rsqrt(row_mean(stream[0] * stream[0], stream[1] * stream[1]) + EPSILON)

            def store(columns, value):
                blocked_store(out_ref, rows, depth, columns, value.astype(jnp.bfloat16))

            norm_back(rows, total, stream, inverse, gain_ref, base, store, gain_sum)

        strip_loop(piece, finish)

    return pl.pallas_call(
        kernel,
        out_shape=[bf(cols, piece, depth), fl(1, D)],
        in_specs=[VMEM, ANY, VMEM, VMEM, VMEM],
        out_specs=[VMEM, VMEM],
        scratch_shapes=scatter_scratch(size, piece)
        + [pltpu.VMEM((3, D, width), jnp.bfloat16), pltpu.SemaphoreType.DMA((cols,))],
        compiler_params=comm_params(7),
        cost_estimate=pl.CostEstimate(flops=6 * GLEN * D * width, bytes_accessed=50_000_000, transcendentals=0),
        name="stream_back",
    )(grads, w_all, x, grad_middle, gain)


def unblock_kernel(x_ref, gain_ref, tokens_ref, normed_ref):
    cols, rows, depth = x_ref.shape
    total = jnp.zeros((rows, 1), jnp.float32)
    for c in range(cols):
        part = x_ref[c].astype(jnp.float32)
        tokens_ref[:, c * depth : (c + 1) * depth] = x_ref[c]
        total += jnp.sum(part * part, axis=1, keepdims=True)
    inverse = lax.rsqrt(total / D + EPSILON)
    for c in range(cols):
        columns = slice(c * depth, (c + 1) * depth)
        normed_ref[:, columns] = (
            x_ref[c].astype(jnp.float32) * inverse * gain_ref[:, columns]
        ).astype(jnp.bfloat16)


def enter(blocks, gain):
    cols, piece, depth = blocks.shape
    rows = piece // 4
    return pl.pallas_call(
        unblock_kernel,
        grid=(4,),
        in_specs=[
            pl.BlockSpec((cols, rows, depth), lambda i: (0, i, 0)),
            pl.BlockSpec((1, D), lambda i: (0, 0)),
        ],
        out_specs=[pl.BlockSpec((rows, D), lambda i: (i, 0))] * 2,
        out_shape=[bf(piece, D), bf(piece, D)],
        cost_estimate=pl.CostEstimate(flops=6 * piece * D, bytes_accessed=6 * piece * D, transcendentals=0),
        name="enter",
    )(blocks, gain)


def to_blocks(block):
    row_size = lax.axis_size("row")
    features = block.shape[1]
    groups = block.shape[0] // GLEN
    piece = GLEN // row_size
    split = block.reshape(groups, row_size, piece, features)
    split = lax.all_to_all(split, "row", split_axis=1, concat_axis=0, tiled=True)
    split = split.reshape(row_size * groups, piece, features)
    return lax.all_to_all(split, "col", split_axis=0, concat_axis=0, tiled=True)


def from_blocks(blocks):
    row_size = lax.axis_size("row")
    cols, piece, features = blocks.shape
    groups = cols // row_size
    split = lax.all_to_all(blocks, "col", split_axis=0, concat_axis=0, tiled=True)
    split = split.reshape(row_size, groups, piece, features)
    split = lax.all_to_all(split, "row", split_axis=0, concat_axis=2, tiled=True)
    return split.reshape(groups * GLEN, features)


def tokens_contract(left, right):
    return lax.dot_general(left, right, (TN, ((), ())), preferred_element_type=jnp.float32)


def over_col(partial, axis):
    return lax.psum_scatter(
        partial.astype(jnp.bfloat16), "col", scatter_dimension=axis, tiled=True
    ).astype(jnp.float32)


def local(
    stream_in,
    w_qkv,
    w_out,
    w_gate_up,
    w_down,
    gain_attn,
    gain_ffn,
    gate_logit,
    memory,
    memory_norm,
    offsets,
    lengths,
    cotangent,
):
    head_here = memory.shape[1]
    size = lax.axis_size("row")
    row_index = lax.axis_index("row")
    col_index = lax.axis_index("col")
    gains = lax.all_gather(jnp.stack([gain_attn, gain_ffn]), "col", axis=1, tiled=True)
    gain_in, gain_mid = gains[0:1], gains[1:2]
    all_qkv, all_out, all_gu, all_down = (
        lax.all_gather(w, "col", axis=0, tiled=False) for w in (w_qkv, w_out, w_gate_up, w_down)
    )
    gate_value = jax.nn.sigmoid(gate_logit)
    group = (memory[0], memory_norm[0], offsets[0], lengths[0], gate_value)
    stream, normed_in = enter(to_blocks(stream_in), gain_in)
    cot, _ = enter(to_blocks(cotangent), gain_in)
    all_cot = lax.all_gather(cot, "row", axis=0, tiled=True)
    heads_all, all_in = project_heads(size, normed_in, all_qkv)
    attn, dot_part, memory_part, logsum, memory_new, norm_new = attend(heads_all, *group)
    middle, normed_ffn, stat_branch = branch_out(size, attn, all_out, stream, gain_mid)
    hidden, grad_gu, all_ffn = feed_forward(size, normed_ffn, all_gu, all_down, all_cot)
    grad_middle, low_branch, part_gain_ffn = middle_back(size, grad_gu, all_gu, middle, cot, gain_mid)
    blocks_out, stat_ffn = ffn_out(size, hidden, all_down, middle)
    grad_heads, all_branch = branch_back(size, low_branch, all_out)
    grads_qkv, gate_sums = attend_back(
        heads_all, grad_heads, dot_part, memory_part, logsum, *group
    )
    blocks_grad, part_gain_attn = stream_back(size, grads_qkv, all_qkv, stream, grad_middle, gain_in)
    stream_out = from_blocks(blocks_out)
    stream_grad = from_blocks(blocks_grad).astype(jnp.float32)

    def flat(pieces):
        return pieces.reshape(GLEN, D)

    grad_down = over_col(tokens_contract(hidden, all_cot), 1)
    grad_gate_up = over_col(
        jnp.einsum("td,jto->jdo", flat(all_ffn), grad_gu, preferred_element_type=jnp.float32), 1
    )
    grad_out = over_col(tokens_contract(attn, flat(all_branch)), 1)
    grad_qkv = over_col(
        jnp.einsum("td,jto->jdo", flat(all_in), grads_qkv, preferred_element_type=jnp.float32), 1
    )
    logit_part = gate_value * (1.0 - gate_value) * jnp.sum(gate_sums, axis=(1, 2))
    logit_slots = lax.dynamic_update_slice(
        jnp.zeros((size * head_here,), jnp.float32), logit_part, (row_index * head_here,)
    )
    small = lax.psum(
        jnp.concatenate([part_gain_attn[0], part_gain_ffn[0], logit_slots]), ("row", "col")
    )
    features_here = gain_attn.shape[0]
    grad_gain_attn = lax.dynamic_slice(small, (col_index * features_here,), (features_here,))
    grad_gain_ffn = lax.dynamic_slice(small, (D + col_index * features_here,), (features_here,))
    grad_gate_logit = lax.dynamic_slice(small, (2 * D + row_index * head_here,), (head_here,))
    rms_here = jnp.sqrt(jnp.concatenate([stat_branch[:, :2], stat_ffn[:, :2]], axis=1).T)
    rms_all = lax.all_gather(rms_here, ("col", "row"), axis=1, tiled=True)
    rows_here = stream_in.shape[0]
    rms_table = lax.dynamic_slice(rms_all, (0, row_index * rows_here), (4, rows_here))
    return (
        stream_out,
        stream_grad,
        grad_qkv,
        grad_out,
        grad_gate_up,
        grad_down,
        grad_gain_attn,
        grad_gain_ffn,
        grad_gate_logit,
        memory_new[None],
        norm_new.reshape(1, head_here, HD),
        rms_table,
    )


def solution(mesh):
    return jax.shard_map(
        local,
        mesh=mesh,
        in_specs=(
            P("row", "col"),
            P(None, "col", "row"),
            P("row", "col"),
            P(None, "col", "row"),
            P("row", "col"),
            P("col"),
            P("col"),
            P("row"),
            P("col", "row", None, None),
            P("col", "row", None),
            P("col", None),
            P("col", None),
            P("row", "col"),
        ),
        out_specs=(
            P("row", "col"),
            P("row", "col"),
            P(None, "col", "row"),
            P("row", "col"),
            P(None, "col", "row"),
            P("row", "col"),
            P("col"),
            P("col"),
            P("row"),
            P("col", "row", None, None),
            P("col", "row", None),
            P(None, "row"),
        ),
        check_vma=False,
    )
```

```python
import jax
import jax.numpy as jnp
from jax import lax
from jax.experimental import pallas as pl
from jax.experimental.pallas import tpu as pltpu
from jax.sharding import PartitionSpec as P

D = 2048
HD = 128
PROMPT = 1024
CONT = 4
CLEN = 128
GLEN = 1536


EPSILON = 1e-06
MASKED_LOGIT = -1e30
BIG_VMEM = 60 * 1024 * 1024


def feature_map(values):
    return jnp.where(values > 0, values + 1.0, jnp.exp(jnp.minimum(values, 0.0)))


def feature_slope(values):
    return jnp.where(values > 0, 1.0, jnp.exp(jnp.minimum(values, 0.0)))


def split_two(value):
    high = value.astype(jnp.bfloat16)
    return high, (value - high.astype(jnp.float32)).astype(jnp.bfloat16)


def wide_dot(left, right, dims):
    left_high, left_low = split_two(left)
    right_high, right_low = split_two(right)

    def one(a, b):
        return lax.dot_general(a, b, (dims, ((), ())), preferred_element_type=jnp.float32)

    return one(left_high, right_high) + one(left_high, right_low) + one(left_low, right_high)


def narrow_dot(left, right, dims):
    right_high, right_low = split_two(right)

    def one(b):
        return lax.dot_general(left, b, (dims, ((), ())), preferred_element_type=jnp.float32)

    return one(right_high) + one(right_low)


def plain_dot(left, right, dims):
    return lax.dot_general(left, right, (dims, ((), ())), preferred_element_type=jnp.float32)


NN = ((1,), (0,))
NT = ((1,), (1,))
TN = ((0,), (0,))
QT = 256
PROMPT_TILES = PROMPT // QT
TILES = GLEN // QT


def tile_scores(tile, q, k_ref, offsets_ref, lengths_ref):
    scale = HD ** (-0.5)
    row = lax.broadcasted_iota(jnp.int32, (QT, QT), 0)
    column = lax.broadcasted_iota(jnp.int32, (QT, QT), 1)
    seen = min(tile * QT, PROMPT)
    own = plain_dot(q, k_ref[tile * QT : (tile + 1) * QT], NT) * scale
    if tile < PROMPT_TILES:
        own = jnp.where(row >= column, own, MASKED_LOGIT)
        ahead = plain_dot(q, k_ref[:seen], NT) * scale if seen else None
        return ahead, own, seen
    first = (tile - PROMPT_TILES) * (QT // CLEN)
    upper = lax.broadcasted_iota(jnp.int32, (QT, 1), 0) >= CLEN
    limit = jnp.where(upper, offsets_ref[first + 1], offsets_ref[first])
    live = jnp.where(upper, lengths_ref[first + 1] + CLEN, lengths_ref[first])
    same = (row >= CLEN) == (column >= CLEN)
    own = jnp.where((row >= column) & same & (column < live), own, MASKED_LOGIT)
    ahead = plain_dot(q, k_ref[:seen], NT) * scale
    position = lax.broadcasted_iota(jnp.int32, (QT, PROMPT), 1)
    return jnp.where(position < limit, ahead, MASKED_LOGIT), own, seen


def attend_kernel(
    offsets_ref, lengths_ref, gate_ref, qkv_ref, memory_ref, norm_ref,
    attn_ref, dot_ref, part_ref, logsum_ref, memory_new_ref, norm_new_ref,
):
    head = pl.program_id(0)
    gate = gate_ref[head]
    q_ref, k_ref, v_ref = qkv_ref.at[0, 0], qkv_ref.at[1, 0], qkv_ref.at[2, 0]
    memory_one = memory_ref[0]
    norm_one = norm_ref[0]
    for tile in range(TILES):
        rows = slice(tile * QT, (tile + 1) * QT)
        q = q_ref[rows]
        ahead, own, seen = tile_scores(tile, q, k_ref, offsets_ref, lengths_ref)
        peak = jnp.max(own, axis=1, keepdims=True)
        if ahead is not None:
            peak = jnp.maximum(peak, jnp.max(ahead, axis=1, keepdims=True))
        own = jnp.exp(own - peak)
        total = jnp.sum(own, axis=1, keepdims=True)
        dot_part = plain_dot(own.astype(jnp.bfloat16), v_ref[rows], NN)
        if ahead is not None:
            ahead = jnp.exp(ahead - peak)
            total += jnp.sum(ahead, axis=1, keepdims=True)
            dot_part += plain_dot(ahead.astype(jnp.bfloat16), v_ref[:seen], NN)
        dot_part = dot_part / total
        lifted = feature_map(q.astype(jnp.float32))
        memory_part = wide_dot(lifted, memory_one, NN) / jnp.sum(
            lifted * norm_one, axis=1, keepdims=True
        )
        attn_ref[rows, :] = (gate * memory_part + (1.0 - gate) * dot_part).astype(jnp.bfloat16)
        dot_ref[0, rows, :] = dot_part
        part_ref[0, rows, :] = memory_part
        logsum_ref[0, rows, :] = peak + jnp.log(total)
    lifted_keys = feature_map(k_ref[:PROMPT].astype(jnp.float32))
    high, low = split_two(lifted_keys)
    v = v_ref[:PROMPT]
    memory_new_ref[0] = memory_one + (plain_dot(high, v, TN) + plain_dot(low, v, TN)) / PROMPT
    norm_new_ref[0] = norm_one + jnp.mean(lifted_keys, axis=0, keepdims=True)


def head_block(shape, lead=0):
    zeros = (0,) * (len(shape) - 1 - lead)
    return pl.BlockSpec(shape, lambda h: (0,) * lead + (h,) + zeros)


SMEM_SPEC = pl.BlockSpec(memory_space=pltpu.SMEM)


def attend(heads_all, memory_one, norm_one, offsets, lengths, gate_value):
    heads = heads_all.shape[1]
    f32 = jnp.float32
    row_block = head_block((1, GLEN, HD))
    column = pl.BlockSpec((GLEN, HD), lambda h: (0, h))
    return pl.pallas_call(
        attend_kernel,
        grid=(heads,),
        in_specs=[
            SMEM_SPEC, SMEM_SPEC, SMEM_SPEC,
            head_block((3, 1, GLEN, HD), 1), head_block((1, HD, HD)), head_block((1, 1, HD)),
        ],
        out_specs=[
            column, row_block, row_block, head_block((1, GLEN, 1)),
            head_block((1, HD, HD)), head_block((1, 1, HD)),
        ],
        out_shape=[
            jax.ShapeDtypeStruct((GLEN, heads * HD), jnp.bfloat16),
            jax.ShapeDtypeStruct((heads, GLEN, HD), f32),
            jax.ShapeDtypeStruct((heads, GLEN, HD), f32),
            jax.ShapeDtypeStruct((heads, GLEN, 1), f32),
            jax.ShapeDtypeStruct((heads, HD, HD), f32),
            jax.ShapeDtypeStruct((heads, 1, HD), f32),
        ],
        compiler_params=pltpu.CompilerParams(vmem_limit_bytes=BIG_VMEM),
        cost_estimate=pl.CostEstimate(
            flops=heads * 800_000_000, bytes_accessed=heads * 6_000_000, transcendentals=heads * 1_300_000
        ),
        name="attend",
    )(offsets, lengths, gate_value, heads_all, memory_one, norm_one[:, None, :])


def attend_back_kernel(
    offsets_ref, lengths_ref, gate_ref, qkv_ref, grad_ref, dot_ref, part_ref, logsum_ref,
    memory_ref, norm_ref, out_ref, gate_out_ref, key_sum, value_sum,
):
    head = pl.program_id(0)
    gate = gate_ref[head]
    keep = 1.0 - gate
    scale = HD ** (-0.5)
    q_ref, k_ref, v_ref = qkv_ref.at[0, 0], qkv_ref.at[1, 0], qkv_ref.at[2, 0]
    memory_one = memory_ref[0]
    norm_one = norm_ref[0]
    gate_row = jnp.zeros((1, HD), jnp.float32)
    key_sum[...] = jnp.zeros_like(key_sum)
    value_sum[...] = jnp.zeros_like(value_sum)
    for tile in range(TILES):
        rows = slice(tile * QT, (tile + 1) * QT)
        q = q_ref[rows]
        grad = grad_ref[0, rows, :]
        grad_float = grad.astype(jnp.float32)
        memory_part = part_ref[0, rows, :]
        dot_part = dot_ref[0, rows, :]
        against_dot = jnp.sum(grad_float * dot_part, axis=1, keepdims=True)
        gate_row += jnp.sum(grad_float * (memory_part - dot_part), axis=0, keepdims=True)
        logsum = logsum_ref[0, rows, :]
        ahead, own, seen = tile_scores(tile, q, k_ref, offsets_ref, lengths_ref)
        own = jnp.exp(own - logsum)
        value_sum[rows, :] += plain_dot(own.astype(jnp.bfloat16), grad, TN)
        own = (keep * own * (plain_dot(grad, v_ref[rows], NT) - against_dot)).astype(jnp.bfloat16)
        key_sum[rows, :] += plain_dot(own, q, TN)
        grad_q = plain_dot(own, k_ref[rows], NN)
        if ahead is not None:
            ahead = jnp.exp(ahead - logsum)
            value_sum[:seen, :] += plain_dot(ahead.astype(jnp.bfloat16), grad, TN)
            ahead = (keep * ahead * (plain_dot(grad, v_ref[:seen], NT) - against_dot)).astype(
                jnp.bfloat16
            )
            key_sum[:seen, :] += plain_dot(ahead, q, TN)
            grad_q += plain_dot(ahead, k_ref[:seen], NN)
        q_float = q.astype(jnp.float32)
        lifted = feature_map(q_float)
        inverse = gate / jnp.sum(lifted * norm_one, axis=1, keepdims=True)
        against_memory = jnp.sum(grad_float * memory_part, axis=1, keepdims=True)
        grad_lifted = inverse * (narrow_dot(grad, memory_one, NT) - against_memory * norm_one)
        out_ref[0, rows, :] = (grad_q * scale + grad_lifted * feature_slope(q_float)).astype(
            jnp.bfloat16
        )
    out_ref[1, :, :] = (key_sum[...] * scale).astype(jnp.bfloat16)
    out_ref[2, :, :] = (value_sum[...] * keep).astype(jnp.bfloat16)
    gate_out_ref[0] = gate_row


def attend_back(heads_all, grad_heads, dot_part, memory_part, logsum, memory_one, norm_one, offsets, lengths, gate_value):
    heads = heads_all.shape[1]
    f32 = jnp.float32
    row_block = head_block((1, GLEN, HD))
    return pl.pallas_call(
        attend_back_kernel,
        grid=(heads,),
        in_specs=[
            SMEM_SPEC, SMEM_SPEC, SMEM_SPEC,
            head_block((3, 1, GLEN, HD), 1), row_block, row_block, row_block,
            head_block((1, GLEN, 1)), head_block((1, HD, HD)), head_block((1, 1, HD)),
        ],
        out_specs=[
            pl.BlockSpec((3, GLEN, HD), lambda h: (0, 0, h)),
            head_block((1, 1, HD)),
        ],
        out_shape=[
            jax.ShapeDtypeStruct((3, GLEN, heads * HD), jnp.bfloat16),
            jax.ShapeDtypeStruct((heads, 1, HD), f32),
        ],
        scratch_shapes=[pltpu.VMEM((GLEN, HD), f32), pltpu.VMEM((GLEN, HD), f32)],
        compiler_params=pltpu.CompilerParams(vmem_limit_bytes=BIG_VMEM),
        cost_estimate=pl.CostEstimate(
            flops=heads * 2_000_000_000, bytes_accessed=heads * 6_000_000, transcendentals=heads * 1_300_000
        ),
        name="attend_back",
    )(
        offsets, lengths, gate_value, heads_all, grad_heads, dot_part, memory_part, logsum,
        memory_one, norm_one[:, None, :],
    )


ANY = pl.BlockSpec(memory_space=pl.ANY)
VMEM = pl.BlockSpec(memory_space=pltpu.VMEM)
MESH_ID = pl.DeviceIdType.MESH
HALF = D // 2
AG_CUTS = 4


def remote(source, target, send, receive, device):
    return pltpu.make_async_remote_copy(
        src_ref=source, dst_ref=target, send_sem=send, recv_sem=receive,
        device_id=device, device_id_type=MESH_ID,
    )


def greet(peers):
    barrier = pltpu.get_barrier_semaphore()
    for peer in peers:
        pl.semaphore_signal(barrier, inc=1, device_id=peer, device_id_type=MESH_ID)
    pl.semaphore_wait(barrier, len(peers))


def square(row):
    along_x = (row // 2) * 2 + (1 - lax.rem(row, 2))
    along_y = lax.rem(row + 2, 4)
    across = (along_y // 2) * 2 + (1 - lax.rem(along_y, 2))
    return along_x, along_y, across


class Gather:
    def __init__(self, size, source, land, send, receive, own):
        self.size, self.source, self.land = size, source, land
        self.send, self.receive, self.own = send, receive, own
        self.row, self.col = lax.axis_index("row"), lax.axis_index("col")
        self.piece = source.shape[0]

    @staticmethod
    def semaphores(size):
        return 3 * AG_CUTS if size == 4 else size - 1

    def at(self, cut):
        height = self.piece // AG_CUTS
        return pl.ds(cut * height, height)

    def start(self, greeted=False):
        row, col = self.row, self.col
        if self.size != 4:
            peers = [lax.rem(row + d, self.size) for d in range(1, self.size)]
            if not greeted:
                greet([(peer, col) for peer in peers])
            self.order = [lax.rem(row + self.size - d, self.size) for d in range(1, self.size)]
            self.copies = [
                remote(self.source, self.land.at[row], self.send.at[i], self.receive.at[i], (peer, col))
                for i, peer in enumerate(peers)
            ]
            for copy in self.copies:
                copy.start()
        else:
            rx, ry, rd = square(row)
            self.order = [rx, ry, rd]
            self.px, self.py = (rx, col), (ry, col)
            if not greeted:
                greet([self.px, self.py])
            self.to_x, self.to_y, self.onward = {}, {}, []
            for step in range(AG_CUTS):
                for table, peer, base, cut in (
                    (self.to_x, self.px, 0, step),
                    (self.to_y, self.py, AG_CUTS, (step + AG_CUTS // 2) % AG_CUTS),
                ):
                    table[cut] = remote(
                        self.source.at[self.at(cut)], self.land.at[row, self.at(cut)],
                        self.send.at[base + cut], self.receive.at[base + cut], peer,
                    )
                    table[cut].start()
        self.keep = pltpu.make_async_copy(self.source, self.land.at[row], self.own)
        self.keep.start()
        self.keep.wait()

    def forward(self):
        if self.size != 4:
            return
        rx, ry, _ = self.order
        for step in range(AG_CUTS // 2):
            for table, peer, owner, cut in (
                (self.to_x, self.py, rx, step),
                (self.to_y, self.px, ry, step + AG_CUTS // 2),
            ):
                table[cut].wait_recv()
                place = self.land.at[owner, self.at(cut)]
                copy = remote(
                    place, place, self.send.at[2 * AG_CUTS + cut], self.receive.at[2 * AG_CUTS + cut], peer
                )
                copy.start()
                self.onward.append(copy)

    def wait(self, step):
        if self.size != 4:
            self.copies[step].wait_recv()
        elif step == 0:
            for cut in range(AG_CUTS // 2, AG_CUTS):
                self.to_x[cut].wait_recv()
        elif step == 1:
            for cut in range(AG_CUTS // 2):
                self.to_y[cut].wait_recv()
        else:
            for copy in self.onward:
                copy.wait_recv()
        return self.order[step]

    def finish(self):
        if self.size != 4:
            for copy in self.copies:
                copy.wait_send()
            return
        for copy in [*self.to_x.values(), *self.to_y.values(), *self.onward]:
            copy.wait_send()


class Scatter:
    def __init__(self, size, stage, land, total, send, receive):
        self.size, self.stage, self.land, self.total = size, stage, land, total
        self.send, self.receive = send, receive
        self.row, self.col = lax.axis_index("row"), lax.axis_index("col")

    @staticmethod
    def semaphores(size):
        return 6 if size == 4 else size - 1

    @staticmethod
    def stage_shape(size, piece):
        return (3 if size == 4 else size - 1, 2, piece, HALF)

    @staticmethod
    def land_shape(size, piece):
        return (6, piece, HALF) if size == 4 else (size - 1, 2, piece, HALF)

    def copy(self, index, source, peer):
        return remote(source, self.land.at[index], self.send.at[index], self.receive.at[index], peer)

    def run(self, partial, between=None, late=None):
        row, col = self.row, self.col

        def into(slot):
            def store(half, columns, value):
                self.stage[slot, half, :, columns] = value.astype(jnp.bfloat16)

            return store

        def into_total(half, columns, value):
            self.total[half, :, columns] = value

        if self.size != 4:
            peers = [lax.rem(row + d, self.size) for d in range(1, self.size)]
            greet([(peer, col) for peer in peers])
            copies = []
            for slot, peer in enumerate(peers):
                partial(peer, into(slot))
                copies.append(self.copy(slot, self.stage.at[slot], (peer, col)))
                copies[-1].start()
            partial(row, into_total)
            if between is not None:
                between()
            if late is not None:
                late()
            for slot, copy in enumerate(copies):
                copy.wait_recv()
                self.add_total(0, self.land.at[slot, 0])
                self.add_total(1, self.land.at[slot, 1])
            for copy in copies:
                copy.wait_send()
            return
        rx, ry, rd = square(row)
        px, py = (rx, col), (ry, col)
        greet([px, py])
        partial(rd, into(0))
        first = [self.copy(0, self.stage.at[0, 0], px), self.copy(1, self.stage.at[0, 1], py)]
        for copy in first:
            copy.start()
        partial(rx, into(1))
        first.append(self.copy(2, self.stage.at[1, 0], px))
        first[2].start()
        partial(ry, into(2))
        first.append(self.copy(3, self.stage.at[2, 1], py))
        first[3].start()
        if between is not None:
            between()
        first[0].wait_recv()
        self.add_stage(2, 0, self.land.at[0])
        second = [self.copy(4, self.stage.at[2, 0], py)]
        second[0].start()
        first[1].wait_recv()
        self.add_stage(1, 1, self.land.at[1])
        second.append(self.copy(5, self.stage.at[1, 1], px))
        second[1].start()
        partial(row, into_total)
        if late is not None:
            late()
        first[2].wait_recv()
        self.add_total(0, self.land.at[2])
        first[3].wait_recv()
        self.add_total(1, self.land.at[3])
        second[0].wait_recv()
        self.add_total(0, self.land.at[4])
        second[1].wait_recv()
        self.add_total(1, self.land.at[5])
        for copy in first + second:
            copy.wait_send()

    def add_stage(self, slot, half, landed):
        @pl.loop(0, landed.shape[0] // STRIP)
        def _(i):
            rows = pl.ds(pl.multiple_of(i * STRIP, STRIP), STRIP)
            value = self.stage[slot, half, rows, :].astype(jnp.float32) + landed[rows, :].astype(jnp.float32)
            self.stage[slot, half, rows, :] = value.astype(jnp.bfloat16)

    def add_total(self, half, landed):
        @pl.loop(0, landed.shape[0] // STRIP)
        def _(i):
            rows = pl.ds(pl.multiple_of(i * STRIP, STRIP), STRIP)
            self.total[half, rows, :] += landed[rows, :].astype(jnp.float32)


STRIP = 32


def scatter_scratch(size, piece):
    count = Scatter.semaphores(size)
    return [
        pltpu.VMEM(Scatter.stage_shape(size, piece), jnp.bfloat16),
        pltpu.VMEM(Scatter.land_shape(size, piece), jnp.bfloat16),
        pltpu.VMEM((2, piece, HALF), jnp.float32),
        pltpu.SemaphoreType.DMA((count,)),
        pltpu.SemaphoreType.DMA((count,)),
    ]


def gather_scratch(size, piece):
    count = Gather.semaphores(size)
    return [
        pltpu.VMEM((size, piece, D), jnp.bfloat16),
        pltpu.SemaphoreType.DMA((count,)),
        pltpu.SemaphoreType.DMA((count,)),
        pltpu.SemaphoreType.DMA,
    ]


def fetches(pairs, semaphores):
    copies = [pltpu.make_async_copy(a, b, semaphores.at[i]) for i, (a, b) in enumerate(pairs)]
    for copy in copies:
        copy.start()
    return copies


def wait_all(copies):
    for copy in copies:
        copy.wait()


def tiles_of(width, tile):
    def run(body):
        @pl.loop(0, width // tile)
        def _(t):
            body(t, pl.ds(pl.multiple_of(t * tile, tile), tile))

    return run


def comm_params(identity):
    return pltpu.CompilerParams(
        collective_id=identity, has_side_effects=True, vmem_limit_bytes=BIG_VMEM
    )


def bf(*shape):
    return jax.ShapeDtypeStruct(shape, jnp.bfloat16)


def fl(*shape):
    return jax.ShapeDtypeStruct(shape, jnp.float32)


def project_heads(size, normed, w_all):
    piece = normed.shape[0]
    cols, _, depth, width = w_all.shape
    heads = width // HD

    def kernel(x_ref, w_ref, heads_ref, all_ref, land, send, receive, own, w, w_sem, all_sem):
        loads = fetches([(w_ref.at[c], w.at[:, pl.ds(c * depth, depth), :]) for c in range(cols)], w_sem)
        gather = Gather(size, x_ref, land, send, receive, own)
        gather.start()

        def compute(row, slot):
            store = pltpu.make_async_copy(land.at[row], all_ref.at[row], all_sem.at[slot])
            store.start()
            rows = pl.ds(pl.multiple_of(row * piece, piece), piece)

            @pl.loop(0, 3)
            def _(j):
                value = jnp.dot(land[row], w[j], preferred_element_type=jnp.float32).astype(jnp.bfloat16)
                for head in range(heads):
                    heads_ref[j, head, rows, :] = value[:, head * HD : (head + 1) * HD]

            return store

        wait_all(loads)
        stores = [compute(gather.row, 0)]
        gather.forward()
        for step in range(size - 1):
            stores.append(compute(gather.wait(step), step + 1))
        wait_all(stores)
        gather.finish()

    return pl.pallas_call(
        kernel,
        out_shape=[bf(3, heads, GLEN, HD), bf(size, piece, D)],
        in_specs=[ANY, ANY],
        out_specs=[VMEM, ANY],
        scratch_shapes=gather_scratch(size, piece)
        + [
            pltpu.VMEM((3, D, width), jnp.bfloat16),
            pltpu.SemaphoreType.DMA((cols,)),
            pltpu.SemaphoreType.DMA((size,)),
        ],
        compiler_params=comm_params(1),
        cost_estimate=pl.CostEstimate(flops=6 * GLEN * D * width, bytes_accessed=40_000_000, transcendentals=0),
        name="project_heads",
    )(normed, w_all)


def strip_loop(piece, body):
    @pl.loop(0, piece // STRIP)
    def _(i):
        body(pl.ds(pl.multiple_of(i * STRIP, STRIP), STRIP))


def row_mean(first, second):
    return (jnp.sum(first, axis=1, keepdims=True) + jnp.sum(second, axis=1, keepdims=True)) / D


def lanes(first, second):
    lane = lax.broadcasted_iota(jnp.int32, (STRIP, HD), 1)
    return jnp.where(lane == 0, first, jnp.where(lane == 1, second, 0.0))


LEFT, RIGHT = slice(0, HALF), slice(HALF, D)


def branch_out(size, attn, w_all, x, gain):
    piece = GLEN // size
    cols, width, depth = w_all.shape

    def kernel(attn_ref, w_ref, x_ref, gain_ref, middle_ref, normed_ref, stat_ref, stage, land, total, send, receive, w, w_sem):
        loads = fetches([(w_ref.at[c], w.at[:, pl.ds(c * depth, depth)]) for c in range(cols)], w_sem)
        scatter = Scatter(size, stage, land, total, send, receive)
        wait_all(loads)

        def partial(row, store):
            rows = pl.ds(pl.multiple_of(row * piece, piece), piece)
            left = attn_ref[rows, :]
            for half in range(2):
                for t in range(2):
                    columns = slice(half * HALF + t * HALF // 2, half * HALF + (t + 1) * HALF // 2)
                    store(
                        half, slice(t * HALF // 2, (t + 1) * HALF // 2),
                        jnp.dot(left, w[:, columns], preferred_element_type=jnp.float32),
                    )

        scatter.run(partial)

        def finish(rows):
            branch = (total[0, rows, :], total[1, rows, :])
            middle = (
                x_ref[rows, LEFT].astype(jnp.float32) + branch[0],
                x_ref[rows, RIGHT].astype(jnp.float32) + branch[1],
            )
            mean = row_mean(middle[0] * middle[0], middle[1] * middle[1])
            inverse = lax.rsqrt(mean + EPSILON)
            for part, columns in zip(middle, (LEFT, RIGHT)):
                middle_ref[rows, columns] = part
                normed_ref[rows, columns] = (part * inverse * gain_ref[:, columns]).astype(jnp.bfloat16)
            stat_ref[rows, :] = lanes(row_mean(branch[0] * branch[0], branch[1] * branch[1]), mean)

        strip_loop(piece, finish)

    return pl.pallas_call(
        kernel,
        out_shape=[fl(piece, D), bf(piece, D), fl(piece, HD)],
        in_specs=[VMEM, ANY, VMEM, VMEM],
        out_specs=[VMEM, VMEM, VMEM],
        scratch_shapes=scatter_scratch(size, piece)
        + [pltpu.VMEM((width, D), jnp.bfloat16), pltpu.SemaphoreType.DMA((cols,))],
        compiler_params=comm_params(2),
        cost_estimate=pl.CostEstimate(flops=2 * GLEN * D * width, bytes_accessed=40_000_000, transcendentals=0),
        name="branch_out",
    )(attn, w_all, x, gain)


def feed_forward(size, normed, w_gu, w_down, cot):
    piece = normed.shape[0]
    cols, _, depth, wide = w_gu.shape
    tile = min(wide, 512)

    def kernel(
        x_ref, gu_ref, down_ref, cot_ref, hidden_ref, grad_ref, all_ref,
        land, send, receive, own, gu, down, cot_all, back, stage, gu_sem, down_sem, cot_sem, out_sem, all_sem,
    ):
        down_loads = fetches(
            [(down_ref.at[c], down.at[:, pl.ds(c * depth, depth)]) for c in range(cols)], down_sem
        )
        cot_load = pltpu.make_async_copy(cot_ref, cot_all, cot_sem)
        cot_load.start()
        gu_loads = fetches([(gu_ref.at[c], gu.at[:, pl.ds(c * depth, depth), :]) for c in range(cols)], gu_sem)
        gather = Gather(size, x_ref, land, send, receive, own)
        gather.start()
        wait_all(down_loads)
        cot_load.wait()

        def backward(row):
            @tiles_of(wide, tile)
            def _(t, columns):
                back[row, :, columns] = plain_dot(cot_all[row], down[columns, :], NT).astype(jnp.bfloat16)

        def moves(row, slot, columns):
            rows = pl.ds(pl.multiple_of(row * piece, piece), piece)
            return [
                pltpu.make_async_copy(stage.at[slot, 0], hidden_ref.at[rows, columns], out_sem.at[slot, 0]),
                pltpu.make_async_copy(stage.at[slot, 1], grad_ref.at[0, rows, columns], out_sem.at[slot, 1]),
                pltpu.make_async_copy(stage.at[slot, 2], grad_ref.at[1, rows, columns], out_sem.at[slot, 2]),
            ]

        count = wide // tile

        def compute(row, first):
            pltpu.make_async_copy(land.at[row], all_ref.at[row], all_sem).start()

            @pl.loop(0, count)
            def _(t):
                columns = pl.ds(pl.multiple_of(t * tile, tile), tile)
                slot = lax.rem(t, 2)
                x = land[row]
                gate_pre = jnp.dot(x, gu[0, :, columns], preferred_element_type=jnp.float32)
                up_pre = jnp.dot(x, gu[1, :, columns], preferred_element_type=jnp.float32)
                sigmoid = jax.nn.sigmoid(gate_pre)
                silu = gate_pre * sigmoid
                grad_hidden = back[row, :, columns].astype(jnp.float32)

                @pl.when(t >= 2)
                def _():
                    wait_all(moves(row, slot, columns))

                stage[slot, 0] = (silu * up_pre).astype(jnp.bfloat16)
                stage[slot, 1] = (grad_hidden * up_pre * (sigmoid + silu * (1.0 - sigmoid))).astype(jnp.bfloat16)
                stage[slot, 2] = (grad_hidden * silu).astype(jnp.bfloat16)
                for move in moves(row, slot, columns):
                    move.start()

            for slot in range(min(2, count)):
                wait_all(moves(row, slot, pl.ds(slot * tile, tile)))
            pltpu.make_async_copy(land.at[row], all_ref.at[row], all_sem).wait()

        backward(gather.row)
        gather.forward()
        for step in range(size - 1):
            backward(gather.order[step])
        wait_all(gu_loads)
        compute(gather.row, True)
        for step in range(size - 1):
            compute(gather.wait(step), False)
        gather.finish()

    return pl.pallas_call(
        kernel,
        out_shape=[bf(GLEN, wide), bf(2, GLEN, wide), bf(size, piece, D)],
        in_specs=[ANY, ANY, ANY, ANY],
        out_specs=[ANY, ANY, ANY],
        scratch_shapes=gather_scratch(size, piece)
        + [
            pltpu.VMEM((2, D, wide), jnp.bfloat16),
            pltpu.VMEM((wide, D), jnp.bfloat16),
            pltpu.VMEM((size, piece, D), jnp.bfloat16),
            pltpu.VMEM((size, piece, wide), jnp.bfloat16),
            pltpu.VMEM((2, 3, piece, tile), jnp.bfloat16),
            pltpu.SemaphoreType.DMA((cols,)),
            pltpu.SemaphoreType.DMA((cols,)),
            pltpu.SemaphoreType.DMA,
            pltpu.SemaphoreType.DMA((2, 3)),
            pltpu.SemaphoreType.DMA,
        ],
        compiler_params=comm_params(3),
        cost_estimate=pl.CostEstimate(flops=6 * GLEN * D * wide, bytes_accessed=70_000_000, transcendentals=GLEN * wide),
        name="feed_forward",
    )(normed, w_gu, w_down, cot.reshape(size, piece, D))


def norm_back(rows, total, stream, inverse, gain_ref, base, store, gain_sum):
    u = [total[half, rows, :] * gain_ref[:, columns] for half, columns in enumerate((LEFT, RIGHT))]
    inner = row_mean(u[0] * stream[0], u[1] * stream[1]) * inverse * inverse * inverse
    for half, columns in enumerate((LEFT, RIGHT)):
        store(columns, base[half] + inverse * u[half] - stream[half] * inner)
        gain_sum[:, columns] += jnp.sum(total[half, rows, :] * stream[half] * inverse, axis=0, keepdims=True)


def middle_back(size, grads, w_gu, middle, cot, gain):
    piece = middle.shape[0]
    cols, _, depth, wide = w_gu.shape
    tile = 512

    def kernel(
        g_ref, gu_ref, middle_ref, cot_ref, gain_ref, grad_ref, low_ref, gain_sum,
        stage, land, total, send, receive, gu, g, gu_sem, g_sem,
    ):
        loads = fetches([(gu_ref.at[c], gu.at[:, pl.ds(c * depth, depth), :]) for c in range(cols)], gu_sem)
        scatter = Scatter(size, stage, land, total, send, receive)
        g_loads = fetches([(g_ref.at[j], g.at[j]) for j in range(2)], g_sem)
        wait_all(g_loads)
        wait_all(loads)
        gain_sum[...] = jnp.zeros_like(gain_sum)

        def partial(row, store):
            rows = pl.ds(pl.multiple_of(row * piece, piece), piece)
            for half in range(2):
                @pl.loop(0, HALF // tile)
                def _(t):
                    columns = pl.ds(pl.multiple_of(t * tile, tile), tile)
                    depth_rows = pl.ds(pl.multiple_of(half * HALF + t * tile, tile), tile)
                    value = plain_dot(g[0, rows, :], gu[0, depth_rows, :], NT)
                    value += plain_dot(g[1, rows, :], gu[1, depth_rows, :], NT)
                    store(half, columns, value)

        scatter.run(partial)

        def finish(rows):
            stream = [middle_ref[rows, columns] for columns in (LEFT, RIGHT)]
            base = [cot_ref[rows, columns].astype(jnp.float32) for columns in (LEFT, RIGHT)]
            inverse = lax.rsqrt(row_mean(stream[0] * stream[0], stream[1] * stream[1]) + EPSILON)

            def store(columns, value):
                grad_ref[rows, columns] = value
                low_ref[rows, columns] = value.astype(jnp.bfloat16)

            norm_back(rows, total, stream, inverse, gain_ref, base, store, gain_sum)

        strip_loop(piece, finish)

    return pl.pallas_call(
        kernel,
        out_shape=[fl(piece, D), bf(piece, D), fl(1, D)],
        in_specs=[ANY, ANY, VMEM, VMEM, VMEM],
        out_specs=[VMEM, VMEM, VMEM],
        scratch_shapes=scatter_scratch(size, piece)
        + [
            pltpu.VMEM((2, D, wide), jnp.bfloat16),
            pltpu.VMEM((2, GLEN, wide), jnp.bfloat16),
            pltpu.SemaphoreType.DMA((cols,)),
            pltpu.SemaphoreType.DMA((2,)),
        ],
        compiler_params=comm_params(4),
        cost_estimate=pl.CostEstimate(flops=4 * GLEN * D * wide, bytes_accessed=60_000_000, transcendentals=0),
        name="middle_back",
    )(grads, w_gu, middle, cot, gain)


def blocked_store(ref, rows, depth, columns, value):
    for i in range(value.shape[1] // depth):
        ref[columns.start // depth + i, rows, :] = value[:, i * depth : (i + 1) * depth]


def ffn_out(size, hidden, w_down, middle):
    piece = middle.shape[0]
    cols, wide, depth = w_down.shape
    tile = 512

    def kernel(h_ref, w_ref, middle_ref, out_ref, stat_ref, stage, land, total, send, receive, w, w_sem):
        loads = fetches([(w_ref.at[c], w.at[:, pl.ds(c * depth, depth)]) for c in range(cols)], w_sem)
        scatter = Scatter(size, stage, land, total, send, receive)
        wait_all(loads)

        def partial(row, store):
            rows = pl.ds(pl.multiple_of(row * piece, piece), piece)
            for half in range(2):
                @pl.loop(0, HALF // tile)
                def _(t):
                    columns = pl.ds(pl.multiple_of(t * tile, tile), tile)
                    whole = pl.ds(pl.multiple_of(half * HALF + t * tile, tile), tile)
                    store(half, columns, jnp.dot(h_ref[rows, :], w[:, whole], preferred_element_type=jnp.float32))

        scatter.run(partial)

        def finish(rows):
            ffn = [total[half, rows, :] for half in range(2)]
            result = [middle_ref[rows, columns] + ffn[half] for half, columns in enumerate((LEFT, RIGHT))]
            for half, columns in enumerate((LEFT, RIGHT)):
                blocked_store(out_ref, rows, depth, columns, result[half].astype(jnp.bfloat16))
            stat_ref[rows, :] = lanes(
                row_mean(ffn[0] * ffn[0], ffn[1] * ffn[1]),
                row_mean(result[0] * result[0], result[1] * result[1]),
            )

        strip_loop(piece, finish)

    return pl.pallas_call(
        kernel,
        out_shape=[bf(cols, piece, depth), fl(piece, HD)],
        in_specs=[VMEM, ANY, VMEM],
        out_specs=[VMEM, VMEM],
        scratch_shapes=scatter_scratch(size, piece)
        + [pltpu.VMEM((wide, D), jnp.bfloat16), pltpu.SemaphoreType.DMA((cols,))],
        compiler_params=comm_params(5),
        cost_estimate=pl.CostEstimate(flops=2 * GLEN * D * wide, bytes_accessed=50_000_000, transcendentals=0),
        name="ffn_out",
    )(hidden, w_down, middle)


def branch_back(size, low, w_all):
    piece = low.shape[0]
    cols, width, depth = w_all.shape
    heads = width // HD

    def kernel(x_ref, w_ref, heads_ref, all_ref, land, send, receive, own, w, w_sem, all_sem):
        loads = fetches([(w_ref.at[c], w.at[:, pl.ds(c * depth, depth)]) for c in range(cols)], w_sem)
        gather = Gather(size, x_ref, land, send, receive, own)
        gather.start()

        def compute(row, slot):
            store = pltpu.make_async_copy(land.at[row], all_ref.at[row], all_sem.at[slot])
            store.start()
            rows = pl.ds(pl.multiple_of(row * piece, piece), piece)
            value = plain_dot(land[row], w[...], NT).astype(jnp.bfloat16)
            for head in range(heads):
                heads_ref[head, rows, :] = value[:, head * HD : (head + 1) * HD]
            return store

        wait_all(loads)
        stores = [compute(gather.row, 0)]
        gather.forward()
        for step in range(size - 1):
            stores.append(compute(gather.wait(step), step + 1))
        wait_all(stores)
        gather.finish()

    return pl.pallas_call(
        kernel,
        out_shape=[bf(heads, GLEN, HD), bf(size, piece, D)],
        in_specs=[ANY, ANY],
        out_specs=[VMEM, ANY],
        scratch_shapes=gather_scratch(size, piece)
        + [
            pltpu.VMEM((width, D), jnp.bfloat16),
            pltpu.SemaphoreType.DMA((cols,)),
            pltpu.SemaphoreType.DMA((size,)),
        ],
        compiler_params=comm_params(6),
        cost_estimate=pl.CostEstimate(flops=2 * GLEN * D * width, bytes_accessed=40_000_000, transcendentals=0),
        name="branch_back",
    )(low, w_all)


def stream_back(size, grads, w_all, x, grad_middle, gain):
    piece = x.shape[0]
    cols, _, depth, width = w_all.shape
    tile = 512

    def kernel(
        g_ref, w_ref, x_ref, middle_ref, gain_ref, out_ref, gain_sum,
        stage, land, total, send, receive, w, w_sem,
    ):
        loads = fetches([(w_ref.at[c], w.at[:, pl.ds(c * depth, depth), :]) for c in range(cols)], w_sem)
        scatter = Scatter(size, stage, land, total, send, receive)
        wait_all(loads)
        gain_sum[...] = jnp.zeros_like(gain_sum)

        def partial(row, store):
            rows = pl.ds(pl.multiple_of(row * piece, piece), piece)
            for half in range(2):
                @pl.loop(0, HALF // tile)
                def _(t):
                    columns = pl.ds(pl.multiple_of(t * tile, tile), tile)
                    depth_rows = pl.ds(pl.multiple_of(half * HALF + t * tile, tile), tile)
                    value = plain_dot(g_ref[0, rows, :], w[0, depth_rows, :], NT)
                    for j in (1, 2):
                        value += plain_dot(g_ref[j, rows, :], w[j, depth_rows, :], NT)
                    store(half, columns, value)

        scatter.run(partial)

        def finish(rows):
            stream = [x_ref[rows, columns].astype(jnp.float32) for columns in (LEFT, RIGHT)]
            base = [middle_ref[rows, columns] for columns in (LEFT, RIGHT)]
            inverse = lax.rsqrt(row_mean(stream[0] * stream[0], stream[1] * stream[1]) + EPSILON)

            def store(columns, value):
                blocked_store(out_ref, rows, depth, columns, value.astype(jnp.bfloat16))

            norm_back(rows, total, stream, inverse, gain_ref, base, store, gain_sum)

        strip_loop(piece, finish)

    return pl.pallas_call(
        kernel,
        out_shape=[bf(cols, piece, depth), fl(1, D)],
        in_specs=[VMEM, ANY, VMEM, VMEM, VMEM],
        out_specs=[VMEM, VMEM],
        scratch_shapes=scatter_scratch(size, piece)
        + [pltpu.VMEM((3, D, width), jnp.bfloat16), pltpu.SemaphoreType.DMA((cols,))],
        compiler_params=comm_params(7),
        cost_estimate=pl.CostEstimate(flops=6 * GLEN * D * width, bytes_accessed=50_000_000, transcendentals=0),
        name="stream_back",
    )(grads, w_all, x, grad_middle, gain)


def here():
    return lax.axis_index("row"), lax.axis_index("col")


def row_and_col_peers(size, cols):
    row, col = here()
    return [(lax.rem(row + d, size), col) for d in range(1, size)] + [
        (row, lax.rem(col + e, cols)) for e in range(1, cols)
    ]


def dma(*shape):
    return pltpu.SemaphoreType.DMA(shape)


class Inward:
    def __init__(self, size, cols, source, middle, land, first_send, first_receive, send, receive, own):
        self.size, self.cols, self.groups = size, cols, cols // size
        self.source, self.middle, self.land = source, middle, land
        self.first_send, self.first_receive = first_send, first_receive
        self.send, self.receive, self.own = send, receive, own
        self.row, self.col = here()

    @staticmethod
    def scratch(size, cols, piece, depth):
        return [
            pltpu.VMEM((size, cols // size, piece, depth), jnp.bfloat16),
            pltpu.VMEM((cols, piece, depth), jnp.bfloat16),
            dma(size - 1), dma(size - 1), dma(cols), dma(cols), dma(2),
        ]

    def start(self):
        row, col = self.row, self.col
        self.first = []
        for d in range(1, self.size):
            peer = lax.rem(row + d, self.size)
            self.first.append(
                remote(
                    self.source.at[:, peer], self.middle.at[row],
                    self.first_send.at[d - 1], self.first_receive.at[d - 1], (peer, col),
                )
            )
            self.first[-1].start()
        self.keep = pltpu.make_async_copy(self.source.at[:, row], self.middle.at[row], self.own.at[0])
        self.keep.start()

    def forward(self):
        row, col = self.row, self.col
        for d in range(self.size):
            origin = lax.rem(row + self.size - d, self.size)
            if d == 0:
                self.keep.wait()
            else:
                self.first[d - 1].wait_recv()
            for i in range(self.groups):
                group = origin * self.groups + i

                @pl.when(group != col)
                def _():
                    remote(
                        self.middle.at[origin, i], self.land.at[col],
                        self.send.at[group], self.receive.at[col], (row, group),
                    ).start()

                @pl.when(group == col)
                def _():
                    pltpu.make_async_copy(self.middle.at[origin, i], self.land.at[col], self.own.at[1]).start()

    def finish(self):
        row, col = self.row, self.col
        pltpu.make_async_copy(self.middle.at[0, 0], self.land.at[col], self.own.at[1]).wait()
        for e in range(1, self.cols):
            peer = lax.rem(col + e, self.cols)
            remote(
                self.middle.at[0, 0], self.land.at[peer], self.send.at[peer], self.receive.at[peer], (row, peer)
            ).wait()
        for copy in self.first:
            copy.wait_send()


class Outward:
    def __init__(self, size, cols, source, middle, target, first_send, first_receive, send, receive, own):
        self.size, self.cols, self.groups = size, cols, cols // size
        self.source, self.middle, self.target = source, middle, target
        self.first_send, self.first_receive = first_send, first_receive
        self.send, self.receive, self.own = send, receive, own
        self.row, self.col = here()

    @staticmethod
    def scratch(size, cols, piece, depth):
        return [
            pltpu.VMEM((cols, piece, depth), jnp.bfloat16),
            dma(cols - 1), dma(cols - 1), dma(cols), dma(cols), dma(cols // size),
        ]

    def start(self):
        row, col = self.row, self.col
        self.first = []
        for e in range(1, self.cols):
            peer = lax.rem(col + e, self.cols)
            self.first.append(
                remote(
                    self.source.at[peer], self.middle.at[col],
                    self.first_send.at[e - 1], self.first_receive.at[e - 1], (row, peer),
                )
            )
            self.first[-1].start()

    def forward(self):
        row, col = self.row, self.col
        for e in range(self.cols):
            group = lax.rem(col + self.cols - e, self.cols)
            if e:
                self.first[e - 1].wait_recv()
            block = self.middle.at[group] if e else self.source.at[col]
            home, i = group // self.groups, lax.rem(group, self.groups)

            @pl.when(home != row)
            def _():
                remote(
                    block, self.target.at[i, row],
                    self.send.at[group], self.receive.at[i * self.size + row], (home, col),
                ).start()

            @pl.when(home == row)
            def _():
                pltpu.make_async_copy(block, self.target.at[i, row], self.own.at[i]).start()

    def finish(self):
        row, col = self.row, self.col
        for i in range(self.groups):
            pltpu.make_async_copy(self.middle.at[0], self.target.at[i, row], self.own.at[i]).wait()
            for d in range(1, self.size):
                peer = lax.rem(row + d, self.size)
                remote(
                    self.middle.at[0], self.target.at[i, peer],
                    self.send.at[peer * self.groups + i], self.receive.at[i * self.size + peer], (peer, col),
                ).wait()
        for copy in self.first:
            copy.wait_send()


def by_pieces(block, size):
    return block.reshape(block.shape[0] // GLEN, size, GLEN // size, block.shape[1])


def enter(size, cols, stream_in, gains):
    pieces = by_pieces(stream_in, size)
    piece, depth = pieces.shape[2:]

    def kernel(x_ref, gains_ref, tokens_ref, normed_ref, gain_in_ref, gain_mid_ref, gains_land, gains_send, gains_receive, *rest):
        greet(row_and_col_peers(size, cols))
        exchange = Inward(size, cols, x_ref, *rest)
        exchange.start()
        row, col = here()
        copies = []
        for e in range(1, cols):
            peer = lax.rem(col + e, cols)
            copies.append(
                remote(gains_ref, gains_land.at[col], gains_send.at[e - 1], gains_receive.at[e - 1], (row, peer))
            )
            copies[-1].start()
        gains_land[col] = gains_ref[...]
        exchange.forward()
        for copy in copies:
            copy.wait()
        for c in range(cols):
            gain_in_ref[:, c * depth : (c + 1) * depth] = gains_land[c, 0:1, :]
            gain_mid_ref[:, c * depth : (c + 1) * depth] = gains_land[c, 1:2, :]
        exchange.finish()
        land = exchange.land

        def norm(rows):
            total = jnp.zeros((STRIP, 1), jnp.float32)
            for c in range(cols):
                part = land[c, rows, :]
                tokens_ref[rows, c * depth : (c + 1) * depth] = part
                part = part.astype(jnp.float32)
                total += jnp.sum(part * part, axis=1, keepdims=True)
            inverse = lax.rsqrt(total / D + EPSILON)
            for c in range(cols):
                columns = slice(c * depth, (c + 1) * depth)
                normed_ref[rows, columns] = (
                    land[c, rows, :].astype(jnp.float32) * inverse * gain_in_ref[:, columns]
                ).astype(jnp.bfloat16)

        strip_loop(piece, norm)

    return pl.pallas_call(
        kernel,
        out_shape=[bf(piece, D), bf(piece, D), fl(1, D), fl(1, D)],
        in_specs=[ANY, VMEM],
        out_specs=[VMEM] * 4,
        scratch_shapes=[pltpu.VMEM((cols, 8, depth), jnp.float32), dma(cols - 1), dma(cols - 1)]
        + Inward.scratch(size, cols, piece, depth),
        compiler_params=comm_params(8),
        cost_estimate=pl.CostEstimate(flops=8 * piece * D, bytes_accessed=40_000_000, transcendentals=0),
        name="enter",
    )(pieces, jnp.pad(gains, ((0, 6), (0, 0))))


def spread(size, cols, cotangent):
    pieces = by_pieces(cotangent, size)
    piece, depth = pieces.shape[2:]
    count = Gather.semaphores(size)

    def kernel(x_ref, tokens_ref, all_ref, send, receive, own, *rest):
        greet(row_and_col_peers(size, cols))
        exchange = Inward(size, cols, x_ref, *rest)
        exchange.start()
        exchange.forward()
        exchange.finish()
        land = exchange.land

        def assemble(rows):
            for c in range(cols):
                tokens_ref[rows, c * depth : (c + 1) * depth] = land[c, rows, :]

        strip_loop(piece, assemble)
        gather = Gather(size, tokens_ref, all_ref, send, receive, own)
        gather.start(greeted=True)
        gather.forward()
        for step in range(size - 1):
            gather.wait(step)
        gather.finish()

    return pl.pallas_call(
        kernel,
        out_shape=[bf(piece, D), bf(size, piece, D)],
        in_specs=[ANY],
        out_specs=[VMEM, ANY],
        scratch_shapes=[dma(count), dma(count), pltpu.SemaphoreType.DMA]
        + Inward.scratch(size, cols, piece, depth),
        compiler_params=comm_params(9),
        cost_estimate=pl.CostEstimate(flops=piece * D, bytes_accessed=60_000_000, transcendentals=0),
        name="spread",
    )(pieces)


def leave(size, cols, blocks_out, blocks_grad, stats, sums):
    _, piece, depth = blocks_out.shape
    groups = cols // size
    half = len(Outward.scratch(size, cols, piece, depth))

    def kernel(
        out_ref, grad_ref, stats_ref, sums_ref, out_target, grad_target, stats_target, sums_target,
        stats_row, stats_all, sums_col, sums_part, sums_row,
        a_send, a_receive, b_send, b_receive, c_send, c_receive, d_send, d_receive, *rest,
    ):
        row, col = here()
        greet(row_and_col_peers(size, cols))
        grad = Outward(size, cols, grad_ref, rest[0], grad_target, *rest[1:half])
        out = Outward(size, cols, out_ref, rest[half], out_target, *rest[half + 1 :])
        home, slot = col // groups, lax.rem(col, groups)
        col_peers = [lax.rem(col + e, cols) for e in range(1, cols)]
        row_peers = [lax.rem(row + d, size) for d in range(1, size)]

        def sums_first(peer):
            return remote(sums_ref.at[peer], sums_col.at[col], c_send.at[peer], c_receive.at[col], (row, peer))

        for peer in col_peers:
            sums_first(peer).start()
        sums_col[col] = sums_ref[col]

        @pl.when(home != row)
        def _():
            remote(stats_ref, stats_row.at[row], a_send, a_receive.at[row], (home, col)).start()

        @pl.when(home == row)
        def _():
            stats_row[row] = stats_ref[...]

        grad.start()
        out.start()
        for peer in col_peers:
            remote(sums_ref.at[peer], sums_col.at[peer], c_send.at[peer], c_receive.at[peer], (row, peer)).wait()
        total = sums_col[0]
        for c in range(1, cols):
            total += sums_col[c]
        sums_part[...] = total
        sums_row[row] = total
        for peer in row_peers:
            remote(sums_part, sums_row.at[row], d_send.at[peer], d_receive.at[row], (peer, col)).start()

        @pl.when(home == row)
        def _():
            for peer in row_peers:
                remote(stats_ref, stats_row.at[peer], a_send, a_receive.at[peer], (peer, col)).wait_recv()
            for e, peer in enumerate(col_peers):
                remote(stats_row, stats_all.at[slot], b_send.at[e], b_receive.at[slot], (row, peer)).start()
            stats_all[slot] = stats_row[...]

        grad.forward()
        out.forward()
        for peer in row_peers:
            remote(sums_part, sums_row.at[peer], d_send.at[peer], d_receive.at[peer], (peer, col)).wait()
        whole = sums_row[0]
        for r in range(1, size):
            whole += sums_row[r]
        line = lax.broadcasted_iota(jnp.int32, (8, depth), 0)
        sums_target[...] = jnp.where(line < 2, whole, total)

        @pl.when(home == row)
        def _():
            for e, peer in enumerate(col_peers):
                remote(stats_row, stats_all.at[slot], b_send.at[e], b_receive.at[slot], (row, peer)).wait_send()

        @pl.when(home != row)
        def _():
            remote(stats_ref, stats_row.at[row], a_send, a_receive.at[row], (home, col)).wait_send()

        for i in range(groups):
            group = row * groups + i

            @pl.when(group != col)
            def _():
                remote(stats_row, stats_all.at[i], b_send.at[0], b_receive.at[i], (row, group)).wait_recv()

        stats_target[...] = stats_all[...]
        grad.finish()
        out.finish()

    return pl.pallas_call(
        kernel,
        out_shape=[
            bf(groups, size, piece, depth), bf(groups, size, piece, depth),
            fl(groups, size, 8, piece), fl(8, depth),
        ],
        in_specs=[VMEM] * 4,
        out_specs=[ANY, ANY, VMEM, VMEM],
        scratch_shapes=[
            pltpu.VMEM((size, 8, piece), jnp.float32),
            pltpu.VMEM((groups, size, 8, piece), jnp.float32),
            pltpu.VMEM((cols, 8, depth), jnp.float32),
            pltpu.VMEM((8, depth), jnp.float32),
            pltpu.VMEM((size, 8, depth), jnp.float32),
            pltpu.SemaphoreType.DMA, dma(size), dma(cols - 1), dma(groups), dma(cols), dma(cols), dma(size), dma(size),
        ]
        + Outward.scratch(size, cols, piece, depth) * 2,
        compiler_params=comm_params(10),
        cost_estimate=pl.CostEstimate(flops=piece * D, bytes_accessed=60_000_000, transcendentals=0),
        name="leave",
    )(blocks_out, blocks_grad, stats, sums)


def tokens_contract(left, right):
    return lax.dot_general(left, right, (TN, ((), ())), preferred_element_type=jnp.float32)


def over_col(partial, axis):
    return lax.psum_scatter(
        partial.astype(jnp.bfloat16), "col", scatter_dimension=axis, tiled=True
    ).astype(jnp.float32)


def flat(pieces):
    return pieces.reshape(GLEN, D)


def local(
    stream_in,
    w_qkv,
    w_out,
    w_gate_up,
    w_down,
    gain_attn,
    gain_ffn,
    gate_logit,
    memory,
    memory_norm,
    offsets,
    lengths,
    cotangent,
):
    head_here = memory.shape[1]
    size = lax.axis_size("row")
    cols = lax.axis_size("col")
    all_qkv, all_out, all_gu, all_down = (
        lax.all_gather(w, "col", axis=0, tiled=False) for w in (w_qkv, w_out, w_gate_up, w_down)
    )
    gate_value = jax.nn.sigmoid(gate_logit)
    group = (memory[0], memory_norm[0], offsets[0], lengths[0], gate_value)
    stream, normed_in, gain_in, gain_mid = enter(
        size, cols, stream_in, jnp.stack([gain_attn, gain_ffn])
    )
    heads_all, all_in = project_heads(size, normed_in, all_qkv)
    attn, dot_part, memory_part, logsum, memory_new, norm_new = attend(heads_all, *group)
    cotangent, attn = lax.optimization_barrier((cotangent, attn))
    cot, all_cot = spread(size, cols, cotangent)
    all_cot, attn = lax.optimization_barrier((all_cot, attn))
    all_cot = all_cot.reshape(GLEN, D)
    middle, normed_ffn, stat_branch = branch_out(size, attn, all_out, stream, gain_mid)
    hidden, grad_gu, all_ffn = feed_forward(size, normed_ffn, all_gu, all_down, all_cot)
    part_gu = jnp.einsum(
        "td,jto->jdo", flat(all_ffn), grad_gu, preferred_element_type=jnp.float32
    ).astype(jnp.bfloat16)
    part_down = tokens_contract(hidden, all_cot).astype(jnp.bfloat16)
    grad_gu, part_gu, part_down = lax.optimization_barrier((grad_gu, part_gu, part_down))
    grad_gate_up = over_col(part_gu, 1)
    grad_down = over_col(part_down, 1)
    grad_middle, low_branch, part_gain_ffn = middle_back(size, grad_gu, all_gu, middle, cot, gain_mid)
    grad_heads, all_branch = branch_back(size, low_branch, all_out)
    grads_qkv, gate_sums = attend_back(
        heads_all, grad_heads, dot_part, memory_part, logsum, *group
    )
    hidden, grads_qkv = lax.optimization_barrier((hidden, grads_qkv))
    blocks_out, stat_ffn = ffn_out(size, hidden, all_down, middle)
    blocks_out, grads_qkv, grad_gate_up = lax.optimization_barrier((blocks_out, grads_qkv, grad_gate_up))
    blocks_grad, part_gain_attn = stream_back(size, grads_qkv, all_qkv, stream, grad_middle, gain_in)
    blocks_grad, grad_down = lax.optimization_barrier((blocks_grad, grad_down))
    grad_out = over_col(tokens_contract(attn, flat(all_branch)), 1)
    grad_qkv = over_col(
        jnp.einsum("td,jto->jdo", flat(all_in), grads_qkv, preferred_element_type=jnp.float32), 1
    )
    logit_part = gate_value * (1.0 - gate_value) * jnp.sum(gate_sums, axis=(1, 2))
    features_here = gain_attn.shape[0]
    sums = jnp.concatenate(
        [
            part_gain_attn.reshape(cols, 1, features_here),
            part_gain_ffn.reshape(cols, 1, features_here),
            jnp.broadcast_to(
                jnp.pad(logit_part, (0, features_here - head_here))[None, None], (cols, 6, features_here)
            ),
        ],
        axis=1,
    )
    stats = jnp.sqrt(jnp.concatenate([stat_branch[:, :2], stat_ffn[:, :2]], axis=1).T)
    stream_out, stream_grad, stats_all, sums = leave(
        size, cols, blocks_out, blocks_grad, jnp.pad(stats, ((0, 4), (0, 0))), sums
    )
    stream_out = stream_out.reshape(stream_in.shape)
    stream_grad = stream_grad.reshape(stream_in.shape).astype(jnp.float32)
    rms_table = stats_all[:, :, :4].transpose(2, 0, 1, 3).reshape(4, stream_in.shape[0])
    grad_gain_attn, grad_gain_ffn, grad_gate_logit = sums[0], sums[1], sums[2, :head_here]
    return (
        stream_out,
        stream_grad,
        grad_qkv,
        grad_out,
        grad_gate_up,
        grad_down,
        grad_gain_attn,
        grad_gain_ffn,
        grad_gate_logit,
        memory_new[None],
        norm_new.reshape(1, head_here, HD),
        rms_table,
    )


def solution(mesh):
    return jax.shard_map(
        local,
        mesh=mesh,
        in_specs=(
            P("row", "col"),
            P(None, "col", "row"),
            P("row", "col"),
            P(None, "col", "row"),
            P("row", "col"),
            P("col"),
            P("col"),
            P("row"),
            P("col", "row", None, None),
            P("col", "row", None),
            P("col", None),
            P("col", None),
            P("row", "col"),
        ),
        out_specs=(
            P("row", "col"),
            P("row", "col"),
            P(None, "col", "row"),
            P("row", "col"),
            P(None, "col", "row"),
            P("row", "col"),
            P("col"),
            P("col"),
            P("row"),
            P("col", "row", None, None),
            P("col", "row", None),
            P(None, "row"),
        ),
        check_vma=False,
    )
```

```python
import functools

import jax
import jax.numpy as jnp
from jax import lax
from jax.experimental import pallas as pl
from jax.experimental.pallas import tpu as pltpu
from jax.sharding import PartitionSpec as P

D = 2048
HD = 128
PROMPT = 1024
CONT = 4
CLEN = 128
GLEN = 1536


EPSILON = 1e-06
MASKED_LOGIT = -1e30
BIG_VMEM = 60 * 1024 * 1024
SHORT = pl.CostEstimate(flops=1000, bytes_accessed=1000, transcendentals=0)


def feature_map(values):
    return jnp.where(values > 0, values + 1.0, jnp.exp(jnp.minimum(values, 0.0)))


def feature_slope(values):
    return jnp.where(values > 0, 1.0, jnp.exp(jnp.minimum(values, 0.0)))


def split_two(value):
    high = value.astype(jnp.bfloat16)
    return high, (value - high.astype(jnp.float32)).astype(jnp.bfloat16)


def wide_dot(left, right, dims):
    left_high, left_low = split_two(left)
    right_high, right_low = split_two(right)

    def one(a, b):
        return lax.dot_general(a, b, (dims, ((), ())), preferred_element_type=jnp.float32)

    return one(left_high, right_high) + one(left_high, right_low) + one(left_low, right_high)


def narrow_dot(left, right, dims):
    right_high, right_low = split_two(right)

    def one(b):
        return lax.dot_general(left, b, (dims, ((), ())), preferred_element_type=jnp.float32)

    return one(right_high) + one(right_low)


def plain_dot(left, right, dims):
    return lax.dot_general(left, right, (dims, ((), ())), preferred_element_type=jnp.float32)


NN = ((1,), (0,))
NT = ((1,), (1,))
TN = ((0,), (0,))
QT = 256
PROMPT_TILES = PROMPT // QT
TILES = GLEN // QT


def tile_scores(tile, q, k_ref, offsets_ref, lengths_ref):
    scale = HD ** (-0.5)
    row = lax.broadcasted_iota(jnp.int32, (QT, QT), 0)
    column = lax.broadcasted_iota(jnp.int32, (QT, QT), 1)
    seen = min(tile * QT, PROMPT)
    own = plain_dot(q, k_ref[tile * QT : (tile + 1) * QT], NT) * scale
    if tile < PROMPT_TILES:
        own = jnp.where(row >= column, own, MASKED_LOGIT)
        ahead = plain_dot(q, k_ref[:seen], NT) * scale if seen else None
        return ahead, own, seen
    first = (tile - PROMPT_TILES) * (QT // CLEN)
    upper = lax.broadcasted_iota(jnp.int32, (QT, 1), 0) >= CLEN
    limit = jnp.where(upper, offsets_ref[first + 1], offsets_ref[first])
    live = jnp.where(upper, lengths_ref[first + 1] + CLEN, lengths_ref[first])
    same = (row >= CLEN) == (column >= CLEN)
    own = jnp.where((row >= column) & same & (column < live), own, MASKED_LOGIT)
    ahead = plain_dot(q, k_ref[:seen], NT) * scale
    position = lax.broadcasted_iota(jnp.int32, (QT, PROMPT), 1)
    return jnp.where(position < limit, ahead, MASKED_LOGIT), own, seen


def attend_kernel(
    size, offsets_ref, lengths_ref, gate_ref, qkv_ref, memory_ref, norm_ref, cot_ref,
    attn_ref, dot_ref, part_ref, logsum_ref, memory_new_ref, norm_new_ref, all_cot_ref,
    send, receive, own,
):
    head = pl.program_id(0)
    gather = Gather(size, cot_ref, all_cot_ref, send, receive, own)

    @pl.when(head == 0)
    def _():
        gather.start(hold=False)

    gate = gate_ref[head]
    q_ref, k_ref, v_ref = qkv_ref.at[0, 0], qkv_ref.at[1, 0], qkv_ref.at[2, 0]
    memory_one = memory_ref[0]
    norm_one = norm_ref[0]
    for tile in range(TILES):
        rows = slice(tile * QT, (tile + 1) * QT)
        q = q_ref[rows]
        ahead, own, seen = tile_scores(tile, q, k_ref, offsets_ref, lengths_ref)
        peak = jnp.max(own, axis=1, keepdims=True)
        if ahead is not None:
            peak = jnp.maximum(peak, jnp.max(ahead, axis=1, keepdims=True))
        own = jnp.exp(own - peak)
        total = jnp.sum(own, axis=1, keepdims=True)
        dot_part = plain_dot(own.astype(jnp.bfloat16), v_ref[rows], NN)
        if ahead is not None:
            ahead = jnp.exp(ahead - peak)
            total += jnp.sum(ahead, axis=1, keepdims=True)
            dot_part += plain_dot(ahead.astype(jnp.bfloat16), v_ref[:seen], NN)
        dot_part = dot_part / total
        lifted = feature_map(q.astype(jnp.float32))
        memory_part = wide_dot(lifted, memory_one, NN) / jnp.sum(
            lifted * norm_one, axis=1, keepdims=True
        )
        attn_ref[rows, :] = (gate * memory_part + (1.0 - gate) * dot_part).astype(jnp.bfloat16)
        dot_ref[0, rows, :] = dot_part
        part_ref[0, rows, :] = memory_part
        logsum_ref[0, rows, :] = peak + jnp.log(total)
    lifted_keys = feature_map(k_ref[:PROMPT].astype(jnp.float32))
    high, low = split_two(lifted_keys)
    v = v_ref[:PROMPT]
    memory_new_ref[0] = memory_one + (plain_dot(high, v, TN) + plain_dot(low, v, TN)) / PROMPT
    norm_new_ref[0] = norm_one + jnp.mean(lifted_keys, axis=0, keepdims=True)

    @pl.when(head == pl.num_programs(0) - 1)
    def _():
        gather.forward()
        for step in range(size - 1):
            gather.wait(step)
        gather.keep.wait()
        gather.finish()


def head_block(shape, lead=0):
    zeros = (0,) * (len(shape) - 1 - lead)
    return pl.BlockSpec(shape, lambda h: (0,) * lead + (h,) + zeros)


SMEM_SPEC = pl.BlockSpec(memory_space=pltpu.SMEM)


def attend(size, cot, heads_all, memory_one, norm_one, offsets, lengths, gate_value):
    heads = heads_all.shape[1]
    f32 = jnp.float32
    row_block = head_block((1, GLEN, HD))
    column = pl.BlockSpec((GLEN, HD), lambda h: (0, h))
    return pl.pallas_call(
        functools.partial(attend_kernel, size),
        grid=(heads,),
        in_specs=[
            SMEM_SPEC, SMEM_SPEC, SMEM_SPEC,
            head_block((3, 1, GLEN, HD), 1), head_block((1, HD, HD)), head_block((1, 1, HD)),
            ANY,
        ],
        out_specs=[
            column, row_block, row_block, head_block((1, GLEN, 1)),
            head_block((1, HD, HD)), head_block((1, 1, HD)), ANY,
        ],
        out_shape=[
            jax.ShapeDtypeStruct((GLEN, heads * HD), jnp.bfloat16),
            jax.ShapeDtypeStruct((heads, GLEN, HD), f32),
            jax.ShapeDtypeStruct((heads, GLEN, HD), f32),
            jax.ShapeDtypeStruct((heads, GLEN, 1), f32),
            jax.ShapeDtypeStruct((heads, HD, HD), f32),
            jax.ShapeDtypeStruct((heads, 1, HD), f32),
            bf(size, GLEN // size, D),
        ],
        scratch_shapes=[dma(Gather.semaphores(size)), dma(Gather.semaphores(size)), pltpu.SemaphoreType.DMA],
        compiler_params=comm_params(9),
        cost_estimate=SHORT,
        name="attend",
    )(offsets, lengths, gate_value, heads_all, memory_one, norm_one[:, None, :], cot)


def attend_back_kernel(
    offsets_ref, lengths_ref, gate_ref, qkv_ref, grad_ref, dot_ref, part_ref, logsum_ref,
    memory_ref, norm_ref, out_ref, gate_out_ref, key_sum, value_sum,
):
    head = pl.program_id(0)
    gate = gate_ref[head]
    keep = 1.0 - gate
    scale = HD ** (-0.5)
    q_ref, k_ref, v_ref = qkv_ref.at[0, 0], qkv_ref.at[1, 0], qkv_ref.at[2, 0]
    memory_one = memory_ref[0]
    norm_one = norm_ref[0]
    gate_row = jnp.zeros((1, HD), jnp.float32)
    key_sum[...] = jnp.zeros_like(key_sum)
    value_sum[...] = jnp.zeros_like(value_sum)
    for tile in range(TILES):
        rows = slice(tile * QT, (tile + 1) * QT)
        q = q_ref[rows]
        grad = grad_ref[0, rows, :]
        grad_float = grad.astype(jnp.float32)
        memory_part = part_ref[0, rows, :]
        dot_part = dot_ref[0, rows, :]
        against_dot = jnp.sum(grad_float * dot_part, axis=1, keepdims=True)
        gate_row += jnp.sum(grad_float * (memory_part - dot_part), axis=0, keepdims=True)
        logsum = logsum_ref[0, rows, :]
        ahead, own, seen = tile_scores(tile, q, k_ref, offsets_ref, lengths_ref)
        own = jnp.exp(own - logsum)
        value_sum[rows, :] += plain_dot(own.astype(jnp.bfloat16), grad, TN)
        own = (keep * own * (plain_dot(grad, v_ref[rows], NT) - against_dot)).astype(jnp.bfloat16)
        key_sum[rows, :] += plain_dot(own, q, TN)
        grad_q = plain_dot(own, k_ref[rows], NN)
        if ahead is not None:
            ahead = jnp.exp(ahead - logsum)
            value_sum[:seen, :] += plain_dot(ahead.astype(jnp.bfloat16), grad, TN)
            ahead = (keep * ahead * (plain_dot(grad, v_ref[:seen], NT) - against_dot)).astype(
                jnp.bfloat16
            )
            key_sum[:seen, :] += plain_dot(ahead, q, TN)
            grad_q += plain_dot(ahead, k_ref[:seen], NN)
        q_float = q.astype(jnp.float32)
        lifted = feature_map(q_float)
        inverse = gate / jnp.sum(lifted * norm_one, axis=1, keepdims=True)
        against_memory = jnp.sum(grad_float * memory_part, axis=1, keepdims=True)
        grad_lifted = inverse * (narrow_dot(grad, memory_one, NT) - against_memory * norm_one)
        out_ref[0, rows, :] = (grad_q * scale + grad_lifted * feature_slope(q_float)).astype(
            jnp.bfloat16
        )
    out_ref[1, :, :] = (key_sum[...] * scale).astype(jnp.bfloat16)
    out_ref[2, :, :] = (value_sum[...] * keep).astype(jnp.bfloat16)
    gate_out_ref[0] = gate_row


def attend_back(heads_all, grad_heads, dot_part, memory_part, logsum, memory_one, norm_one, offsets, lengths, gate_value):
    heads = heads_all.shape[1]
    f32 = jnp.float32
    row_block = head_block((1, GLEN, HD))
    return pl.pallas_call(
        attend_back_kernel,
        grid=(heads,),
        in_specs=[
            SMEM_SPEC, SMEM_SPEC, SMEM_SPEC,
            head_block((3, 1, GLEN, HD), 1), row_block, row_block, row_block,
            head_block((1, GLEN, 1)), head_block((1, HD, HD)), head_block((1, 1, HD)),
        ],
        out_specs=[
            pl.BlockSpec((3, GLEN, HD), lambda h: (0, 0, h)),
            head_block((1, 1, HD)),
        ],
        out_shape=[
            jax.ShapeDtypeStruct((3, GLEN, heads * HD), jnp.bfloat16),
            jax.ShapeDtypeStruct((heads, 1, HD), f32),
        ],
        scratch_shapes=[pltpu.VMEM((GLEN, HD), f32), pltpu.VMEM((GLEN, HD), f32)],
        compiler_params=pltpu.CompilerParams(vmem_limit_bytes=BIG_VMEM),
        cost_estimate=SHORT,
        name="attend_back",
    )(
        offsets, lengths, gate_value, heads_all, grad_heads, dot_part, memory_part, logsum,
        memory_one, norm_one[:, None, :],
    )


ANY = pl.BlockSpec(memory_space=pl.ANY)
VMEM = pl.BlockSpec(memory_space=pltpu.VMEM)
MESH_ID = pl.DeviceIdType.MESH
HALF = D // 2
AG_CUTS = 4


def remote(source, target, send, receive, device):
    return pltpu.make_async_remote_copy(
        src_ref=source, dst_ref=target, send_sem=send, recv_sem=receive,
        device_id=device, device_id_type=MESH_ID,
    )


def here():
    return lax.axis_index("row"), lax.axis_index("col")


def greet(peers):
    barrier = pltpu.get_barrier_semaphore()
    for peer in peers:
        pl.semaphore_signal(barrier, inc=1, device_id=peer, device_id_type=MESH_ID)
    pl.semaphore_wait(barrier, len(peers))


def square(row):
    along_x = (row // 2) * 2 + (1 - lax.rem(row, 2))
    along_y = lax.rem(row + 2, 4)
    across = (along_y // 2) * 2 + (1 - lax.rem(along_y, 2))
    return along_x, along_y, across


class Gather:
    def __init__(self, size, source, land, send, receive, own):
        self.size = size
        row, col = self.row, self.col = here()
        piece = source.shape[0]
        self.keep = pltpu.make_async_copy(source, land.at[row], own)
        if size != 4:
            self.peers = [(lax.rem(row + d, size), col) for d in range(1, size)]
            self.order = [lax.rem(row + size - d, size) for d in range(1, size)]
            self.copies = [
                remote(source, land.at[row], send.at[i], receive.at[i], peer) for i, peer in enumerate(self.peers)
            ]
            return
        self.order = rx, ry, rd = square(row)
        px, py = self.peers = [(rx, col), (ry, col)]
        height = piece // AG_CUTS
        cuts = [pl.ds(cut * height, height) for cut in range(AG_CUTS)]

        def out(cut, base, peer):
            return remote(
                source.at[cuts[cut]], land.at[row, cuts[cut]], send.at[base + cut], receive.at[base + cut], peer
            )

        def onward(cut, owner, peer):
            place = land.at[owner, cuts[cut]]
            return remote(place, place, send.at[2 * AG_CUTS + cut], receive.at[2 * AG_CUTS + cut], peer)

        middle = AG_CUTS // 2
        self.to_x = [out(cut, 0, px) for cut in range(AG_CUTS)]
        self.to_y = [out(cut, AG_CUTS, py) for cut in range(AG_CUTS)]
        self.onward = [onward(cut, rx, py) for cut in range(middle)] + [
            onward(cut, ry, px) for cut in range(middle, AG_CUTS)
        ]

    @staticmethod
    def semaphores(size):
        return 3 * AG_CUTS if size == 4 else size - 1

    def start(self, greeted=False, hold=True):
        if not greeted:
            greet(self.peers)
        if self.size != 4:
            for copy in self.copies:
                copy.start()
        else:
            for step in range(AG_CUTS):
                self.to_x[step].start()
                self.to_y[(step + AG_CUTS // 2) % AG_CUTS].start()
        self.keep.start()
        if hold:
            self.keep.wait()

    def forward(self):
        if self.size != 4:
            return
        for step in range(AG_CUTS // 2):
            later = step + AG_CUTS // 2
            self.to_x[step].wait_recv()
            self.onward[step].start()
            self.to_y[later].wait_recv()
            self.onward[later].start()

    def wait(self, step):
        middle = AG_CUTS // 2
        if self.size != 4:
            waits = [self.copies[step]]
        else:
            waits = (self.to_x[middle:], self.to_y[:middle], self.onward)[step]
        for copy in waits:
            copy.wait_recv()
        return self.order[step]

    def finish(self):
        for copy in self.copies if self.size != 4 else [*self.to_x, *self.to_y, *self.onward]:
            copy.wait_send()


class Scatter:
    def __init__(self, size, stage, land, total, send, receive):
        self.size, self.stage, self.land, self.total = size, stage, land, total
        self.send, self.receive = send, receive
        self.row, self.col = lax.axis_index("row"), lax.axis_index("col")

    @staticmethod
    def semaphores(size):
        return 6 if size == 4 else size - 1

    @staticmethod
    def stage_shape(size, piece):
        return (3 if size == 4 else size - 1, 2, piece, HALF)

    @staticmethod
    def land_shape(size, piece):
        return (6, piece, HALF) if size == 4 else (size - 1, 2, piece, HALF)

    def copy(self, index, source, peer):
        return remote(source, self.land.at[index], self.send.at[index], self.receive.at[index], peer)

    def run(self, partial, between=None, late=None):
        row, col = self.row, self.col

        def into(slot):
            def store(half, columns, value):
                self.stage[slot, half, :, columns] = value.astype(jnp.bfloat16)

            return store

        def into_total(half, columns, value):
            self.total[half, :, columns] = value

        if self.size != 4:
            peers = [lax.rem(row + d, self.size) for d in range(1, self.size)]
            greet([(peer, col) for peer in peers])
            copies = []
            for slot, peer in enumerate(peers):
                partial(peer, into(slot))
                copies.append(self.copy(slot, self.stage.at[slot], (peer, col)))
                copies[-1].start()
            partial(row, into_total)
            if between is not None:
                between()
            if late is not None:
                late()
            for slot, copy in enumerate(copies):
                copy.wait_recv()
                self.add_total(0, self.land.at[slot, 0])
                self.add_total(1, self.land.at[slot, 1])
            for copy in copies:
                copy.wait_send()
            return
        rx, ry, rd = square(row)
        px, py = (rx, col), (ry, col)
        greet([px, py])
        partial(rd, into(0))
        first = [self.copy(0, self.stage.at[0, 0], px), self.copy(1, self.stage.at[0, 1], py)]
        for copy in first:
            copy.start()
        partial(rx, into(1))
        first.append(self.copy(2, self.stage.at[1, 0], px))
        first[2].start()
        partial(ry, into(2))
        first.append(self.copy(3, self.stage.at[2, 1], py))
        first[3].start()
        if between is not None:
            between()
        first[0].wait_recv()
        self.add_stage(2, 0, self.land.at[0])
        second = [self.copy(4, self.stage.at[2, 0], py)]
        second[0].start()
        first[1].wait_recv()
        self.add_stage(1, 1, self.land.at[1])
        second.append(self.copy(5, self.stage.at[1, 1], px))
        second[1].start()
        partial(row, into_total)
        if late is not None:
            late()
        first[2].wait_recv()
        self.add_total(0, self.land.at[2])
        first[3].wait_recv()
        self.add_total(1, self.land.at[3])
        second[0].wait_recv()
        self.add_total(0, self.land.at[4])
        second[1].wait_recv()
        self.add_total(1, self.land.at[5])
        for copy in first + second:
            copy.wait_send()

    def add_stage(self, slot, half, landed):
        @pl.loop(0, landed.shape[0] // STRIP)
        def _(i):
            rows = pl.ds(pl.multiple_of(i * STRIP, STRIP), STRIP)
            value = self.stage[slot, half, rows, :].astype(jnp.float32) + landed[rows, :].astype(jnp.float32)
            self.stage[slot, half, rows, :] = value.astype(jnp.bfloat16)

    def add_total(self, half, landed):
        @pl.loop(0, landed.shape[0] // STRIP)
        def _(i):
            rows = pl.ds(pl.multiple_of(i * STRIP, STRIP), STRIP)
            self.total[half, rows, :] += landed[rows, :].astype(jnp.float32)


STRIP = 32


def scatter_scratch(size, piece):
    count = Scatter.semaphores(size)
    return [
        pltpu.VMEM(Scatter.stage_shape(size, piece), jnp.bfloat16),
        pltpu.VMEM(Scatter.land_shape(size, piece), jnp.bfloat16),
        pltpu.VMEM((2, piece, HALF), jnp.float32),
        pltpu.SemaphoreType.DMA((count,)),
        pltpu.SemaphoreType.DMA((count,)),
    ]


def gather_scratch(size, piece):
    count = Gather.semaphores(size)
    return [
        pltpu.VMEM((size, piece, D), jnp.bfloat16),
        pltpu.SemaphoreType.DMA((count,)),
        pltpu.SemaphoreType.DMA((count,)),
        pltpu.SemaphoreType.DMA,
    ]


def fetches(pairs, semaphores):
    copies = [pltpu.make_async_copy(a, b, semaphores.at[i]) for i, (a, b) in enumerate(pairs)]
    for copy in copies:
        copy.start()
    return copies


def wait_all(copies):
    for copy in copies:
        copy.wait()


def tiles_of(width, tile):
    def run(body):
        @pl.loop(0, width // tile)
        def _(t):
            body(t, pl.ds(pl.multiple_of(t * tile, tile), tile))

    return run


def comm_params(identity):
    return pltpu.CompilerParams(
        collective_id=identity, has_side_effects=True, vmem_limit_bytes=BIG_VMEM
    )


def bf(*shape):
    return jax.ShapeDtypeStruct(shape, jnp.bfloat16)


def fl(*shape):
    return jax.ShapeDtypeStruct(shape, jnp.float32)


def project_heads(size, normed, w_all):
    piece = normed.shape[0]
    cols, _, depth, width = w_all.shape
    heads = width // HD

    def kernel(
        x_ref, w_ref, heads_ref, all_ref,
        land, send, receive, own, w, w_sem, all_sem,
    ):
        loads = fetches([(w_ref.at[c], w.at[:, pl.ds(c * depth, depth), :]) for c in range(cols)], w_sem)
        gather = Gather(size, x_ref, land, send, receive, own)
        gather.start()

        def compute(row, slot):
            store = pltpu.make_async_copy(land.at[row], all_ref.at[row], all_sem.at[slot])
            store.start()
            rows = pl.ds(pl.multiple_of(row * piece, piece), piece)

            @pl.loop(0, 3)
            def _(j):
                value = jnp.dot(land[row], w[j], preferred_element_type=jnp.float32).astype(jnp.bfloat16)
                for head in range(heads):
                    heads_ref[j, head, rows, :] = value[:, head * HD : (head + 1) * HD]

            return store

        wait_all(loads)
        stores = [compute(gather.row, 0)]
        gather.forward()
        for step in range(size - 1):
            stores.append(compute(gather.wait(step), step + 1))
        wait_all(stores)
        gather.finish()

    return pl.pallas_call(
        kernel,
        out_shape=[bf(3, heads, GLEN, HD), bf(size, piece, D)],
        in_specs=[ANY, ANY],
        out_specs=[VMEM, ANY],
        scratch_shapes=gather_scratch(size, piece)
        + [
            pltpu.VMEM((3, D, width), jnp.bfloat16),
            pltpu.SemaphoreType.DMA((cols,)),
            pltpu.SemaphoreType.DMA((size,)),
        ],
        compiler_params=comm_params(1),
        cost_estimate=SHORT,
        name="project_heads",
    )(normed, w_all)


def strip_loop(piece, body):
    @pl.loop(0, piece // STRIP)
    def _(i):
        body(pl.ds(pl.multiple_of(i * STRIP, STRIP), STRIP))


def row_mean(first, second):
    return (jnp.sum(first, axis=1, keepdims=True) + jnp.sum(second, axis=1, keepdims=True)) / D


def lanes(first, second):
    lane = lax.broadcasted_iota(jnp.int32, (STRIP, HD), 1)
    return jnp.where(lane == 0, first, jnp.where(lane == 1, second, 0.0))


LEFT, RIGHT = slice(0, HALF), slice(HALF, D)


def branch_out(size, attn, w_all, x, gain):
    piece = GLEN // size
    cols, width, depth = w_all.shape

    def kernel(attn_ref, w_ref, x_ref, gain_ref, middle_ref, normed_ref, stat_ref, stage, land, total, send, receive, w, w_sem):
        loads = fetches([(w_ref.at[c], w.at[:, pl.ds(c * depth, depth)]) for c in range(cols)], w_sem)
        scatter = Scatter(size, stage, land, total, send, receive)
        wait_all(loads)

        def partial(row, store):
            rows = pl.ds(pl.multiple_of(row * piece, piece), piece)
            left = attn_ref[rows, :]
            for half in range(2):
                for t in range(2):
                    columns = slice(half * HALF + t * HALF // 2, half * HALF + (t + 1) * HALF // 2)
                    store(
                        half, slice(t * HALF // 2, (t + 1) * HALF // 2),
                        jnp.dot(left, w[:, columns], preferred_element_type=jnp.float32),
                    )

        scatter.run(partial)

        def finish(rows):
            branch = (total[0, rows, :], total[1, rows, :])
            middle = (
                x_ref[rows, LEFT].astype(jnp.float32) + branch[0],
                x_ref[rows, RIGHT].astype(jnp.float32) + branch[1],
            )
            mean = row_mean(middle[0] * middle[0], middle[1] * middle[1])
            inverse = lax.rsqrt(mean + EPSILON)
            for part, columns in zip(middle, (LEFT, RIGHT)):
                middle_ref[rows, columns] = part
                normed_ref[rows, columns] = (part * inverse * gain_ref[:, columns]).astype(jnp.bfloat16)
            stat_ref[rows, :] = lanes(row_mean(branch[0] * branch[0], branch[1] * branch[1]), mean)

        strip_loop(piece, finish)

    return pl.pallas_call(
        kernel,
        out_shape=[fl(piece, D), bf(piece, D), fl(piece, HD)],
        in_specs=[VMEM, ANY, VMEM, VMEM],
        out_specs=[VMEM, VMEM, VMEM],
        scratch_shapes=scatter_scratch(size, piece)
        + [pltpu.VMEM((width, D), jnp.bfloat16), pltpu.SemaphoreType.DMA((cols,))],
        compiler_params=comm_params(2),
        cost_estimate=SHORT,
        name="branch_out",
    )(attn, w_all, x, gain)


def feed_forward(size, tokens, pack, cot, first):
    piece = GLEN // size
    cols, _, depth, wide = pack.shape
    tile = min(wide, 512)
    count = wide // tile

    def kernel(x_ref, pack_ref, cot_ref, hidden_ref, grad_ref, *rest):
        if first:
            all_ref, land, send, receive, own, all_sem, *rest = rest
        else:
            land, own, *rest = rest
        w, cot_all, back, stage, w_sem, cot_sem, out_sem = rest
        if first:
            gather = Gather(size, x_ref, land, send, receive, own)
            gather.start()
            order = [gather.row, *gather.order]
        else:
            order = list(range(size))
        w_loads = fetches(
            [(pack_ref.at[c, j], w.at[j, pl.ds(c * depth, depth), :]) for j in (2, 0, 1) for c in range(cols)], w_sem
        )
        cot_loads = fetches([(cot_ref.at[row], cot_all.at[row]) for row in order], cot_sem)
        if not first:
            x_loads = fetches([(x_ref.at[row], land.at[row]) for row in order], own)

        def backward(step):
            row = order[step]
            cot_loads[step].wait()

            @tiles_of(wide, tile)
            def _(t, columns):
                back[row, :, columns] = plain_dot(cot_all[row], w[2, :, columns], NN).astype(jnp.bfloat16)

        def moves(row, slot, columns):
            rows = pl.ds(pl.multiple_of(row * piece, piece), piece)
            return [
                pltpu.make_async_copy(stage.at[slot, 0], hidden_ref.at[rows, columns], out_sem.at[slot, 0]),
                pltpu.make_async_copy(stage.at[slot, 1], grad_ref.at[0, rows, columns], out_sem.at[slot, 1]),
                pltpu.make_async_copy(stage.at[slot, 2], grad_ref.at[1, rows, columns], out_sem.at[slot, 2]),
            ]

        def compute(step):
            row = order[step]
            if first:
                store = pltpu.make_async_copy(land.at[row], all_ref.at[row], all_sem)
                store.start()

            @pl.loop(0, count)
            def _(t):
                columns = pl.ds(pl.multiple_of(t * tile, tile), tile)
                slot = lax.rem(t, 2)
                x = land[row]
                gate_pre = jnp.dot(x, w[0, :, columns], preferred_element_type=jnp.float32)
                up_pre = jnp.dot(x, w[1, :, columns], preferred_element_type=jnp.float32)
                sigmoid = jax.nn.sigmoid(gate_pre)
                silu = gate_pre * sigmoid
                grad_hidden = back[row, :, columns].astype(jnp.float32)

                @pl.when(t >= 2)
                def _():
                    wait_all(moves(row, slot, columns))

                stage[slot, 0] = (silu * up_pre).astype(jnp.bfloat16)
                stage[slot, 1] = (grad_hidden * up_pre * (sigmoid + silu * (1.0 - sigmoid))).astype(jnp.bfloat16)
                stage[slot, 2] = (grad_hidden * silu).astype(jnp.bfloat16)
                for move in moves(row, slot, columns):
                    move.start()

            for slot in range(min(2, count)):
                wait_all(moves(row, slot, pl.ds(slot * tile, tile)))
            if first:
                store.wait()

        wait_all(w_loads[:cols])
        backward(0)
        if first:
            gather.forward()
        for step in range(1, size):
            backward(step)
        wait_all(w_loads[cols:])
        for step in range(size):
            if not first:
                x_loads[step].wait()
            elif step:
                gather.wait(step - 1)
            compute(step)
        if first:
            gather.finish()

    out_shape = [bf(GLEN, wide), bf(2, GLEN, wide)]
    if first:
        out_shape.append(bf(size, piece, D))
        scratch = gather_scratch(size, piece) + [pltpu.SemaphoreType.DMA]
    else:
        scratch = [pltpu.VMEM((size, piece, D), jnp.bfloat16), dma(size)]
    return pl.pallas_call(
        kernel,
        out_shape=out_shape,
        in_specs=[ANY] * 3,
        out_specs=[ANY] * len(out_shape),
        scratch_shapes=scratch
        + [
            pltpu.VMEM((3, D, wide), jnp.bfloat16),
            pltpu.VMEM((size, piece, D), jnp.bfloat16),
            pltpu.VMEM((size, piece, wide), jnp.bfloat16),
            pltpu.VMEM((2, 3, piece, tile), jnp.bfloat16),
            dma(3 * cols), dma(size), dma(2, 3),
        ],
        compiler_params=comm_params(3) if first else pltpu.CompilerParams(vmem_limit_bytes=BIG_VMEM),
        cost_estimate=SHORT,
        name="feed_first" if first else "feed_second",
    )(tokens, pack, cot)


def weight_grads_kernel(x_ref, y_ref, g_ref, h_ref, out_ref):
    for j in range(2):
        out_ref[j] = plain_dot(x_ref[...], g_ref[j], TN).astype(jnp.bfloat16)
    out_ref[2] = plain_dot(y_ref[...], h_ref[...], TN).astype(jnp.bfloat16)


def weight_grads(x, grads, y, hidden):
    wide = hidden.shape[1]
    tile = 256
    block = pl.BlockSpec((GLEN, tile), lambda i: (0, i))
    return pl.pallas_call(
        weight_grads_kernel,
        grid=(D // tile,),
        in_specs=[
            block, block,
            pl.BlockSpec((2, GLEN, wide), lambda i: (0, 0, 0), pipeline_mode=pl.Buffered(1)),
            pl.BlockSpec((GLEN, wide), lambda i: (0, 0), pipeline_mode=pl.Buffered(1)),
        ],
        out_specs=pl.BlockSpec((3, tile, wide), lambda i: (0, i, 0)),
        out_shape=bf(3, D, wide),
        compiler_params=pltpu.CompilerParams(vmem_limit_bytes=BIG_VMEM),
        cost_estimate=SHORT,
        name="weight_grads",
    )(x, y, grads, hidden)


def norm_back(rows, total, stream, inverse, gain_ref, base, store, gain_sum):
    u = [total[half, rows, :] * gain_ref[:, columns] for half, columns in enumerate((LEFT, RIGHT))]
    inner = row_mean(u[0] * stream[0], u[1] * stream[1]) * inverse * inverse * inverse
    for half, columns in enumerate((LEFT, RIGHT)):
        store(columns, base[half] + inverse * u[half] - stream[half] * inner)
        gain_sum[:, columns] += jnp.sum(total[half, rows, :] * stream[half] * inverse, axis=0, keepdims=True)


def middle_back(size, grads, packs, middle, cot, gain):
    piece = middle.shape[0]
    cols, _, depth, wide = packs[0].shape
    tile = 512
    halves = len(packs)

    def kernel(
        *refs,
    ):
        g_refs, pack_refs, refs = refs[:halves], refs[halves : 2 * halves], refs[2 * halves :]
        (middle_ref, cot_ref, gain_ref, grad_ref, low_ref, gain_sum,
         stage, land, total, send, receive, w, g, w_sem, g_sem) = refs
        row, _ = here()
        rows_order = [*reversed(square(row)), row] if size == 4 else [lax.rem(row + d, size) for d in range(size)]
        if size == 4:
            rows_order = [rows_order[0], rows_order[2], rows_order[1], row]

        def piece_rows(at):
            return pl.ds(pl.multiple_of(at * piece, piece), piece)

        def g_load(h, at):
            return pltpu.make_async_copy(
                g_refs[h].at[:, piece_rows(at)], g.at[h, :, piece_rows(at)], g_sem.at[h, at]
            )

        def w_load(h, c):
            return pltpu.make_async_copy(
                pack_refs[h].at[c, pl.ds(0, 2)], w.at[h, :, pl.ds(c * depth, depth), :], w_sem.at[h, c]
            )

        for h in range(halves):
            g_load(h, rows_order[0]).start()
        for c in range(cols):
            for h in range(halves):
                w_load(h, c).start()
        for at in rows_order[1:]:
            for h in range(halves):
                g_load(h, at).start()
        scatter = Scatter(size, stage, land, total, send, receive)
        gain_sum[...] = jnp.zeros_like(gain_sum)
        calls = []

        def one(rows, depth_rows, store, half, columns):
            value = 0.0
            for h in range(halves):
                for j in range(2):
                    value += plain_dot(g[h, j, rows, :], w[h, j, depth_rows, :], NT)
            store(half, columns, value)

        def partial(at, store):
            fresh = not calls
            calls.append(at)
            for h in range(halves):
                g_load(h, at).wait()
            rows = piece_rows(at)
            if fresh:
                for t in range(D // tile):
                    for c in range(t * tile // depth, (t + 1) * tile // depth):
                        for h in range(halves):
                            w_load(h, c).wait()
                    half, inside = divmod(t * tile, HALF)
                    one(rows, slice(t * tile, (t + 1) * tile), store, half, slice(inside, inside + tile))
                return
            for half in range(2):
                @pl.loop(0, HALF // tile)
                def _(t):
                    columns = pl.ds(pl.multiple_of(t * tile, tile), tile)
                    one(rows, pl.ds(pl.multiple_of(half * HALF + t * tile, tile), tile), store, half, columns)

        scatter.run(partial)

        def finish(rows):
            stream = [middle_ref[rows, columns] for columns in (LEFT, RIGHT)]
            base = [cot_ref[rows, columns].astype(jnp.float32) for columns in (LEFT, RIGHT)]
            inverse = lax.rsqrt(row_mean(stream[0] * stream[0], stream[1] * stream[1]) + EPSILON)

            def store(columns, value):
                grad_ref[rows, columns] = value
                low_ref[rows, columns] = value.astype(jnp.bfloat16)

            norm_back(rows, total, stream, inverse, gain_ref, base, store, gain_sum)

        strip_loop(piece, finish)

    return pl.pallas_call(
        kernel,
        out_shape=[fl(piece, D), bf(piece, D), fl(1, D)],
        in_specs=[ANY] * (2 * halves) + [VMEM] * 3,
        out_specs=[VMEM, VMEM, VMEM],
        scratch_shapes=scatter_scratch(size, piece)
        + [
            pltpu.VMEM((halves, 2, D, wide), jnp.bfloat16),
            pltpu.VMEM((halves, 2, GLEN, wide), jnp.bfloat16),
            dma(halves, cols), dma(halves, size),
        ],
        compiler_params=comm_params(4),
        cost_estimate=SHORT,
        name="middle_back",
    )(*grads, *packs, middle, cot, gain)


def blocked_store(ref, rows, depth, columns, value):
    for i in range(value.shape[1] // depth):
        ref[columns.start // depth + i, rows, :] = value[:, i * depth : (i + 1) * depth]


def ffn_out(size, hiddens, packs, middle):
    piece = middle.shape[0]
    cols, _, depth, wide = packs[0].shape
    tile = 512
    halves = len(packs)

    def kernel(*refs):
        h_refs, pack_refs, refs = refs[:halves], refs[halves : 2 * halves], refs[2 * halves :]
        middle_ref, out_ref, stat_ref, stage, land, total, send, receive, w, w_sem = refs

        def w_load(h, c):
            return pltpu.make_async_copy(
                pack_refs[h].at[c, 2], w.at[h, pl.ds(c * depth, depth), :], w_sem.at[h, c]
            )

        for c in range(cols):
            for h in range(halves):
                w_load(h, c).start()
        scatter = Scatter(size, stage, land, total, send, receive)
        calls = []

        def one(rows, depth_rows, store, half, columns):
            value = 0.0
            for h in range(halves):
                value += plain_dot(h_refs[h][rows, :], w[h, depth_rows, :], NT)
            store(half, columns, value)

        def partial(at, store):
            fresh = not calls
            calls.append(at)
            rows = pl.ds(pl.multiple_of(at * piece, piece), piece)
            if fresh:
                for c in range(cols):
                    for h in range(halves):
                        w_load(h, c).wait()
            for half in range(2):
                @pl.loop(0, HALF // tile)
                def _(t):
                    columns = pl.ds(pl.multiple_of(t * tile, tile), tile)
                    one(rows, pl.ds(pl.multiple_of(half * HALF + t * tile, tile), tile), store, half, columns)

        scatter.run(partial)

        def finish(rows):
            ffn = [total[half, rows, :] for half in range(2)]
            result = [middle_ref[rows, columns] + ffn[half] for half, columns in enumerate((LEFT, RIGHT))]
            for half, columns in enumerate((LEFT, RIGHT)):
                blocked_store(out_ref, rows, depth, columns, result[half].astype(jnp.bfloat16))
            stat_ref[rows, :] = lanes(
                row_mean(ffn[0] * ffn[0], ffn[1] * ffn[1]),
                row_mean(result[0] * result[0], result[1] * result[1]),
            )

        strip_loop(piece, finish)

    return pl.pallas_call(
        kernel,
        out_shape=[bf(cols, piece, depth), fl(piece, HD)],
        in_specs=[VMEM] * halves + [ANY] * halves + [VMEM],
        out_specs=[VMEM, VMEM],
        scratch_shapes=scatter_scratch(size, piece)
        + [pltpu.VMEM((halves, D, wide), jnp.bfloat16), dma(halves, cols)],
        compiler_params=comm_params(5),
        cost_estimate=SHORT,
        name="ffn_out",
    )(*hiddens, *packs, middle)


def branch_back(size, low, w_all):
    piece = low.shape[0]
    cols, width, depth = w_all.shape
    heads = width // HD

    def kernel(x_ref, w_ref, heads_ref, all_ref, land, send, receive, own, w, w_sem, all_sem):
        loads = fetches([(w_ref.at[c], w.at[:, pl.ds(c * depth, depth)]) for c in range(cols)], w_sem)
        gather = Gather(size, x_ref, land, send, receive, own)
        gather.start()

        def compute(row, slot):
            store = pltpu.make_async_copy(land.at[row], all_ref.at[row], all_sem.at[slot])
            store.start()
            rows = pl.ds(pl.multiple_of(row * piece, piece), piece)
            value = plain_dot(land[row], w[...], NT).astype(jnp.bfloat16)
            for head in range(heads):
                heads_ref[head, rows, :] = value[:, head * HD : (head + 1) * HD]
            return store

        wait_all(loads)
        stores = [compute(gather.row, 0)]
        gather.forward()
        for step in range(size - 1):
            stores.append(compute(gather.wait(step), step + 1))
        wait_all(stores)
        gather.finish()

    return pl.pallas_call(
        kernel,
        out_shape=[bf(heads, GLEN, HD), bf(size, piece, D)],
        in_specs=[ANY, ANY],
        out_specs=[VMEM, ANY],
        scratch_shapes=gather_scratch(size, piece)
        + [
            pltpu.VMEM((width, D), jnp.bfloat16),
            pltpu.SemaphoreType.DMA((cols,)),
            pltpu.SemaphoreType.DMA((size,)),
        ],
        compiler_params=comm_params(6),
        cost_estimate=SHORT,
        name="branch_back",
    )(low, w_all)


def stream_back(size, grads, w_all, x, grad_middle, gain):
    piece = x.shape[0]
    cols, _, depth, width = w_all.shape
    tile = 512

    def kernel(
        g_ref, w_ref, x_ref, middle_ref, gain_ref, out_ref, gain_sum,
        stage, land, total, send, receive, w, w_sem,
    ):
        loads = fetches([(w_ref.at[c], w.at[:, pl.ds(c * depth, depth), :]) for c in range(cols)], w_sem)
        scatter = Scatter(size, stage, land, total, send, receive)
        wait_all(loads)
        gain_sum[...] = jnp.zeros_like(gain_sum)

        def partial(row, store):
            rows = pl.ds(pl.multiple_of(row * piece, piece), piece)
            for half in range(2):
                @pl.loop(0, HALF // tile)
                def _(t):
                    columns = pl.ds(pl.multiple_of(t * tile, tile), tile)
                    depth_rows = pl.ds(pl.multiple_of(half * HALF + t * tile, tile), tile)
                    value = plain_dot(g_ref[0, rows, :], w[0, depth_rows, :], NT)
                    for j in (1, 2):
                        value += plain_dot(g_ref[j, rows, :], w[j, depth_rows, :], NT)
                    store(half, columns, value)

        scatter.run(partial)

        def finish(rows):
            stream = [x_ref[rows, columns].astype(jnp.float32) for columns in (LEFT, RIGHT)]
            base = [middle_ref[rows, columns] for columns in (LEFT, RIGHT)]
            inverse = lax.rsqrt(row_mean(stream[0] * stream[0], stream[1] * stream[1]) + EPSILON)

            def store(columns, value):
                blocked_store(out_ref, rows, depth, columns, value.astype(jnp.bfloat16))

            norm_back(rows, total, stream, inverse, gain_ref, base, store, gain_sum)

        strip_loop(piece, finish)

    return pl.pallas_call(
        kernel,
        out_shape=[bf(cols, piece, depth), fl(1, D)],
        in_specs=[VMEM, ANY, VMEM, VMEM, VMEM],
        out_specs=[VMEM, VMEM],
        scratch_shapes=scatter_scratch(size, piece)
        + [pltpu.VMEM((3, D, width), jnp.bfloat16), pltpu.SemaphoreType.DMA((cols,))],
        compiler_params=comm_params(7),
        cost_estimate=SHORT,
        name="stream_back",
    )(grads, w_all, x, grad_middle, gain)


def row_and_col_peers(size, cols):
    row, col = here()
    return [(lax.rem(row + d, size), col) for d in range(1, size)] + [
        (row, lax.rem(col + e, cols)) for e in range(1, cols)
    ]


def dma(*shape):
    return pltpu.SemaphoreType.DMA(shape)


class Inward:
    def __init__(self, size, cols, source, middle, land, first_send, first_receive, send, receive, own):
        self.size, self.cols, self.groups = size, cols, cols // size
        self.source, self.middle, self.land = source, middle, land
        self.first_send, self.first_receive = first_send, first_receive
        self.send, self.receive, self.own = send, receive, own
        self.row, self.col = here()

    @staticmethod
    def scratch(size, cols, piece, depth):
        return [
            pltpu.VMEM((size, cols // size, piece, depth), jnp.bfloat16),
            pltpu.VMEM((cols, piece, depth), jnp.bfloat16),
            dma(size - 1), dma(size - 1), dma(cols), dma(cols), dma(2),
        ]

    def start(self):
        row, col = self.row, self.col
        self.first = []
        for d in range(1, self.size):
            peer = lax.rem(row + d, self.size)
            self.first.append(
                remote(
                    self.source.at[:, peer], self.middle.at[row],
                    self.first_send.at[d - 1], self.first_receive.at[d - 1], (peer, col),
                )
            )
            self.first[-1].start()
        self.keep = pltpu.make_async_copy(self.source.at[:, row], self.middle.at[row], self.own.at[0])
        self.keep.start()

    def forward(self):
        row, col = self.row, self.col
        for d in range(self.size):
            origin = lax.rem(row + self.size - d, self.size)
            if d == 0:
                self.keep.wait()
            else:
                self.first[d - 1].wait_recv()
            for i in range(self.groups):
                group = origin * self.groups + i

                @pl.when(group != col)
                def _():
                    remote(
                        self.middle.at[origin, i], self.land.at[col],
                        self.send.at[group], self.receive.at[col], (row, group),
                    ).start()

                @pl.when(group == col)
                def _():
                    pltpu.make_async_copy(self.middle.at[origin, i], self.land.at[col], self.own.at[1]).start()

    def finish(self):
        row, col = self.row, self.col
        pltpu.make_async_copy(self.middle.at[0, 0], self.land.at[col], self.own.at[1]).wait()
        for e in range(1, self.cols):
            peer = lax.rem(col + e, self.cols)
            remote(
                self.middle.at[0, 0], self.land.at[peer], self.send.at[peer], self.receive.at[peer], (row, peer)
            ).wait()
        for copy in self.first:
            copy.wait_send()


class Outward:
    def __init__(self, size, cols, source, middle, target, first_send, first_receive, send, receive, own):
        self.size, self.cols, self.groups = size, cols, cols // size
        self.source, self.middle, self.target = source, middle, target
        self.first_send, self.first_receive = first_send, first_receive
        self.send, self.receive, self.own = send, receive, own
        self.row, self.col = here()

    @staticmethod
    def scratch(size, cols, piece, depth):
        return [
            pltpu.VMEM((cols, piece, depth), jnp.bfloat16),
            dma(cols - 1), dma(cols - 1), dma(cols), dma(cols), dma(cols // size),
        ]

    def start(self):
        row, col = self.row, self.col
        self.first = []
        for e in range(1, self.cols):
            peer = lax.rem(col + e, self.cols)
            self.first.append(
                remote(
                    self.source.at[peer], self.middle.at[col],
                    self.first_send.at[e - 1], self.first_receive.at[e - 1], (row, peer),
                )
            )
            self.first[-1].start()

    def forward(self):
        row, col = self.row, self.col
        for e in range(self.cols):
            group = lax.rem(col + self.cols - e, self.cols)
            if e:
                self.first[e - 1].wait_recv()
            block = self.middle.at[group] if e else self.source.at[col]
            home, i = group // self.groups, lax.rem(group, self.groups)

            @pl.when(home != row)
            def _():
                remote(
                    block, self.target.at[i, row],
                    self.send.at[group], self.receive.at[i * self.size + row], (home, col),
                ).start()

            @pl.when(home == row)
            def _():
                pltpu.make_async_copy(block, self.target.at[i, row], self.own.at[i]).start()

    def finish(self):
        row, col = self.row, self.col
        for i in range(self.groups):
            pltpu.make_async_copy(self.middle.at[0], self.target.at[i, row], self.own.at[i]).wait()
            for d in range(1, self.size):
                peer = lax.rem(row + d, self.size)
                remote(
                    self.middle.at[0], self.target.at[i, peer],
                    self.send.at[peer * self.groups + i], self.receive.at[i * self.size + peer], (peer, col),
                ).wait()
        for copy in self.first:
            copy.wait_send()


def by_pieces(block, size):
    return block.reshape(block.shape[0] // GLEN, size, GLEN // size, block.shape[1])


def enter(size, cols, stream_in, cotangent, gains):
    pieces = by_pieces(stream_in, size)
    piece, depth = pieces.shape[2:]
    scratch = Inward.scratch(size, cols, piece, depth)

    def kernel(
        x_ref, cot_ref, gains_ref, tokens_ref, normed_ref, gain_in_ref, gain_mid_ref, cot_tokens_ref,
        gains_land, gains_send, gains_receive, *rest,
    ):
        greet(row_and_col_peers(size, cols))
        exchange = Inward(size, cols, x_ref, *rest[: len(scratch)])
        second = Inward(size, cols, cot_ref, *rest[len(scratch) :])
        exchange.start()
        row, col = here()
        copies = []
        for e in range(1, cols):
            peer = lax.rem(col + e, cols)
            copies.append(
                remote(gains_ref, gains_land.at[col], gains_send.at[e - 1], gains_receive.at[e - 1], (row, peer))
            )
            copies[-1].start()
        gains_land[col] = gains_ref[...]
        second.start()
        exchange.forward()
        second.forward()
        for copy in copies:
            copy.wait()
        for c in range(cols):
            gain_in_ref[:, c * depth : (c + 1) * depth] = gains_land[c, 0:1, :]
            gain_mid_ref[:, c * depth : (c + 1) * depth] = gains_land[c, 1:2, :]
        exchange.finish()
        land = exchange.land

        def norm(rows):
            total = jnp.zeros((STRIP, 1), jnp.float32)
            for c in range(cols):
                part = land[c, rows, :]
                tokens_ref[rows, c * depth : (c + 1) * depth] = part
                part = part.astype(jnp.float32)
                total += jnp.sum(part * part, axis=1, keepdims=True)
            inverse = lax.rsqrt(total / D + EPSILON)
            for c in range(cols):
                columns = slice(c * depth, (c + 1) * depth)
                normed_ref[rows, columns] = (
                    land[c, rows, :].astype(jnp.float32) * inverse * gain_in_ref[:, columns]
                ).astype(jnp.bfloat16)

        strip_loop(piece, norm)
        second.finish()

        def assemble(rows):
            for c in range(cols):
                cot_tokens_ref[rows, c * depth : (c + 1) * depth] = second.land[c, rows, :]

        strip_loop(piece, assemble)

    return pl.pallas_call(
        kernel,
        out_shape=[bf(piece, D), bf(piece, D), fl(1, D), fl(1, D), bf(piece, D)],
        in_specs=[ANY, ANY, VMEM],
        out_specs=[VMEM] * 5,
        scratch_shapes=[pltpu.VMEM((cols, 8, depth), jnp.float32), dma(cols - 1), dma(cols - 1)]
        + scratch * 2,
        compiler_params=comm_params(8),
        cost_estimate=SHORT,
        name="enter",
    )(pieces, by_pieces(cotangent, size), jnp.pad(gains, ((0, 6), (0, 0))))


def leave(size, cols, blocks_out, blocks_grad, stats, sums):
    _, piece, depth = blocks_out.shape
    groups = cols // size
    half = len(Outward.scratch(size, cols, piece, depth))

    def kernel(
        out_ref, grad_ref, stats_ref, sums_ref, out_target, grad_target, stats_target, sums_target,
        stats_row, stats_all, sums_col, sums_part, sums_row,
        a_send, a_receive, b_send, b_receive, c_send, c_receive, d_send, d_receive, *rest,
    ):
        row, col = here()
        greet(row_and_col_peers(size, cols))
        grad = Outward(size, cols, grad_ref, rest[0], grad_target, *rest[1:half])
        out = Outward(size, cols, out_ref, rest[half], out_target, *rest[half + 1 :])
        home, slot = col // groups, lax.rem(col, groups)
        col_peers = [lax.rem(col + e, cols) for e in range(1, cols)]
        row_peers = [lax.rem(row + d, size) for d in range(1, size)]

        def sums_first(peer):
            return remote(sums_ref.at[peer], sums_col.at[col], c_send.at[peer], c_receive.at[col], (row, peer))

        for peer in col_peers:
            sums_first(peer).start()
        sums_col[col] = sums_ref[col]

        @pl.when(home != row)
        def _():
            remote(stats_ref, stats_row.at[row], a_send, a_receive.at[row], (home, col)).start()

        @pl.when(home == row)
        def _():
            stats_row[row] = stats_ref[...]

        grad.start()
        out.start()
        for peer in col_peers:
            remote(sums_ref.at[peer], sums_col.at[peer], c_send.at[peer], c_receive.at[peer], (row, peer)).wait()
        total = sums_col[0]
        for c in range(1, cols):
            total += sums_col[c]
        sums_part[...] = total
        sums_row[row] = total
        for peer in row_peers:
            remote(sums_part, sums_row.at[row], d_send.at[peer], d_receive.at[row], (peer, col)).start()

        @pl.when(home == row)
        def _():
            for peer in row_peers:
                remote(stats_ref, stats_row.at[peer], a_send, a_receive.at[peer], (peer, col)).wait_recv()
            for e, peer in enumerate(col_peers):
                remote(stats_row, stats_all.at[slot], b_send.at[e], b_receive.at[slot], (row, peer)).start()
            stats_all[slot] = stats_row[...]

        grad.forward()
        out.forward()
        for peer in row_peers:
            remote(sums_part, sums_row.at[peer], d_send.at[peer], d_receive.at[peer], (peer, col)).wait()
        whole = sums_row[0]
        for r in range(1, size):
            whole += sums_row[r]
        line = lax.broadcasted_iota(jnp.int32, (8, depth), 0)
        sums_target[...] = jnp.where(line < 2, whole, total)

        @pl.when(home == row)
        def _():
            for e, peer in enumerate(col_peers):
                remote(stats_row, stats_all.at[slot], b_send.at[e], b_receive.at[slot], (row, peer)).wait_send()

        @pl.when(home != row)
        def _():
            remote(stats_ref, stats_row.at[row], a_send, a_receive.at[row], (home, col)).wait_send()

        for i in range(groups):
            group = row * groups + i

            @pl.when(group != col)
            def _():
                remote(stats_row, stats_all.at[i], b_send.at[0], b_receive.at[i], (row, group)).wait_recv()

        stats_target[...] = stats_all[...]
        grad.finish()
        out.finish()

    return pl.pallas_call(
        kernel,
        out_shape=[
            bf(groups, size, piece, depth), bf(groups, size, piece, depth),
            fl(groups, size, 8, piece), fl(8, depth),
        ],
        in_specs=[VMEM] * 4,
        out_specs=[ANY, ANY, VMEM, VMEM],
        scratch_shapes=[
            pltpu.VMEM((size, 8, piece), jnp.float32),
            pltpu.VMEM((groups, size, 8, piece), jnp.float32),
            pltpu.VMEM((cols, 8, depth), jnp.float32),
            pltpu.VMEM((8, depth), jnp.float32),
            pltpu.VMEM((size, 8, depth), jnp.float32),
            pltpu.SemaphoreType.DMA, dma(size), dma(cols - 1), dma(groups), dma(cols), dma(cols), dma(size), dma(size),
        ]
        + Outward.scratch(size, cols, piece, depth) * 2,
        compiler_params=comm_params(10),
        cost_estimate=SHORT,
        name="leave",
    )(blocks_out, blocks_grad, stats, sums)


def tokens_contract(left, right):
    return lax.dot_general(left, right, (TN, ((), ())), preferred_element_type=jnp.float32)


def over_col(partial, axis):
    return lax.psum_scatter(partial.astype(jnp.bfloat16), "col", scatter_dimension=axis, tiled=True)


def flat(pieces):
    return pieces.reshape(GLEN, D)


def local(
    stream_in,
    w_qkv,
    w_out,
    w_gate_up,
    w_down,
    gain_attn,
    gain_ffn,
    gate_logit,
    memory,
    memory_norm,
    offsets,
    lengths,
    cotangent,
):
    head_here = memory.shape[1]
    size = lax.axis_size("row")
    cols = lax.axis_size("col")
    all_qkv, all_out = (lax.all_gather(w, "col", axis=0, tiled=False) for w in (w_qkv, w_out))
    gate_value = jax.nn.sigmoid(gate_logit)
    group = (memory[0], memory_norm[0], offsets[0], lengths[0], gate_value)
    stream, normed_in, gain_in, gain_mid, cot = enter(
        size, cols, stream_in, cotangent, jnp.stack([gain_attn, gain_ffn])
    )
    normed_in, w_gate_up, w_down = lax.optimization_barrier((normed_in, w_gate_up, w_down))
    units = w_down.shape[0] // 2
    packs = [
        jnp.concatenate([w_gate_up[:, :, part], w_down[part].T[None]], axis=0)
        for part in (slice(0, units), slice(units, None))
    ]
    all_packs = [lax.all_gather(pack, "col", axis=0, tiled=False) for pack in packs]
    heads_all, all_in = project_heads(size, normed_in, all_qkv)
    attn, dot_part, memory_part, logsum, memory_new, norm_new, all_cot = attend(size, cot, heads_all, *group)
    middle, normed_ffn, stat_branch = branch_out(size, attn, all_out, stream, gain_mid)
    hidden_first, grads_first, all_ffn = feed_forward(size, normed_ffn, all_packs[0], all_cot, True)
    part_first = weight_grads(flat(all_ffn), grads_first, flat(all_cot), hidden_first)
    part_first, all_ffn = lax.optimization_barrier((part_first, all_ffn))
    scattered_first = over_col(part_first, 1)
    hidden_second, grads_second = feed_forward(size, all_ffn, all_packs[1], all_cot, False)
    part_second = weight_grads(flat(all_ffn), grads_second, flat(all_cot), hidden_second)
    part_second, grads_second = lax.optimization_barrier((part_second, grads_second))
    scattered_second = over_col(part_second, 1)
    grad_middle, low_branch, part_gain_ffn = middle_back(
        size, (grads_first, grads_second), all_packs, middle, cot, gain_mid
    )
    grad_heads, all_branch = branch_back(size, low_branch, all_out)
    grads_qkv, gate_sums = attend_back(
        heads_all, grad_heads, dot_part, memory_part, logsum, *group
    )
    part_qkv = jnp.einsum(
        "td,jto->jdo", flat(all_in), grads_qkv, preferred_element_type=jnp.float32
    ).astype(jnp.bfloat16)
    part_out = tokens_contract(attn, flat(all_branch)).astype(jnp.bfloat16)
    hidden_first, grads_qkv, part_qkv, part_out, scattered_first = lax.optimization_barrier(
        (hidden_first, grads_qkv, part_qkv, part_out, scattered_first)
    )
    blocks_out, stat_ffn = ffn_out(size, (hidden_first, hidden_second), all_packs, middle)
    scattered_out, scattered_qkv = over_col(part_out, 1), over_col(part_qkv, 1)
    blocks_out, grads_qkv, scattered_second = lax.optimization_barrier(
        (blocks_out, grads_qkv, scattered_second)
    )
    blocks_grad, part_gain_attn = stream_back(size, grads_qkv, all_qkv, stream, grad_middle, gain_in)
    grad_out, grad_qkv = scattered_out.astype(jnp.float32), scattered_qkv.astype(jnp.float32)
    grad_gate_up = jnp.concatenate([scattered_first[:2], scattered_second[:2]], axis=2).astype(jnp.float32)
    grad_down = jnp.concatenate([scattered_first[2], scattered_second[2]], axis=1).T.astype(jnp.float32)
    logit_part = gate_value * (1.0 - gate_value) * jnp.sum(gate_sums, axis=(1, 2))
    features_here = gain_attn.shape[0]
    sums = jnp.concatenate(
        [
            part_gain_attn.reshape(cols, 1, features_here),
            part_gain_ffn.reshape(cols, 1, features_here),
            jnp.broadcast_to(
                jnp.pad(logit_part, (0, features_here - head_here))[None, None], (cols, 6, features_here)
            ),
        ],
        axis=1,
    )
    stats = jnp.sqrt(jnp.concatenate([stat_branch[:, :2], stat_ffn[:, :2]], axis=1).T)
    stream_out, stream_grad, stats_all, sums = leave(
        size, cols, blocks_out, blocks_grad, jnp.pad(stats, ((0, 4), (0, 0))), sums
    )
    stream_out = stream_out.reshape(stream_in.shape)
    stream_grad = stream_grad.reshape(stream_in.shape).astype(jnp.float32)
    rms_table = stats_all[:, :, :4].transpose(2, 0, 1, 3).reshape(4, stream_in.shape[0])
    grad_gain_attn, grad_gain_ffn, grad_gate_logit = sums[0], sums[1], sums[2, :head_here]
    return (
        stream_out,
        stream_grad,
        grad_qkv,
        grad_out,
        grad_gate_up,
        grad_down,
        grad_gain_attn,
        grad_gain_ffn,
        grad_gate_logit,
        memory_new[None],
        norm_new.reshape(1, head_here, HD),
        rms_table,
    )


def solution(mesh):
    return jax.shard_map(
        local,
        mesh=mesh,
        in_specs=(
            P("row", "col"),
            P(None, "col", "row"),
            P("row", "col"),
            P(None, "col", "row"),
            P("row", "col"),
            P("col"),
            P("col"),
            P("row"),
            P("col", "row", None, None),
            P("col", "row", None),
            P("col", None),
            P("col", None),
            P("row", "col"),
        ),
        out_specs=(
            P("row", "col"),
            P("row", "col"),
            P(None, "col", "row"),
            P("row", "col"),
            P(None, "col", "row"),
            P("row", "col"),
            P("col"),
            P("col"),
            P("row"),
            P("col", "row", None, None),
            P("col", "row", None),
            P(None, "row"),
        ),
        check_vma=False,
    )
```

```python
import functools

import jax
import jax.numpy as jnp
from jax import lax
from jax.experimental import pallas as pl
from jax.experimental.pallas import tpu as pltpu
from jax.sharding import PartitionSpec as P

D = 2048
HD = 128
PROMPT = 1024
CONT = 4
CLEN = 128
GLEN = 1536


EPSILON = 1e-06
MASKED_LOGIT = -1e30
BIG_VMEM = 60 * 1024 * 1024
SHORT = pl.CostEstimate(flops=1000, bytes_accessed=1000, transcendentals=0)


def feature_map(values):
    return jnp.where(values > 0, values + 1.0, jnp.exp(jnp.minimum(values, 0.0)))


def feature_slope(values):
    return jnp.where(values > 0, 1.0, jnp.exp(jnp.minimum(values, 0.0)))


def split_two(value):
    high = value.astype(jnp.bfloat16)
    return high, (value - high.astype(jnp.float32)).astype(jnp.bfloat16)


def wide_dot(left, right, dims):
    left_high, left_low = split_two(left)
    right_high, right_low = split_two(right)

    def one(a, b):
        return lax.dot_general(a, b, (dims, ((), ())), preferred_element_type=jnp.float32)

    return one(left_high, right_high) + one(left_high, right_low) + one(left_low, right_high)


def narrow_dot(left, right, dims):
    right_high, right_low = split_two(right)

    def one(b):
        return lax.dot_general(left, b, (dims, ((), ())), preferred_element_type=jnp.float32)

    return one(right_high) + one(right_low)


def plain_dot(left, right, dims):
    return lax.dot_general(left, right, (dims, ((), ())), preferred_element_type=jnp.float32)


NN = ((1,), (0,))
NT = ((1,), (1,))
TN = ((0,), (0,))
QT = 256
PROMPT_TILES = PROMPT // QT
TILES = GLEN // QT


def tile_scores(tile, q, k_ref, offsets_ref, lengths_ref):
    scale = HD ** (-0.5)
    row = lax.broadcasted_iota(jnp.int32, (QT, QT), 0)
    column = lax.broadcasted_iota(jnp.int32, (QT, QT), 1)
    seen = min(tile * QT, PROMPT)
    own = plain_dot(q, k_ref[tile * QT : (tile + 1) * QT], NT) * scale
    if tile < PROMPT_TILES:
        own = jnp.where(row >= column, own, MASKED_LOGIT)
        ahead = plain_dot(q, k_ref[:seen], NT) * scale if seen else None
        return ahead, own, seen
    first = (tile - PROMPT_TILES) * (QT // CLEN)
    upper = lax.broadcasted_iota(jnp.int32, (QT, 1), 0) >= CLEN
    limit = jnp.where(upper, offsets_ref[first + 1], offsets_ref[first])
    live = jnp.where(upper, lengths_ref[first + 1] + CLEN, lengths_ref[first])
    same = (row >= CLEN) == (column >= CLEN)
    own = jnp.where((row >= column) & same & (column < live), own, MASKED_LOGIT)
    ahead = plain_dot(q, k_ref[:seen], NT) * scale
    position = lax.broadcasted_iota(jnp.int32, (QT, PROMPT), 1)
    return jnp.where(position < limit, ahead, MASKED_LOGIT), own, seen


def attend_kernel(
    offsets_ref, lengths_ref, gate_ref, qkv_ref, memory_ref, norm_ref,
    attn_ref, dot_ref, part_ref, logsum_ref, memory_new_ref, norm_new_ref,
):
    head = pl.program_id(0)
    gate = gate_ref[head]
    q_ref, k_ref, v_ref = qkv_ref.at[0, 0], qkv_ref.at[1, 0], qkv_ref.at[2, 0]
    memory_one = memory_ref[0]
    norm_one = norm_ref[0]
    for tile in range(TILES):
        rows = slice(tile * QT, (tile + 1) * QT)
        q = q_ref[rows]
        ahead, own, seen = tile_scores(tile, q, k_ref, offsets_ref, lengths_ref)
        peak = jnp.max(own, axis=1, keepdims=True)
        if ahead is not None:
            peak = jnp.maximum(peak, jnp.max(ahead, axis=1, keepdims=True))
        own = jnp.exp(own - peak)
        total = jnp.sum(own, axis=1, keepdims=True)
        dot_part = plain_dot(own.astype(jnp.bfloat16), v_ref[rows], NN)
        if ahead is not None:
            ahead = jnp.exp(ahead - peak)
            total += jnp.sum(ahead, axis=1, keepdims=True)
            dot_part += plain_dot(ahead.astype(jnp.bfloat16), v_ref[:seen], NN)
        dot_part = dot_part / total
        lifted = feature_map(q.astype(jnp.float32))
        memory_part = wide_dot(lifted, memory_one, NN) / jnp.sum(
            lifted * norm_one, axis=1, keepdims=True
        )
        attn_ref[rows, :] = (gate * memory_part + (1.0 - gate) * dot_part).astype(jnp.bfloat16)
        dot_ref[0, rows, :] = dot_part
        part_ref[0, rows, :] = memory_part
        logsum_ref[0, rows, :] = peak + jnp.log(total)
    lifted_keys = feature_map(k_ref[:PROMPT].astype(jnp.float32))
    high, low = split_two(lifted_keys)
    v = v_ref[:PROMPT]
    memory_new_ref[0] = memory_one + (plain_dot(high, v, TN) + plain_dot(low, v, TN)) / PROMPT
    norm_new_ref[0] = norm_one + jnp.mean(lifted_keys, axis=0, keepdims=True)


def head_block(shape, lead=0):
    zeros = (0,) * (len(shape) - 1 - lead)
    return pl.BlockSpec(shape, lambda h: (0,) * lead + (h,) + zeros)


SMEM_SPEC = pl.BlockSpec(memory_space=pltpu.SMEM)


def attend(heads_all, memory_one, norm_one, offsets, lengths, gate_value):
    heads = heads_all.shape[1]
    f32 = jnp.float32
    row_block = head_block((1, GLEN, HD))
    column = pl.BlockSpec((GLEN, HD), lambda h: (0, h))
    return pl.pallas_call(
        attend_kernel,
        grid=(heads,),
        in_specs=[
            SMEM_SPEC, SMEM_SPEC, SMEM_SPEC,
            head_block((3, 1, GLEN, HD), 1), head_block((1, HD, HD)), head_block((1, 1, HD)),
        ],
        out_specs=[
            column, row_block, row_block, head_block((1, GLEN, 1)),
            head_block((1, HD, HD)), head_block((1, 1, HD)),
        ],
        out_shape=[
            jax.ShapeDtypeStruct((GLEN, heads * HD), jnp.bfloat16),
            jax.ShapeDtypeStruct((heads, GLEN, HD), f32),
            jax.ShapeDtypeStruct((heads, GLEN, HD), f32),
            jax.ShapeDtypeStruct((heads, GLEN, 1), f32),
            jax.ShapeDtypeStruct((heads, HD, HD), f32),
            jax.ShapeDtypeStruct((heads, 1, HD), f32),
        ],
        compiler_params=pltpu.CompilerParams(vmem_limit_bytes=BIG_VMEM),
        cost_estimate=SHORT,
        name="attend",
    )(offsets, lengths, gate_value, heads_all, memory_one, norm_one[:, None, :])


def attend_back_kernel(
    size, cols, depth, wide,
    offsets_ref, lengths_ref, gate_ref, qkv_ref, grad_ref, dot_ref, part_ref, logsum_ref,
    memory_ref, norm_ref, middle_ref, hidden_a, hidden_b, pack_a, pack_b,
    out_ref, gate_out_ref, blocks_ref, stat_ref,
    key_sum, value_sum, stage, land, total, send, receive, h, w, h_sem, w_sem,
):
    head = pl.program_id(0)
    piece = GLEN // size
    span = 512
    scatter = Scatter(size, stage, land, total, send, receive)

    def h_load(i, step):
        rows = pl.ds(pl.multiple_of(scatter.order[step] * piece, piece), piece)
        return pltpu.make_async_copy((hidden_a, hidden_b)[i].at[rows], h.at[i, rows], h_sem.at[i, step])

    def w_load(i, c):
        return pltpu.make_async_copy(
            (pack_a, pack_b)[i].at[c, 2], w.at[i, pl.ds(c * depth, depth), :], w_sem.at[i, c]
        )

    def partial(step, at, store):
        for i in range(2):
            h_load(i, step).wait()

        def one(depth_rows, half, columns):
            rows = pl.ds(pl.multiple_of(at * piece, piece), piece)
            store(
                half, columns,
                plain_dot(h[0, rows, :], w[0, depth_rows, :], NT) + plain_dot(h[1, rows, :], w[1, depth_rows, :], NT),
            )

        if step == 0:
            for t in range(D // span):
                for c in range(t * span // depth, (t + 1) * span // depth):
                    for i in range(2):
                        w_load(i, c).wait()
                half, inside = divmod(t * span, HALF)
                one(slice(t * span, (t + 1) * span), half, slice(inside, inside + span))
            return
        for half in range(2):
            @pl.loop(0, HALF // span)
            def _(t):
                columns = pl.ds(pl.multiple_of(t * span, span), span)
                one(pl.ds(pl.multiple_of(half * HALF + t * span, span), span), half, columns)

    @pl.when(head == 0)
    def _():
        for i in range(2):
            h_load(i, 0).start()
        for c in range(cols):
            for i in range(2):
                w_load(i, c).start()
        for step in range(1, size):
            for i in range(2):
                h_load(i, step).start()
        scatter.begin(partial)

    @pl.when(head == pl.num_programs(0) // 2)
    def _():
        scatter.middle()

    gate = gate_ref[head]
    keep = 1.0 - gate
    scale = HD ** (-0.5)
    q_ref, k_ref, v_ref = qkv_ref.at[0, 0], qkv_ref.at[1, 0], qkv_ref.at[2, 0]
    memory_one = memory_ref[0]
    norm_one = norm_ref[0]
    gate_row = jnp.zeros((1, HD), jnp.float32)
    key_sum[...] = jnp.zeros_like(key_sum)
    value_sum[...] = jnp.zeros_like(value_sum)
    for tile in range(TILES):
        rows = slice(tile * QT, (tile + 1) * QT)
        q = q_ref[rows]
        grad = grad_ref[0, rows, :]
        grad_float = grad.astype(jnp.float32)
        memory_part = part_ref[0, rows, :]
        dot_part = dot_ref[0, rows, :]
        against_dot = jnp.sum(grad_float * dot_part, axis=1, keepdims=True)
        gate_row += jnp.sum(grad_float * (memory_part - dot_part), axis=0, keepdims=True)
        logsum = logsum_ref[0, rows, :]
        ahead, own, seen = tile_scores(tile, q, k_ref, offsets_ref, lengths_ref)
        own = jnp.exp(own - logsum)
        value_sum[rows, :] += plain_dot(own.astype(jnp.bfloat16), grad, TN)
        own = (keep * own * (plain_dot(grad, v_ref[rows], NT) - against_dot)).astype(jnp.bfloat16)
        key_sum[rows, :] += plain_dot(own, q, TN)
        grad_q = plain_dot(own, k_ref[rows], NN)
        if ahead is not None:
            ahead = jnp.exp(ahead - logsum)
            value_sum[:seen, :] += plain_dot(ahead.astype(jnp.bfloat16), grad, TN)
            ahead = (keep * ahead * (plain_dot(grad, v_ref[:seen], NT) - against_dot)).astype(
                jnp.bfloat16
            )
            key_sum[:seen, :] += plain_dot(ahead, q, TN)
            grad_q += plain_dot(ahead, k_ref[:seen], NN)
        q_float = q.astype(jnp.float32)
        lifted = feature_map(q_float)
        inverse = gate / jnp.sum(lifted * norm_one, axis=1, keepdims=True)
        against_memory = jnp.sum(grad_float * memory_part, axis=1, keepdims=True)
        grad_lifted = inverse * (narrow_dot(grad, memory_one, NT) - against_memory * norm_one)
        out_ref[0, rows, :] = (grad_q * scale + grad_lifted * feature_slope(q_float)).astype(
            jnp.bfloat16
        )
    out_ref[1, :, :] = (key_sum[...] * scale).astype(jnp.bfloat16)
    out_ref[2, :, :] = (value_sum[...] * keep).astype(jnp.bfloat16)
    gate_out_ref[0] = gate_row

    def finish(rows):
        ffn = [total[half, rows, :] for half in range(2)]
        result = [middle_ref[rows, columns] + ffn[half] for half, columns in enumerate((LEFT, RIGHT))]
        for half, columns in enumerate((LEFT, RIGHT)):
            blocked_store(blocks_ref, rows, depth, columns, result[half].astype(jnp.bfloat16))
        stat_ref[rows, :] = lanes(
            row_mean(ffn[0] * ffn[0], ffn[1] * ffn[1]),
            row_mean(result[0] * result[0], result[1] * result[1]),
        )

    @pl.when(head == pl.num_programs(0) - 1)
    def _():
        scatter.own(partial)
        scatter.end()
        strip_loop(piece, finish)


def whole_block(shape):
    return pl.BlockSpec(shape, lambda h: (0,) * len(shape), pipeline_mode=pl.Buffered(1))


def attend_back(
    size, heads_all, grad_heads, dot_part, memory_part, logsum, memory_one, norm_one, offsets, lengths, gate_value,
    hiddens, packs, middle,
):
    heads = heads_all.shape[1]
    piece = middle.shape[0]
    cols, _, depth, wide = packs[0].shape
    row_block = head_block((1, GLEN, HD))
    return pl.pallas_call(
        functools.partial(attend_back_kernel, size, cols, depth, wide),
        grid=(heads,),
        in_specs=[
            SMEM_SPEC, SMEM_SPEC, SMEM_SPEC,
            head_block((3, 1, GLEN, HD), 1), row_block, row_block, row_block,
            head_block((1, GLEN, 1)), head_block((1, HD, HD)), head_block((1, 1, HD)),
            whole_block((piece, D)), ANY, ANY, ANY, ANY,
        ],
        out_specs=[
            pl.BlockSpec((3, GLEN, HD), lambda h: (0, 0, h)),
            head_block((1, 1, HD)),
            whole_block((cols, piece, depth)), whole_block((piece, HD)),
        ],
        out_shape=[bf(3, GLEN, heads * HD), fl(heads, 1, HD), bf(cols, piece, depth), fl(piece, HD)],
        scratch_shapes=[pltpu.VMEM((GLEN, HD), jnp.float32), pltpu.VMEM((GLEN, HD), jnp.float32)]
        + scatter_scratch(size, piece)
        + [
            pltpu.VMEM((2, GLEN, wide), jnp.bfloat16),
            pltpu.VMEM((2, D, wide), jnp.bfloat16),
            dma(2, size), dma(2, cols),
        ],
        compiler_params=comm_params(5),
        cost_estimate=SHORT,
        name="attend_back",
    )(
        offsets, lengths, gate_value, heads_all, grad_heads, dot_part, memory_part, logsum,
        memory_one, norm_one[:, None, :], middle, *hiddens, *packs,
    )


ANY = pl.BlockSpec(memory_space=pl.ANY)
VMEM = pl.BlockSpec(memory_space=pltpu.VMEM)
MESH_ID = pl.DeviceIdType.MESH
HALF = D // 2
AG_CUTS = 4


def remote(source, target, send, receive, device):
    return pltpu.make_async_remote_copy(
        src_ref=source, dst_ref=target, send_sem=send, recv_sem=receive,
        device_id=device, device_id_type=MESH_ID,
    )


def here():
    return lax.axis_index("row"), lax.axis_index("col")


def greet(peers):
    barrier = pltpu.get_barrier_semaphore()
    for peer in peers:
        pl.semaphore_signal(barrier, inc=1, device_id=peer, device_id_type=MESH_ID)
    pl.semaphore_wait(barrier, len(peers))


def square(row):
    along_x = (row // 2) * 2 + (1 - lax.rem(row, 2))
    along_y = lax.rem(row + 2, 4)
    across = (along_y // 2) * 2 + (1 - lax.rem(along_y, 2))
    return along_x, along_y, across


class Gather:
    def __init__(self, size, source, land, send, receive, own):
        self.size = size
        row, col = self.row, self.col = here()
        piece = source.shape[0]
        self.keep = pltpu.make_async_copy(source, land.at[row], own)
        if size != 4:
            self.peers = [(lax.rem(row + d, size), col) for d in range(1, size)]
            self.order = [lax.rem(row + size - d, size) for d in range(1, size)]
            self.copies = [
                remote(source, land.at[row], send.at[i], receive.at[i], peer) for i, peer in enumerate(self.peers)
            ]
            return
        self.order = rx, ry, rd = square(row)
        px, py = self.peers = [(rx, col), (ry, col)]
        height = piece // AG_CUTS
        cuts = [pl.ds(cut * height, height) for cut in range(AG_CUTS)]

        def out(cut, base, peer):
            return remote(
                source.at[cuts[cut]], land.at[row, cuts[cut]], send.at[base + cut], receive.at[base + cut], peer
            )

        def onward(cut, owner, peer):
            place = land.at[owner, cuts[cut]]
            return remote(place, place, send.at[2 * AG_CUTS + cut], receive.at[2 * AG_CUTS + cut], peer)

        middle = AG_CUTS // 2
        self.to_x = [out(cut, 0, px) for cut in range(AG_CUTS)]
        self.to_y = [out(cut, AG_CUTS, py) for cut in range(AG_CUTS)]
        self.onward = [onward(cut, rx, py) for cut in range(middle)] + [
            onward(cut, ry, px) for cut in range(middle, AG_CUTS)
        ]

    @staticmethod
    def semaphores(size):
        return 3 * AG_CUTS if size == 4 else size - 1

    def start(self, greeted=False, hold=True):
        if not greeted:
            greet(self.peers)
        if self.size != 4:
            for copy in self.copies:
                copy.start()
        else:
            for step in range(AG_CUTS):
                self.to_x[step].start()
                self.to_y[(step + AG_CUTS // 2) % AG_CUTS].start()
        self.keep.start()
        if hold:
            self.keep.wait()

    def forward(self):
        if self.size != 4:
            return
        for step in range(AG_CUTS // 2):
            later = step + AG_CUTS // 2
            self.to_x[step].wait_recv()
            self.onward[step].start()
            self.to_y[later].wait_recv()
            self.onward[later].start()

    def wait(self, step):
        middle = AG_CUTS // 2
        if self.size != 4:
            waits = [self.copies[step]]
        else:
            waits = (self.to_x[middle:], self.to_y[:middle], self.onward)[step]
        for copy in waits:
            copy.wait_recv()
        return self.order[step]

    def finish(self):
        for copy in self.copies if self.size != 4 else [*self.to_x, *self.to_y, *self.onward]:
            copy.wait_send()


class Scatter:
    def __init__(self, size, stage, land, total, send, receive):
        self.size, self.stage, self.land, self.total = size, stage, land, total
        self.send, self.receive = send, receive
        self.row, self.col = here()
        self.plan()

    @staticmethod
    def semaphores(size):
        return 6 if size == 4 else size - 1

    @staticmethod
    def stage_shape(size, piece):
        return (3 if size == 4 else size - 1, 2, piece, HALF)

    @staticmethod
    def land_shape(size, piece):
        return (6, piece, HALF) if size == 4 else (size - 1, 2, piece, HALF)

    def plan(self):
        row, col, stage = self.row, self.col, self.stage

        def copy(index, source, peer):
            return remote(source, self.land.at[index], self.send.at[index], self.receive.at[index], peer)

        if self.size != 4:
            others = [lax.rem(row + d, self.size) for d in range(1, self.size)]
            self.peers = [(peer, col) for peer in others]
            self.order = [*others, row]
            self.copies = [copy(slot, stage.at[slot], peer) for slot, peer in enumerate(self.peers)]
            self.after = [[slot] for slot in range(self.size - 1)]
            return
        rx, ry, rd = square(row)
        px, py = self.peers = [(rx, col), (ry, col)]
        self.order = [rd, rx, ry, row]
        self.copies = [
            copy(0, stage.at[0, 0], px), copy(1, stage.at[0, 1], py), copy(2, stage.at[1, 0], px),
            copy(3, stage.at[2, 1], py), copy(4, stage.at[2, 0], py), copy(5, stage.at[1, 1], px),
        ]
        self.after = [[0, 1], [2], [3]]

    def begin(self, partial, greeted=False):
        if not greeted:
            greet(self.peers)
        for step, row in enumerate(self.order[:-1]):

            def store(half, columns, value):
                self.stage[step, half, :, columns] = value.astype(jnp.bfloat16)

            partial(step, row, store)
            for index in self.after[step]:
                self.copies[index].start()

    def middle(self):
        if self.size != 4:
            return
        self.copies[0].wait_recv()
        self.add_stage(2, 0, self.land.at[0])
        self.copies[4].start()
        self.copies[1].wait_recv()
        self.add_stage(1, 1, self.land.at[1])
        self.copies[5].start()

    def own(self, partial):
        def store(half, columns, value):
            self.total[half, :, columns] = value

        partial(self.size - 1, self.order[-1], store)

    def end(self):
        if self.size != 4:
            for slot, copy in enumerate(self.copies):
                copy.wait_recv()
                self.add_total(0, self.land.at[slot, 0])
                self.add_total(1, self.land.at[slot, 1])
        else:
            for index, half in ((2, 0), (3, 1), (4, 0), (5, 1)):
                self.copies[index].wait_recv()
                self.add_total(half, self.land.at[index])
        for copy in self.copies:
            copy.wait_send()

    def run(self, partial, late=None, greeted=False):
        self.begin(partial, greeted)
        self.middle()
        self.own(partial)
        if late is not None:
            late()
        self.end()

    def add_stage(self, slot, half, landed):
        @pl.loop(0, landed.shape[0] // STRIP)
        def _(i):
            rows = pl.ds(pl.multiple_of(i * STRIP, STRIP), STRIP)
            value = self.stage[slot, half, rows, :].astype(jnp.float32) + landed[rows, :].astype(jnp.float32)
            self.stage[slot, half, rows, :] = value.astype(jnp.bfloat16)

    def add_total(self, half, landed):
        @pl.loop(0, landed.shape[0] // STRIP)
        def _(i):
            rows = pl.ds(pl.multiple_of(i * STRIP, STRIP), STRIP)
            self.total[half, rows, :] += landed[rows, :].astype(jnp.float32)


STRIP = 32


def scatter_scratch(size, piece):
    count = Scatter.semaphores(size)
    return [
        pltpu.VMEM(Scatter.stage_shape(size, piece), jnp.bfloat16),
        pltpu.VMEM(Scatter.land_shape(size, piece), jnp.bfloat16),
        pltpu.VMEM((2, piece, HALF), jnp.float32),
        pltpu.SemaphoreType.DMA((count,)),
        pltpu.SemaphoreType.DMA((count,)),
    ]


def gather_scratch(size, piece):
    count = Gather.semaphores(size)
    return [
        pltpu.VMEM((size, piece, D), jnp.bfloat16),
        pltpu.SemaphoreType.DMA((count,)),
        pltpu.SemaphoreType.DMA((count,)),
        pltpu.SemaphoreType.DMA,
    ]


def fetches(pairs, semaphores):
    copies = [pltpu.make_async_copy(a, b, semaphores.at[i]) for i, (a, b) in enumerate(pairs)]
    for copy in copies:
        copy.start()
    return copies


def wait_all(copies):
    for copy in copies:
        copy.wait()


def tiles_of(width, tile):
    def run(body):
        @pl.loop(0, width // tile)
        def _(t):
            body(t, pl.ds(pl.multiple_of(t * tile, tile), tile))

    return run


def comm_params(identity):
    return pltpu.CompilerParams(
        collective_id=identity, has_side_effects=True, vmem_limit_bytes=BIG_VMEM
    )


def bf(*shape):
    return jax.ShapeDtypeStruct(shape, jnp.bfloat16)


def fl(*shape):
    return jax.ShapeDtypeStruct(shape, jnp.float32)


def project_heads(size, normed, w_all):
    piece = normed.shape[0]
    cols, _, depth, width = w_all.shape
    heads = width // HD

    def kernel(
        x_ref, w_ref, heads_ref, all_ref,
        land, send, receive, own, w, w_sem, all_sem,
    ):
        loads = fetches([(w_ref.at[c], w.at[:, pl.ds(c * depth, depth), :]) for c in range(cols)], w_sem)
        gather = Gather(size, x_ref, land, send, receive, own)
        gather.start()

        def compute(row, slot):
            store = pltpu.make_async_copy(land.at[row], all_ref.at[row], all_sem.at[slot])
            store.start()
            rows = pl.ds(pl.multiple_of(row * piece, piece), piece)

            @pl.loop(0, 3)
            def _(j):
                value = jnp.dot(land[row], w[j], preferred_element_type=jnp.float32).astype(jnp.bfloat16)
                for head in range(heads):
                    heads_ref[j, head, rows, :] = value[:, head * HD : (head + 1) * HD]

            return store

        wait_all(loads)
        stores = [compute(gather.row, 0)]
        gather.forward()
        for step in range(size - 1):
            stores.append(compute(gather.wait(step), step + 1))
        wait_all(stores)
        gather.finish()

    return pl.pallas_call(
        kernel,
        out_shape=[bf(3, heads, GLEN, HD), bf(size, piece, D)],
        in_specs=[ANY, ANY],
        out_specs=[VMEM, ANY],
        scratch_shapes=gather_scratch(size, piece)
        + [
            pltpu.VMEM((3, D, width), jnp.bfloat16),
            pltpu.SemaphoreType.DMA((cols,)),
            pltpu.SemaphoreType.DMA((size,)),
        ],
        compiler_params=comm_params(1),
        cost_estimate=SHORT,
        name="project_heads",
    )(normed, w_all)


def strip_loop(piece, body):
    @pl.loop(0, piece // STRIP)
    def _(i):
        body(pl.ds(pl.multiple_of(i * STRIP, STRIP), STRIP))


def row_mean(first, second):
    return (jnp.sum(first, axis=1, keepdims=True) + jnp.sum(second, axis=1, keepdims=True)) / D


def lanes(first, second):
    lane = lax.broadcasted_iota(jnp.int32, (STRIP, HD), 1)
    return jnp.where(lane == 0, first, jnp.where(lane == 1, second, 0.0))


LEFT, RIGHT = slice(0, HALF), slice(HALF, D)


def branch_out(size, attn, w_all, x, gain):
    piece = GLEN // size
    cols, width, depth = w_all.shape

    def kernel(attn_ref, w_ref, x_ref, gain_ref, middle_ref, normed_ref, stat_ref, stage, land, total, send, receive, w, w_sem):
        loads = fetches([(w_ref.at[c], w.at[:, pl.ds(c * depth, depth)]) for c in range(cols)], w_sem)
        scatter = Scatter(size, stage, land, total, send, receive)
        wait_all(loads)

        def partial(step, row, store):
            rows = pl.ds(pl.multiple_of(row * piece, piece), piece)
            left = attn_ref[rows, :]
            for half in range(2):
                for t in range(2):
                    columns = slice(half * HALF + t * HALF // 2, half * HALF + (t + 1) * HALF // 2)
                    store(
                        half, slice(t * HALF // 2, (t + 1) * HALF // 2),
                        jnp.dot(left, w[:, columns], preferred_element_type=jnp.float32),
                    )

        scatter.run(partial)

        def finish(rows):
            branch = (total[0, rows, :], total[1, rows, :])
            middle = (
                x_ref[rows, LEFT].astype(jnp.float32) + branch[0],
                x_ref[rows, RIGHT].astype(jnp.float32) + branch[1],
            )
            mean = row_mean(middle[0] * middle[0], middle[1] * middle[1])
            inverse = lax.rsqrt(mean + EPSILON)
            for part, columns in zip(middle, (LEFT, RIGHT)):
                middle_ref[rows, columns] = part
                normed_ref[rows, columns] = (part * inverse * gain_ref[:, columns]).astype(jnp.bfloat16)
            stat_ref[rows, :] = lanes(row_mean(branch[0] * branch[0], branch[1] * branch[1]), mean)

        strip_loop(piece, finish)

    return pl.pallas_call(
        kernel,
        out_shape=[fl(piece, D), bf(piece, D), fl(piece, HD)],
        in_specs=[VMEM, ANY, VMEM, VMEM],
        out_specs=[VMEM, VMEM, VMEM],
        scratch_shapes=scatter_scratch(size, piece)
        + [pltpu.VMEM((width, D), jnp.bfloat16), pltpu.SemaphoreType.DMA((cols,))],
        compiler_params=comm_params(2),
        cost_estimate=SHORT,
        name="branch_out",
    )(attn, w_all, x, gain)


def feed_forward(size, tokens, pack, cot, first):
    piece = GLEN // size
    cols, _, depth, wide = pack.shape
    tile = min(wide, 512)
    count = wide // tile

    def kernel(x_ref, pack_ref, cot_ref, hidden_ref, grad_ref, *rest):
        if first:
            all_ref, land, send, receive, own, all_sem, *rest = rest
        else:
            land, own, *rest = rest
        w, cot_all, back, stage, w_sem, cot_sem, out_sem = rest
        if first:
            gather = Gather(size, x_ref, land, send, receive, own)
            gather.start()
            order = [gather.row, *gather.order]
        else:
            order = list(range(size))
        w_loads = fetches(
            [(pack_ref.at[c, j], w.at[j, pl.ds(c * depth, depth), :]) for j in (2, 0, 1) for c in range(cols)], w_sem
        )
        cot_loads = fetches([(cot_ref.at[row], cot_all.at[row]) for row in order], cot_sem)
        if not first:
            x_loads = fetches([(x_ref.at[row], land.at[row]) for row in order], own)

        def backward(step):
            row = order[step]
            cot_loads[step].wait()

            @tiles_of(wide, tile)
            def _(t, columns):
                back[row, :, columns] = plain_dot(cot_all[row], w[2, :, columns], NN).astype(jnp.bfloat16)

        def moves(row, slot, columns):
            rows = pl.ds(pl.multiple_of(row * piece, piece), piece)
            return [
                pltpu.make_async_copy(stage.at[slot, 0], hidden_ref.at[rows, columns], out_sem.at[slot, 0]),
                pltpu.make_async_copy(stage.at[slot, 1], grad_ref.at[0, rows, columns], out_sem.at[slot, 1]),
                pltpu.make_async_copy(stage.at[slot, 2], grad_ref.at[1, rows, columns], out_sem.at[slot, 2]),
            ]

        def compute(step):
            row = order[step]
            if first:
                store = pltpu.make_async_copy(land.at[row], all_ref.at[row], all_sem)
                store.start()

            @pl.loop(0, count)
            def _(t):
                columns = pl.ds(pl.multiple_of(t * tile, tile), tile)
                slot = lax.rem(t, 2)
                x = land[row]
                gate_pre = jnp.dot(x, w[0, :, columns], preferred_element_type=jnp.float32)
                up_pre = jnp.dot(x, w[1, :, columns], preferred_element_type=jnp.float32)
                sigmoid = jax.nn.sigmoid(gate_pre)
                silu = gate_pre * sigmoid
                grad_hidden = back[row, :, columns].astype(jnp.float32)

                @pl.when(t >= 2)
                def _():
                    wait_all(moves(row, slot, columns))

                stage[slot, 0] = (silu * up_pre).astype(jnp.bfloat16)
                stage[slot, 1] = (grad_hidden * up_pre * (sigmoid + silu * (1.0 - sigmoid))).astype(jnp.bfloat16)
                stage[slot, 2] = (grad_hidden * silu).astype(jnp.bfloat16)
                for move in moves(row, slot, columns):
                    move.start()

            for slot in range(min(2, count)):
                wait_all(moves(row, slot, pl.ds(slot * tile, tile)))
            if first:
                store.wait()

        wait_all(w_loads[:cols])
        backward(0)
        if first:
            gather.forward()
        for step in range(1, size):
            backward(step)
        wait_all(w_loads[cols:])
        for step in range(size):
            if not first:
                x_loads[step].wait()
            elif step:
                gather.wait(step - 1)
            compute(step)
        if first:
            gather.finish()

    out_shape = [bf(GLEN, wide), bf(2, GLEN, wide)]
    if first:
        out_shape.append(bf(size, piece, D))
        scratch = gather_scratch(size, piece) + [pltpu.SemaphoreType.DMA]
    else:
        scratch = [pltpu.VMEM((size, piece, D), jnp.bfloat16), dma(size)]
    return pl.pallas_call(
        kernel,
        out_shape=out_shape,
        in_specs=[ANY] * 3,
        out_specs=[ANY] * len(out_shape),
        scratch_shapes=scratch
        + [
            pltpu.VMEM((3, D, wide), jnp.bfloat16),
            pltpu.VMEM((size, piece, D), jnp.bfloat16),
            pltpu.VMEM((size, piece, wide), jnp.bfloat16),
            pltpu.VMEM((2, 3, piece, tile), jnp.bfloat16),
            dma(3 * cols), dma(size), dma(2, 3),
        ],
        compiler_params=comm_params(3) if first else pltpu.CompilerParams(vmem_limit_bytes=BIG_VMEM),
        cost_estimate=SHORT,
        name="feed_first" if first else "feed_second",
    )(tokens, pack, cot)


def weight_grads_kernel(x_ref, y_ref, g_ref, h_ref, out_ref):
    for j in range(2):
        out_ref[j] = plain_dot(x_ref[...], g_ref[j], TN).astype(jnp.bfloat16)
    out_ref[2] = plain_dot(y_ref[...], h_ref[...], TN).astype(jnp.bfloat16)


def weight_grads(x, grads, y, hidden):
    wide = hidden.shape[1]
    tile = 256
    block = pl.BlockSpec((GLEN, tile), lambda i: (0, i))
    return pl.pallas_call(
        weight_grads_kernel,
        grid=(D // tile,),
        in_specs=[
            block, block,
            pl.BlockSpec((2, GLEN, wide), lambda i: (0, 0, 0), pipeline_mode=pl.Buffered(1)),
            pl.BlockSpec((GLEN, wide), lambda i: (0, 0), pipeline_mode=pl.Buffered(1)),
        ],
        out_specs=pl.BlockSpec((3, tile, wide), lambda i: (0, i, 0)),
        out_shape=bf(3, D, wide),
        compiler_params=pltpu.CompilerParams(vmem_limit_bytes=BIG_VMEM),
        cost_estimate=SHORT,
        name="weight_grads",
    )(x, y, grads, hidden)


def norm_back(rows, total, stream, inverse, gain_ref, base, store, gain_sum):
    u = [total[half, rows, :] * gain_ref[:, columns] for half, columns in enumerate((LEFT, RIGHT))]
    inner = row_mean(u[0] * stream[0], u[1] * stream[1]) * inverse * inverse * inverse
    for half, columns in enumerate((LEFT, RIGHT)):
        store(columns, base[half] + inverse * u[half] - stream[half] * inner)
        gain_sum[:, columns] += jnp.sum(total[half, rows, :] * stream[half] * inverse, axis=0, keepdims=True)


def middle_back(size, grads, packs, middle, cot, gain, tokens, all_cot, hidden):
    piece = middle.shape[0]
    cols, _, depth, wide = packs[0].shape
    tile = 512
    block = 256

    def kernel(
        first_ref, second_ref, pack_a, pack_b, middle_ref, cot_ref, gain_ref, x_ref, y_ref, hidden_ref,
        grad_ref, low_ref, gain_sum, part_ref,
        stage, land, total, send, receive, w, g_first, g_second, h, x, part,
        w_sem, first_sem, second_sem, h_sem, x_sem, part_sem,
    ):
        pack_refs = (pack_a, pack_b)
        scatter = Scatter(size, stage, land, total, send, receive)

        def piece_rows(at):
            return pl.ds(pl.multiple_of(at * piece, piece), piece)

        def first_load(step):
            return pltpu.make_async_copy(
                first_ref.at[:, piece_rows(scatter.order[step])], g_first.at[step % 2], first_sem.at[step % 2]
            )

        def second_load(step):
            rows = piece_rows(scatter.order[step])
            return pltpu.make_async_copy(second_ref.at[:, rows], g_second.at[:, rows], second_sem.at[step])

        def w_load(i, c):
            return pltpu.make_async_copy(
                pack_refs[i].at[c, pl.ds(0, 2)], w.at[i, :, pl.ds(c * depth, depth), :], w_sem.at[i, c]
            )

        first_load(0).start()
        second_load(0).start()
        for c in range(cols):
            for i in range(2):
                w_load(i, c).start()
        first_load(1).start()
        for step in range(1, size):
            second_load(step).start()
        h_load = pltpu.make_async_copy(hidden_ref, h, h_sem)
        h_load.start()
        gain_sum[...] = jnp.zeros_like(gain_sum)

        def one(step, rows, depth_rows, store, half, columns):
            value = 0.0
            for j in range(2):
                value += plain_dot(g_first[step % 2, j], w[0, j, depth_rows, :], NT)
                value += plain_dot(g_second[j, rows, :], w[1, j, depth_rows, :], NT)
            store(half, columns, value)

        def partial(step, at, store):
            first_load(step).wait()
            second_load(step).wait()
            rows = piece_rows(at)
            if step == 0:
                for t in range(D // tile):
                    for c in range(t * tile // depth, (t + 1) * tile // depth):
                        for i in range(2):
                            w_load(i, c).wait()
                    half, inside = divmod(t * tile, HALF)
                    one(step, rows, slice(t * tile, (t + 1) * tile), store, half, slice(inside, inside + tile))
            else:
                for half in range(2):
                    @pl.loop(0, HALF // tile)
                    def _(t):
                        columns = pl.ds(pl.multiple_of(t * tile, tile), tile)
                        depth_rows = pl.ds(pl.multiple_of(half * HALF + t * tile, tile), tile)
                        one(step, rows, depth_rows, store, half, columns)
            if step + 2 < size:
                first_load(step + 2).start()

        def x_loads(i, slot):
            columns = pl.ds(pl.multiple_of(i * block, block), block)
            return [
                pltpu.make_async_copy(source.at[:, :, columns], x.at[slot, k], x_sem.at[slot, k])
                for k, source in enumerate((x_ref, y_ref))
            ]

        def part_move(i, slot):
            columns = pl.ds(pl.multiple_of(i * block, block), block)
            return pltpu.make_async_copy(part.at[slot], part_ref.at[:, columns, :], part_sem.at[slot])

        def weights():
            count = D // block
            for load in x_loads(0, 0):
                load.start()
            h_load.wait()

            @pl.loop(0, count)
            def _(i):
                slot = lax.rem(i, 2)

                @pl.when(i + 1 < count)
                def _():
                    for load in x_loads(i + 1, 1 - slot):
                        load.start()

                wait_all(x_loads(i, slot))

                @pl.when(i >= 2)
                def _():
                    part_move(i, slot).wait()

                left = x[slot, 0].reshape(GLEN, block)
                for j in range(2):
                    part[slot, j] = plain_dot(left, g_second[j], TN).astype(jnp.bfloat16)
                part[slot, 2] = plain_dot(x[slot, 1].reshape(GLEN, block), h[...], TN).astype(jnp.bfloat16)
                part_move(i, slot).start()

            for slot in range(2):
                part_move(slot, slot).wait()

        scatter.run(partial, weights)

        def finish(rows):
            stream = [middle_ref[rows, columns] for columns in (LEFT, RIGHT)]
            base = [cot_ref[rows, columns].astype(jnp.float32) for columns in (LEFT, RIGHT)]
            inverse = lax.rsqrt(row_mean(stream[0] * stream[0], stream[1] * stream[1]) + EPSILON)

            def store(columns, value):
                grad_ref[rows, columns] = value
                low_ref[rows, columns] = value.astype(jnp.bfloat16)

            norm_back(rows, total, stream, inverse, gain_ref, base, store, gain_sum)

        strip_loop(piece, finish)

    return pl.pallas_call(
        kernel,
        out_shape=[fl(piece, D), bf(piece, D), fl(1, D), bf(3, D, wide)],
        in_specs=[ANY] * 4 + [VMEM] * 3 + [ANY] * 3,
        out_specs=[VMEM, VMEM, VMEM, ANY],
        scratch_shapes=scatter_scratch(size, piece)
        + [
            pltpu.VMEM((2, 2, D, wide), jnp.bfloat16),
            pltpu.VMEM((2, 2, piece, wide), jnp.bfloat16),
            pltpu.VMEM((2, GLEN, wide), jnp.bfloat16),
            pltpu.VMEM((GLEN, wide), jnp.bfloat16),
            pltpu.VMEM((2, 2, size, piece, block), jnp.bfloat16),
            pltpu.VMEM((2, 3, block, wide), jnp.bfloat16),
            dma(2, cols), dma(2), dma(size), pltpu.SemaphoreType.DMA, dma(2, 2), dma(2),
        ],
        compiler_params=comm_params(4),
        cost_estimate=SHORT,
        name="middle_back",
    )(*grads, *packs, middle, cot, gain, tokens, all_cot, hidden)


def blocked_store(ref, rows, depth, columns, value):
    for i in range(value.shape[1] // depth):
        ref[columns.start // depth + i, rows, :] = value[:, i * depth : (i + 1) * depth]


def branch_back(size, low, w_all):
    piece = low.shape[0]
    cols, width, depth = w_all.shape
    heads = width // HD

    def kernel(x_ref, w_ref, heads_ref, all_ref, land, send, receive, own, w, w_sem, all_sem):
        loads = fetches([(w_ref.at[c], w.at[:, pl.ds(c * depth, depth)]) for c in range(cols)], w_sem)
        gather = Gather(size, x_ref, land, send, receive, own)
        gather.start()

        def compute(row, slot):
            store = pltpu.make_async_copy(land.at[row], all_ref.at[row], all_sem.at[slot])
            store.start()
            rows = pl.ds(pl.multiple_of(row * piece, piece), piece)
            value = plain_dot(land[row], w[...], NT).astype(jnp.bfloat16)
            for head in range(heads):
                heads_ref[head, rows, :] = value[:, head * HD : (head + 1) * HD]
            return store

        wait_all(loads)
        stores = [compute(gather.row, 0)]
        gather.forward()
        for step in range(size - 1):
            stores.append(compute(gather.wait(step), step + 1))
        wait_all(stores)
        gather.finish()

    return pl.pallas_call(
        kernel,
        out_shape=[bf(heads, GLEN, HD), bf(size, piece, D)],
        in_specs=[ANY, ANY],
        out_specs=[VMEM, ANY],
        scratch_shapes=gather_scratch(size, piece)
        + [
            pltpu.VMEM((width, D), jnp.bfloat16),
            pltpu.SemaphoreType.DMA((cols,)),
            pltpu.SemaphoreType.DMA((size,)),
        ],
        compiler_params=comm_params(6),
        cost_estimate=SHORT,
        name="branch_back",
    )(low, w_all)


def stream_back(size, grads, w_all, x, grad_middle, gain, blocks_out):
    piece = x.shape[0]
    cols, _, depth, width = w_all.shape
    tile = 512

    def kernel(
        g_ref, w_ref, x_ref, middle_ref, gain_ref, blocks_ref, out_ref, gain_sum, target_ref,
        stage, land, total, send, receive, w, w_sem, *rest,
    ):
        greet(row_and_col_peers(size, cols))
        outward = Outward(size, cols, blocks_ref, rest[0], target_ref, *rest[1:])
        outward.start()
        loads = fetches([(w_ref.at[c], w.at[:, pl.ds(c * depth, depth), :]) for c in range(cols)], w_sem)
        scatter = Scatter(size, stage, land, total, send, receive)
        wait_all(loads)
        gain_sum[...] = jnp.zeros_like(gain_sum)

        def partial(step, row, store):
            rows = pl.ds(pl.multiple_of(row * piece, piece), piece)
            for half in range(2):
                @pl.loop(0, HALF // tile)
                def _(t):
                    columns = pl.ds(pl.multiple_of(t * tile, tile), tile)
                    depth_rows = pl.ds(pl.multiple_of(half * HALF + t * tile, tile), tile)
                    value = plain_dot(g_ref[0, rows, :], w[0, depth_rows, :], NT)
                    for j in (1, 2):
                        value += plain_dot(g_ref[j, rows, :], w[j, depth_rows, :], NT)
                    store(half, columns, value)

        scatter.run(partial, outward.forward, greeted=True)

        def finish(rows):
            stream = [x_ref[rows, columns].astype(jnp.float32) for columns in (LEFT, RIGHT)]
            base = [middle_ref[rows, columns] for columns in (LEFT, RIGHT)]
            inverse = lax.rsqrt(row_mean(stream[0] * stream[0], stream[1] * stream[1]) + EPSILON)

            def store(columns, value):
                blocked_store(out_ref, rows, depth, columns, value.astype(jnp.bfloat16))

            norm_back(rows, total, stream, inverse, gain_ref, base, store, gain_sum)

        strip_loop(piece, finish)
        outward.finish()

    return pl.pallas_call(
        kernel,
        out_shape=[bf(cols, piece, depth), fl(1, D), bf(cols // size, size, piece, depth)],
        in_specs=[VMEM, ANY, VMEM, VMEM, VMEM, VMEM],
        out_specs=[VMEM, VMEM, ANY],
        scratch_shapes=scatter_scratch(size, piece)
        + [pltpu.VMEM((3, D, width), jnp.bfloat16), pltpu.SemaphoreType.DMA((cols,))]
        + Outward.scratch(size, cols, piece, depth),
        compiler_params=comm_params(7),
        cost_estimate=SHORT,
        name="stream_back",
    )(grads, w_all, x, grad_middle, gain, blocks_out)


def row_and_col_peers(size, cols):
    row, col = here()
    return [(lax.rem(row + d, size), col) for d in range(1, size)] + [
        (row, lax.rem(col + e, cols)) for e in range(1, cols)
    ]


def dma(*shape):
    return pltpu.SemaphoreType.DMA(shape)


class Inward:
    def __init__(self, size, cols, source, middle, land, first_send, first_receive, send, receive, own):
        self.size, self.cols, self.groups = size, cols, cols // size
        self.source, self.middle, self.land = source, middle, land
        self.first_send, self.first_receive = first_send, first_receive
        self.send, self.receive, self.own = send, receive, own
        self.row, self.col = here()

    @staticmethod
    def scratch(size, cols, piece, depth):
        return [
            pltpu.VMEM((size, cols // size, piece, depth), jnp.bfloat16),
            pltpu.VMEM((cols, piece, depth), jnp.bfloat16),
            dma(size - 1), dma(size - 1), dma(cols), dma(cols), dma(2),
        ]

    def start(self):
        row, col = self.row, self.col
        self.first = []
        for d in range(1, self.size):
            peer = lax.rem(row + d, self.size)
            self.first.append(
                remote(
                    self.source.at[:, peer], self.middle.at[row],
                    self.first_send.at[d - 1], self.first_receive.at[d - 1], (peer, col),
                )
            )
            self.first[-1].start()
        self.keep = pltpu.make_async_copy(self.source.at[:, row], self.middle.at[row], self.own.at[0])
        self.keep.start()

    def forward(self):
        row, col = self.row, self.col
        for d in range(self.size):
            origin = lax.rem(row + self.size - d, self.size)
            if d == 0:
                self.keep.wait()
            else:
                self.first[d - 1].wait_recv()
            for i in range(self.groups):
                group = origin * self.groups + i

                @pl.when(group != col)
                def _():
                    remote(
                        self.middle.at[origin, i], self.land.at[col],
                        self.send.at[group], self.receive.at[col], (row, group),
                    ).start()

                @pl.when(group == col)
                def _():
                    pltpu.make_async_copy(self.middle.at[origin, i], self.land.at[col], self.own.at[1]).start()

    def finish(self):
        row, col = self.row, self.col
        pltpu.make_async_copy(self.middle.at[0, 0], self.land.at[col], self.own.at[1]).wait()
        for e in range(1, self.cols):
            peer = lax.rem(col + e, self.cols)
            remote(
                self.middle.at[0, 0], self.land.at[peer], self.send.at[peer], self.receive.at[peer], (row, peer)
            ).wait()
        for copy in self.first:
            copy.wait_send()


class Outward:
    def __init__(self, size, cols, source, middle, target, first_send, first_receive, send, receive, own):
        self.size, self.cols, self.groups = size, cols, cols // size
        self.source, self.middle, self.target = source, middle, target
        self.first_send, self.first_receive = first_send, first_receive
        self.send, self.receive, self.own = send, receive, own
        self.row, self.col = here()

    @staticmethod
    def scratch(size, cols, piece, depth):
        return [
            pltpu.VMEM((cols, piece, depth), jnp.bfloat16),
            dma(cols - 1), dma(cols - 1), dma(cols), dma(cols), dma(cols // size),
        ]

    def start(self):
        row, col = self.row, self.col
        self.first = []
        for e in range(1, self.cols):
            peer = lax.rem(col + e, self.cols)
            self.first.append(
                remote(
                    self.source.at[peer], self.middle.at[col],
                    self.first_send.at[e - 1], self.first_receive.at[e - 1], (row, peer),
                )
            )
            self.first[-1].start()

    def forward(self):
        row, col = self.row, self.col
        for e in range(self.cols):
            group = lax.rem(col + self.cols - e, self.cols)
            if e:
                self.first[e - 1].wait_recv()
            block = self.middle.at[group] if e else self.source.at[col]
            home, i = group // self.groups, lax.rem(group, self.groups)

            @pl.when(home != row)
            def _():
                remote(
                    block, self.target.at[i, row],
                    self.send.at[group], self.receive.at[i * self.size + row], (home, col),
                ).start()

            @pl.when(home == row)
            def _():
                pltpu.make_async_copy(block, self.target.at[i, row], self.own.at[i]).start()

    def finish(self):
        row, col = self.row, self.col
        for i in range(self.groups):
            pltpu.make_async_copy(self.middle.at[0], self.target.at[i, row], self.own.at[i]).wait()
            for d in range(1, self.size):
                peer = lax.rem(row + d, self.size)
                remote(
                    self.middle.at[0], self.target.at[i, peer],
                    self.send.at[peer * self.groups + i], self.receive.at[i * self.size + peer], (peer, col),
                ).wait()
        for copy in self.first:
            copy.wait_send()


def by_pieces(block, size):
    return block.reshape(block.shape[0] // GLEN, size, GLEN // size, block.shape[1])


def enter(size, cols, stream_in, cotangent, gains):
    pieces = by_pieces(stream_in, size)
    piece, depth = pieces.shape[2:]
    scratch = Inward.scratch(size, cols, piece, depth)

    def kernel(
        x_ref, cot_ref, gains_ref, tokens_ref, normed_ref, gain_in_ref, gain_mid_ref, cot_tokens_ref, all_cot_ref,
        gains_land, gains_send, gains_receive, gather_send, gather_receive, gather_own, *rest,
    ):
        greet(row_and_col_peers(size, cols))
        exchange = Inward(size, cols, x_ref, *rest[: len(scratch)])
        second = Inward(size, cols, cot_ref, *rest[len(scratch) :])
        gather = Gather(size, cot_tokens_ref, all_cot_ref, gather_send, gather_receive, gather_own)
        second.start()
        exchange.start()
        row, col = here()
        copies = []
        for e in range(1, cols):
            peer = lax.rem(col + e, cols)
            copies.append(
                remote(gains_ref, gains_land.at[col], gains_send.at[e - 1], gains_receive.at[e - 1], (row, peer))
            )
            copies[-1].start()
        gains_land[col] = gains_ref[...]
        second.forward()
        exchange.forward()
        second.finish()

        def assemble(rows):
            for c in range(cols):
                cot_tokens_ref[rows, c * depth : (c + 1) * depth] = second.land[c, rows, :]

        strip_loop(piece, assemble)
        gather.start(greeted=True, hold=False)
        gather.forward()
        for copy in copies:
            copy.wait()
        for c in range(cols):
            gain_in_ref[:, c * depth : (c + 1) * depth] = gains_land[c, 0:1, :]
            gain_mid_ref[:, c * depth : (c + 1) * depth] = gains_land[c, 1:2, :]
        exchange.finish()
        land = exchange.land

        def norm(rows):
            total = jnp.zeros((STRIP, 1), jnp.float32)
            for c in range(cols):
                part = land[c, rows, :]
                tokens_ref[rows, c * depth : (c + 1) * depth] = part
                part = part.astype(jnp.float32)
                total += jnp.sum(part * part, axis=1, keepdims=True)
            inverse = lax.rsqrt(total / D + EPSILON)
            for c in range(cols):
                columns = slice(c * depth, (c + 1) * depth)
                normed_ref[rows, columns] = (
                    land[c, rows, :].astype(jnp.float32) * inverse * gain_in_ref[:, columns]
                ).astype(jnp.bfloat16)

        strip_loop(piece, norm)
        for step in range(size - 1):
            gather.wait(step)
        gather.keep.wait()
        gather.finish()

    return pl.pallas_call(
        kernel,
        out_shape=[bf(piece, D), bf(piece, D), fl(1, D), fl(1, D), bf(piece, D), bf(size, piece, D)],
        in_specs=[ANY, ANY, VMEM],
        out_specs=[VMEM] * 5 + [ANY],
        scratch_shapes=[pltpu.VMEM((cols, 8, depth), jnp.float32), dma(cols - 1), dma(cols - 1)]
        + [dma(Gather.semaphores(size)), dma(Gather.semaphores(size)), pltpu.SemaphoreType.DMA]
        + scratch * 2,
        compiler_params=comm_params(8),
        cost_estimate=SHORT,
        name="enter",
    )(pieces, by_pieces(cotangent, size), jnp.pad(gains, ((0, 6), (0, 0))))


def leave(size, cols, blocks_grad, stats, sums):
    _, piece, depth = blocks_grad.shape
    groups = cols // size

    def kernel(
        grad_ref, stats_ref, sums_ref, grad_target, stats_target, sums_target,
        stats_row, stats_all, sums_col, sums_part, sums_row,
        a_send, a_receive, b_send, b_receive, c_send, c_receive, d_send, d_receive, *rest,
    ):
        row, col = here()
        greet(row_and_col_peers(size, cols))
        grad = Outward(size, cols, grad_ref, rest[0], grad_target, *rest[1:])
        home, slot = col // groups, lax.rem(col, groups)
        col_peers = [lax.rem(col + e, cols) for e in range(1, cols)]
        row_peers = [lax.rem(row + d, size) for d in range(1, size)]

        def sums_first(peer):
            return remote(sums_ref.at[peer], sums_col.at[col], c_send.at[peer], c_receive.at[col], (row, peer))

        for peer in col_peers:
            sums_first(peer).start()
        sums_col[col] = sums_ref[col]

        @pl.when(home != row)
        def _():
            remote(stats_ref, stats_row.at[row], a_send, a_receive.at[row], (home, col)).start()

        @pl.when(home == row)
        def _():
            stats_row[row] = stats_ref[...]

        grad.start()
        for peer in col_peers:
            remote(sums_ref.at[peer], sums_col.at[peer], c_send.at[peer], c_receive.at[peer], (row, peer)).wait()
        total = sums_col[0]
        for c in range(1, cols):
            total += sums_col[c]
        sums_part[...] = total
        sums_row[row] = total
        for peer in row_peers:
            remote(sums_part, sums_row.at[row], d_send.at[peer], d_receive.at[row], (peer, col)).start()

        @pl.when(home == row)
        def _():
            for peer in row_peers:
                remote(stats_ref, stats_row.at[peer], a_send, a_receive.at[peer], (peer, col)).wait_recv()
            for e, peer in enumerate(col_peers):
                remote(stats_row, stats_all.at[slot], b_send.at[e], b_receive.at[slot], (row, peer)).start()
            stats_all[slot] = stats_row[...]

        grad.forward()
        for peer in row_peers:
            remote(sums_part, sums_row.at[peer], d_send.at[peer], d_receive.at[peer], (peer, col)).wait()
        whole = sums_row[0]
        for r in range(1, size):
            whole += sums_row[r]
        line = lax.broadcasted_iota(jnp.int32, (8, depth), 0)
        sums_target[...] = jnp.where(line < 2, whole, total)

        @pl.when(home == row)
        def _():
            for e, peer in enumerate(col_peers):
                remote(stats_row, stats_all.at[slot], b_send.at[e], b_receive.at[slot], (row, peer)).wait_send()

        @pl.when(home != row)
        def _():
            remote(stats_ref, stats_row.at[row], a_send, a_receive.at[row], (home, col)).wait_send()

        for i in range(groups):
            group = row * groups + i

            @pl.when(group != col)
            def _():
                remote(stats_row, stats_all.at[i], b_send.at[0], b_receive.at[i], (row, group)).wait_recv()

        stats_target[...] = stats_all[...]
        grad.finish()

    return pl.pallas_call(
        kernel,
        out_shape=[
            bf(groups, size, piece, depth),
            fl(groups, size, 8, piece), fl(8, depth),
        ],
        in_specs=[VMEM] * 3,
        out_specs=[ANY, VMEM, VMEM],
        scratch_shapes=[
            pltpu.VMEM((size, 8, piece), jnp.float32),
            pltpu.VMEM((groups, size, 8, piece), jnp.float32),
            pltpu.VMEM((cols, 8, depth), jnp.float32),
            pltpu.VMEM((8, depth), jnp.float32),
            pltpu.VMEM((size, 8, depth), jnp.float32),
            pltpu.SemaphoreType.DMA, dma(size), dma(cols - 1), dma(groups), dma(cols), dma(cols), dma(size), dma(size),
        ]
        + Outward.scratch(size, cols, piece, depth),
        compiler_params=comm_params(10),
        cost_estimate=SHORT,
        name="leave",
    )(blocks_grad, stats, sums)


def tokens_contract(left, right):
    return lax.dot_general(left, right, (TN, ((), ())), preferred_element_type=jnp.float32)


def over_col(partial, axis):
    return lax.psum_scatter(partial.astype(jnp.bfloat16), "col", scatter_dimension=axis, tiled=True)


def flat(pieces):
    return pieces.reshape(GLEN, D)


def local(
    stream_in,
    w_qkv,
    w_out,
    w_gate_up,
    w_down,
    gain_attn,
    gain_ffn,
    gate_logit,
    memory,
    memory_norm,
    offsets,
    lengths,
    cotangent,
):
    head_here = memory.shape[1]
    size = lax.axis_size("row")
    cols = lax.axis_size("col")
    all_qkv, all_out = (lax.all_gather(w, "col", axis=0, tiled=False) for w in (w_qkv, w_out))
    gate_value = jax.nn.sigmoid(gate_logit)
    group = (memory[0], memory_norm[0], offsets[0], lengths[0], gate_value)
    stream, normed_in, gain_in, gain_mid, cot, all_cot = enter(
        size, cols, stream_in, cotangent, jnp.stack([gain_attn, gain_ffn])
    )
    normed_in, w_gate_up, w_down = lax.optimization_barrier((normed_in, w_gate_up, w_down))
    units = w_down.shape[0] // 2
    packs = [
        jnp.concatenate([w_gate_up[:, :, part], w_down[part].T[None]], axis=0)
        for part in (slice(0, units), slice(units, None))
    ]
    all_packs = [lax.all_gather(pack, "col", axis=0, tiled=False) for pack in packs]
    heads_all, all_in = project_heads(size, normed_in, all_qkv)
    attn, dot_part, memory_part, logsum, memory_new, norm_new = attend(heads_all, *group)
    middle, normed_ffn, stat_branch = branch_out(size, attn, all_out, stream, gain_mid)
    hidden_first, grads_first, all_ffn = feed_forward(size, normed_ffn, all_packs[0], all_cot, True)
    part_first = weight_grads(flat(all_ffn), grads_first, flat(all_cot), hidden_first)
    part_first, all_ffn = lax.optimization_barrier((part_first, all_ffn))
    scattered_first = over_col(part_first, 1)
    hidden_second, grads_second = feed_forward(size, all_ffn, all_packs[1], all_cot, False)
    grad_middle, low_branch, part_gain_ffn, part_second = middle_back(
        size, (grads_first, grads_second), all_packs, middle, cot, gain_mid, all_ffn, all_cot, hidden_second
    )
    scattered_second = over_col(part_second, 1)
    grad_heads, all_branch = branch_back(size, low_branch, all_out)
    part_out = tokens_contract(attn, flat(all_branch)).astype(jnp.bfloat16)
    part_out, grad_heads = lax.optimization_barrier((part_out, grad_heads))
    grads_qkv, gate_sums, blocks_out, stat_ffn = attend_back(
        size, heads_all, grad_heads, dot_part, memory_part, logsum, *group,
        (hidden_first, hidden_second), all_packs, middle,
    )
    part_qkv = jnp.einsum(
        "td,jto->jdo", flat(all_in), grads_qkv, preferred_element_type=jnp.float32
    ).astype(jnp.bfloat16)
    grads_qkv, part_qkv, part_out, scattered_first = lax.optimization_barrier(
        (grads_qkv, part_qkv, part_out, scattered_first)
    )
    scattered_out, scattered_qkv = over_col(part_out, 1), over_col(part_qkv, 1)
    blocks_grad, part_gain_attn, stream_out = stream_back(
        size, grads_qkv, all_qkv, stream, grad_middle, gain_in, blocks_out
    )
    blocks_grad, scattered_second = lax.optimization_barrier((blocks_grad, scattered_second))
    grad_out, grad_qkv = scattered_out.astype(jnp.float32), scattered_qkv.astype(jnp.float32)
    grad_gate_up = jnp.concatenate([scattered_first[:2], scattered_second[:2]], axis=2).astype(jnp.float32)
    grad_down = jnp.concatenate([scattered_first[2], scattered_second[2]], axis=1).T.astype(jnp.float32)
    logit_part = gate_value * (1.0 - gate_value) * jnp.sum(gate_sums, axis=(1, 2))
    features_here = gain_attn.shape[0]
    sums = jnp.concatenate(
        [
            part_gain_attn.reshape(cols, 1, features_here),
            part_gain_ffn.reshape(cols, 1, features_here),
            jnp.broadcast_to(
                jnp.pad(logit_part, (0, features_here - head_here))[None, None], (cols, 6, features_here)
            ),
        ],
        axis=1,
    )
    stats = jnp.sqrt(jnp.concatenate([stat_branch[:, :2], stat_ffn[:, :2]], axis=1).T)
    stream_grad, stats_all, sums = leave(
        size, cols, blocks_grad, jnp.pad(stats, ((0, 4), (0, 0))), sums
    )
    stream_out = stream_out.reshape(stream_in.shape)
    stream_grad = stream_grad.reshape(stream_in.shape).astype(jnp.float32)
    rms_table = stats_all[:, :, :4].transpose(2, 0, 1, 3).reshape(4, stream_in.shape[0])
    grad_gain_attn, grad_gain_ffn, grad_gate_logit = sums[0], sums[1], sums[2, :head_here]
    return (
        stream_out,
        stream_grad,
        grad_qkv,
        grad_out,
        grad_gate_up,
        grad_down,
        grad_gain_attn,
        grad_gain_ffn,
        grad_gate_logit,
        memory_new[None],
        norm_new.reshape(1, head_here, HD),
        rms_table,
    )


def solution(mesh):
    return jax.shard_map(
        local,
        mesh=mesh,
        in_specs=(
            P("row", "col"),
            P(None, "col", "row"),
            P("row", "col"),
            P(None, "col", "row"),
            P("row", "col"),
            P("col"),
            P("col"),
            P("row"),
            P("col", "row", None, None),
            P("col", "row", None),
            P("col", None),
            P("col", None),
            P("row", "col"),
        ),
        out_specs=(
            P("row", "col"),
            P("row", "col"),
            P(None, "col", "row"),
            P("row", "col"),
            P(None, "col", "row"),
            P("row", "col"),
            P("col"),
            P("col"),
            P("row"),
            P("col", "row", None, None),
            P("col", "row", None),
            P(None, "row"),
        ),
        check_vma=False,
    )
```

```python
import functools

import jax
import jax.numpy as jnp
from jax import lax
from jax.experimental import pallas as pl
from jax.experimental.pallas import tpu as pltpu
from jax.sharding import PartitionSpec as P

D = 2048
HD = 128
PROMPT = 1024
CONT = 4
CLEN = 128
GLEN = 1536


EPSILON = 1e-06
MASKED_LOGIT = -1e30
BIG_VMEM = 60 * 1024 * 1024
SHORT = pl.CostEstimate(flops=1000, bytes_accessed=1000, transcendentals=0)


def feature_map(values):
    return jnp.where(values > 0, values + 1.0, jnp.exp(jnp.minimum(values, 0.0)))


def feature_slope(values):
    return jnp.where(values > 0, 1.0, jnp.exp(jnp.minimum(values, 0.0)))


def split_two(value):
    high = value.astype(jnp.bfloat16)
    return high, (value - high.astype(jnp.float32)).astype(jnp.bfloat16)


def wide_dot(left, right, dims):
    left_high, left_low = split_two(left)
    right_high, right_low = split_two(right)

    def one(a, b):
        return lax.dot_general(a, b, (dims, ((), ())), preferred_element_type=jnp.float32)

    return one(left_high, right_high) + one(left_high, right_low) + one(left_low, right_high)


def narrow_dot(left, right, dims):
    right_high, right_low = split_two(right)

    def one(b):
        return lax.dot_general(left, b, (dims, ((), ())), preferred_element_type=jnp.float32)

    return one(right_high) + one(right_low)


def plain_dot(left, right, dims):
    return lax.dot_general(left, right, (dims, ((), ())), preferred_element_type=jnp.float32)


NN = ((1,), (0,))
NT = ((1,), (1,))
TN = ((0,), (0,))
QT = 256
PROMPT_TILES = PROMPT // QT
TILES = GLEN // QT


def tile_scores(tile, q, k_ref, offsets_ref, lengths_ref):
    scale = HD ** (-0.5)
    row = lax.broadcasted_iota(jnp.int32, (QT, QT), 0)
    column = lax.broadcasted_iota(jnp.int32, (QT, QT), 1)
    seen = min(tile * QT, PROMPT)
    own = plain_dot(q, k_ref[tile * QT : (tile + 1) * QT], NT) * scale
    if tile < PROMPT_TILES:
        own = jnp.where(row >= column, own, MASKED_LOGIT)
        ahead = plain_dot(q, k_ref[:seen], NT) * scale if seen else None
        return ahead, own, seen
    first = (tile - PROMPT_TILES) * (QT // CLEN)
    upper = lax.broadcasted_iota(jnp.int32, (QT, 1), 0) >= CLEN
    limit = jnp.where(upper, offsets_ref[first + 1], offsets_ref[first])
    live = jnp.where(upper, lengths_ref[first + 1] + CLEN, lengths_ref[first])
    same = (row >= CLEN) == (column >= CLEN)
    own = jnp.where((row >= column) & same & (column < live), own, MASKED_LOGIT)
    ahead = plain_dot(q, k_ref[:seen], NT) * scale
    position = lax.broadcasted_iota(jnp.int32, (QT, PROMPT), 1)
    return jnp.where(position < limit, ahead, MASKED_LOGIT), own, seen


def attend_kernel(
    offsets_ref, lengths_ref, gate_ref, qkv_ref, memory_ref, norm_ref,
    attn_ref, dot_ref, part_ref, logsum_ref, memory_new_ref, norm_new_ref,
):
    head = pl.program_id(0)
    gate = gate_ref[head]
    q_ref, k_ref, v_ref = qkv_ref.at[0, 0], qkv_ref.at[1, 0], qkv_ref.at[2, 0]
    memory_one = memory_ref[0]
    norm_one = norm_ref[0]
    for tile in range(TILES):
        rows = slice(tile * QT, (tile + 1) * QT)
        q = q_ref[rows]
        ahead, own, seen = tile_scores(tile, q, k_ref, offsets_ref, lengths_ref)
        peak = jnp.max(own, axis=1, keepdims=True)
        if ahead is not None:
            peak = jnp.maximum(peak, jnp.max(ahead, axis=1, keepdims=True))
        own = jnp.exp(own - peak)
        total = jnp.sum(own, axis=1, keepdims=True)
        dot_part = plain_dot(own.astype(jnp.bfloat16), v_ref[rows], NN)
        if ahead is not None:
            ahead = jnp.exp(ahead - peak)
            total += jnp.sum(ahead, axis=1, keepdims=True)
            dot_part += plain_dot(ahead.astype(jnp.bfloat16), v_ref[:seen], NN)
        dot_part = dot_part / total
        lifted = feature_map(q.astype(jnp.float32))
        memory_part = wide_dot(lifted, memory_one, NN) / jnp.sum(
            lifted * norm_one, axis=1, keepdims=True
        )
        attn_ref[rows, :] = (gate * memory_part + (1.0 - gate) * dot_part).astype(jnp.bfloat16)
        dot_ref[0, rows, :] = dot_part
        part_ref[0, rows, :] = memory_part
        logsum_ref[0, rows, :] = peak + jnp.log(total)
    lifted_keys = feature_map(k_ref[:PROMPT].astype(jnp.float32))
    high, low = split_two(lifted_keys)
    v = v_ref[:PROMPT]
    memory_new_ref[0] = memory_one + (plain_dot(high, v, TN) + plain_dot(low, v, TN)) / PROMPT
    norm_new_ref[0] = norm_one + jnp.mean(lifted_keys, axis=0, keepdims=True)


def head_block(shape, lead=0):
    zeros = (0,) * (len(shape) - 1 - lead)
    return pl.BlockSpec(shape, lambda h: (0,) * lead + (h,) + zeros)


SMEM_SPEC = pl.BlockSpec(memory_space=pltpu.SMEM)


def attend(heads_all, memory_one, norm_one, offsets, lengths, gate_value):
    heads = heads_all.shape[1]
    f32 = jnp.float32
    row_block = head_block((1, GLEN, HD))
    column = pl.BlockSpec((GLEN, HD), lambda h: (0, h))
    return pl.pallas_call(
        attend_kernel,
        grid=(heads,),
        in_specs=[
            SMEM_SPEC, SMEM_SPEC, SMEM_SPEC,
            head_block((3, 1, GLEN, HD), 1), head_block((1, HD, HD)), head_block((1, 1, HD)),
        ],
        out_specs=[
            column, row_block, row_block, head_block((1, GLEN, 1)),
            head_block((1, HD, HD)), head_block((1, 1, HD)),
        ],
        out_shape=[
            jax.ShapeDtypeStruct((GLEN, heads * HD), jnp.bfloat16),
            jax.ShapeDtypeStruct((heads, GLEN, HD), f32),
            jax.ShapeDtypeStruct((heads, GLEN, HD), f32),
            jax.ShapeDtypeStruct((heads, GLEN, 1), f32),
            jax.ShapeDtypeStruct((heads, HD, HD), f32),
            jax.ShapeDtypeStruct((heads, 1, HD), f32),
        ],
        compiler_params=pltpu.CompilerParams(vmem_limit_bytes=BIG_VMEM),
        cost_estimate=SHORT,
        name="attend",
    )(offsets, lengths, gate_value, heads_all, memory_one, norm_one[:, None, :])


def attend_back_kernel(
    size, cols, depth, wide,
    offsets_ref, lengths_ref, gate_ref, qkv_ref, grad_ref, dot_ref, part_ref, logsum_ref,
    memory_ref, norm_ref, middle_ref, hidden_a, hidden_b, pack_a, pack_b,
    out_ref, gate_out_ref, blocks_ref, stat_ref,
    key_sum, value_sum, stage, land, total, send, receive, h, w, h_sem, w_sem,
):
    head = pl.program_id(0)
    piece = GLEN // size
    scatter = Scatter(size, stage, land, total, send, receive)

    def h_load(i, step):
        rows = pl.ds(pl.multiple_of(scatter.order[step] * piece, piece), piece)
        return pltpu.make_async_copy((hidden_a, hidden_b)[i].at[rows], h.at[i, rows], h_sem.at[i, step])

    def w_load(i, c):
        return pltpu.make_async_copy(
            (pack_a, pack_b)[i].at[c, 2], w.at[i, pl.ds(pl.multiple_of(c * depth, depth), depth), :], w_sem.at[i, c]
        )

    def partial(step, at, store):
        for i in range(2):
            h_load(i, step).wait()

        @span_loop
        def _(t, half, columns, depth_rows):
            if step == 0:
                for k in range(SPAN // depth):
                    for i in range(2):
                        w_load(i, t * (SPAN // depth) + k).wait()
            rows = pl.ds(pl.multiple_of(at * piece, piece), piece)
            store(
                half, columns,
                plain_dot(h[0, rows, :], w[0, depth_rows, :], NT) + plain_dot(h[1, rows, :], w[1, depth_rows, :], NT),
            )

    @pl.when(head == 0)
    def _():
        for i in range(2):
            h_load(i, 0).start()
        for c in range(cols):
            for i in range(2):
                w_load(i, c).start()
        for step in range(1, size):
            for i in range(2):
                h_load(i, step).start()
        scatter.begin(partial)

    @pl.when(head == pl.num_programs(0) // 2)
    def _():
        scatter.middle()

    gate = gate_ref[head]
    keep = 1.0 - gate
    scale = HD ** (-0.5)
    q_ref, k_ref, v_ref = qkv_ref.at[0, 0], qkv_ref.at[1, 0], qkv_ref.at[2, 0]
    memory_one = memory_ref[0]
    norm_one = norm_ref[0]
    gate_row = jnp.zeros((1, HD), jnp.float32)
    key_sum[...] = jnp.zeros_like(key_sum)
    value_sum[...] = jnp.zeros_like(value_sum)
    for tile in range(TILES):
        rows = slice(tile * QT, (tile + 1) * QT)
        q = q_ref[rows]
        grad = grad_ref[0, rows, :]
        grad_float = grad.astype(jnp.float32)
        memory_part = part_ref[0, rows, :]
        dot_part = dot_ref[0, rows, :]
        against_dot = jnp.sum(grad_float * dot_part, axis=1, keepdims=True)
        gate_row += jnp.sum(grad_float * (memory_part - dot_part), axis=0, keepdims=True)
        logsum = logsum_ref[0, rows, :]
        ahead, own, seen = tile_scores(tile, q, k_ref, offsets_ref, lengths_ref)
        own = jnp.exp(own - logsum)
        value_sum[rows, :] += plain_dot(own.astype(jnp.bfloat16), grad, TN)
        own = (keep * own * (plain_dot(grad, v_ref[rows], NT) - against_dot)).astype(jnp.bfloat16)
        key_sum[rows, :] += plain_dot(own, q, TN)
        grad_q = plain_dot(own, k_ref[rows], NN)
        if ahead is not None:
            ahead = jnp.exp(ahead - logsum)
            value_sum[:seen, :] += plain_dot(ahead.astype(jnp.bfloat16), grad, TN)
            ahead = (keep * ahead * (plain_dot(grad, v_ref[:seen], NT) - against_dot)).astype(
                jnp.bfloat16
            )
            key_sum[:seen, :] += plain_dot(ahead, q, TN)
            grad_q += plain_dot(ahead, k_ref[:seen], NN)
        q_float = q.astype(jnp.float32)
        lifted = feature_map(q_float)
        inverse = gate / jnp.sum(lifted * norm_one, axis=1, keepdims=True)
        against_memory = jnp.sum(grad_float * memory_part, axis=1, keepdims=True)
        grad_lifted = inverse * (narrow_dot(grad, memory_one, NT) - against_memory * norm_one)
        out_ref[0, rows, :] = (grad_q * scale + grad_lifted * feature_slope(q_float)).astype(
            jnp.bfloat16
        )
    out_ref[1, :, :] = (key_sum[...] * scale).astype(jnp.bfloat16)
    out_ref[2, :, :] = (value_sum[...] * keep).astype(jnp.bfloat16)
    gate_out_ref[0] = gate_row

    def finish(rows):
        ffn = [total[half, rows, :] for half in range(2)]
        result = [middle_ref[rows, columns] + ffn[half] for half, columns in enumerate((LEFT, RIGHT))]
        for half, columns in enumerate((LEFT, RIGHT)):
            blocked_store(blocks_ref, rows, depth, columns, result[half].astype(jnp.bfloat16))
        stat_ref[rows, :] = lanes(
            row_mean(ffn[0] * ffn[0], ffn[1] * ffn[1]),
            row_mean(result[0] * result[0], result[1] * result[1]),
        )

    @pl.when(head == pl.num_programs(0) - 1)
    def _():
        scatter.own(partial)
        scatter.end()
        strip_loop(piece, finish)


def whole_block(shape):
    return pl.BlockSpec(shape, lambda h: (0,) * len(shape), pipeline_mode=pl.Buffered(1))


def attend_back(
    size, heads_all, grad_heads, dot_part, memory_part, logsum, memory_one, norm_one, offsets, lengths, gate_value,
    hiddens, packs, middle,
):
    heads = heads_all.shape[1]
    piece = middle.shape[0]
    cols, _, depth, wide = packs[0].shape
    row_block = head_block((1, GLEN, HD))
    return pl.pallas_call(
        functools.partial(attend_back_kernel, size, cols, depth, wide),
        grid=(heads,),
        in_specs=[
            SMEM_SPEC, SMEM_SPEC, SMEM_SPEC,
            head_block((3, 1, GLEN, HD), 1), row_block, row_block, row_block,
            head_block((1, GLEN, 1)), head_block((1, HD, HD)), head_block((1, 1, HD)),
            whole_block((piece, D)), ANY, ANY, ANY, ANY,
        ],
        out_specs=[
            pl.BlockSpec((3, GLEN, HD), lambda h: (0, 0, h)),
            head_block((1, 1, HD)),
            whole_block((cols, piece, depth)), whole_block((piece, HD)),
        ],
        out_shape=[bf(3, GLEN, heads * HD), fl(heads, 1, HD), bf(cols, piece, depth), fl(piece, HD)],
        scratch_shapes=[pltpu.VMEM((GLEN, HD), jnp.float32), pltpu.VMEM((GLEN, HD), jnp.float32)]
        + scatter_scratch(size, piece)
        + [
            pltpu.VMEM((2, GLEN, wide), jnp.bfloat16),
            pltpu.VMEM((2, D, wide), jnp.bfloat16),
            dma(2, size), dma(2, cols),
        ],
        compiler_params=comm_params(5),
        cost_estimate=SHORT,
        name="attend_back",
    )(
        offsets, lengths, gate_value, heads_all, grad_heads, dot_part, memory_part, logsum,
        memory_one, norm_one[:, None, :], middle, *hiddens, *packs,
    )


ANY = pl.BlockSpec(memory_space=pl.ANY)
VMEM = pl.BlockSpec(memory_space=pltpu.VMEM)
MESH_ID = pl.DeviceIdType.MESH
HALF = D // 2
AG_CUTS = 4


def remote(source, target, send, receive, device):
    return pltpu.make_async_remote_copy(
        src_ref=source, dst_ref=target, send_sem=send, recv_sem=receive,
        device_id=device, device_id_type=MESH_ID,
    )


def dma(*shape):
    return pltpu.SemaphoreType.DMA(shape)


def here():
    return lax.axis_index("row"), lax.axis_index("col")


def greet(peers):
    barrier = pltpu.get_barrier_semaphore()
    for peer in peers:
        pl.semaphore_signal(barrier, inc=1, device_id=peer, device_id_type=MESH_ID)
    pl.semaphore_wait(barrier, len(peers))


def square(row):
    along_x = (row // 2) * 2 + (1 - lax.rem(row, 2))
    along_y = lax.rem(row + 2, 4)
    across = (along_y // 2) * 2 + (1 - lax.rem(along_y, 2))
    return along_x, along_y, across


class Gather:
    def __init__(self, size, source, land, send, receive, own):
        self.size = size
        row, col = self.row, self.col = here()
        piece = source.shape[0]
        self.keep = pltpu.make_async_copy(source, land.at[row], own)
        if size != 4:
            self.peers = [(lax.rem(row + d, size), col) for d in range(1, size)]
            self.order = [lax.rem(row + size - d, size) for d in range(1, size)]
            self.copies = [
                remote(source, land.at[row], send.at[i], receive.at[i], peer) for i, peer in enumerate(self.peers)
            ]
            return
        self.order = rx, ry, rd = square(row)
        px, py = self.peers = [(rx, col), (ry, col)]
        height = piece // AG_CUTS
        cuts = [pl.ds(cut * height, height) for cut in range(AG_CUTS)]

        def out(cut, base, peer):
            return remote(
                source.at[cuts[cut]], land.at[row, cuts[cut]], send.at[base + cut], receive.at[base + cut], peer
            )

        def onward(cut, owner, peer):
            place = land.at[owner, cuts[cut]]
            return remote(place, place, send.at[2 * AG_CUTS + cut], receive.at[2 * AG_CUTS + cut], peer)

        middle = AG_CUTS // 2
        self.to_x = [out(cut, 0, px) for cut in range(AG_CUTS)]
        self.to_y = [out(cut, AG_CUTS, py) for cut in range(AG_CUTS)]
        self.onward = [onward(cut, rx, py) for cut in range(middle)] + [
            onward(cut, ry, px) for cut in range(middle, AG_CUTS)
        ]

    @staticmethod
    def semaphores(size):
        return 3 * AG_CUTS if size == 4 else size - 1

    def start(self, greeted=False, hold=True):
        if not greeted:
            greet(self.peers)
        if self.size != 4:
            for copy in self.copies:
                copy.start()
        else:
            for step in range(AG_CUTS):
                self.to_x[step].start()
                self.to_y[(step + AG_CUTS // 2) % AG_CUTS].start()
        self.keep.start()
        if hold:
            self.keep.wait()

    def forward(self):
        if self.size != 4:
            return
        for step in range(AG_CUTS // 2):
            later = step + AG_CUTS // 2
            self.to_x[step].wait_recv()
            self.onward[step].start()
            self.to_y[later].wait_recv()
            self.onward[later].start()

    def wait(self, step):
        middle = AG_CUTS // 2
        if self.size != 4:
            waits = [self.copies[step]]
        else:
            waits = (self.to_x[middle:], self.to_y[:middle], self.onward)[step]
        for copy in waits:
            copy.wait_recv()
        return self.order[step]

    def finish(self):
        for copy in self.copies if self.size != 4 else [*self.to_x, *self.to_y, *self.onward]:
            copy.wait_send()


class CoreGather:
    def __init__(self, cols, source, target, far_send, far_receive, near_send, near_receive, own):
        row, col = here()
        pair = (col // 2) * 2 + 1 - lax.rem(col, 2)
        chips = cols // 2
        self.greets = [(row, lax.rem(col + 2 * e, cols)) for e in range(1, chips)] + [(row, pair)]
        self.far = [
            remote(source, target.at[col], far_send.at[e], far_receive.at[e], peer)
            for e, peer in enumerate(self.greets[:-1])
        ]
        self.near = [remote(source, target.at[col], near_send.at[0], near_receive.at[0], (row, pair))]
        for e in range(1, chips):
            place = target.at[lax.rem(col + cols - 2 * e, cols)]
            self.near.append(remote(place, place, near_send.at[e], near_receive.at[e], (row, pair)))
        self.keep = pltpu.make_async_copy(source, target.at[col], own)

    @staticmethod
    def scratch(cols):
        far, near = cols // 2 - 1, cols // 2
        return [dma(far), dma(far), dma(near), dma(near), pltpu.SemaphoreType.DMA]

    def start(self):
        for copy in [*self.far, self.near[0], self.keep]:
            copy.start()

    def forward(self):
        for e, copy in enumerate(self.far):
            copy.wait_recv()
            self.near[e + 1].start()

    def finish(self):
        for copy in self.near:
            copy.wait()
        for copy in self.far:
            copy.wait_send()
        self.keep.wait()


class Scatter:
    def __init__(self, size, stage, land, total, send, receive):
        self.size, self.stage, self.land, self.total = size, stage, land, total
        self.send, self.receive = send, receive
        self.row, self.col = here()
        self.plan()

    @staticmethod
    def semaphores(size):
        return 6 if size == 4 else size - 1

    @staticmethod
    def stage_shape(size, piece):
        return (3 if size == 4 else size - 1, 2, piece, HALF)

    @staticmethod
    def land_shape(size, piece):
        return (6, piece, HALF) if size == 4 else (size - 1, 2, piece, HALF)

    def plan(self):
        row, col, stage = self.row, self.col, self.stage

        def copy(index, source, peer):
            return remote(source, self.land.at[index], self.send.at[index], self.receive.at[index], peer)

        if self.size != 4:
            others = [lax.rem(row + d, self.size) for d in range(1, self.size)]
            self.peers = [(peer, col) for peer in others]
            self.order = [*others, row]
            self.copies = [copy(slot, stage.at[slot], peer) for slot, peer in enumerate(self.peers)]
            self.after = [[slot] for slot in range(self.size - 1)]
            return
        rx, ry, rd = square(row)
        px, py = self.peers = [(rx, col), (ry, col)]
        self.order = [rd, rx, ry, row]
        self.copies = [
            copy(0, stage.at[0, 0], px), copy(1, stage.at[0, 1], py), copy(2, stage.at[1, 0], px),
            copy(3, stage.at[2, 1], py), copy(4, stage.at[2, 0], py), copy(5, stage.at[1, 1], px),
        ]
        self.after = [[0, 1], [2], [3]]

    def begin(self, partial, greeted=False):
        if not greeted:
            greet(self.peers)
        for step, row in enumerate(self.order[:-1]):

            def store(half, columns, value):
                self.stage[step, half, :, columns] = value.astype(jnp.bfloat16)

            partial(step, row, store)
            for index in self.after[step]:
                self.copies[index].start()

    def middle(self):
        if self.size != 4:
            return
        self.copies[0].wait_recv()
        self.add_stage(2, 0, self.land.at[0])
        self.copies[4].start()
        self.copies[1].wait_recv()
        self.add_stage(1, 1, self.land.at[1])
        self.copies[5].start()

    def own(self, partial):
        def store(half, columns, value):
            self.total[half, :, columns] = value

        partial(self.size - 1, self.order[-1], store)

    def end(self):
        if self.size != 4:
            for slot, copy in enumerate(self.copies):
                copy.wait_recv()
                self.add_total(0, self.land.at[slot, 0])
                self.add_total(1, self.land.at[slot, 1])
        else:
            for index, half in ((2, 0), (3, 1), (4, 0), (5, 1)):
                self.copies[index].wait_recv()
                self.add_total(half, self.land.at[index])
        for copy in self.copies:
            copy.wait_send()

    def run(self, partial, late=None, greeted=False):
        self.begin(partial, greeted)
        self.middle()
        self.own(partial)
        if late is not None:
            late()
        self.end()

    def add_stage(self, slot, half, landed):
        @pl.loop(0, landed.shape[0] // STRIP)
        def _(i):
            rows = pl.ds(pl.multiple_of(i * STRIP, STRIP), STRIP)
            value = self.stage[slot, half, rows, :].astype(jnp.float32) + landed[rows, :].astype(jnp.float32)
            self.stage[slot, half, rows, :] = value.astype(jnp.bfloat16)

    def add_total(self, half, landed):
        @pl.loop(0, landed.shape[0] // STRIP)
        def _(i):
            rows = pl.ds(pl.multiple_of(i * STRIP, STRIP), STRIP)
            self.total[half, rows, :] += landed[rows, :].astype(jnp.float32)


STRIP = 32


def scatter_scratch(size, piece):
    count = Scatter.semaphores(size)
    return [
        pltpu.VMEM(Scatter.stage_shape(size, piece), jnp.bfloat16),
        pltpu.VMEM(Scatter.land_shape(size, piece), jnp.bfloat16),
        pltpu.VMEM((2, piece, HALF), jnp.float32),
        pltpu.SemaphoreType.DMA((count,)),
        pltpu.SemaphoreType.DMA((count,)),
    ]


def gather_scratch(size, piece):
    count = Gather.semaphores(size)
    return [
        pltpu.VMEM((size, piece, D), jnp.bfloat16),
        pltpu.SemaphoreType.DMA((count,)),
        pltpu.SemaphoreType.DMA((count,)),
        pltpu.SemaphoreType.DMA,
    ]


def fetches(pairs, semaphores):
    copies = [pltpu.make_async_copy(a, b, semaphores.at[i]) for i, (a, b) in enumerate(pairs)]
    for copy in copies:
        copy.start()
    return copies


def wait_all(copies):
    for copy in copies:
        copy.wait()


def tiles_of(width, tile):
    def run(body):
        @pl.loop(0, width // tile)
        def _(t):
            body(t, pl.ds(pl.multiple_of(t * tile, tile), tile))

    return run


SPAN = 512


def span_loop(body):
    inside = HALF // SPAN

    @pl.loop(0, D // SPAN)
    def _(t):
        body(
            t, t // inside,
            pl.ds(pl.multiple_of(lax.rem(t, inside) * SPAN, SPAN), SPAN),
            pl.ds(pl.multiple_of(t * SPAN, SPAN), SPAN),
        )


def comm_params(identity):
    return pltpu.CompilerParams(
        collective_id=identity, has_side_effects=True, vmem_limit_bytes=BIG_VMEM
    )


def bf(*shape):
    return jax.ShapeDtypeStruct(shape, jnp.bfloat16)


def fl(*shape):
    return jax.ShapeDtypeStruct(shape, jnp.float32)


def project_heads(size, normed, w_all, w_out):
    piece = normed.shape[0]
    cols, _, depth, width = w_all.shape
    heads = width // HD

    def kernel(
        x_ref, w_ref, out_ref, heads_ref, all_ref, all_out_ref,
        land, send, receive, own, w, w_sem, all_sem, *rest,
    ):
        loads = fetches([(w_ref.at[c], w.at[:, pl.ds(c * depth, depth), :]) for c in range(cols)], w_sem)
        gather = Gather(size, x_ref, land, send, receive, own)
        beside = CoreGather(cols, out_ref, all_out_ref, *rest)
        greet([*gather.peers, *beside.greets])
        gather.start(greeted=True)
        beside.start()

        def compute(row, slot):
            store = pltpu.make_async_copy(land.at[row], all_ref.at[row], all_sem.at[slot])
            store.start()
            rows = pl.ds(pl.multiple_of(row * piece, piece), piece)

            @pl.loop(0, 3)
            def _(j):
                value = jnp.dot(land[row], w[j], preferred_element_type=jnp.float32).astype(jnp.bfloat16)
                for head in range(heads):
                    heads_ref[j, head, rows, :] = value[:, head * HD : (head + 1) * HD]

            return store

        wait_all(loads)
        stores = [compute(gather.row, 0)]
        gather.forward()
        beside.forward()
        for step in range(size - 1):
            stores.append(compute(gather.wait(step), step + 1))
        beside.finish()
        wait_all(stores)
        gather.finish()

    return pl.pallas_call(
        kernel,
        out_shape=[bf(3, heads, GLEN, HD), bf(size, piece, D), bf(cols, *w_out.shape)],
        in_specs=[ANY, ANY, ANY],
        out_specs=[VMEM, ANY, ANY],
        scratch_shapes=gather_scratch(size, piece)
        + [
            pltpu.VMEM((3, D, width), jnp.bfloat16),
            pltpu.SemaphoreType.DMA((cols,)),
            pltpu.SemaphoreType.DMA((size,)),
        ]
        + CoreGather.scratch(cols),
        compiler_params=comm_params(1),
        cost_estimate=SHORT,
        name="project_heads",
    )(normed, w_all, w_out)


def strip_loop(piece, body):
    @pl.loop(0, piece // STRIP)
    def _(i):
        body(pl.ds(pl.multiple_of(i * STRIP, STRIP), STRIP))


def row_mean(first, second):
    return (jnp.sum(first, axis=1, keepdims=True) + jnp.sum(second, axis=1, keepdims=True)) / D


def lanes(first, second):
    lane = lax.broadcasted_iota(jnp.int32, (STRIP, HD), 1)
    return jnp.where(lane == 0, first, jnp.where(lane == 1, second, 0.0))


LEFT, RIGHT = slice(0, HALF), slice(HALF, D)


def branch_out(size, attn, w_all, x, gain):
    piece = GLEN // size
    cols, width, depth = w_all.shape

    def kernel(attn_ref, w_ref, x_ref, gain_ref, middle_ref, normed_ref, stat_ref, stage, land, total, send, receive, w, w_sem):
        loads = fetches([(w_ref.at[c], w.at[:, pl.ds(c * depth, depth)]) for c in range(cols)], w_sem)
        scatter = Scatter(size, stage, land, total, send, receive)
        wait_all(loads)

        def partial(step, row, store):
            rows = pl.ds(pl.multiple_of(row * piece, piece), piece)
            left = attn_ref[rows, :]

            @span_loop
            def _(t, half, columns, depth_rows):
                store(half, columns, plain_dot(left, w[:, depth_rows], NN))

        scatter.run(partial)

        def finish(rows):
            branch = (total[0, rows, :], total[1, rows, :])
            middle = (
                x_ref[rows, LEFT].astype(jnp.float32) + branch[0],
                x_ref[rows, RIGHT].astype(jnp.float32) + branch[1],
            )
            mean = row_mean(middle[0] * middle[0], middle[1] * middle[1])
            inverse = lax.rsqrt(mean + EPSILON)
            for part, columns in zip(middle, (LEFT, RIGHT)):
                middle_ref[rows, columns] = part
                normed_ref[rows, columns] = (part * inverse * gain_ref[:, columns]).astype(jnp.bfloat16)
            stat_ref[rows, :] = lanes(row_mean(branch[0] * branch[0], branch[1] * branch[1]), mean)

        strip_loop(piece, finish)

    return pl.pallas_call(
        kernel,
        out_shape=[fl(piece, D), bf(piece, D), fl(piece, HD)],
        in_specs=[VMEM, ANY, VMEM, VMEM],
        out_specs=[VMEM, VMEM, VMEM],
        scratch_shapes=scatter_scratch(size, piece)
        + [pltpu.VMEM((width, D), jnp.bfloat16), pltpu.SemaphoreType.DMA((cols,))],
        compiler_params=comm_params(2),
        cost_estimate=SHORT,
        name="branch_out",
    )(attn, w_all, x, gain)


def feed_forward(size, tokens, pack, cot, first):
    piece = GLEN // size
    cols, _, depth, wide = pack.shape
    tile = min(wide, 512)
    count = wide // tile

    def kernel(x_ref, pack_ref, cot_ref, hidden_ref, grad_ref, *rest):
        if first:
            all_ref, land, send, receive, own, all_sem, *rest = rest
        else:
            land, own, *rest = rest
        w, cot_all, back, stage, w_sem, cot_sem, out_sem = rest
        if first:
            gather = Gather(size, x_ref, land, send, receive, own)
            gather.start()
            order = [gather.row, *gather.order]
        else:
            order = list(range(size))
        w_loads = fetches(
            [(pack_ref.at[c, j], w.at[j, pl.ds(c * depth, depth), :]) for j in (2, 0, 1) for c in range(cols)], w_sem
        )
        cot_loads = fetches([(cot_ref.at[row], cot_all.at[row]) for row in order], cot_sem)
        if not first:
            x_loads = fetches([(x_ref.at[row], land.at[row]) for row in order], own)

        def backward(row):
            @tiles_of(wide, tile)
            def _(t, columns):
                back[row, :, columns] = plain_dot(cot_all[row], w[2, :, columns], NN).astype(jnp.bfloat16)

        def moves(row, slot, columns):
            rows = pl.ds(pl.multiple_of(row * piece, piece), piece)
            return [
                pltpu.make_async_copy(stage.at[slot, 0], hidden_ref.at[rows, columns], out_sem.at[slot, 0]),
                pltpu.make_async_copy(stage.at[slot, 1], grad_ref.at[0, rows, columns], out_sem.at[slot, 1]),
                pltpu.make_async_copy(stage.at[slot, 2], grad_ref.at[1, rows, columns], out_sem.at[slot, 2]),
            ]

        def compute(row):
            if first:
                store = pltpu.make_async_copy(land.at[row], all_ref.at[row], all_sem)
                store.start()

            @pl.loop(0, count)
            def _(t):
                columns = pl.ds(pl.multiple_of(t * tile, tile), tile)
                slot = lax.rem(t, 2)
                x = land[row]
                gate_pre = jnp.dot(x, w[0, :, columns], preferred_element_type=jnp.float32)
                up_pre = jnp.dot(x, w[1, :, columns], preferred_element_type=jnp.float32)
                sigmoid = jax.nn.sigmoid(gate_pre)
                silu = gate_pre * sigmoid
                grad_hidden = back[row, :, columns].astype(jnp.float32)

                @pl.when(t >= 2)
                def _():
                    wait_all(moves(row, slot, columns))

                stage[slot, 0] = (silu * up_pre).astype(jnp.bfloat16)
                stage[slot, 1] = (grad_hidden * up_pre * (sigmoid + silu * (1.0 - sigmoid))).astype(jnp.bfloat16)
                stage[slot, 2] = (grad_hidden * silu).astype(jnp.bfloat16)
                for move in moves(row, slot, columns):
                    move.start()

            for slot in range(min(2, count)):
                wait_all(moves(row, slot, pl.ds(slot * tile, tile)))
            if first:
                store.wait()

        wait_all(w_loads[:cols])
        if first:
            cot_loads[0].wait()
            backward(order[0])
            gather.forward()
            wait_all(cot_loads[1:])

            @pl.loop(1, size)
            def _(d):
                backward(lax.rem(gather.row + d, size))

            wait_all(w_loads[cols:])
            for step in range(size):
                if step:
                    gather.wait(step - 1)
                compute(order[step])
            gather.finish()
            return

        @pl.loop(0, size)
        def _(row):
            pltpu.make_async_copy(cot_ref.at[row], cot_all.at[row], cot_sem.at[row]).wait()
            backward(row)

        wait_all(w_loads[cols:])

        @pl.loop(0, size)
        def _(row):
            pltpu.make_async_copy(x_ref.at[row], land.at[row], own.at[row]).wait()
            compute(row)

    out_shape = [bf(GLEN, wide), bf(2, GLEN, wide)]
    if first:
        out_shape.append(bf(size, piece, D))
        scratch = gather_scratch(size, piece) + [pltpu.SemaphoreType.DMA]
    else:
        scratch = [pltpu.VMEM((size, piece, D), jnp.bfloat16), dma(size)]
    return pl.pallas_call(
        kernel,
        out_shape=out_shape,
        in_specs=[ANY] * 3,
        out_specs=[ANY] * len(out_shape),
        scratch_shapes=scratch
        + [
            pltpu.VMEM((3, D, wide), jnp.bfloat16),
            pltpu.VMEM((size, piece, D), jnp.bfloat16),
            pltpu.VMEM((size, piece, wide), jnp.bfloat16),
            pltpu.VMEM((2, 3, piece, tile), jnp.bfloat16),
            dma(3 * cols), dma(size), dma(2, 3),
        ],
        compiler_params=comm_params(3) if first else pltpu.CompilerParams(vmem_limit_bytes=BIG_VMEM),
        cost_estimate=SHORT,
        name="feed_first" if first else "feed_second",
    )(tokens, pack, cot)


def weight_grads_kernel(x_ref, y_ref, g_ref, h_ref, out_ref):
    count = g_ref.shape[0]
    for j in range(count):
        out_ref[j] = plain_dot(x_ref[...], g_ref[j], TN).astype(jnp.bfloat16)
    out_ref[count] = plain_dot(y_ref[...], h_ref[...], TN).astype(jnp.bfloat16)


def weight_grads(x, grads, y, hidden):
    count, _, wide = grads.shape
    tile = 256
    block = pl.BlockSpec((GLEN, tile), lambda i: (0, i))
    return pl.pallas_call(
        weight_grads_kernel,
        grid=(D // tile,),
        in_specs=[
            block, block,
            pl.BlockSpec((count, GLEN, wide), lambda i: (0, 0, 0), pipeline_mode=pl.Buffered(1)),
            pl.BlockSpec((GLEN, wide), lambda i: (0, 0), pipeline_mode=pl.Buffered(1)),
        ],
        out_specs=pl.BlockSpec((count + 1, tile, wide), lambda i: (0, i, 0)),
        out_shape=bf(count + 1, D, wide),
        compiler_params=pltpu.CompilerParams(vmem_limit_bytes=BIG_VMEM),
        cost_estimate=SHORT,
        name="weight_grads",
    )(x, y, grads, hidden)


def norm_back(rows, total, stream, inverse, gain_ref, base, store, gain_sum):
    u = [total[half, rows, :] * gain_ref[:, columns] for half, columns in enumerate((LEFT, RIGHT))]
    inner = row_mean(u[0] * stream[0], u[1] * stream[1]) * inverse * inverse * inverse
    for half, columns in enumerate((LEFT, RIGHT)):
        store(columns, base[half] + inverse * u[half] - stream[half] * inner)
        gain_sum[:, columns] += jnp.sum(total[half, rows, :] * stream[half] * inverse, axis=0, keepdims=True)


def middle_back(size, grads, packs, middle, cot, gain, tokens, all_cot, hidden):
    piece = middle.shape[0]
    cols, _, depth, wide = packs[0].shape
    block = 256

    def kernel(
        first_ref, second_ref, pack_a, pack_b, middle_ref, cot_ref, gain_ref, x_ref, y_ref, hidden_ref,
        grad_ref, low_ref, gain_sum, part_ref,
        stage, land, total, send, receive, w, g_first, g_second, h, x, part,
        w_sem, first_sem, second_sem, h_sem, x_sem, part_sem,
    ):
        pack_refs = (pack_a, pack_b)
        scatter = Scatter(size, stage, land, total, send, receive)

        def piece_rows(at):
            return pl.ds(pl.multiple_of(at * piece, piece), piece)

        def first_load(step):
            return pltpu.make_async_copy(
                first_ref.at[:, piece_rows(scatter.order[step])], g_first.at[step % 2], first_sem.at[step % 2]
            )

        def second_load(step):
            rows = piece_rows(scatter.order[step])
            return pltpu.make_async_copy(second_ref.at[:, rows], g_second.at[:, rows], second_sem.at[step])

        def w_load(i, c):
            return pltpu.make_async_copy(
                pack_refs[i].at[c, pl.ds(0, 2)], w.at[i, :, pl.ds(pl.multiple_of(c * depth, depth), depth), :], w_sem.at[i, c]
            )

        first_load(0).start()
        second_load(0).start()
        for c in range(cols):
            for i in range(2):
                w_load(i, c).start()
        first_load(1).start()
        for step in range(1, size):
            second_load(step).start()
        h_load = pltpu.make_async_copy(hidden_ref, h, h_sem)
        h_load.start()
        gain_sum[...] = jnp.zeros_like(gain_sum)

        def partial(step, at, store):
            first_load(step).wait()
            second_load(step).wait()

            @span_loop
            def _(t, half, columns, depth_rows):
                if step == 0:
                    for k in range(SPAN // depth):
                        for i in range(2):
                            w_load(i, t * (SPAN // depth) + k).wait()
                rows = piece_rows(at)
                value = 0.0
                for j in range(2):
                    value += plain_dot(g_first[step % 2, j], w[0, j, depth_rows, :], NT)
                    value += plain_dot(g_second[j, rows, :], w[1, j, depth_rows, :], NT)
                store(half, columns, value)

            if step + 2 < size:
                first_load(step + 2).start()

        def x_loads(i, slot):
            columns = pl.ds(pl.multiple_of(i * block, block), block)
            return [
                pltpu.make_async_copy(source.at[:, :, columns], x.at[slot, k], x_sem.at[slot, k])
                for k, source in enumerate((x_ref, y_ref))
            ]

        def part_move(i, slot):
            columns = pl.ds(pl.multiple_of(i * block, block), block)
            return pltpu.make_async_copy(part.at[slot], part_ref.at[:, columns, :], part_sem.at[slot])

        def weights():
            count = D // block
            for load in x_loads(0, 0):
                load.start()
            h_load.wait()

            @pl.loop(0, count)
            def _(i):
                slot = lax.rem(i, 2)

                @pl.when(i + 1 < count)
                def _():
                    for load in x_loads(i + 1, 1 - slot):
                        load.start()

                wait_all(x_loads(i, slot))

                @pl.when(i >= 2)
                def _():
                    part_move(i, slot).wait()

                left = x[slot, 0].reshape(GLEN, block)
                for j in range(2):
                    part[slot, j] = plain_dot(left, g_second[j], TN).astype(jnp.bfloat16)
                part[slot, 2] = plain_dot(x[slot, 1].reshape(GLEN, block), h[...], TN).astype(jnp.bfloat16)
                part_move(i, slot).start()

            for slot in range(2):
                part_move(slot, slot).wait()

        scatter.run(partial, weights)

        def finish(rows):
            stream = [middle_ref[rows, columns] for columns in (LEFT, RIGHT)]
            base = [cot_ref[rows, columns].astype(jnp.float32) for columns in (LEFT, RIGHT)]
            inverse = lax.rsqrt(row_mean(stream[0] * stream[0], stream[1] * stream[1]) + EPSILON)

            def store(columns, value):
                grad_ref[rows, columns] = value
                low_ref[rows, columns] = value.astype(jnp.bfloat16)

            norm_back(rows, total, stream, inverse, gain_ref, base, store, gain_sum)

        strip_loop(piece, finish)

    return pl.pallas_call(
        kernel,
        out_shape=[fl(piece, D), bf(piece, D), fl(1, D), bf(3, D, wide)],
        in_specs=[ANY] * 4 + [VMEM] * 3 + [ANY] * 3,
        out_specs=[VMEM, VMEM, VMEM, ANY],
        scratch_shapes=scatter_scratch(size, piece)
        + [
            pltpu.VMEM((2, 2, D, wide), jnp.bfloat16),
            pltpu.VMEM((2, 2, piece, wide), jnp.bfloat16),
            pltpu.VMEM((2, GLEN, wide), jnp.bfloat16),
            pltpu.VMEM((GLEN, wide), jnp.bfloat16),
            pltpu.VMEM((2, 2, size, piece, block), jnp.bfloat16),
            pltpu.VMEM((2, 3, block, wide), jnp.bfloat16),
            dma(2, cols), dma(2), dma(size), pltpu.SemaphoreType.DMA, dma(2, 2), dma(2),
        ],
        compiler_params=comm_params(4),
        cost_estimate=SHORT,
        name="middle_back",
    )(*grads, *packs, middle, cot, gain, tokens, all_cot, hidden)


def blocked_store(ref, rows, depth, columns, value):
    for i in range(value.shape[1] // depth):
        ref[columns.start // depth + i, rows, :] = value[:, i * depth : (i + 1) * depth]


def branch_back(size, low, w_all):
    piece = low.shape[0]
    cols, width, depth = w_all.shape
    heads = width // HD

    def kernel(x_ref, w_ref, heads_ref, all_ref, land, send, receive, own, w, w_sem, all_sem):
        loads = fetches([(w_ref.at[c], w.at[:, pl.ds(c * depth, depth)]) for c in range(cols)], w_sem)
        gather = Gather(size, x_ref, land, send, receive, own)
        gather.start()

        def compute(row, slot):
            store = pltpu.make_async_copy(land.at[row], all_ref.at[row], all_sem.at[slot])
            store.start()
            rows = pl.ds(pl.multiple_of(row * piece, piece), piece)
            value = plain_dot(land[row], w[...], NT).astype(jnp.bfloat16)
            for head in range(heads):
                heads_ref[head, rows, :] = value[:, head * HD : (head + 1) * HD]
            return store

        wait_all(loads)
        stores = [compute(gather.row, 0)]
        gather.forward()
        for step in range(size - 1):
            stores.append(compute(gather.wait(step), step + 1))
        wait_all(stores)
        gather.finish()

    return pl.pallas_call(
        kernel,
        out_shape=[bf(heads, GLEN, HD), bf(size, piece, D)],
        in_specs=[ANY, ANY],
        out_specs=[VMEM, ANY],
        scratch_shapes=gather_scratch(size, piece)
        + [
            pltpu.VMEM((width, D), jnp.bfloat16),
            pltpu.SemaphoreType.DMA((cols,)),
            pltpu.SemaphoreType.DMA((size,)),
        ],
        compiler_params=comm_params(6),
        cost_estimate=SHORT,
        name="branch_back",
    )(low, w_all)


def stream_back(size, grads, w_all, x, grad_middle, gain, blocks_out):
    piece = x.shape[0]
    cols, _, depth, width = w_all.shape

    def kernel(
        g_ref, w_ref, x_ref, middle_ref, gain_ref, blocks_ref, out_ref, gain_sum, target_ref,
        stage, land, total, send, receive, w, w_sem, *rest,
    ):
        greet(row_and_col_peers(size, cols))
        outward = Outward(size, cols, blocks_ref, rest[0], target_ref, *rest[1:])
        outward.start()
        loads = fetches([(w_ref.at[c], w.at[:, pl.ds(c * depth, depth), :]) for c in range(cols)], w_sem)
        scatter = Scatter(size, stage, land, total, send, receive)
        wait_all(loads)
        gain_sum[...] = jnp.zeros_like(gain_sum)

        def partial(step, row, store):
            @span_loop
            def _(t, half, columns, depth_rows):
                rows = pl.ds(pl.multiple_of(row * piece, piece), piece)
                value = plain_dot(g_ref[0, rows, :], w[0, depth_rows, :], NT)
                for j in (1, 2):
                    value += plain_dot(g_ref[j, rows, :], w[j, depth_rows, :], NT)
                store(half, columns, value)

        scatter.run(partial, outward.forward, greeted=True)

        def finish(rows):
            stream = [x_ref[rows, columns].astype(jnp.float32) for columns in (LEFT, RIGHT)]
            base = [middle_ref[rows, columns] for columns in (LEFT, RIGHT)]
            inverse = lax.rsqrt(row_mean(stream[0] * stream[0], stream[1] * stream[1]) + EPSILON)

            def store(columns, value):
                blocked_store(out_ref, rows, depth, columns, value.astype(jnp.bfloat16))

            norm_back(rows, total, stream, inverse, gain_ref, base, store, gain_sum)

        strip_loop(piece, finish)
        outward.finish()

    return pl.pallas_call(
        kernel,
        out_shape=[bf(cols, piece, depth), fl(1, D), bf(cols // size, size, piece, depth)],
        in_specs=[VMEM, ANY, VMEM, VMEM, VMEM, VMEM],
        out_specs=[VMEM, VMEM, ANY],
        scratch_shapes=scatter_scratch(size, piece)
        + [pltpu.VMEM((3, D, width), jnp.bfloat16), pltpu.SemaphoreType.DMA((cols,))]
        + Outward.scratch(size, cols, piece, depth),
        compiler_params=comm_params(7),
        cost_estimate=SHORT,
        name="stream_back",
    )(grads, w_all, x, grad_middle, gain, blocks_out)


def row_and_col_peers(size, cols):
    row, col = here()
    return [(lax.rem(row + d, size), col) for d in range(1, size)] + [
        (row, lax.rem(col + e, cols)) for e in range(1, cols)
    ]


class Inward:
    def __init__(self, size, cols, source, middle, land, first_send, first_receive, send, receive, own):
        self.size, self.cols, self.groups = size, cols, cols // size
        self.source, self.middle, self.land = source, middle, land
        self.first_send, self.first_receive = first_send, first_receive
        self.send, self.receive, self.own = send, receive, own
        self.row, self.col = here()

    @staticmethod
    def scratch(size, cols, piece, depth):
        return [
            pltpu.VMEM((size, cols // size, piece, depth), jnp.bfloat16),
            pltpu.VMEM((cols, piece, depth), jnp.bfloat16),
            dma(size - 1), dma(size - 1), dma(cols), dma(cols), dma(2),
        ]

    def start(self):
        row, col = self.row, self.col
        self.first = []
        for d in range(1, self.size):
            peer = lax.rem(row + d, self.size)
            self.first.append(
                remote(
                    self.source.at[:, peer], self.middle.at[row],
                    self.first_send.at[d - 1], self.first_receive.at[d - 1], (peer, col),
                )
            )
            self.first[-1].start()
        self.keep = pltpu.make_async_copy(self.source.at[:, row], self.middle.at[row], self.own.at[0])
        self.keep.start()

    def forward(self):
        row, col = self.row, self.col
        for d in range(self.size):
            origin = lax.rem(row + self.size - d, self.size)
            if d == 0:
                self.keep.wait()
            else:
                self.first[d - 1].wait_recv()
            for i in range(self.groups):
                group = origin * self.groups + i

                @pl.when(group != col)
                def _():
                    remote(
                        self.middle.at[origin, i], self.land.at[col],
                        self.send.at[group], self.receive.at[col], (row, group),
                    ).start()

                @pl.when(group == col)
                def _():
                    pltpu.make_async_copy(self.middle.at[origin, i], self.land.at[col], self.own.at[1]).start()

    def finish(self):
        row, col = self.row, self.col
        pltpu.make_async_copy(self.middle.at[0, 0], self.land.at[col], self.own.at[1]).wait()
        for e in range(1, self.cols):
            peer = lax.rem(col + e, self.cols)
            remote(
                self.middle.at[0, 0], self.land.at[peer], self.send.at[peer], self.receive.at[peer], (row, peer)
            ).wait()
        for copy in self.first:
            copy.wait_send()


class Outward:
    def __init__(self, size, cols, source, middle, target, first_send, first_receive, send, receive, own):
        self.size, self.cols, self.groups = size, cols, cols // size
        self.source, self.middle, self.target = source, middle, target
        self.first_send, self.first_receive = first_send, first_receive
        self.send, self.receive, self.own = send, receive, own
        self.row, self.col = here()

    @staticmethod
    def scratch(size, cols, piece, depth):
        return [
            pltpu.VMEM((cols, piece, depth), jnp.bfloat16),
            dma(cols - 1), dma(cols - 1), dma(cols), dma(cols), dma(cols // size),
        ]

    def start(self):
        row, col = self.row, self.col
        self.first = []
        for e in range(1, self.cols):
            peer = lax.rem(col + e, self.cols)
            self.first.append(
                remote(
                    self.source.at[peer], self.middle.at[col],
                    self.first_send.at[e - 1], self.first_receive.at[e - 1], (row, peer),
                )
            )
            self.first[-1].start()

    def forward(self):
        row, col = self.row, self.col
        for e in range(self.cols):
            group = lax.rem(col + self.cols - e, self.cols)
            if e:
                self.first[e - 1].wait_recv()
            block = self.middle.at[group] if e else self.source.at[col]
            home, i = group // self.groups, lax.rem(group, self.groups)

            @pl.when(home != row)
            def _():
                remote(
                    block, self.target.at[i, row],
                    self.send.at[group], self.receive.at[i * self.size + row], (home, col),
                ).start()

            @pl.when(home == row)
            def _():
                pltpu.make_async_copy(block, self.target.at[i, row], self.own.at[i]).start()

    def finish(self):
        row, col = self.row, self.col
        for i in range(self.groups):
            pltpu.make_async_copy(self.middle.at[0], self.target.at[i, row], self.own.at[i]).wait()
            for d in range(1, self.size):
                peer = lax.rem(row + d, self.size)
                remote(
                    self.middle.at[0], self.target.at[i, peer],
                    self.send.at[peer * self.groups + i], self.receive.at[i * self.size + peer], (peer, col),
                ).wait()
        for copy in self.first:
            copy.wait_send()


def by_pieces(block, size):
    return block.reshape(block.shape[0] // GLEN, size, GLEN // size, block.shape[1])


def enter(size, cols, stream_in, cotangent, gains):
    pieces = by_pieces(stream_in, size)
    piece, depth = pieces.shape[2:]
    scratch = Inward.scratch(size, cols, piece, depth)

    def kernel(
        x_ref, cot_ref, gains_ref, tokens_ref, normed_ref, gain_in_ref, gain_mid_ref, cot_tokens_ref, all_cot_ref,
        gains_land, gains_send, gains_receive, gather_send, gather_receive, gather_own, *rest,
    ):
        greet(row_and_col_peers(size, cols))
        exchange = Inward(size, cols, x_ref, *rest[: len(scratch)])
        second = Inward(size, cols, cot_ref, *rest[len(scratch) :])
        gather = Gather(size, cot_tokens_ref, all_cot_ref, gather_send, gather_receive, gather_own)
        second.start()
        exchange.start()
        row, col = here()
        copies = []
        for e in range(1, cols):
            peer = lax.rem(col + e, cols)
            copies.append(
                remote(gains_ref, gains_land.at[col], gains_send.at[e - 1], gains_receive.at[e - 1], (row, peer))
            )
            copies[-1].start()
        gains_land[col] = gains_ref[...]
        second.forward()
        exchange.forward()
        second.finish()

        def assemble(rows):
            for c in range(cols):
                cot_tokens_ref[rows, c * depth : (c + 1) * depth] = second.land[c, rows, :]

        strip_loop(piece, assemble)
        gather.start(greeted=True, hold=False)
        gather.forward()
        for copy in copies:
            copy.wait()
        for c in range(cols):
            gain_in_ref[:, c * depth : (c + 1) * depth] = gains_land[c, 0:1, :]
            gain_mid_ref[:, c * depth : (c + 1) * depth] = gains_land[c, 1:2, :]
        exchange.finish()
        land = exchange.land

        def norm(rows):
            total = jnp.zeros((STRIP, 1), jnp.float32)
            for c in range(cols):
                part = land[c, rows, :]
                tokens_ref[rows, c * depth : (c + 1) * depth] = part
                part = part.astype(jnp.float32)
                total += jnp.sum(part * part, axis=1, keepdims=True)
            inverse = lax.rsqrt(total / D + EPSILON)
            for c in range(cols):
                columns = slice(c * depth, (c + 1) * depth)
                normed_ref[rows, columns] = (
                    land[c, rows, :].astype(jnp.float32) * inverse * gain_in_ref[:, columns]
                ).astype(jnp.bfloat16)

        strip_loop(piece, norm)
        for step in range(size - 1):
            gather.wait(step)
        gather.keep.wait()
        gather.finish()

    return pl.pallas_call(
        kernel,
        out_shape=[bf(piece, D), bf(piece, D), fl(1, D), fl(1, D), bf(piece, D), bf(size, piece, D)],
        in_specs=[ANY, ANY, VMEM],
        out_specs=[VMEM] * 5 + [ANY],
        scratch_shapes=[pltpu.VMEM((cols, 8, depth), jnp.float32), dma(cols - 1), dma(cols - 1)]
        + [dma(Gather.semaphores(size)), dma(Gather.semaphores(size)), pltpu.SemaphoreType.DMA]
        + scratch * 2,
        compiler_params=comm_params(8),
        cost_estimate=SHORT,
        name="enter",
    )(pieces, by_pieces(cotangent, size), jnp.pad(gains, ((0, 6), (0, 0))))


def leave(size, cols, blocks_grad, stats, sums):
    _, piece, depth = blocks_grad.shape
    groups = cols // size

    def kernel(
        grad_ref, stats_ref, sums_ref, grad_target, stats_target, sums_target,
        stats_row, stats_all, sums_col, sums_part, sums_row,
        a_send, a_receive, b_send, b_receive, c_send, c_receive, d_send, d_receive, *rest,
    ):
        row, col = here()
        greet(row_and_col_peers(size, cols))
        grad = Outward(size, cols, grad_ref, rest[0], grad_target, *rest[1:])
        home, slot = col // groups, lax.rem(col, groups)
        col_peers = [lax.rem(col + e, cols) for e in range(1, cols)]
        row_peers = [lax.rem(row + d, size) for d in range(1, size)]

        def sums_first(peer):
            return remote(sums_ref.at[peer], sums_col.at[col], c_send.at[peer], c_receive.at[col], (row, peer))

        for peer in col_peers:
            sums_first(peer).start()
        sums_col[col] = sums_ref[col]

        @pl.when(home != row)
        def _():
            remote(stats_ref, stats_row.at[row], a_send, a_receive.at[row], (home, col)).start()

        @pl.when(home == row)
        def _():
            stats_row[row] = stats_ref[...]

        grad.start()
        for peer in col_peers:
            remote(sums_ref.at[peer], sums_col.at[peer], c_send.at[peer], c_receive.at[peer], (row, peer)).wait()
        total = sums_col[0]
        for c in range(1, cols):
            total += sums_col[c]
        sums_part[...] = total
        sums_row[row] = total
        for peer in row_peers:
            remote(sums_part, sums_row.at[row], d_send.at[peer], d_receive.at[row], (peer, col)).start()

        @pl.when(home == row)
        def _():
            for peer in row_peers:
                remote(stats_ref, stats_row.at[peer], a_send, a_receive.at[peer], (peer, col)).wait_recv()
            for e, peer in enumerate(col_peers):
                remote(stats_row, stats_all.at[slot], b_send.at[e], b_receive.at[slot], (row, peer)).start()
            stats_all[slot] = stats_row[...]

        grad.forward()
        for peer in row_peers:
            remote(sums_part, sums_row.at[peer], d_send.at[peer], d_receive.at[peer], (peer, col)).wait()
        whole = sums_row[0]
        for r in range(1, size):
            whole += sums_row[r]
        line = lax.broadcasted_iota(jnp.int32, (8, depth), 0)
        sums_target[...] = jnp.where(line < 2, whole, total)

        @pl.when(home == row)
        def _():
            for e, peer in enumerate(col_peers):
                remote(stats_row, stats_all.at[slot], b_send.at[e], b_receive.at[slot], (row, peer)).wait_send()

        @pl.when(home != row)
        def _():
            remote(stats_ref, stats_row.at[row], a_send, a_receive.at[row], (home, col)).wait_send()

        for i in range(groups):
            group = row * groups + i

            @pl.when(group != col)
            def _():
                remote(stats_row, stats_all.at[i], b_send.at[0], b_receive.at[i], (row, group)).wait_recv()

        stats_target[...] = stats_all[...]
        grad.finish()

    return pl.pallas_call(
        kernel,
        out_shape=[
            bf(groups, size, piece, depth),
            fl(groups, size, 8, piece), fl(8, depth),
        ],
        in_specs=[VMEM] * 3,
        out_specs=[ANY, VMEM, VMEM],
        scratch_shapes=[
            pltpu.VMEM((size, 8, piece), jnp.float32),
            pltpu.VMEM((groups, size, 8, piece), jnp.float32),
            pltpu.VMEM((cols, 8, depth), jnp.float32),
            pltpu.VMEM((8, depth), jnp.float32),
            pltpu.VMEM((size, 8, depth), jnp.float32),
            pltpu.SemaphoreType.DMA, dma(size), dma(cols - 1), dma(groups), dma(cols), dma(cols), dma(size), dma(size),
        ]
        + Outward.scratch(size, cols, piece, depth),
        compiler_params=comm_params(10),
        cost_estimate=SHORT,
        name="leave",
    )(blocks_grad, stats, sums)


def over_col(partial, axis):
    return lax.psum_scatter(partial.astype(jnp.bfloat16), "col", scatter_dimension=axis, tiled=True)


def flat(pieces):
    return pieces.reshape(GLEN, D)


def local(
    stream_in,
    w_qkv,
    w_out,
    w_gate_up,
    w_down,
    gain_attn,
    gain_ffn,
    gate_logit,
    memory,
    memory_norm,
    offsets,
    lengths,
    cotangent,
):
    head_here = memory.shape[1]
    size = lax.axis_size("row")
    cols = lax.axis_size("col")
    all_qkv = lax.all_gather(w_qkv, "col", axis=0, tiled=False)
    units = w_down.shape[0] // 2
    packs = [
        jnp.concatenate([w_gate_up[:, :, part], w_down[part].T[None]], axis=0)
        for part in (slice(0, units), slice(units, None))
    ]
    all_packs = [lax.all_gather(pack, "col", axis=0, tiled=False) for pack in packs]
    gate_value = jax.nn.sigmoid(gate_logit)
    group = (memory[0], memory_norm[0], offsets[0], lengths[0], gate_value)
    stream, normed_in, gain_in, gain_mid, cot, all_cot = enter(
        size, cols, stream_in, cotangent, jnp.stack([gain_attn, gain_ffn])
    )
    heads_all, all_in, all_out = project_heads(size, normed_in, all_qkv, w_out)
    attn, dot_part, memory_part, logsum, memory_new, norm_new = attend(heads_all, *group)
    middle, normed_ffn, stat_branch = branch_out(size, attn, all_out, stream, gain_mid)
    hidden_first, grads_first, all_ffn = feed_forward(size, normed_ffn, all_packs[0], all_cot, True)
    part_first = weight_grads(flat(all_ffn), grads_first, flat(all_cot), hidden_first)
    part_first, all_ffn = lax.optimization_barrier((part_first, all_ffn))
    scattered_first = over_col(part_first, 1)
    hidden_second, grads_second = feed_forward(size, all_ffn, all_packs[1], all_cot, False)
    grad_middle, low_branch, part_gain_ffn, part_second = middle_back(
        size, (grads_first, grads_second), all_packs, middle, cot, gain_mid, all_ffn, all_cot, hidden_second
    )
    scattered_second = over_col(part_second, 1)
    grad_heads, all_branch = branch_back(size, low_branch, all_out)
    grads_qkv, gate_sums, blocks_out, stat_ffn = attend_back(
        size, heads_all, grad_heads, dot_part, memory_part, logsum, *group,
        (hidden_first, hidden_second), all_packs, middle,
    )
    part_attn = weight_grads(flat(all_in), grads_qkv, flat(all_branch), attn)
    grads_qkv, part_attn, scattered_first = lax.optimization_barrier((grads_qkv, part_attn, scattered_first))
    scattered_attn = over_col(part_attn, 1)
    blocks_grad, part_gain_attn, stream_out = stream_back(
        size, grads_qkv, all_qkv, stream, grad_middle, gain_in, blocks_out
    )
    grad_gate_up = jnp.concatenate([scattered_first[:2], scattered_second[:2]], axis=2).astype(jnp.float32)
    grad_down = jnp.concatenate([scattered_first[2], scattered_second[2]], axis=1).T.astype(jnp.float32)
    blocks_grad, grad_gate_up, grad_down = lax.optimization_barrier((blocks_grad, grad_gate_up, grad_down))
    grad_qkv, grad_out = scattered_attn[:3].astype(jnp.float32), scattered_attn[3].T.astype(jnp.float32)
    logit_part = gate_value * (1.0 - gate_value) * jnp.sum(gate_sums, axis=(1, 2))
    features_here = gain_attn.shape[0]
    sums = jnp.concatenate(
        [
            part_gain_attn.reshape(cols, 1, features_here),
            part_gain_ffn.reshape(cols, 1, features_here),
            jnp.broadcast_to(
                jnp.pad(logit_part, (0, features_here - head_here))[None, None], (cols, 6, features_here)
            ),
        ],
        axis=1,
    )
    stats = jnp.sqrt(jnp.concatenate([stat_branch[:, :2], stat_ffn[:, :2]], axis=1).T)
    stream_grad, stats_all, sums = leave(
        size, cols, blocks_grad, jnp.pad(stats, ((0, 4), (0, 0))), sums
    )
    stream_out = stream_out.reshape(stream_in.shape)
    stream_grad = stream_grad.reshape(stream_in.shape).astype(jnp.float32)
    rms_table = stats_all[:, :, :4].transpose(2, 0, 1, 3).reshape(4, stream_in.shape[0])
    grad_gain_attn, grad_gain_ffn, grad_gate_logit = sums[0], sums[1], sums[2, :head_here]
    return (
        stream_out,
        stream_grad,
        grad_qkv,
        grad_out,
        grad_gate_up,
        grad_down,
        grad_gain_attn,
        grad_gain_ffn,
        grad_gate_logit,
        memory_new[None],
        norm_new.reshape(1, head_here, HD),
        rms_table,
    )


def solution(mesh):
    return jax.shard_map(
        local,
        mesh=mesh,
        in_specs=(
            P("row", "col"),
            P(None, "col", "row"),
            P("row", "col"),
            P(None, "col", "row"),
            P("row", "col"),
            P("col"),
            P("col"),
            P("row"),
            P("col", "row", None, None),
            P("col", "row", None),
            P("col", None),
            P("col", None),
            P("row", "col"),
        ),
        out_specs=(
            P("row", "col"),
            P("row", "col"),
            P(None, "col", "row"),
            P("row", "col"),
            P(None, "col", "row"),
            P("row", "col"),
            P("col"),
            P("col"),
            P("row"),
            P("col", "row", None, None),
            P("col", "row", None),
            P(None, "row"),
        ),
        check_vma=False,
    )
```

```python
import functools

import jax
import jax.numpy as jnp
from jax import lax
from jax.experimental import pallas as pl
from jax.experimental.pallas import tpu as pltpu
from jax.sharding import PartitionSpec as P

D = 2048
HD = 128
PROMPT = 1024
CONT = 4
CLEN = 128
GLEN = 1536


EPSILON = 1e-06
MASKED_LOGIT = -1e30
BIG_VMEM = 60 * 1024 * 1024
SHORT = pl.CostEstimate(flops=1000, bytes_accessed=1000, transcendentals=0)


def feature_map(values):
    return jnp.where(values > 0, values + 1.0, jnp.exp(jnp.minimum(values, 0.0)))


def feature_slope(values):
    return jnp.where(values > 0, 1.0, jnp.exp(jnp.minimum(values, 0.0)))


def split_two(value):
    high = value.astype(jnp.bfloat16)
    return high, (value - high.astype(jnp.float32)).astype(jnp.bfloat16)


def wide_dot(left, right, dims):
    left_high, left_low = split_two(left)
    right_high, right_low = split_two(right)

    def one(a, b):
        return lax.dot_general(a, b, (dims, ((), ())), preferred_element_type=jnp.float32)

    return one(left_high, right_high) + one(left_high, right_low) + one(left_low, right_high)


def narrow_dot(left, right, dims):
    right_high, right_low = split_two(right)

    def one(b):
        return lax.dot_general(left, b, (dims, ((), ())), preferred_element_type=jnp.float32)

    return one(right_high) + one(right_low)


def plain_dot(left, right, dims):
    return lax.dot_general(left, right, (dims, ((), ())), preferred_element_type=jnp.float32)


NN = ((1,), (0,))
NT = ((1,), (1,))
TN = ((0,), (0,))
QT = 256
PROMPT_TILES = PROMPT // QT
TILES = GLEN // QT


def tile_rows(tile):
    return pl.ds(pl.multiple_of(tile * QT, QT), QT) if not isinstance(tile, int) else slice(tile * QT, (tile + 1) * QT)


def tile_scores(tile, q, k_ref, offsets_ref, lengths_ref):
    scale = HD ** (-0.5)
    row = lax.broadcasted_iota(jnp.int32, (QT, QT), 0)
    column = lax.broadcasted_iota(jnp.int32, (QT, QT), 1)
    own = plain_dot(q, k_ref[tile_rows(tile)], NT) * scale
    if isinstance(tile, int) and tile < PROMPT_TILES:
        seen = tile * QT
        own = jnp.where(row >= column, own, MASKED_LOGIT)
        ahead = plain_dot(q, k_ref[:seen], NT) * scale if seen else None
        return ahead, own, seen
    first = (tile - PROMPT_TILES) * (QT // CLEN)
    upper = lax.broadcasted_iota(jnp.int32, (QT, 1), 0) >= CLEN
    limit = jnp.where(upper, offsets_ref[first + 1], offsets_ref[first])
    live = jnp.where(upper, lengths_ref[first + 1] + CLEN, lengths_ref[first])
    same = (row >= CLEN) == (column >= CLEN)
    own = jnp.where((row >= column) & same & (column < live), own, MASKED_LOGIT)
    ahead = plain_dot(q, k_ref[:PROMPT], NT) * scale
    position = lax.broadcasted_iota(jnp.int32, (QT, PROMPT), 1)
    return jnp.where(position < limit, ahead, MASKED_LOGIT), own, PROMPT


def each_tile(body):
    for tile in range(PROMPT_TILES):
        body(tile)
    pl.loop(PROMPT_TILES, TILES)(body)


def attend_kernel(
    offsets_ref, lengths_ref, gate_ref, qkv_ref, memory_ref, norm_ref,
    attn_ref, dot_ref, part_ref, logsum_ref, memory_new_ref, norm_new_ref,
):
    head = pl.program_id(0)
    gate = gate_ref[head]
    q_ref, k_ref, v_ref = qkv_ref.at[0, 0], qkv_ref.at[1, 0], qkv_ref.at[2, 0]
    memory_one = memory_ref[0]
    norm_one = norm_ref[0]
    for tile in range(TILES):
        rows = slice(tile * QT, (tile + 1) * QT)
        q = q_ref[rows]
        ahead, own, seen = tile_scores(tile, q, k_ref, offsets_ref, lengths_ref)
        peak = jnp.max(own, axis=1, keepdims=True)
        if ahead is not None:
            peak = jnp.maximum(peak, jnp.max(ahead, axis=1, keepdims=True))
        own = jnp.exp(own - peak)
        total = jnp.sum(own, axis=1, keepdims=True)
        dot_part = plain_dot(own.astype(jnp.bfloat16), v_ref[rows], NN)
        if ahead is not None:
            ahead = jnp.exp(ahead - peak)
            total += jnp.sum(ahead, axis=1, keepdims=True)
            dot_part += plain_dot(ahead.astype(jnp.bfloat16), v_ref[:seen], NN)
        dot_part = dot_part / total
        lifted = feature_map(q.astype(jnp.float32))
        memory_part = wide_dot(lifted, memory_one, NN) / jnp.sum(
            lifted * norm_one, axis=1, keepdims=True
        )
        attn_ref[rows, :] = (gate * memory_part + (1.0 - gate) * dot_part).astype(jnp.bfloat16)
        dot_ref[0, rows, :] = dot_part
        part_ref[0, rows, :] = memory_part
        logsum_ref[0, rows, :] = peak + jnp.log(total)
    lifted_keys = feature_map(k_ref[:PROMPT].astype(jnp.float32))
    high, low = split_two(lifted_keys)
    v = v_ref[:PROMPT]
    memory_new_ref[0] = memory_one + (plain_dot(high, v, TN) + plain_dot(low, v, TN)) / PROMPT
    norm_new_ref[0] = norm_one + jnp.mean(lifted_keys, axis=0, keepdims=True)


def head_block(shape, lead=0):
    zeros = (0,) * (len(shape) - 1 - lead)
    return pl.BlockSpec(shape, lambda h: (0,) * lead + (h,) + zeros)


SMEM_SPEC = pl.BlockSpec(memory_space=pltpu.SMEM)


def attend(heads_all, memory_one, norm_one, offsets, lengths, gate_value):
    heads = heads_all.shape[1]
    f32 = jnp.float32
    row_block = head_block((1, GLEN, HD))
    column = pl.BlockSpec((GLEN, HD), lambda h: (0, h))
    return pl.pallas_call(
        attend_kernel,
        grid=(heads,),
        in_specs=[
            SMEM_SPEC, SMEM_SPEC, SMEM_SPEC,
            head_block((3, 1, GLEN, HD), 1), head_block((1, HD, HD)), head_block((1, 1, HD)),
        ],
        out_specs=[
            column, row_block, row_block, head_block((1, GLEN, 1)),
            head_block((1, HD, HD)), head_block((1, 1, HD)),
        ],
        out_shape=[
            jax.ShapeDtypeStruct((GLEN, heads * HD), jnp.bfloat16),
            jax.ShapeDtypeStruct((heads, GLEN, HD), f32),
            jax.ShapeDtypeStruct((heads, GLEN, HD), f32),
            jax.ShapeDtypeStruct((heads, GLEN, 1), f32),
            jax.ShapeDtypeStruct((heads, HD, HD), f32),
            jax.ShapeDtypeStruct((heads, 1, HD), f32),
        ],
        compiler_params=pltpu.CompilerParams(vmem_limit_bytes=BIG_VMEM),
        cost_estimate=SHORT,
        name="attend",
    )(offsets, lengths, gate_value, heads_all, memory_one, norm_one[:, None, :])


def attend_back_kernel(
    size, cols, depth, wide,
    offsets_ref, lengths_ref, gate_ref, qkv_ref, grad_ref, dot_ref, part_ref, logsum_ref,
    memory_ref, norm_ref, middle_ref, hidden_a, hidden_b, pack_a, pack_b,
    out_ref, gate_out_ref, blocks_ref, stat_ref,
    key_sum, value_sum, query_sum, stage, land, total, send, receive, h, w, h_sem, w_sem,
):
    head = pl.program_id(0)
    piece = GLEN // size
    scatter = Scatter(size, stage, land, total, send, receive)

    def h_load(i, step):
        rows = pl.ds(pl.multiple_of(scatter.row_at(step) * piece, piece), piece)
        return pltpu.make_async_copy((hidden_a, hidden_b)[i].at[rows], h.at[i, rows], h_sem.at[i, step])

    def w_load(i, c):
        return pltpu.make_async_copy(
            (pack_a, pack_b)[i].at[c, 2], w.at[i, pl.ds(pl.multiple_of(c * depth, depth), depth), :], w_sem.at[i, c]
        )

    def partial(step, at, store):
        for i in range(2):
            h_load(i, step).wait()

        @span_loop
        def _(t, half, columns, depth_rows):
            @pl.when(step == 0)
            def _():
                for k in range(SPAN // depth):
                    for i in range(2):
                        w_load(i, t * (SPAN // depth) + k).wait()

            rows = pl.ds(pl.multiple_of(at * piece, piece), piece)
            store(
                half, columns,
                plain_dot(h[0, rows, :], w[0, depth_rows, :], NT) + plain_dot(h[1, rows, :], w[1, depth_rows, :], NT),
            )

    @pl.when(head == 0)
    def _():
        for i in range(2):
            h_load(i, 0).start()
        for c in range(cols):
            for i in range(2):
                w_load(i, c).start()
        for step in range(1, size):
            for i in range(2):
                h_load(i, step).start()
        scatter.begin(partial)

    @pl.when(head == pl.num_programs(0) // 2)
    def _():
        scatter.middle()

    gate = gate_ref[head]
    keep = 1.0 - gate
    scale = HD ** (-0.5)
    q_ref, k_ref, v_ref = qkv_ref.at[0, 0], qkv_ref.at[1, 0], qkv_ref.at[2, 0]
    memory_one = memory_ref[0]
    norm_one = norm_ref[0]
    gate_out_ref[0] = jnp.zeros((1, HD), jnp.float32)
    key_sum[...] = jnp.zeros_like(key_sum)
    value_sum[...] = jnp.zeros_like(value_sum)

    @pl.loop(0, TILES)
    def _(tile):
        rows = tile_rows(tile)
        grad = grad_ref[0, rows, :]
        grad_float = grad.astype(jnp.float32)
        memory_part = part_ref[0, rows, :]
        gate_out_ref[0] += jnp.sum(grad_float * (memory_part - dot_ref[0, rows, :]), axis=0, keepdims=True)
        q_float = q_ref[rows].astype(jnp.float32)
        lifted = feature_map(q_float)
        inverse = gate / jnp.sum(lifted * norm_one, axis=1, keepdims=True)
        against_memory = jnp.sum(grad_float * memory_part, axis=1, keepdims=True)
        grad_lifted = inverse * (narrow_dot(grad, memory_one, NT) - against_memory * norm_one)
        query_sum[rows, :] = grad_lifted * feature_slope(q_float)

    def one(tile):
        rows = tile_rows(tile)
        q = q_ref[rows]
        grad = grad_ref[0, rows, :]
        grad_float = grad.astype(jnp.float32)
        against_dot = jnp.sum(grad_float * dot_ref[0, rows, :], axis=1, keepdims=True)
        logsum = logsum_ref[0, rows, :]
        ahead, own, seen = tile_scores(tile, q, k_ref, offsets_ref, lengths_ref)
        own = jnp.exp(own - logsum)
        value_sum[rows, :] += plain_dot(own.astype(jnp.bfloat16), grad, TN)
        own = (keep * own * (plain_dot(grad, v_ref[rows], NT) - against_dot)).astype(jnp.bfloat16)
        key_sum[rows, :] += plain_dot(own, q, TN)
        grad_q = plain_dot(own, k_ref[rows], NN)
        if ahead is not None:
            ahead = jnp.exp(ahead - logsum)
            value_sum[:seen, :] += plain_dot(ahead.astype(jnp.bfloat16), grad, TN)
            ahead = (keep * ahead * (plain_dot(grad, v_ref[:seen], NT) - against_dot)).astype(
                jnp.bfloat16
            )
            key_sum[:seen, :] += plain_dot(ahead, q, TN)
            grad_q += plain_dot(ahead, k_ref[:seen], NN)
        out_ref[0, rows, :] = (grad_q * scale + query_sum[rows, :]).astype(jnp.bfloat16)

    each_tile(one)
    out_ref[1, :, :] = (key_sum[...] * scale).astype(jnp.bfloat16)
    out_ref[2, :, :] = (value_sum[...] * keep).astype(jnp.bfloat16)

    def finish(rows):
        ffn = [total[half, rows, :] for half in range(2)]
        result = [middle_ref[rows, columns] + ffn[half] for half, columns in enumerate((LEFT, RIGHT))]
        for half, columns in enumerate((LEFT, RIGHT)):
            blocked_store(blocks_ref, rows, depth, columns, result[half].astype(jnp.bfloat16))
        stat_ref[rows, :] = lanes(
            row_mean(ffn[0] * ffn[0], ffn[1] * ffn[1]),
            row_mean(result[0] * result[0], result[1] * result[1]),
        )

    @pl.when(head == pl.num_programs(0) - 1)
    def _():
        scatter.own(partial)
        scatter.end()
        strip_loop(piece, finish)


def whole_block(shape):
    return pl.BlockSpec(shape, lambda h: (0,) * len(shape), pipeline_mode=pl.Buffered(1))


def attend_back(
    size, heads_all, grad_heads, dot_part, memory_part, logsum, memory_one, norm_one, offsets, lengths, gate_value,
    hiddens, packs, middle,
):
    heads = heads_all.shape[1]
    piece = middle.shape[0]
    cols, _, depth, wide = packs[0].shape
    row_block = head_block((1, GLEN, HD))
    return pl.pallas_call(
        functools.partial(attend_back_kernel, size, cols, depth, wide),
        grid=(heads,),
        in_specs=[
            SMEM_SPEC, SMEM_SPEC, SMEM_SPEC,
            head_block((3, 1, GLEN, HD), 1), row_block, row_block, row_block,
            head_block((1, GLEN, 1)), head_block((1, HD, HD)), head_block((1, 1, HD)),
            whole_block((piece, D)), ANY, ANY, ANY, ANY,
        ],
        out_specs=[
            pl.BlockSpec((3, GLEN, HD), lambda h: (0, 0, h)),
            head_block((1, 1, HD)),
            whole_block((cols, piece, depth)), whole_block((piece, HD)),
        ],
        out_shape=[bf(3, GLEN, heads * HD), fl(heads, 1, HD), bf(cols, piece, depth), fl(piece, HD)],
        scratch_shapes=[pltpu.VMEM((GLEN, HD), jnp.float32)] * 3
        + scatter_scratch(size, piece)
        + [
            pltpu.VMEM((2, GLEN, wide), jnp.bfloat16),
            pltpu.VMEM((2, D, wide), jnp.bfloat16),
            dma(2, size), dma(2, cols),
        ],
        compiler_params=comm_params(5),
        cost_estimate=SHORT,
        name="attend_back",
    )(
        offsets, lengths, gate_value, heads_all, grad_heads, dot_part, memory_part, logsum,
        memory_one, norm_one[:, None, :], middle, *hiddens, *packs,
    )


ANY = pl.BlockSpec(memory_space=pl.ANY)
VMEM = pl.BlockSpec(memory_space=pltpu.VMEM)
MESH_ID = pl.DeviceIdType.MESH
HALF = D // 2
AG_CUTS = 4


def remote(source, target, send, receive, device):
    return pltpu.make_async_remote_copy(
        src_ref=source, dst_ref=target, send_sem=send, recv_sem=receive,
        device_id=device, device_id_type=MESH_ID,
    )


def dma(*shape):
    return pltpu.SemaphoreType.DMA(shape)


def here():
    return lax.axis_index("row"), lax.axis_index("col")


def greet(peers):
    barrier = pltpu.get_barrier_semaphore()
    for peer in peers:
        pl.semaphore_signal(barrier, inc=1, device_id=peer, device_id_type=MESH_ID)
    pl.semaphore_wait(barrier, len(peers))


def square(row):
    along_x = (row // 2) * 2 + (1 - lax.rem(row, 2))
    along_y = lax.rem(row + 2, 4)
    across = (along_y // 2) * 2 + (1 - lax.rem(along_y, 2))
    return along_x, along_y, across


class Gather:
    def __init__(self, size, source, land, send, receive, own):
        self.size = size
        row, col = self.row, self.col = here()
        piece = source.shape[0]
        self.keep = pltpu.make_async_copy(source, land.at[row], own)
        if size != 4:
            self.peers = [(lax.rem(row + d, size), col) for d in range(1, size)]
            self.order = [lax.rem(row + size - d, size) for d in range(1, size)]
            self.copies = [
                remote(source, land.at[row], send.at[i], receive.at[i], peer) for i, peer in enumerate(self.peers)
            ]
            return
        self.order = rx, ry, rd = square(row)
        px, py = self.peers = [(rx, col), (ry, col)]
        height = piece // AG_CUTS
        cuts = [pl.ds(cut * height, height) for cut in range(AG_CUTS)]

        def out(cut, base, peer):
            return remote(
                source.at[cuts[cut]], land.at[row, cuts[cut]], send.at[base + cut], receive.at[base + cut], peer
            )

        def onward(cut, owner, peer):
            place = land.at[owner, cuts[cut]]
            return remote(place, place, send.at[2 * AG_CUTS + cut], receive.at[2 * AG_CUTS + cut], peer)

        middle = AG_CUTS // 2
        self.to_x = [out(cut, 0, px) for cut in range(AG_CUTS)]
        self.to_y = [out(cut, AG_CUTS, py) for cut in range(AG_CUTS)]
        self.onward = [onward(cut, rx, py) for cut in range(middle)] + [
            onward(cut, ry, px) for cut in range(middle, AG_CUTS)
        ]

    @staticmethod
    def semaphores(size):
        return 3 * AG_CUTS if size == 4 else size - 1

    def start(self, greeted=False, hold=True):
        if not greeted:
            greet(self.peers)
        if self.size != 4:
            for copy in self.copies:
                copy.start()
        else:
            for step in range(AG_CUTS):
                self.to_x[step].start()
                self.to_y[(step + AG_CUTS // 2) % AG_CUTS].start()
        self.keep.start()
        if hold:
            self.keep.wait()

    def forward(self):
        if self.size != 4:
            return
        for step in range(AG_CUTS // 2):
            later = step + AG_CUTS // 2
            self.to_x[step].wait_recv()
            self.onward[step].start()
            self.to_y[later].wait_recv()
            self.onward[later].start()

    def wait(self, step):
        middle = AG_CUTS // 2
        if self.size != 4:
            waits = [self.copies[step]]
        else:
            waits = (self.to_x[middle:], self.to_y[:middle], self.onward)[step]
        for copy in waits:
            copy.wait_recv()
        return self.order[step]

    def row_at(self, step):
        if self.size != 4:
            return lax.rem(self.row + self.size - step, self.size)
        along_x = lax.rem(lax.rem(self.row, 2) + lax.rem(step, 2), 2)
        return 2 * lax.rem(self.row // 2 + step // 2, 2) + along_x

    def each(self, body, between):
        @pl.loop(0, self.size)
        def _(step):
            for k in range(1, self.size):

                @pl.when(step == k)
                def _():
                    if k == 1:
                        between()
                    self.wait(k - 1)

            body(step, self.row_at(step))

    def finish(self):
        for copy in self.copies if self.size != 4 else [*self.to_x, *self.to_y, *self.onward]:
            copy.wait_send()


class CoreGather:
    def __init__(self, cols, source, target, far_send, far_receive, near_send, near_receive, own):
        row, col = here()
        pair = (col // 2) * 2 + 1 - lax.rem(col, 2)
        chips = cols // 2
        self.greets = [(row, lax.rem(col + 2 * e, cols)) for e in range(1, chips)] + [(row, pair)]
        self.far = [
            remote(source, target.at[col], far_send.at[e], far_receive.at[e], peer)
            for e, peer in enumerate(self.greets[:-1])
        ]
        self.near = [remote(source, target.at[col], near_send.at[0], near_receive.at[0], (row, pair))]
        for e in range(1, chips):
            place = target.at[lax.rem(col + cols - 2 * e, cols)]
            self.near.append(remote(place, place, near_send.at[e], near_receive.at[e], (row, pair)))
        self.keep = pltpu.make_async_copy(source, target.at[col], own)

    @staticmethod
    def scratch(cols):
        far, near = cols // 2 - 1, cols // 2
        return [dma(far), dma(far), dma(near), dma(near), pltpu.SemaphoreType.DMA]

    def start(self):
        for copy in [*self.far, self.near[0], self.keep]:
            copy.start()

    def forward(self):
        for e, copy in enumerate(self.far):
            copy.wait_recv()
            self.near[e + 1].start()

    def finish(self):
        for copy in self.near:
            copy.wait()
        for copy in self.far:
            copy.wait_send()
        self.keep.wait()


class Scatter:
    def __init__(self, size, stage, land, total, send, receive):
        self.size, self.stage, self.land, self.total = size, stage, land, total
        self.send, self.receive = send, receive
        self.row, self.col = here()
        self.plan()

    @staticmethod
    def semaphores(size):
        return 6 if size == 4 else size - 1

    @staticmethod
    def stage_shape(size, piece):
        return (3 if size == 4 else size - 1, 2, piece, HALF)

    @staticmethod
    def land_shape(size, piece):
        return (6, piece, HALF) if size == 4 else (size - 1, 2, piece, HALF)

    def plan(self):
        row, col, stage = self.row, self.col, self.stage

        def copy(index, source, peer):
            return remote(source, self.land.at[index], self.send.at[index], self.receive.at[index], peer)

        if self.size != 4:
            others = [lax.rem(row + d, self.size) for d in range(1, self.size)]
            self.peers = [(peer, col) for peer in others]
            self.order = [*others, row]
            self.copies = [copy(slot, stage.at[slot], peer) for slot, peer in enumerate(self.peers)]
            self.after = [[slot] for slot in range(self.size - 1)]
            return
        rx, ry, rd = square(row)
        px, py = self.peers = [(rx, col), (ry, col)]
        self.order = [rd, rx, ry, row]
        self.copies = [
            copy(0, stage.at[0, 0], px), copy(1, stage.at[0, 1], py), copy(2, stage.at[1, 0], px),
            copy(3, stage.at[2, 1], py), copy(4, stage.at[2, 0], py), copy(5, stage.at[1, 1], px),
        ]
        self.after = [[0, 1], [2], [3]]

    def begin(self, partial, greeted=False):
        if not greeted:
            greet(self.peers)

        @pl.loop(0, self.size - 1)
        def _(step):
            def store(half, columns, value):
                self.stage[step, half, :, columns] = value.astype(jnp.bfloat16)

            partial(step, self.row_at(step), store)
            for k, indices in enumerate(self.after):

                @pl.when(step == k)
                def _():
                    for index in indices:
                        self.copies[index].start()

    def row_at(self, step):
        if self.size != 4:
            return lax.rem(self.row + 1 + step, self.size)
        along_x = lax.rem(lax.rem(self.row, 2) + 3 - step // 2, 2)
        return 2 * lax.rem(self.row // 2 + 3 - lax.rem(step, 2), 2) + along_x

    def middle(self):
        if self.size != 4:
            return
        self.copies[0].wait_recv()
        self.add_stage(2, 0, self.land.at[0])
        self.copies[4].start()
        self.copies[1].wait_recv()
        self.add_stage(1, 1, self.land.at[1])
        self.copies[5].start()

    def own(self, partial):
        def store(half, columns, value):
            self.total[half, :, columns] = value

        partial(self.size - 1, self.order[-1], store)

    def end(self):
        if self.size != 4:
            for slot, copy in enumerate(self.copies):
                copy.wait_recv()
                self.add_total(0, self.land.at[slot, 0])
                self.add_total(1, self.land.at[slot, 1])
        else:
            for index, half in ((2, 0), (3, 1), (4, 0), (5, 1)):
                self.copies[index].wait_recv()
                self.add_total(half, self.land.at[index])
        for copy in self.copies:
            copy.wait_send()

    def run(self, partial, late=None, greeted=False):
        self.begin(partial, greeted)
        self.middle()
        self.own(partial)
        if late is not None:
            late()
        self.end()

    def run_short(self, partial, late=None, greeted=False):
        if not greeted:
            greet(self.peers)

        @pl.loop(0, self.size)
        def _(step):
            @pl.when(step == self.size - 1)
            def _():
                self.middle()

            def store(half, columns, value):
                self.total[half, :, columns] = value
                self.stage[step, half, :, columns] = value.astype(jnp.bfloat16)

            partial(step, self.row_at(step), store)
            for k, indices in enumerate(self.after):

                @pl.when(step == k)
                def _():
                    for index in indices:
                        self.copies[index].start()

        if late is not None:
            late()
        self.end()

    def add_stage(self, slot, half, landed):
        @pl.loop(0, landed.shape[0] // STRIP)
        def _(i):
            rows = pl.ds(pl.multiple_of(i * STRIP, STRIP), STRIP)
            value = self.stage[slot, half, rows, :].astype(jnp.float32) + landed[rows, :].astype(jnp.float32)
            self.stage[slot, half, rows, :] = value.astype(jnp.bfloat16)

    def add_total(self, half, landed):
        @pl.loop(0, landed.shape[0] // STRIP)
        def _(i):
            rows = pl.ds(pl.multiple_of(i * STRIP, STRIP), STRIP)
            self.total[half, rows, :] += landed[rows, :].astype(jnp.float32)


STRIP = 32


def scatter_scratch(size, piece, spare=0):
    count = Scatter.semaphores(size)
    slots, *shape = Scatter.stage_shape(size, piece)
    return [
        pltpu.VMEM((slots + spare, *shape), jnp.bfloat16),
        pltpu.VMEM(Scatter.land_shape(size, piece), jnp.bfloat16),
        pltpu.VMEM((2, piece, HALF), jnp.float32),
        pltpu.SemaphoreType.DMA((count,)),
        pltpu.SemaphoreType.DMA((count,)),
    ]


def gather_scratch(size, piece):
    count = Gather.semaphores(size)
    return [
        pltpu.VMEM((size, piece, D), jnp.bfloat16),
        pltpu.SemaphoreType.DMA((count,)),
        pltpu.SemaphoreType.DMA((count,)),
        pltpu.SemaphoreType.DMA,
    ]


def fetches(pairs, semaphores):
    copies = [pltpu.make_async_copy(a, b, semaphores.at[i]) for i, (a, b) in enumerate(pairs)]
    for copy in copies:
        copy.start()
    return copies


def wait_all(copies):
    for copy in copies:
        copy.wait()


def tiles_of(width, tile):
    def run(body):
        @pl.loop(0, width // tile)
        def _(t):
            body(t, pl.ds(pl.multiple_of(t * tile, tile), tile))

    return run


SPAN = 512


def span_loop(body):
    inside = HALF // SPAN

    @pl.loop(0, D // SPAN)
    def _(t):
        body(
            t, t // inside,
            pl.ds(pl.multiple_of(lax.rem(t, inside) * SPAN, SPAN), SPAN),
            pl.ds(pl.multiple_of(t * SPAN, SPAN), SPAN),
        )


def comm_params(identity):
    return pltpu.CompilerParams(
        collective_id=identity, has_side_effects=True, vmem_limit_bytes=BIG_VMEM
    )


def bf(*shape):
    return jax.ShapeDtypeStruct(shape, jnp.bfloat16)


def fl(*shape):
    return jax.ShapeDtypeStruct(shape, jnp.float32)


def project_heads(size, normed, w_all, w_out):
    piece = normed.shape[0]
    cols, _, depth, width = w_all.shape
    heads = width // HD

    def kernel(
        x_ref, w_ref, out_ref, heads_ref, all_ref, all_out_ref,
        land, send, receive, own, w, w_sem, all_sem, *rest,
    ):
        loads = fetches([(w_ref.at[c], w.at[:, pl.ds(c * depth, depth), :]) for c in range(cols)], w_sem)
        gather = Gather(size, x_ref, land, send, receive, own)
        beside = CoreGather(cols, out_ref, all_out_ref, *rest)
        greet([*gather.peers, *beside.greets])
        gather.start(greeted=True)
        beside.start()

        def keep(step, row):
            return pltpu.make_async_copy(land.at[row], all_ref.at[row], all_sem.at[step])

        def compute(step, row):
            keep(step, row).start()
            rows = pl.ds(pl.multiple_of(row * piece, piece), piece)

            @pl.loop(0, 3)
            def _(j):
                value = jnp.dot(land[row], w[j], preferred_element_type=jnp.float32).astype(jnp.bfloat16)
                for head in range(heads):
                    heads_ref[j, head, rows, :] = value[:, head * HD : (head + 1) * HD]

        def between():
            gather.forward()
            beside.forward()

        wait_all(loads)
        gather.each(compute, between)
        beside.finish()
        for step in range(size):
            keep(step, gather.row_at(step)).wait()
        gather.finish()

    return pl.pallas_call(
        kernel,
        out_shape=[bf(3, heads, GLEN, HD), bf(size, piece, D), bf(cols, *w_out.shape)],
        in_specs=[ANY, ANY, ANY],
        out_specs=[VMEM, ANY, ANY],
        scratch_shapes=gather_scratch(size, piece)
        + [
            pltpu.VMEM((3, D, width), jnp.bfloat16),
            pltpu.SemaphoreType.DMA((cols,)),
            pltpu.SemaphoreType.DMA((size,)),
        ]
        + CoreGather.scratch(cols),
        compiler_params=comm_params(1),
        cost_estimate=SHORT,
        name="project_heads",
    )(normed, w_all, w_out)


def strip_loop(piece, body):
    @pl.loop(0, piece // STRIP)
    def _(i):
        body(pl.ds(pl.multiple_of(i * STRIP, STRIP), STRIP))


def row_mean(first, second):
    return (jnp.sum(first, axis=1, keepdims=True) + jnp.sum(second, axis=1, keepdims=True)) / D


def lanes(first, second):
    lane = lax.broadcasted_iota(jnp.int32, (STRIP, HD), 1)
    return jnp.where(lane == 0, first, jnp.where(lane == 1, second, 0.0))


LEFT, RIGHT = slice(0, HALF), slice(HALF, D)


def branch_out(size, attn, w_all, x, gain):
    piece = GLEN // size
    cols, width, depth = w_all.shape

    def kernel(attn_ref, w_ref, x_ref, gain_ref, middle_ref, normed_ref, stat_ref, stage, land, total, send, receive, w, w_sem):
        loads = fetches([(w_ref.at[c], w.at[:, pl.ds(c * depth, depth)]) for c in range(cols)], w_sem)
        scatter = Scatter(size, stage, land, total, send, receive)
        wait_all(loads)

        def partial(step, row, store):
            rows = pl.ds(pl.multiple_of(row * piece, piece), piece)
            left = attn_ref[rows, :]

            @span_loop
            def _(t, half, columns, depth_rows):
                store(half, columns, plain_dot(left, w[:, depth_rows], NN))

        scatter.run_short(partial)

        def finish(rows):
            branch = (total[0, rows, :], total[1, rows, :])
            middle = (
                x_ref[rows, LEFT].astype(jnp.float32) + branch[0],
                x_ref[rows, RIGHT].astype(jnp.float32) + branch[1],
            )
            mean = row_mean(middle[0] * middle[0], middle[1] * middle[1])
            inverse = lax.rsqrt(mean + EPSILON)
            for part, columns in zip(middle, (LEFT, RIGHT)):
                middle_ref[rows, columns] = part
                normed_ref[rows, columns] = (part * inverse * gain_ref[:, columns]).astype(jnp.bfloat16)
            stat_ref[rows, :] = lanes(row_mean(branch[0] * branch[0], branch[1] * branch[1]), mean)

        strip_loop(piece, finish)

    return pl.pallas_call(
        kernel,
        out_shape=[fl(piece, D), bf(piece, D), fl(piece, HD)],
        in_specs=[VMEM, ANY, VMEM, VMEM],
        out_specs=[VMEM, VMEM, VMEM],
        scratch_shapes=scatter_scratch(size, piece, 1)
        + [pltpu.VMEM((width, D), jnp.bfloat16), pltpu.SemaphoreType.DMA((cols,))],
        compiler_params=comm_params(2),
        cost_estimate=SHORT,
        name="branch_out",
    )(attn, w_all, x, gain)


def feed_forward(size, tokens, pack, cot, first):
    piece = GLEN // size
    cols, _, depth, wide = pack.shape
    tile = min(wide, 512)
    count = wide // tile

    def kernel(x_ref, pack_ref, cot_ref, hidden_ref, grad_ref, *rest):
        if first:
            all_ref, land, send, receive, own, all_sem, *rest = rest
        else:
            land, own, *rest = rest
        w, cot_all, back, stage, w_sem, cot_sem, out_sem = rest
        if first:
            gather = Gather(size, x_ref, land, send, receive, own)
            gather.start()
            order = [gather.row, *gather.order]
        else:
            order = list(range(size))
        w_loads = fetches(
            [(pack_ref.at[c, j], w.at[j, pl.ds(c * depth, depth), :]) for j in (2, 0, 1) for c in range(cols)], w_sem
        )
        cot_loads = fetches([(cot_ref.at[row], cot_all.at[row]) for row in order], cot_sem)
        if not first:
            x_loads = fetches([(x_ref.at[row], land.at[row]) for row in order], own)

        def backward(row):
            @tiles_of(wide, tile)
            def _(t, columns):
                back[row, :, columns] = plain_dot(cot_all[row], w[2, :, columns], NN).astype(jnp.bfloat16)

        def moves(row, slot, columns):
            rows = pl.ds(pl.multiple_of(row * piece, piece), piece)
            return [
                pltpu.make_async_copy(stage.at[slot, 0], hidden_ref.at[rows, columns], out_sem.at[slot, 0]),
                pltpu.make_async_copy(stage.at[slot, 1], grad_ref.at[0, rows, columns], out_sem.at[slot, 1]),
                pltpu.make_async_copy(stage.at[slot, 2], grad_ref.at[1, rows, columns], out_sem.at[slot, 2]),
            ]

        def compute(row):
            if first:
                store = pltpu.make_async_copy(land.at[row], all_ref.at[row], all_sem)
                store.start()

            @pl.loop(0, count)
            def _(t):
                columns = pl.ds(pl.multiple_of(t * tile, tile), tile)
                slot = lax.rem(t, 2)
                x = land[row]
                gate_pre = jnp.dot(x, w[0, :, columns], preferred_element_type=jnp.float32)
                up_pre = jnp.dot(x, w[1, :, columns], preferred_element_type=jnp.float32)
                sigmoid = jax.nn.sigmoid(gate_pre)
                silu = gate_pre * sigmoid
                grad_hidden = back[row, :, columns].astype(jnp.float32)

                @pl.when(t >= 2)
                def _():
                    wait_all(moves(row, slot, columns))

                stage[slot, 0] = (silu * up_pre).astype(jnp.bfloat16)
                stage[slot, 1] = (grad_hidden * up_pre * (sigmoid + silu * (1.0 - sigmoid))).astype(jnp.bfloat16)
                stage[slot, 2] = (grad_hidden * silu).astype(jnp.bfloat16)
                for move in moves(row, slot, columns):
                    move.start()

            for slot in range(min(2, count)):
                wait_all(moves(row, slot, pl.ds(slot * tile, tile)))
            if first:
                store.wait()

        wait_all(w_loads[:cols])
        if first:
            cot_loads[0].wait()

            @pl.loop(0, size)
            def _(d):
                @pl.when(d == 1)
                def _():
                    gather.forward()
                    wait_all(cot_loads[1:])

                backward(lax.rem(gather.row + d, size))

            wait_all(w_loads[cols:])
            gather.each(lambda step, row: compute(row), lambda: None)
            gather.finish()
            return

        @pl.loop(0, size)
        def _(row):
            pltpu.make_async_copy(cot_ref.at[row], cot_all.at[row], cot_sem.at[row]).wait()
            backward(row)

        wait_all(w_loads[cols:])

        @pl.loop(0, size)
        def _(row):
            pltpu.make_async_copy(x_ref.at[row], land.at[row], own.at[row]).wait()
            compute(row)

    out_shape = [bf(GLEN, wide), bf(2, GLEN, wide)]
    if first:
        out_shape.append(bf(size, piece, D))
        scratch = gather_scratch(size, piece) + [pltpu.SemaphoreType.DMA]
    else:
        scratch = [pltpu.VMEM((size, piece, D), jnp.bfloat16), dma(size)]
    return pl.pallas_call(
        kernel,
        out_shape=out_shape,
        in_specs=[ANY] * 3,
        out_specs=[ANY] * len(out_shape),
        scratch_shapes=scratch
        + [
            pltpu.VMEM((3, D, wide), jnp.bfloat16),
            pltpu.VMEM((size, piece, D), jnp.bfloat16),
            pltpu.VMEM((size, piece, wide), jnp.bfloat16),
            pltpu.VMEM((2, 3, piece, tile), jnp.bfloat16),
            dma(3 * cols), dma(size), dma(2, 3),
        ],
        compiler_params=comm_params(3) if first else pltpu.CompilerParams(vmem_limit_bytes=BIG_VMEM),
        cost_estimate=SHORT,
        name="feed_first" if first else "feed_second",
    )(tokens, pack, cot)


def weight_grads_kernel(x_ref, y_ref, g_ref, h_ref, out_ref):
    count = g_ref.shape[0]
    for j in range(count):
        out_ref[j] = plain_dot(x_ref[...], g_ref[j], TN).astype(jnp.bfloat16)
    out_ref[count] = plain_dot(y_ref[...], h_ref[...], TN).astype(jnp.bfloat16)


def weight_grads(x, grads, y, hidden):
    count, _, wide = grads.shape
    tile = 256
    block = pl.BlockSpec((GLEN, tile), lambda i: (0, i))
    return pl.pallas_call(
        weight_grads_kernel,
        grid=(D // tile,),
        in_specs=[
            block, block,
            pl.BlockSpec((count, GLEN, wide), lambda i: (0, 0, 0), pipeline_mode=pl.Buffered(1)),
            pl.BlockSpec((GLEN, wide), lambda i: (0, 0), pipeline_mode=pl.Buffered(1)),
        ],
        out_specs=pl.BlockSpec((count + 1, tile, wide), lambda i: (0, i, 0)),
        out_shape=bf(count + 1, D, wide),
        compiler_params=pltpu.CompilerParams(vmem_limit_bytes=BIG_VMEM),
        cost_estimate=SHORT,
        name="weight_grads",
    )(x, y, grads, hidden)


def norm_back(rows, total, stream, inverse, gain_ref, base, store, gain_sum):
    u = [total[half, rows, :] * gain_ref[:, columns] for half, columns in enumerate((LEFT, RIGHT))]
    inner = row_mean(u[0] * stream[0], u[1] * stream[1]) * inverse * inverse * inverse
    for half, columns in enumerate((LEFT, RIGHT)):
        store(columns, base[half] + inverse * u[half] - stream[half] * inner)
        gain_sum[:, columns] += jnp.sum(total[half, rows, :] * stream[half] * inverse, axis=0, keepdims=True)


def middle_back(size, grads, packs, middle, cot, gain, tokens, all_cot, hidden):
    piece = middle.shape[0]
    cols, _, depth, wide = packs[0].shape
    block = 256

    def kernel(
        first_ref, second_ref, pack_a, pack_b, middle_ref, cot_ref, gain_ref, x_ref, y_ref, hidden_ref,
        grad_ref, low_ref, gain_sum, part_ref,
        stage, land, total, send, receive, w, g_first, g_second, h, x, part,
        w_sem, first_sem, second_sem, h_sem, x_sem, part_sem,
    ):
        pack_refs = (pack_a, pack_b)
        scatter = Scatter(size, stage, land, total, send, receive)

        def piece_rows(at):
            return pl.ds(pl.multiple_of(at * piece, piece), piece)

        def first_load(step):
            slot = lax.rem(step, 2)
            return pltpu.make_async_copy(
                first_ref.at[:, piece_rows(scatter.row_at(step))], g_first.at[slot], first_sem.at[slot]
            )

        def second_load(step):
            rows = piece_rows(scatter.row_at(step))
            return pltpu.make_async_copy(second_ref.at[:, rows], g_second.at[:, rows], second_sem.at[step])

        def w_load(i, c):
            return pltpu.make_async_copy(
                pack_refs[i].at[c, pl.ds(0, 2)], w.at[i, :, pl.ds(pl.multiple_of(c * depth, depth), depth), :], w_sem.at[i, c]
            )

        first_load(0).start()
        second_load(0).start()
        for c in range(cols):
            for i in range(2):
                w_load(i, c).start()
        first_load(1).start()
        for step in range(1, size):
            second_load(step).start()
        h_load = pltpu.make_async_copy(hidden_ref, h, h_sem)
        h_load.start()
        gain_sum[...] = jnp.zeros_like(gain_sum)

        def partial(step, at, store):
            first_load(step).wait()
            second_load(step).wait()

            @span_loop
            def _(t, half, columns, depth_rows):
                @pl.when(step == 0)
                def _():
                    for k in range(SPAN // depth):
                        for i in range(2):
                            w_load(i, t * (SPAN // depth) + k).wait()

                rows = piece_rows(at)
                value = 0.0
                for j in range(2):
                    value += plain_dot(g_first[lax.rem(step, 2), j], w[0, j, depth_rows, :], NT)
                    value += plain_dot(g_second[j, rows, :], w[1, j, depth_rows, :], NT)
                store(half, columns, value)

            @pl.when(step + 2 < size)
            def _():
                first_load(step + 2).start()

        def x_loads(i, slot):
            columns = pl.ds(pl.multiple_of(i * block, block), block)
            return [
                pltpu.make_async_copy(source.at[:, :, columns], x.at[slot, k], x_sem.at[slot, k])
                for k, source in enumerate((x_ref, y_ref))
            ]

        def part_move(i, slot):
            columns = pl.ds(pl.multiple_of(i * block, block), block)
            return pltpu.make_async_copy(part.at[slot], part_ref.at[:, columns, :], part_sem.at[slot])

        def weights():
            count = D // block
            for load in x_loads(0, 0):
                load.start()
            h_load.wait()

            @pl.loop(0, count)
            def _(i):
                slot = lax.rem(i, 2)

                @pl.when(i + 1 < count)
                def _():
                    for load in x_loads(i + 1, 1 - slot):
                        load.start()

                wait_all(x_loads(i, slot))

                @pl.when(i >= 2)
                def _():
                    part_move(i, slot).wait()


                @pl.loop(0, 2)
                def _(j):
                    part[slot, j] = plain_dot(x[slot, 0].reshape(GLEN, block), g_second[j], TN).astype(jnp.bfloat16)

                part[slot, 2] = plain_dot(x[slot, 1].reshape(GLEN, block), h[...], TN).astype(jnp.bfloat16)
                part_move(i, slot).start()

            for slot in range(2):
                part_move(slot, slot).wait()

        scatter.run_short(partial, weights)

        def finish(rows):
            stream = [middle_ref[rows, columns] for columns in (LEFT, RIGHT)]
            base = [cot_ref[rows, columns].astype(jnp.float32) for columns in (LEFT, RIGHT)]
            inverse = lax.rsqrt(row_mean(stream[0] * stream[0], stream[1] * stream[1]) + EPSILON)

            def store(columns, value):
                grad_ref[rows, columns] = value
                low_ref[rows, columns] = value.astype(jnp.bfloat16)

            norm_back(rows, total, stream, inverse, gain_ref, base, store, gain_sum)

        strip_loop(piece, finish)

    return pl.pallas_call(
        kernel,
        out_shape=[fl(piece, D), bf(piece, D), fl(1, D), bf(3, D, wide)],
        in_specs=[ANY] * 4 + [VMEM] * 3 + [ANY] * 3,
        out_specs=[VMEM, VMEM, VMEM, ANY],
        scratch_shapes=scatter_scratch(size, piece, 1)
        + [
            pltpu.VMEM((2, 2, D, wide), jnp.bfloat16),
            pltpu.VMEM((2, 2, piece, wide), jnp.bfloat16),
            pltpu.VMEM((2, GLEN, wide), jnp.bfloat16),
            pltpu.VMEM((GLEN, wide), jnp.bfloat16),
            pltpu.VMEM((2, 2, size, piece, block), jnp.bfloat16),
            pltpu.VMEM((2, 3, block, wide), jnp.bfloat16),
            dma(2, cols), dma(2), dma(size), pltpu.SemaphoreType.DMA, dma(2, 2), dma(2),
        ],
        compiler_params=comm_params(4),
        cost_estimate=SHORT,
        name="middle_back",
    )(*grads, *packs, middle, cot, gain, tokens, all_cot, hidden)


def blocked_store(ref, rows, depth, columns, value):
    for i in range(value.shape[1] // depth):
        ref[columns.start // depth + i, rows, :] = value[:, i * depth : (i + 1) * depth]


def branch_back(size, low, w_all):
    piece = low.shape[0]
    cols, width, depth = w_all.shape
    heads = width // HD

    def kernel(x_ref, w_ref, heads_ref, all_ref, land, send, receive, own, w, w_sem, all_sem):
        loads = fetches([(w_ref.at[c], w.at[:, pl.ds(c * depth, depth)]) for c in range(cols)], w_sem)
        gather = Gather(size, x_ref, land, send, receive, own)
        gather.start()

        def keep(step, row):
            return pltpu.make_async_copy(land.at[row], all_ref.at[row], all_sem.at[step])

        def compute(step, row):
            keep(step, row).start()
            rows = pl.ds(pl.multiple_of(row * piece, piece), piece)
            value = plain_dot(land[row], w[...], NT).astype(jnp.bfloat16)
            for head in range(heads):
                heads_ref[head, rows, :] = value[:, head * HD : (head + 1) * HD]

        wait_all(loads)
        gather.each(compute, gather.forward)
        for step in range(size):
            keep(step, gather.row_at(step)).wait()
        gather.finish()

    return pl.pallas_call(
        kernel,
        out_shape=[bf(heads, GLEN, HD), bf(size, piece, D)],
        in_specs=[ANY, ANY],
        out_specs=[VMEM, ANY],
        scratch_shapes=gather_scratch(size, piece)
        + [
            pltpu.VMEM((width, D), jnp.bfloat16),
            pltpu.SemaphoreType.DMA((cols,)),
            pltpu.SemaphoreType.DMA((size,)),
        ],
        compiler_params=comm_params(6),
        cost_estimate=SHORT,
        name="branch_back",
    )(low, w_all)


def stream_back(size, grads, w_all, x, grad_middle, gain, blocks_out):
    piece = x.shape[0]
    cols, _, depth, width = w_all.shape

    def kernel(
        g_ref, w_ref, x_ref, middle_ref, gain_ref, blocks_ref, out_ref, gain_sum, target_ref,
        stage, land, total, send, receive, w, w_sem, *rest,
    ):
        greet(row_and_col_peers(size, cols))
        outward = Outward(size, cols, blocks_ref, rest[0], target_ref, *rest[1:])
        outward.start()
        loads = fetches([(w_ref.at[c], w.at[:, pl.ds(c * depth, depth), :]) for c in range(cols)], w_sem)
        scatter = Scatter(size, stage, land, total, send, receive)
        wait_all(loads)
        gain_sum[...] = jnp.zeros_like(gain_sum)

        def partial(step, row, store):
            @span_loop
            def _(t, half, columns, depth_rows):
                rows = pl.ds(pl.multiple_of(row * piece, piece), piece)
                value = plain_dot(g_ref[0, rows, :], w[0, depth_rows, :], NT)
                for j in (1, 2):
                    value += plain_dot(g_ref[j, rows, :], w[j, depth_rows, :], NT)
                store(half, columns, value)

        scatter.run_short(partial, outward.forward, greeted=True)

        def finish(rows):
            stream = [x_ref[rows, columns].astype(jnp.float32) for columns in (LEFT, RIGHT)]
            base = [middle_ref[rows, columns] for columns in (LEFT, RIGHT)]
            inverse = lax.rsqrt(row_mean(stream[0] * stream[0], stream[1] * stream[1]) + EPSILON)

            def store(columns, value):
                blocked_store(out_ref, rows, depth, columns, value.astype(jnp.bfloat16))

            norm_back(rows, total, stream, inverse, gain_ref, base, store, gain_sum)

        strip_loop(piece, finish)
        outward.finish()

    return pl.pallas_call(
        kernel,
        out_shape=[bf(cols, piece, depth), fl(1, D), bf(cols // size, size, piece, depth)],
        in_specs=[VMEM, ANY, VMEM, VMEM, VMEM, VMEM],
        out_specs=[VMEM, VMEM, ANY],
        scratch_shapes=scatter_scratch(size, piece, 1)
        + [pltpu.VMEM((3, D, width), jnp.bfloat16), pltpu.SemaphoreType.DMA((cols,))]
        + Outward.scratch(size, cols, piece, depth),
        compiler_params=comm_params(7),
        cost_estimate=SHORT,
        name="stream_back",
    )(grads, w_all, x, grad_middle, gain, blocks_out)


def row_and_col_peers(size, cols):
    row, col = here()
    return [(lax.rem(row + d, size), col) for d in range(1, size)] + [
        (row, lax.rem(col + e, cols)) for e in range(1, cols)
    ]


class Inward:
    def __init__(self, size, cols, source, middle, land, first_send, first_receive, send, receive, own):
        self.size, self.cols, self.groups = size, cols, cols // size
        self.source, self.middle, self.land = source, middle, land
        self.first_send, self.first_receive = first_send, first_receive
        self.send, self.receive, self.own = send, receive, own
        self.row, self.col = here()

    @staticmethod
    def scratch(size, cols, piece, depth):
        return [
            pltpu.VMEM((size, cols // size, piece, depth), jnp.bfloat16),
            pltpu.VMEM((cols, piece, depth), jnp.bfloat16),
            dma(size - 1), dma(size - 1), dma(cols), dma(cols), dma(2),
        ]

    def start(self):
        row, col = self.row, self.col
        self.first = []
        for d in range(1, self.size):
            peer = lax.rem(row + d, self.size)
            self.first.append(
                remote(
                    self.source.at[:, peer], self.middle.at[row],
                    self.first_send.at[d - 1], self.first_receive.at[d - 1], (peer, col),
                )
            )
            self.first[-1].start()
        self.keep = pltpu.make_async_copy(self.source.at[:, row], self.middle.at[row], self.own.at[0])
        self.keep.start()

    def forward(self):
        row, col = self.row, self.col
        for d in range(self.size):
            origin = lax.rem(row + self.size - d, self.size)
            if d == 0:
                self.keep.wait()
            else:
                self.first[d - 1].wait_recv()
            for i in range(self.groups):
                group = origin * self.groups + i

                @pl.when(group != col)
                def _():
                    remote(
                        self.middle.at[origin, i], self.land.at[col],
                        self.send.at[group], self.receive.at[col], (row, group),
                    ).start()

                @pl.when(group == col)
                def _():
                    pltpu.make_async_copy(self.middle.at[origin, i], self.land.at[col], self.own.at[1]).start()

    def finish(self):
        row, col = self.row, self.col
        pltpu.make_async_copy(self.middle.at[0, 0], self.land.at[col], self.own.at[1]).wait()
        for e in range(1, self.cols):
            peer = lax.rem(col + e, self.cols)
            remote(
                self.middle.at[0, 0], self.land.at[peer], self.send.at[peer], self.receive.at[peer], (row, peer)
            ).wait()
        for copy in self.first:
            copy.wait_send()


class Outward:
    def __init__(self, size, cols, source, middle, target, first_send, first_receive, send, receive, own):
        self.size, self.cols, self.groups = size, cols, cols // size
        self.source, self.middle, self.target = source, middle, target
        self.first_send, self.first_receive = first_send, first_receive
        self.send, self.receive, self.own = send, receive, own
        self.row, self.col = here()

    @staticmethod
    def scratch(size, cols, piece, depth):
        return [
            pltpu.VMEM((cols, piece, depth), jnp.bfloat16),
            dma(cols - 1), dma(cols - 1), dma(cols), dma(cols), dma(cols // size),
        ]

    def start(self):
        row, col = self.row, self.col
        self.first = []
        for e in range(1, self.cols):
            peer = lax.rem(col + e, self.cols)
            self.first.append(
                remote(
                    self.source.at[peer], self.middle.at[col],
                    self.first_send.at[e - 1], self.first_receive.at[e - 1], (row, peer),
                )
            )
            self.first[-1].start()

    def forward(self):
        row, col = self.row, self.col
        for e in range(self.cols):
            group = lax.rem(col + self.cols - e, self.cols)
            if e:
                self.first[e - 1].wait_recv()
            block = self.middle.at[group] if e else self.source.at[col]
            home, i = group // self.groups, lax.rem(group, self.groups)

            @pl.when(home != row)
            def _():
                remote(
                    block, self.target.at[i, row],
                    self.send.at[group], self.receive.at[i * self.size + row], (home, col),
                ).start()

            @pl.when(home == row)
            def _():
                pltpu.make_async_copy(block, self.target.at[i, row], self.own.at[i]).start()

    def finish(self):
        row, col = self.row, self.col
        for i in range(self.groups):
            pltpu.make_async_copy(self.middle.at[0], self.target.at[i, row], self.own.at[i]).wait()
            for d in range(1, self.size):
                peer = lax.rem(row + d, self.size)
                remote(
                    self.middle.at[0], self.target.at[i, peer],
                    self.send.at[peer * self.groups + i], self.receive.at[i * self.size + peer], (peer, col),
                ).wait()
        for copy in self.first:
            copy.wait_send()


def by_pieces(block, size):
    return block.reshape(block.shape[0] // GLEN, size, GLEN // size, block.shape[1])


def enter(size, cols, stream_in, cotangent, gains):
    pieces = by_pieces(stream_in, size)
    piece, depth = pieces.shape[2:]
    scratch = Inward.scratch(size, cols, piece, depth)

    def kernel(
        x_ref, cot_ref, gains_ref, tokens_ref, normed_ref, gain_in_ref, gain_mid_ref, cot_tokens_ref, all_cot_ref,
        gains_land, gains_send, gains_receive, gather_send, gather_receive, gather_own, *rest,
    ):
        greet(row_and_col_peers(size, cols))
        exchange = Inward(size, cols, x_ref, *rest[: len(scratch)])
        second = Inward(size, cols, cot_ref, *rest[len(scratch) :])
        gather = Gather(size, cot_tokens_ref, all_cot_ref, gather_send, gather_receive, gather_own)
        second.start()
        exchange.start()
        row, col = here()
        copies = []
        for e in range(1, cols):
            peer = lax.rem(col + e, cols)
            copies.append(
                remote(gains_ref, gains_land.at[col], gains_send.at[e - 1], gains_receive.at[e - 1], (row, peer))
            )
            copies[-1].start()
        gains_land[col] = gains_ref[...]
        second.forward()
        exchange.forward()
        second.finish()

        def assemble(rows):
            for c in range(cols):
                cot_tokens_ref[rows, c * depth : (c + 1) * depth] = second.land[c, rows, :]

        strip_loop(piece, assemble)
        gather.start(greeted=True, hold=False)
        gather.forward()
        for copy in copies:
            copy.wait()
        for c in range(cols):
            gain_in_ref[:, c * depth : (c + 1) * depth] = gains_land[c, 0:1, :]
            gain_mid_ref[:, c * depth : (c + 1) * depth] = gains_land[c, 1:2, :]
        exchange.finish()
        land = exchange.land

        def norm(rows):
            total = jnp.zeros((STRIP, 1), jnp.float32)
            for c in range(cols):
                part = land[c, rows, :]
                tokens_ref[rows, c * depth : (c + 1) * depth] = part
                part = part.astype(jnp.float32)
                total += jnp.sum(part * part, axis=1, keepdims=True)
            inverse = lax.rsqrt(total / D + EPSILON)
            for c in range(cols):
                columns = slice(c * depth, (c + 1) * depth)
                normed_ref[rows, columns] = (
                    land[c, rows, :].astype(jnp.float32) * inverse * gain_in_ref[:, columns]
                ).astype(jnp.bfloat16)

        strip_loop(piece, norm)
        for step in range(size - 1):
            gather.wait(step)
        gather.keep.wait()
        gather.finish()

    return pl.pallas_call(
        kernel,
        out_shape=[bf(piece, D), bf(piece, D), fl(1, D), fl(1, D), bf(piece, D), bf(size, piece, D)],
        in_specs=[ANY, ANY, VMEM],
        out_specs=[VMEM] * 5 + [ANY],
        scratch_shapes=[pltpu.VMEM((cols, 8, depth), jnp.float32), dma(cols - 1), dma(cols - 1)]
        + [dma(Gather.semaphores(size)), dma(Gather.semaphores(size)), pltpu.SemaphoreType.DMA]
        + scratch * 2,
        compiler_params=comm_params(8),
        cost_estimate=SHORT,
        name="enter",
    )(pieces, by_pieces(cotangent, size), jnp.pad(gains, ((0, 6), (0, 0))))


def leave(size, cols, blocks_grad, stats, sums):
    _, piece, depth = blocks_grad.shape
    groups = cols // size

    def kernel(
        grad_ref, stats_ref, sums_ref, grad_target, stats_target, sums_target,
        stats_row, stats_all, sums_col, sums_part, sums_row,
        a_send, a_receive, b_send, b_receive, c_send, c_receive, d_send, d_receive, *rest,
    ):
        row, col = here()
        greet(row_and_col_peers(size, cols))
        grad = Outward(size, cols, grad_ref, rest[0], grad_target, *rest[1:])
        home, slot = col // groups, lax.rem(col, groups)
        col_peers = [lax.rem(col + e, cols) for e in range(1, cols)]
        row_peers = [lax.rem(row + d, size) for d in range(1, size)]

        def sums_first(peer):
            return remote(sums_ref.at[peer], sums_col.at[col], c_send.at[peer], c_receive.at[col], (row, peer))

        for peer in col_peers:
            sums_first(peer).start()
        sums_col[col] = sums_ref[col]

        @pl.when(home != row)
        def _():
            remote(stats_ref, stats_row.at[row], a_send, a_receive.at[row], (home, col)).start()

        @pl.when(home == row)
        def _():
            stats_row[row] = stats_ref[...]

        grad.start()
        for peer in col_peers:
            remote(sums_ref.at[peer], sums_col.at[peer], c_send.at[peer], c_receive.at[peer], (row, peer)).wait()
        total = sums_col[0]
        for c in range(1, cols):
            total += sums_col[c]
        sums_part[...] = total
        sums_row[row] = total
        for peer in row_peers:
            remote(sums_part, sums_row.at[row], d_send.at[peer], d_receive.at[row], (peer, col)).start()

        @pl.when(home == row)
        def _():
            for peer in row_peers:
                remote(stats_ref, stats_row.at[peer], a_send, a_receive.at[peer], (peer, col)).wait_recv()
            for e, peer in enumerate(col_peers):
                remote(stats_row, stats_all.at[slot], b_send.at[e], b_receive.at[slot], (row, peer)).start()
            stats_all[slot] = stats_row[...]

        grad.forward()
        for peer in row_peers:
            remote(sums_part, sums_row.at[peer], d_send.at[peer], d_receive.at[peer], (peer, col)).wait()
        whole = sums_row[0]
        for r in range(1, size):
            whole += sums_row[r]
        line = lax.broadcasted_iota(jnp.int32, (8, depth), 0)
        sums_target[...] = jnp.where(line < 2, whole, total)

        @pl.when(home == row)
        def _():
            for e, peer in enumerate(col_peers):
                remote(stats_row, stats_all.at[slot], b_send.at[e], b_receive.at[slot], (row, peer)).wait_send()

        @pl.when(home != row)
        def _():
            remote(stats_ref, stats_row.at[row], a_send, a_receive.at[row], (home, col)).wait_send()

        for i in range(groups):
            group = row * groups + i

            @pl.when(group != col)
            def _():
                remote(stats_row, stats_all.at[i], b_send.at[0], b_receive.at[i], (row, group)).wait_recv()

        stats_target[...] = stats_all[...]
        grad.finish()

    return pl.pallas_call(
        kernel,
        out_shape=[
            bf(groups, size, piece, depth),
            fl(groups, size, 8, piece), fl(8, depth),
        ],
        in_specs=[VMEM] * 3,
        out_specs=[ANY, VMEM, VMEM],
        scratch_shapes=[
            pltpu.VMEM((size, 8, piece), jnp.float32),
            pltpu.VMEM((groups, size, 8, piece), jnp.float32),
            pltpu.VMEM((cols, 8, depth), jnp.float32),
            pltpu.VMEM((8, depth), jnp.float32),
            pltpu.VMEM((size, 8, depth), jnp.float32),
            pltpu.SemaphoreType.DMA, dma(size), dma(cols - 1), dma(groups), dma(cols), dma(cols), dma(size), dma(size),
        ]
        + Outward.scratch(size, cols, piece, depth),
        compiler_params=comm_params(10),
        cost_estimate=SHORT,
        name="leave",
    )(blocks_grad, stats, sums)


def over_col(partial, axis):
    return lax.psum_scatter(partial.astype(jnp.bfloat16), "col", scatter_dimension=axis, tiled=True)


def flat(pieces):
    return pieces.reshape(GLEN, D)


def local(
    stream_in,
    w_qkv,
    w_out,
    w_gate_up,
    w_down,
    gain_attn,
    gain_ffn,
    gate_logit,
    memory,
    memory_norm,
    offsets,
    lengths,
    cotangent,
):
    head_here = memory.shape[1]
    size = lax.axis_size("row")
    cols = lax.axis_size("col")
    all_qkv = lax.all_gather(w_qkv, "col", axis=0, tiled=False)
    units = w_down.shape[0] // 2
    packs = [
        jnp.concatenate([w_gate_up[:, :, part], w_down[part].T[None]], axis=0)
        for part in (slice(0, units), slice(units, None))
    ]
    all_packs = [lax.all_gather(pack, "col", axis=0, tiled=False) for pack in packs]
    gate_value = jax.nn.sigmoid(gate_logit)
    group = (memory[0], memory_norm[0], offsets[0], lengths[0], gate_value)
    stream, normed_in, gain_in, gain_mid, cot, all_cot = enter(
        size, cols, stream_in, cotangent, jnp.stack([gain_attn, gain_ffn])
    )
    heads_all, all_in, all_out = project_heads(size, normed_in, all_qkv, w_out)
    attn, dot_part, memory_part, logsum, memory_new, norm_new = attend(heads_all, *group)
    middle, normed_ffn, stat_branch = branch_out(size, attn, all_out, stream, gain_mid)
    hidden_first, grads_first, all_ffn = feed_forward(size, normed_ffn, all_packs[0], all_cot, True)
    part_first = weight_grads(flat(all_ffn), grads_first, flat(all_cot), hidden_first)
    part_first, all_ffn = lax.optimization_barrier((part_first, all_ffn))
    scattered_first = over_col(part_first, 1)
    hidden_second, grads_second = feed_forward(size, all_ffn, all_packs[1], all_cot, False)
    grad_middle, low_branch, part_gain_ffn, part_second = middle_back(
        size, (grads_first, grads_second), all_packs, middle, cot, gain_mid, all_ffn, all_cot, hidden_second
    )
    scattered_second = over_col(part_second, 1)
    grad_heads, all_branch = branch_back(size, low_branch, all_out)
    grads_qkv, gate_sums, blocks_out, stat_ffn = attend_back(
        size, heads_all, grad_heads, dot_part, memory_part, logsum, *group,
        (hidden_first, hidden_second), all_packs, middle,
    )
    part_attn = weight_grads(flat(all_in), grads_qkv, flat(all_branch), attn)
    grads_qkv, part_attn, scattered_first = lax.optimization_barrier((grads_qkv, part_attn, scattered_first))
    scattered_attn = over_col(part_attn, 1)
    blocks_grad, part_gain_attn, stream_out = stream_back(
        size, grads_qkv, all_qkv, stream, grad_middle, gain_in, blocks_out
    )
    grad_gate_up = jnp.concatenate([scattered_first[:2], scattered_second[:2]], axis=2).astype(jnp.float32)
    grad_down = jnp.concatenate([scattered_first[2], scattered_second[2]], axis=1).T.astype(jnp.float32)
    blocks_grad, grad_gate_up, grad_down = lax.optimization_barrier((blocks_grad, grad_gate_up, grad_down))
    grad_qkv, grad_out = scattered_attn[:3].astype(jnp.float32), scattered_attn[3].T.astype(jnp.float32)
    logit_part = gate_value * (1.0 - gate_value) * jnp.sum(gate_sums, axis=(1, 2))
    features_here = gain_attn.shape[0]
    sums = jnp.concatenate(
        [
            part_gain_attn.reshape(cols, 1, features_here),
            part_gain_ffn.reshape(cols, 1, features_here),
            jnp.broadcast_to(
                jnp.pad(logit_part, (0, features_here - head_here))[None, None], (cols, 6, features_here)
            ),
        ],
        axis=1,
    )
    stats = jnp.sqrt(jnp.concatenate([stat_branch[:, :2], stat_ffn[:, :2]], axis=1).T)
    stream_grad, stats_all, sums = leave(
        size, cols, blocks_grad, jnp.pad(stats, ((0, 4), (0, 0))), sums
    )
    stream_out = stream_out.reshape(stream_in.shape)
    stream_grad = stream_grad.reshape(stream_in.shape).astype(jnp.float32)
    rms_table = stats_all[:, :, :4].transpose(2, 0, 1, 3).reshape(4, stream_in.shape[0])
    grad_gain_attn, grad_gain_ffn, grad_gate_logit = sums[0], sums[1], sums[2, :head_here]
    return (
        stream_out,
        stream_grad,
        grad_qkv,
        grad_out,
        grad_gate_up,
        grad_down,
        grad_gain_attn,
        grad_gain_ffn,
        grad_gate_logit,
        memory_new[None],
        norm_new.reshape(1, head_here, HD),
        rms_table,
    )


def solution(mesh):
    return jax.shard_map(
        local,
        mesh=mesh,
        in_specs=(
            P("row", "col"),
            P(None, "col", "row"),
            P("row", "col"),
            P(None, "col", "row"),
            P("row", "col"),
            P("col"),
            P("col"),
            P("row"),
            P("col", "row", None, None),
            P("col", "row", None),
            P("col", None),
            P("col", None),
            P("row", "col"),
        ),
        out_specs=(
            P("row", "col"),
            P("row", "col"),
            P(None, "col", "row"),
            P("row", "col"),
            P(None, "col", "row"),
            P("row", "col"),
            P("col"),
            P("col"),
            P("row"),
            P("col", "row", None, None),
            P("col", "row", None),
            P(None, "row"),
        ),
        check_vma=False,
    )
```

```python
import functools

import jax
import jax.numpy as jnp
from jax import lax
from jax.experimental import pallas as pl
from jax.experimental.pallas import tpu as pltpu
from jax.sharding import PartitionSpec as P

D = 2048
HD = 128
PROMPT = 1024
CONT = 4
CLEN = 128
GLEN = 1536


EPSILON = 1e-06
MASKED_LOGIT = -1e30
BIG_VMEM = 60 * 1024 * 1024
SHORT = pl.CostEstimate(flops=1000, bytes_accessed=1000, transcendentals=0)


def feature_map(values):
    return jnp.where(values > 0, values + 1.0, jnp.exp(jnp.minimum(values, 0.0)))


def feature_slope(values):
    return jnp.where(values > 0, 1.0, jnp.exp(jnp.minimum(values, 0.0)))


def split_two(value):
    high = value.astype(jnp.bfloat16)
    return high, (value - high.astype(jnp.float32)).astype(jnp.bfloat16)


def wide_dot(left, right, dims):
    left_high, left_low = split_two(left)
    right_high, right_low = split_two(right)

    def one(a, b):
        return lax.dot_general(a, b, (dims, ((), ())), preferred_element_type=jnp.float32)

    return one(left_high, right_high) + one(left_high, right_low) + one(left_low, right_high)


def narrow_dot(left, right, dims):
    right_high, right_low = split_two(right)

    def one(b):
        return lax.dot_general(left, b, (dims, ((), ())), preferred_element_type=jnp.float32)

    return one(right_high) + one(right_low)


def plain_dot(left, right, dims):
    return lax.dot_general(left, right, (dims, ((), ())), preferred_element_type=jnp.float32)


NN = ((1,), (0,))
NT = ((1,), (1,))
TN = ((0,), (0,))
QT = 256
PROMPT_TILES = PROMPT // QT
TILES = GLEN // QT


def tile_rows(tile):
    return pl.ds(pl.multiple_of(tile * QT, QT), QT) if not isinstance(tile, int) else slice(tile * QT, (tile + 1) * QT)


def tile_scores(tile, q, k_ref, offsets_ref, lengths_ref):
    scale = HD ** (-0.5)
    row = lax.broadcasted_iota(jnp.int32, (QT, QT), 0)
    column = lax.broadcasted_iota(jnp.int32, (QT, QT), 1)
    own = plain_dot(q, k_ref[tile_rows(tile)], NT) * scale
    if isinstance(tile, int) and tile < PROMPT_TILES:
        seen = tile * QT
        own = jnp.where(row >= column, own, MASKED_LOGIT)
        ahead = plain_dot(q, k_ref[:seen], NT) * scale if seen else None
        return ahead, own, seen
    first = (tile - PROMPT_TILES) * (QT // CLEN)
    upper = lax.broadcasted_iota(jnp.int32, (QT, 1), 0) >= CLEN
    limit = jnp.where(upper, offsets_ref[first + 1], offsets_ref[first])
    live = jnp.where(upper, lengths_ref[first + 1] + CLEN, lengths_ref[first])
    same = (row >= CLEN) == (column >= CLEN)
    own = jnp.where((row >= column) & same & (column < live), own, MASKED_LOGIT)
    ahead = plain_dot(q, k_ref[:PROMPT], NT) * scale
    position = lax.broadcasted_iota(jnp.int32, (QT, PROMPT), 1)
    return jnp.where(position < limit, ahead, MASKED_LOGIT), own, PROMPT


def each_tile(body):
    for tile in range(PROMPT_TILES):
        body(tile)
    pl.loop(PROMPT_TILES, TILES)(body)


def attend_kernel(
    offsets_ref, lengths_ref, gate_ref, qkv_ref, memory_ref, norm_ref,
    attn_ref, dot_ref, part_ref, logsum_ref, memory_new_ref, norm_new_ref,
):
    head = pl.program_id(0)
    gate = gate_ref[head]
    q_ref, k_ref, v_ref = qkv_ref.at[0, 0], qkv_ref.at[1, 0], qkv_ref.at[2, 0]
    memory_one = memory_ref[0]
    norm_one = norm_ref[0]
    for tile in range(TILES):
        rows = slice(tile * QT, (tile + 1) * QT)
        q = q_ref[rows]
        ahead, own, seen = tile_scores(tile, q, k_ref, offsets_ref, lengths_ref)
        peak = jnp.max(own, axis=1, keepdims=True)
        if ahead is not None:
            peak = jnp.maximum(peak, jnp.max(ahead, axis=1, keepdims=True))
        own = jnp.exp(own - peak)
        total = jnp.sum(own, axis=1, keepdims=True)
        dot_part = plain_dot(own.astype(jnp.bfloat16), v_ref[rows], NN)
        if ahead is not None:
            ahead = jnp.exp(ahead - peak)
            total += jnp.sum(ahead, axis=1, keepdims=True)
            dot_part += plain_dot(ahead.astype(jnp.bfloat16), v_ref[:seen], NN)
        dot_part = dot_part / total
        lifted = feature_map(q.astype(jnp.float32))
        memory_part = wide_dot(lifted, memory_one, NN) / jnp.sum(
            lifted * norm_one, axis=1, keepdims=True
        )
        attn_ref[rows, :] = (gate * memory_part + (1.0 - gate) * dot_part).astype(jnp.bfloat16)
        dot_ref[0, rows, :] = dot_part
        part_ref[0, rows, :] = memory_part
        logsum_ref[0, rows, :] = peak + jnp.log(total)
    lifted_keys = feature_map(k_ref[:PROMPT].astype(jnp.float32))
    high, low = split_two(lifted_keys)
    v = v_ref[:PROMPT]
    memory_new_ref[0] = memory_one + (plain_dot(high, v, TN) + plain_dot(low, v, TN)) / PROMPT
    norm_new_ref[0] = norm_one + jnp.mean(lifted_keys, axis=0, keepdims=True)


def head_block(shape, lead=0):
    zeros = (0,) * (len(shape) - 1 - lead)
    return pl.BlockSpec(shape, lambda h: (0,) * lead + (h,) + zeros)


SMEM_SPEC = pl.BlockSpec(memory_space=pltpu.SMEM)


def attend(heads_all, memory_one, norm_one, offsets, lengths, gate_value):
    heads = heads_all.shape[1]
    f32 = jnp.float32
    row_block = head_block((1, GLEN, HD))
    column = pl.BlockSpec((GLEN, HD), lambda h: (0, h))
    return pl.pallas_call(
        attend_kernel,
        grid=(heads,),
        in_specs=[
            SMEM_SPEC, SMEM_SPEC, SMEM_SPEC,
            head_block((3, 1, GLEN, HD), 1), head_block((1, HD, HD)), head_block((1, 1, HD)),
        ],
        out_specs=[
            column, row_block, row_block, head_block((1, GLEN, 1)),
            head_block((1, HD, HD)), head_block((1, 1, HD)),
        ],
        out_shape=[
            jax.ShapeDtypeStruct((GLEN, heads * HD), jnp.bfloat16),
            jax.ShapeDtypeStruct((heads, GLEN, HD), f32),
            jax.ShapeDtypeStruct((heads, GLEN, HD), f32),
            jax.ShapeDtypeStruct((heads, GLEN, 1), f32),
            jax.ShapeDtypeStruct((heads, HD, HD), f32),
            jax.ShapeDtypeStruct((heads, 1, HD), f32),
        ],
        compiler_params=pltpu.CompilerParams(vmem_limit_bytes=BIG_VMEM),
        cost_estimate=SHORT,
        name="attend",
    )(offsets, lengths, gate_value, heads_all, memory_one, norm_one[:, None, :])


def attend_back_kernel(
    size, cols, depth, wide,
    offsets_ref, lengths_ref, gate_ref, qkv_ref, grad_ref, dot_ref, part_ref, logsum_ref,
    memory_ref, norm_ref, middle_hbm, hidden_a, hidden_b, pack_a, pack_b,
    out_ref, gate_out_ref, blocks_ref, stat_ref,
    key_sum, value_sum, query_sum, stage, land, total, send, receive, h, w, h_sem, w_sem, middle_ref, middle_sem,
):
    head = pl.program_id(0)
    piece = GLEN // size
    scatter = Scatter(size, stage, land, total, send, receive)

    def h_load(i, step):
        rows = pl.ds(pl.multiple_of(scatter.row_at(step) * piece, piece), piece)
        return pltpu.make_async_copy((hidden_a, hidden_b)[i].at[rows], h.at[i, rows], h_sem.at[i, step])

    def w_load(i, c):
        return pltpu.make_async_copy(
            (pack_a, pack_b)[i].at[c, 2], w.at[i, pl.ds(pl.multiple_of(c * depth, depth), depth), :], w_sem.at[i, c]
        )

    def partial(step, at, store):
        for i in range(2):
            h_load(i, step).wait()

        @span_loop
        def _(t, half, columns, depth_rows):
            @pl.when(step == 0)
            def _():
                for k in range(SPAN // depth):
                    for i in range(2):
                        w_load(i, t * (SPAN // depth) + k).wait()

            rows = pl.ds(pl.multiple_of(at * piece, piece), piece)
            store(
                half, columns,
                plain_dot(h[0, rows, :], w[0, depth_rows, :], NT) + plain_dot(h[1, rows, :], w[1, depth_rows, :], NT),
            )

    middle_load = pltpu.make_async_copy(middle_hbm, middle_ref, middle_sem)

    @pl.when(head == 0)
    def _():
        for i in range(2):
            h_load(i, 0).start()
        for c in range(cols):
            for i in range(2):
                w_load(i, c).start()
        for step in range(1, size):
            for i in range(2):
                h_load(i, step).start()
        middle_load.start()
        scatter.begin(partial)

    @pl.when(head == pl.num_programs(0) // 2)
    def _():
        scatter.middle()

    gate = gate_ref[head]
    keep = 1.0 - gate
    scale = HD ** (-0.5)
    q_ref, k_ref, v_ref = qkv_ref.at[0, 0], qkv_ref.at[1, 0], qkv_ref.at[2, 0]
    memory_one = memory_ref[0]
    norm_one = norm_ref[0]
    gate_out_ref[0] = jnp.zeros((1, HD), jnp.float32)
    key_sum[...] = jnp.zeros_like(key_sum)
    value_sum[...] = jnp.zeros_like(value_sum)

    @pl.loop(0, TILES)
    def _(tile):
        rows = tile_rows(tile)
        grad = grad_ref[0, rows, :]
        grad_float = grad.astype(jnp.float32)
        memory_part = part_ref[0, rows, :]
        gate_out_ref[0] += jnp.sum(grad_float * (memory_part - dot_ref[0, rows, :]), axis=0, keepdims=True)
        q_float = q_ref[rows].astype(jnp.float32)
        lifted = feature_map(q_float)
        inverse = gate / jnp.sum(lifted * norm_one, axis=1, keepdims=True)
        against_memory = jnp.sum(grad_float * memory_part, axis=1, keepdims=True)
        grad_lifted = inverse * (narrow_dot(grad, memory_one, NT) - against_memory * norm_one)
        query_sum[rows, :] = grad_lifted * feature_slope(q_float)

    def one(tile):
        rows = tile_rows(tile)
        q = q_ref[rows]
        grad = grad_ref[0, rows, :]
        grad_float = grad.astype(jnp.float32)
        against_dot = jnp.sum(grad_float * dot_ref[0, rows, :], axis=1, keepdims=True)
        logsum = logsum_ref[0, rows, :]
        ahead, own, seen = tile_scores(tile, q, k_ref, offsets_ref, lengths_ref)
        own = jnp.exp(own - logsum)
        value_sum[rows, :] += plain_dot(own.astype(jnp.bfloat16), grad, TN)
        own = (keep * own * (plain_dot(grad, v_ref[rows], NT) - against_dot)).astype(jnp.bfloat16)
        key_sum[rows, :] += plain_dot(own, q, TN)
        grad_q = plain_dot(own, k_ref[rows], NN)
        if ahead is not None:
            ahead = jnp.exp(ahead - logsum)
            value_sum[:seen, :] += plain_dot(ahead.astype(jnp.bfloat16), grad, TN)
            ahead = (keep * ahead * (plain_dot(grad, v_ref[:seen], NT) - against_dot)).astype(
                jnp.bfloat16
            )
            key_sum[:seen, :] += plain_dot(ahead, q, TN)
            grad_q += plain_dot(ahead, k_ref[:seen], NN)
        out_ref[0, rows, :] = (grad_q * scale + query_sum[rows, :]).astype(jnp.bfloat16)

    each_tile(one)
    out_ref[1, :, :] = (key_sum[...] * scale).astype(jnp.bfloat16)
    out_ref[2, :, :] = (value_sum[...] * keep).astype(jnp.bfloat16)

    def finish(rows):
        ffn = [total[half, rows, :] for half in range(2)]
        result = [middle_ref[rows, columns] + ffn[half] for half, columns in enumerate((LEFT, RIGHT))]
        for half, columns in enumerate((LEFT, RIGHT)):
            blocked_store(blocks_ref, rows, depth, columns, result[half].astype(jnp.bfloat16))
        stat_ref[rows, :] = lanes(
            row_mean(ffn[0] * ffn[0], ffn[1] * ffn[1]),
            row_mean(result[0] * result[0], result[1] * result[1]),
        )

    @pl.when(head == pl.num_programs(0) - 1)
    def _():
        scatter.own(partial)
        scatter.end()
        middle_load.wait()
        strip_loop(piece, finish)


def whole_block(shape):
    return pl.BlockSpec(shape, lambda h: (0,) * len(shape), pipeline_mode=pl.Buffered(1))


def attend_back(
    size, heads_all, grad_heads, dot_part, memory_part, logsum, memory_one, norm_one, offsets, lengths, gate_value,
    hiddens, packs, middle,
):
    heads = heads_all.shape[1]
    piece = middle.shape[0]
    cols, _, depth, wide = packs[0].shape
    row_block = head_block((1, GLEN, HD))
    return pl.pallas_call(
        functools.partial(attend_back_kernel, size, cols, depth, wide),
        grid=(heads,),
        in_specs=[
            SMEM_SPEC, SMEM_SPEC, SMEM_SPEC,
            head_block((3, 1, GLEN, HD), 1), row_block, row_block, row_block,
            head_block((1, GLEN, 1)), head_block((1, HD, HD)), head_block((1, 1, HD)),
            ANY, ANY, ANY, ANY, ANY,
        ],
        out_specs=[
            pl.BlockSpec((3, GLEN, HD), lambda h: (0, 0, h)),
            head_block((1, 1, HD)),
            whole_block((cols, piece, depth)), whole_block((piece, HD)),
        ],
        out_shape=[bf(3, GLEN, heads * HD), fl(heads, 1, HD), bf(cols, piece, depth), fl(piece, HD)],
        scratch_shapes=[pltpu.VMEM((GLEN, HD), jnp.float32)] * 3
        + scatter_scratch(size, piece)
        + [
            pltpu.VMEM((2, GLEN, wide), jnp.bfloat16),
            pltpu.VMEM((2, D, wide), jnp.bfloat16),
            dma(2, size), dma(2, cols), pltpu.VMEM((piece, D), jnp.float32), pltpu.SemaphoreType.DMA,
        ],
        compiler_params=comm_params(5),
        cost_estimate=SHORT,
        name="attend_back",
    )(
        offsets, lengths, gate_value, heads_all, grad_heads, dot_part, memory_part, logsum,
        memory_one, norm_one[:, None, :], middle, *hiddens, *packs,
    )


ANY = pl.BlockSpec(memory_space=pl.ANY)
VMEM = pl.BlockSpec(memory_space=pltpu.VMEM)
MESH_ID = pl.DeviceIdType.MESH
HALF = D // 2
AG_CUTS = 4


def remote(source, target, send, receive, device):
    return pltpu.make_async_remote_copy(
        src_ref=source, dst_ref=target, send_sem=send, recv_sem=receive,
        device_id=device, device_id_type=MESH_ID,
    )


def dma(*shape):
    return pltpu.SemaphoreType.DMA(shape)


def here():
    return lax.axis_index("row"), lax.axis_index("col")


def greet(peers):
    barrier = pltpu.get_barrier_semaphore()
    for peer in peers:
        pl.semaphore_signal(barrier, inc=1, device_id=peer, device_id_type=MESH_ID)
    pl.semaphore_wait(barrier, len(peers))


def square(row):
    along_x = (row // 2) * 2 + (1 - lax.rem(row, 2))
    along_y = lax.rem(row + 2, 4)
    across = (along_y // 2) * 2 + (1 - lax.rem(along_y, 2))
    return along_x, along_y, across


class Gather:
    def __init__(self, size, source, land, send, receive, own):
        self.size = size
        row, col = self.row, self.col = here()
        piece = source.shape[0]
        self.keep = pltpu.make_async_copy(source, land.at[row], own)
        if size != 4:
            self.peers = [(lax.rem(row + d, size), col) for d in range(1, size)]
            self.order = [lax.rem(row + size - d, size) for d in range(1, size)]
            self.copies = [
                remote(source, land.at[row], send.at[i], receive.at[i], peer) for i, peer in enumerate(self.peers)
            ]
            return
        self.order = rx, ry, rd = square(row)
        px, py = self.peers = [(rx, col), (ry, col)]
        height = piece // AG_CUTS
        cuts = [pl.ds(cut * height, height) for cut in range(AG_CUTS)]

        def out(cut, base, peer):
            return remote(
                source.at[cuts[cut]], land.at[row, cuts[cut]], send.at[base + cut], receive.at[base + cut], peer
            )

        def onward(cut, owner, peer):
            place = land.at[owner, cuts[cut]]
            return remote(place, place, send.at[2 * AG_CUTS + cut], receive.at[2 * AG_CUTS + cut], peer)

        middle = AG_CUTS // 2
        self.to_x = [out(cut, 0, px) for cut in range(AG_CUTS)]
        self.to_y = [out(cut, AG_CUTS, py) for cut in range(AG_CUTS)]
        self.onward = [onward(cut, rx, py) for cut in range(middle)] + [
            onward(cut, ry, px) for cut in range(middle, AG_CUTS)
        ]

    @staticmethod
    def semaphores(size):
        return 3 * AG_CUTS if size == 4 else size - 1

    def start(self, greeted=False, hold=True):
        if not greeted:
            greet(self.peers)
        if self.size != 4:
            for copy in self.copies:
                copy.start()
        else:
            for step in range(AG_CUTS):
                self.to_x[step].start()
                self.to_y[(step + AG_CUTS // 2) % AG_CUTS].start()
        self.keep.start()
        if hold:
            self.keep.wait()

    def forward(self):
        if self.size != 4:
            return
        for step in range(AG_CUTS // 2):
            later = step + AG_CUTS // 2
            self.to_x[step].wait_recv()
            self.onward[step].start()
            self.to_y[later].wait_recv()
            self.onward[later].start()

    def wait(self, step):
        middle = AG_CUTS // 2
        if self.size != 4:
            waits = [self.copies[step]]
        else:
            waits = (self.to_x[middle:], self.to_y[:middle], self.onward)[step]
        for copy in waits:
            copy.wait_recv()
        return self.order[step]

    def row_at(self, step):
        if self.size != 4:
            return lax.rem(self.row + self.size - step, self.size)
        along_x = lax.rem(lax.rem(self.row, 2) + lax.rem(step, 2), 2)
        return 2 * lax.rem(self.row // 2 + step // 2, 2) + along_x

    def each(self, body, between):
        @pl.loop(0, self.size)
        def _(step):
            for k in range(1, self.size):

                @pl.when(step == k)
                def _():
                    if k == 1:
                        between()
                    self.wait(k - 1)

            body(step, self.row_at(step))

    def finish(self):
        for copy in self.copies if self.size != 4 else [*self.to_x, *self.to_y, *self.onward]:
            copy.wait_send()


class CoreGather:
    def __init__(self, cols, source, target, far_send, far_receive, near_send, near_receive, own):
        row, col = here()
        pair = (col // 2) * 2 + 1 - lax.rem(col, 2)
        chips = cols // 2
        self.greets = [(row, lax.rem(col + 2 * e, cols)) for e in range(1, chips)] + [(row, pair)]
        self.far = [
            remote(source, target.at[col], far_send.at[e], far_receive.at[e], peer)
            for e, peer in enumerate(self.greets[:-1])
        ]
        self.near = [remote(source, target.at[col], near_send.at[0], near_receive.at[0], (row, pair))]
        for e in range(1, chips):
            place = target.at[lax.rem(col + cols - 2 * e, cols)]
            self.near.append(remote(place, place, near_send.at[e], near_receive.at[e], (row, pair)))
        self.keep = pltpu.make_async_copy(source, target.at[col], own)

    @staticmethod
    def scratch(cols):
        far, near = cols // 2 - 1, cols // 2
        return [dma(far), dma(far), dma(near), dma(near), pltpu.SemaphoreType.DMA]

    def start(self):
        for copy in [*self.far, self.near[0], self.keep]:
            copy.start()

    def forward(self):
        for e, copy in enumerate(self.far):
            copy.wait_recv()
            self.near[e + 1].start()

    def finish(self):
        for copy in self.near:
            copy.wait()
        for copy in self.far:
            copy.wait_send()
        self.keep.wait()


class Scatter:
    def __init__(self, size, stage, land, total, send, receive):
        self.size, self.stage, self.land, self.total = size, stage, land, total
        self.send, self.receive = send, receive
        self.row, self.col = here()
        self.plan()

    @staticmethod
    def semaphores(size):
        return 6 if size == 4 else size - 1

    @staticmethod
    def stage_shape(size, piece):
        return (3 if size == 4 else size - 1, 2, piece, HALF)

    @staticmethod
    def land_shape(size, piece):
        return (6, piece, HALF) if size == 4 else (size - 1, 2, piece, HALF)

    def plan(self):
        row, col, stage = self.row, self.col, self.stage

        def copy(index, source, peer):
            return remote(source, self.land.at[index], self.send.at[index], self.receive.at[index], peer)

        if self.size != 4:
            others = [lax.rem(row + d, self.size) for d in range(1, self.size)]
            self.peers = [(peer, col) for peer in others]
            self.order = [*others, row]
            self.copies = [copy(slot, stage.at[slot], peer) for slot, peer in enumerate(self.peers)]
            self.after = [[slot] for slot in range(self.size - 1)]
            return
        rx, ry, rd = square(row)
        px, py = self.peers = [(rx, col), (ry, col)]
        self.order = [rd, rx, ry, row]
        self.copies = [
            copy(0, stage.at[0, 0], px), copy(1, stage.at[0, 1], py), copy(2, stage.at[1, 0], px),
            copy(3, stage.at[2, 1], py), copy(4, stage.at[2, 0], py), copy(5, stage.at[1, 1], px),
        ]
        self.after = [[0, 1], [2], [3]]

    def begin(self, partial, greeted=False):
        if not greeted:
            greet(self.peers)

        @pl.loop(0, self.size - 1)
        def _(step):
            def store(half, columns, value):
                self.stage[step, half, :, columns] = value.astype(jnp.bfloat16)

            partial(step, self.row_at(step), store)
            for k, indices in enumerate(self.after):

                @pl.when(step == k)
                def _():
                    for index in indices:
                        self.copies[index].start()

    def row_at(self, step):
        if self.size != 4:
            return lax.rem(self.row + 1 + step, self.size)
        along_x = lax.rem(lax.rem(self.row, 2) + 3 - step // 2, 2)
        return 2 * lax.rem(self.row // 2 + 3 - lax.rem(step, 2), 2) + along_x

    def middle(self):
        if self.size != 4:
            return
        self.copies[0].wait_recv()
        self.add_stage(2, 0, self.land.at[0])
        self.copies[4].start()
        self.copies[1].wait_recv()
        self.add_stage(1, 1, self.land.at[1])
        self.copies[5].start()

    def own(self, partial):
        def store(half, columns, value):
            self.total[half, :, columns] = value

        partial(self.size - 1, self.order[-1], store)

    def end(self):
        if self.size != 4:
            for slot, copy in enumerate(self.copies):
                copy.wait_recv()
                self.add_total(0, self.land.at[slot, 0])
                self.add_total(1, self.land.at[slot, 1])
        else:
            for index, half in ((2, 0), (3, 1), (4, 0), (5, 1)):
                self.copies[index].wait_recv()
                self.add_total(half, self.land.at[index])
        for copy in self.copies:
            copy.wait_send()

    def run(self, partial, late=None, greeted=False):
        self.begin(partial, greeted)
        self.middle()
        self.own(partial)
        if late is not None:
            late()
        self.end()

    def run_short(self, partial, late=None, greeted=False):
        if not greeted:
            greet(self.peers)

        @pl.loop(0, self.size)
        def _(step):
            @pl.when(step == self.size - 1)
            def _():
                self.middle()

            def store(half, columns, value):
                self.total[half, :, columns] = value
                self.stage[step, half, :, columns] = value.astype(jnp.bfloat16)

            partial(step, self.row_at(step), store)
            for k, indices in enumerate(self.after):

                @pl.when(step == k)
                def _():
                    for index in indices:
                        self.copies[index].start()

        if late is not None:
            late()
        self.end()

    def add_stage(self, slot, half, landed):
        @pl.loop(0, landed.shape[0] // STRIP)
        def _(i):
            rows = pl.ds(pl.multiple_of(i * STRIP, STRIP), STRIP)
            value = self.stage[slot, half, rows, :].astype(jnp.float32) + landed[rows, :].astype(jnp.float32)
            self.stage[slot, half, rows, :] = value.astype(jnp.bfloat16)

    def add_total(self, half, landed):
        @pl.loop(0, landed.shape[0] // STRIP)
        def _(i):
            rows = pl.ds(pl.multiple_of(i * STRIP, STRIP), STRIP)
            self.total[half, rows, :] += landed[rows, :].astype(jnp.float32)


STRIP = 32


def scatter_scratch(size, piece, spare=0):
    count = Scatter.semaphores(size)
    slots, *shape = Scatter.stage_shape(size, piece)
    return [
        pltpu.VMEM((slots + spare, *shape), jnp.bfloat16),
        pltpu.VMEM(Scatter.land_shape(size, piece), jnp.bfloat16),
        pltpu.VMEM((2, piece, HALF), jnp.float32),
        pltpu.SemaphoreType.DMA((count,)),
        pltpu.SemaphoreType.DMA((count,)),
    ]


def gather_scratch(size, piece):
    count = Gather.semaphores(size)
    return [
        pltpu.VMEM((size, piece, D), jnp.bfloat16),
        pltpu.SemaphoreType.DMA((count,)),
        pltpu.SemaphoreType.DMA((count,)),
        pltpu.SemaphoreType.DMA,
    ]


def fetches(pairs, semaphores):
    copies = [pltpu.make_async_copy(a, b, semaphores.at[i]) for i, (a, b) in enumerate(pairs)]
    for copy in copies:
        copy.start()
    return copies


def wait_all(copies):
    for copy in copies:
        copy.wait()


def tiles_of(width, tile):
    def run(body):
        @pl.loop(0, width // tile)
        def _(t):
            body(t, pl.ds(pl.multiple_of(t * tile, tile), tile))

    return run


SPAN = 512


def span_loop(body):
    inside = HALF // SPAN

    @pl.loop(0, D // SPAN)
    def _(t):
        body(
            t, t // inside,
            pl.ds(pl.multiple_of(lax.rem(t, inside) * SPAN, SPAN), SPAN),
            pl.ds(pl.multiple_of(t * SPAN, SPAN), SPAN),
        )


def comm_params(identity):
    return pltpu.CompilerParams(
        collective_id=identity, has_side_effects=True, vmem_limit_bytes=BIG_VMEM
    )


def bf(*shape):
    return jax.ShapeDtypeStruct(shape, jnp.bfloat16)


def fl(*shape):
    return jax.ShapeDtypeStruct(shape, jnp.float32)


def project_heads(size, normed, w_all, w_out):
    piece = normed.shape[0]
    cols, _, depth, width = w_all.shape
    heads = width // HD

    def kernel(
        x_ref, w_ref, out_ref, heads_ref, all_ref, all_out_ref,
        land, send, receive, own, w, w_sem, all_sem, *rest,
    ):
        loads = fetches([(w_ref.at[c], w.at[:, pl.ds(c * depth, depth), :]) for c in range(cols)], w_sem)
        gather = Gather(size, x_ref, land, send, receive, own)
        beside = CoreGather(cols, out_ref, all_out_ref, *rest)
        greet([*gather.peers, *beside.greets])
        gather.start(greeted=True)
        beside.start()

        def keep(step, row):
            return pltpu.make_async_copy(land.at[row], all_ref.at[row], all_sem.at[step])

        def compute(step, row):
            keep(step, row).start()
            rows = pl.ds(pl.multiple_of(row * piece, piece), piece)

            @pl.loop(0, 3)
            def _(j):
                value = jnp.dot(land[row], w[j], preferred_element_type=jnp.float32).astype(jnp.bfloat16)
                for head in range(heads):
                    heads_ref[j, head, rows, :] = value[:, head * HD : (head + 1) * HD]

        wait_all(loads)
        gather.each(compute, gather.forward)
        beside.forward()
        beside.finish()
        for step in range(size):
            keep(step, gather.row_at(step)).wait()
        gather.finish()

    return pl.pallas_call(
        kernel,
        out_shape=[bf(3, heads, GLEN, HD), bf(size, piece, D), bf(cols, *w_out.shape)],
        in_specs=[ANY, ANY, ANY],
        out_specs=[VMEM, ANY, ANY],
        scratch_shapes=gather_scratch(size, piece)
        + [
            pltpu.VMEM((3, D, width), jnp.bfloat16),
            pltpu.SemaphoreType.DMA((cols,)),
            pltpu.SemaphoreType.DMA((size,)),
        ]
        + CoreGather.scratch(cols),
        compiler_params=comm_params(1),
        cost_estimate=SHORT,
        name="project_heads",
    )(normed, w_all, w_out)


def strip_loop(piece, body):
    @pl.loop(0, piece // STRIP)
    def _(i):
        body(pl.ds(pl.multiple_of(i * STRIP, STRIP), STRIP))


def row_mean(first, second):
    return (jnp.sum(first, axis=1, keepdims=True) + jnp.sum(second, axis=1, keepdims=True)) / D


def lanes(first, second):
    lane = lax.broadcasted_iota(jnp.int32, (STRIP, HD), 1)
    return jnp.where(lane == 0, first, jnp.where(lane == 1, second, 0.0))


LEFT, RIGHT = slice(0, HALF), slice(HALF, D)


def branch_out(size, attn, w_all, x, gain):
    piece = GLEN // size
    cols, width, depth = w_all.shape

    def kernel(
        attn_ref, w_ref, x_hbm, gain_ref, middle_ref, normed_ref, stat_ref,
        stage, land, total, send, receive, w, w_sem, x_ref, x_sem,
    ):
        loads = fetches([(w_ref.at[c], w.at[:, pl.ds(c * depth, depth)]) for c in range(cols)], w_sem)
        x_load = fetches([(x_hbm, x_ref)], x_sem)
        scatter = Scatter(size, stage, land, total, send, receive)
        wait_all(loads)

        def partial(step, row, store):
            rows = pl.ds(pl.multiple_of(row * piece, piece), piece)
            left = attn_ref[rows, :]

            @span_loop
            def _(t, half, columns, depth_rows):
                store(half, columns, plain_dot(left, w[:, depth_rows], NN))

        scatter.run_short(partial)

        def finish(rows):
            branch = (total[0, rows, :], total[1, rows, :])
            middle = (
                x_ref[rows, LEFT].astype(jnp.float32) + branch[0],
                x_ref[rows, RIGHT].astype(jnp.float32) + branch[1],
            )
            mean = row_mean(middle[0] * middle[0], middle[1] * middle[1])
            inverse = lax.rsqrt(mean + EPSILON)
            for part, columns in zip(middle, (LEFT, RIGHT)):
                middle_ref[rows, columns] = part
                normed_ref[rows, columns] = (part * inverse * gain_ref[:, columns]).astype(jnp.bfloat16)
            stat_ref[rows, :] = lanes(row_mean(branch[0] * branch[0], branch[1] * branch[1]), mean)

        wait_all(x_load)
        strip_loop(piece, finish)

    return pl.pallas_call(
        kernel,
        out_shape=[fl(piece, D), bf(piece, D), fl(piece, HD)],
        in_specs=[VMEM, ANY, ANY, VMEM],
        out_specs=[VMEM, VMEM, VMEM],
        scratch_shapes=scatter_scratch(size, piece, 1)
        + [pltpu.VMEM((width, D), jnp.bfloat16), dma(cols), pltpu.VMEM((piece, D), jnp.bfloat16), dma(1)],
        compiler_params=comm_params(2),
        cost_estimate=SHORT,
        name="branch_out",
    )(attn, w_all, x, gain)


def feed_forward(size, tokens, pack, cot, first):
    piece = GLEN // size
    cols, _, depth, wide = pack.shape
    tile = min(wide, 512)
    count = wide // tile

    def kernel(x_ref, pack_ref, cot_ref, hidden_ref, grad_ref, *rest):
        if first:
            all_ref, land, send, receive, own, all_sem, *rest = rest
        else:
            land, own, *rest = rest
        w, cot_all, back, stage, w_sem, cot_sem, out_sem = rest
        if first:
            gather = Gather(size, x_ref, land, send, receive, own)
            gather.start()
            order = [gather.row, *gather.order]
        else:
            order = list(range(size))
        w_loads = fetches(
            [(pack_ref.at[c, j], w.at[j, pl.ds(c * depth, depth), :]) for j in (2, 0, 1) for c in range(cols)], w_sem
        )
        cot_loads = fetches([(cot_ref.at[row], cot_all.at[row]) for row in order], cot_sem)
        if not first:
            x_loads = fetches([(x_ref.at[row], land.at[row]) for row in order], own)

        def backward(row):
            @tiles_of(wide, tile)
            def _(t, columns):
                back[row, :, columns] = plain_dot(cot_all[row], w[2, :, columns], NN).astype(jnp.bfloat16)

        def moves(row, slot, columns):
            rows = pl.ds(pl.multiple_of(row * piece, piece), piece)
            return [
                pltpu.make_async_copy(stage.at[slot, 0], hidden_ref.at[rows, columns], out_sem.at[slot, 0]),
                pltpu.make_async_copy(stage.at[slot, 1], grad_ref.at[0, rows, columns], out_sem.at[slot, 1]),
                pltpu.make_async_copy(stage.at[slot, 2], grad_ref.at[1, rows, columns], out_sem.at[slot, 2]),
            ]

        def compute(row):
            if first:
                store = pltpu.make_async_copy(land.at[row], all_ref.at[row], all_sem)
                store.start()

            @pl.loop(0, count)
            def _(t):
                columns = pl.ds(pl.multiple_of(t * tile, tile), tile)
                slot = lax.rem(t, 2)
                x = land[row]
                gate_pre = jnp.dot(x, w[0, :, columns], preferred_element_type=jnp.float32)
                up_pre = jnp.dot(x, w[1, :, columns], preferred_element_type=jnp.float32)
                sigmoid = jax.nn.sigmoid(gate_pre)
                silu = gate_pre * sigmoid
                grad_hidden = back[row, :, columns].astype(jnp.float32)

                @pl.when(t >= 2)
                def _():
                    wait_all(moves(row, slot, columns))

                stage[slot, 0] = (silu * up_pre).astype(jnp.bfloat16)
                stage[slot, 1] = (grad_hidden * up_pre * (sigmoid + silu * (1.0 - sigmoid))).astype(jnp.bfloat16)
                stage[slot, 2] = (grad_hidden * silu).astype(jnp.bfloat16)
                for move in moves(row, slot, columns):
                    move.start()

            for slot in range(min(2, count)):
                wait_all(moves(row, slot, pl.ds(slot * tile, tile)))
            if first:
                store.wait()

        wait_all(w_loads[:cols])
        if first:
            cot_loads[0].wait()

            @pl.loop(0, size)
            def _(d):
                @pl.when(d == 1)
                def _():
                    gather.forward()
                    wait_all(cot_loads[1:])

                backward(lax.rem(gather.row + d, size))

            wait_all(w_loads[cols:])
            gather.each(lambda step, row: compute(row), lambda: None)
            gather.finish()
            return

        @pl.loop(0, size)
        def _(row):
            pltpu.make_async_copy(cot_ref.at[row], cot_all.at[row], cot_sem.at[row]).wait()
            backward(row)

        wait_all(w_loads[cols:])

        @pl.loop(0, size)
        def _(row):
            pltpu.make_async_copy(x_ref.at[row], land.at[row], own.at[row]).wait()
            compute(row)

    out_shape = [bf(GLEN, wide), bf(2, GLEN, wide)]
    if first:
        out_shape.append(bf(size, piece, D))
        scratch = gather_scratch(size, piece) + [pltpu.SemaphoreType.DMA]
    else:
        scratch = [pltpu.VMEM((size, piece, D), jnp.bfloat16), dma(size)]
    return pl.pallas_call(
        kernel,
        out_shape=out_shape,
        in_specs=[ANY] * 3,
        out_specs=[ANY] * len(out_shape),
        scratch_shapes=scratch
        + [
            pltpu.VMEM((3, D, wide), jnp.bfloat16),
            pltpu.VMEM((size, piece, D), jnp.bfloat16),
            pltpu.VMEM((size, piece, wide), jnp.bfloat16),
            pltpu.VMEM((2, 3, piece, tile), jnp.bfloat16),
            dma(3 * cols), dma(size), dma(2, 3),
        ],
        compiler_params=comm_params(3) if first else pltpu.CompilerParams(vmem_limit_bytes=BIG_VMEM),
        cost_estimate=SHORT,
        name="feed_first" if first else "feed_second",
    )(tokens, pack, cot)


def weight_grads_kernel(x_ref, y_ref, g_ref, h_ref, out_ref):
    count = g_ref.shape[0]
    for j in range(count):
        out_ref[j] = plain_dot(x_ref[...], g_ref[j], TN).astype(jnp.bfloat16)
    out_ref[count] = plain_dot(y_ref[...], h_ref[...], TN).astype(jnp.bfloat16)


def weight_grads(x, grads, y, hidden):
    count, _, wide = grads.shape
    tile = 256
    block = pl.BlockSpec((GLEN, tile), lambda i: (0, i))
    return pl.pallas_call(
        weight_grads_kernel,
        grid=(D // tile,),
        in_specs=[
            block, block,
            pl.BlockSpec((count, GLEN, wide), lambda i: (0, 0, 0), pipeline_mode=pl.Buffered(1)),
            pl.BlockSpec((GLEN, wide), lambda i: (0, 0), pipeline_mode=pl.Buffered(1)),
        ],
        out_specs=pl.BlockSpec((count + 1, tile, wide), lambda i: (0, i, 0)),
        out_shape=bf(count + 1, D, wide),
        compiler_params=pltpu.CompilerParams(vmem_limit_bytes=BIG_VMEM),
        cost_estimate=SHORT,
        name="weight_grads",
    )(x, y, grads, hidden)


def norm_back(rows, total, stream, inverse, gain_ref, base, store, gain_sum):
    u = [total[half, rows, :] * gain_ref[:, columns] for half, columns in enumerate((LEFT, RIGHT))]
    inner = row_mean(u[0] * stream[0], u[1] * stream[1]) * inverse * inverse * inverse
    for half, columns in enumerate((LEFT, RIGHT)):
        store(columns, base[half] + inverse * u[half] - stream[half] * inner)
        gain_sum[:, columns] += jnp.sum(total[half, rows, :] * stream[half] * inverse, axis=0, keepdims=True)


def middle_back(size, grads, packs, middle, cot, gain, tokens, all_cot, hidden):
    piece = middle.shape[0]
    cols, _, depth, wide = packs[0].shape
    block = 256

    def kernel(
        first_ref, second_ref, pack_a, pack_b, middle_hbm, cot_hbm, gain_ref, x_ref, y_ref, hidden_ref,
        grad_ref, low_ref, gain_sum, part_ref,
        stage, land, total, send, receive, w, g_first, g_second, h, x, part,
        w_sem, first_sem, second_sem, h_sem, x_sem, part_sem, middle_ref, cot_ref, late_sem,
    ):
        pack_refs = (pack_a, pack_b)
        scatter = Scatter(size, stage, land, total, send, receive)

        def piece_rows(at):
            return pl.ds(pl.multiple_of(at * piece, piece), piece)

        def first_load(step):
            slot = lax.rem(step, 2)
            return pltpu.make_async_copy(
                first_ref.at[:, piece_rows(scatter.row_at(step))], g_first.at[slot], first_sem.at[slot]
            )

        def second_load(step):
            rows = piece_rows(scatter.row_at(step))
            return pltpu.make_async_copy(second_ref.at[:, rows], g_second.at[:, rows], second_sem.at[step])

        def w_load(i, c):
            return pltpu.make_async_copy(
                pack_refs[i].at[c, pl.ds(0, 2)], w.at[i, :, pl.ds(pl.multiple_of(c * depth, depth), depth), :], w_sem.at[i, c]
            )

        first_load(0).start()
        second_load(0).start()
        for c in range(cols):
            for i in range(2):
                w_load(i, c).start()
        first_load(1).start()
        for step in range(1, size):
            second_load(step).start()
        h_load = pltpu.make_async_copy(hidden_ref, h, h_sem)
        h_load.start()
        late = fetches([(middle_hbm, middle_ref), (cot_hbm, cot_ref)], late_sem)
        gain_sum[...] = jnp.zeros_like(gain_sum)

        def partial(step, at, store):
            first_load(step).wait()
            second_load(step).wait()

            @span_loop
            def _(t, half, columns, depth_rows):
                @pl.when(step == 0)
                def _():
                    for k in range(SPAN // depth):
                        for i in range(2):
                            w_load(i, t * (SPAN // depth) + k).wait()

                rows = piece_rows(at)
                value = 0.0
                for j in range(2):
                    value += plain_dot(g_first[lax.rem(step, 2), j], w[0, j, depth_rows, :], NT)
                    value += plain_dot(g_second[j, rows, :], w[1, j, depth_rows, :], NT)
                store(half, columns, value)

            @pl.when(step + 2 < size)
            def _():
                first_load(step + 2).start()

        def x_loads(i, slot):
            columns = pl.ds(pl.multiple_of(i * block, block), block)
            return [
                pltpu.make_async_copy(source.at[:, :, columns], x.at[slot, k], x_sem.at[slot, k])
                for k, source in enumerate((x_ref, y_ref))
            ]

        def part_move(i, slot):
            columns = pl.ds(pl.multiple_of(i * block, block), block)
            return pltpu.make_async_copy(part.at[slot], part_ref.at[:, columns, :], part_sem.at[slot])

        def weights():
            count = D // block
            for load in x_loads(0, 0):
                load.start()
            h_load.wait()

            @pl.loop(0, count)
            def _(i):
                slot = lax.rem(i, 2)

                @pl.when(i + 1 < count)
                def _():
                    for load in x_loads(i + 1, 1 - slot):
                        load.start()

                wait_all(x_loads(i, slot))

                @pl.when(i >= 2)
                def _():
                    part_move(i, slot).wait()


                @pl.loop(0, 2)
                def _(j):
                    part[slot, j] = plain_dot(x[slot, 0].reshape(GLEN, block), g_second[j], TN).astype(jnp.bfloat16)

                part[slot, 2] = plain_dot(x[slot, 1].reshape(GLEN, block), h[...], TN).astype(jnp.bfloat16)
                part_move(i, slot).start()

            for slot in range(2):
                part_move(slot, slot).wait()

        scatter.run_short(partial, weights)

        def finish(rows):
            stream = [middle_ref[rows, columns] for columns in (LEFT, RIGHT)]
            base = [cot_ref[rows, columns].astype(jnp.float32) for columns in (LEFT, RIGHT)]
            inverse = lax.rsqrt(row_mean(stream[0] * stream[0], stream[1] * stream[1]) + EPSILON)

            def store(columns, value):
                grad_ref[rows, columns] = value
                low_ref[rows, columns] = value.astype(jnp.bfloat16)

            norm_back(rows, total, stream, inverse, gain_ref, base, store, gain_sum)

        wait_all(late)
        strip_loop(piece, finish)

    return pl.pallas_call(
        kernel,
        out_shape=[fl(piece, D), bf(piece, D), fl(1, D), bf(3, D, wide)],
        in_specs=[ANY] * 6 + [VMEM] + [ANY] * 3,
        out_specs=[VMEM, VMEM, VMEM, ANY],
        scratch_shapes=scatter_scratch(size, piece, 1)
        + [
            pltpu.VMEM((2, 2, D, wide), jnp.bfloat16),
            pltpu.VMEM((2, 2, piece, wide), jnp.bfloat16),
            pltpu.VMEM((2, GLEN, wide), jnp.bfloat16),
            pltpu.VMEM((GLEN, wide), jnp.bfloat16),
            pltpu.VMEM((2, 2, size, piece, block), jnp.bfloat16),
            pltpu.VMEM((2, 3, block, wide), jnp.bfloat16),
            dma(2, cols), dma(2), dma(size), pltpu.SemaphoreType.DMA, dma(2, 2), dma(2),
            pltpu.VMEM((piece, D), jnp.float32), pltpu.VMEM((piece, D), jnp.bfloat16), dma(2),
        ],
        compiler_params=comm_params(4),
        cost_estimate=SHORT,
        name="middle_back",
    )(*grads, *packs, middle, cot, gain, tokens, all_cot, hidden)


def blocked_store(ref, rows, depth, columns, value):
    for i in range(value.shape[1] // depth):
        ref[columns.start // depth + i, rows, :] = value[:, i * depth : (i + 1) * depth]


def branch_back(size, low, w_all):
    piece = low.shape[0]
    cols, width, depth = w_all.shape
    heads = width // HD

    def kernel(x_ref, w_ref, heads_ref, all_ref, land, send, receive, own, w, w_sem, all_sem):
        loads = fetches([(w_ref.at[c], w.at[:, pl.ds(c * depth, depth)]) for c in range(cols)], w_sem)
        gather = Gather(size, x_ref, land, send, receive, own)
        gather.start()

        def keep(step, row):
            return pltpu.make_async_copy(land.at[row], all_ref.at[row], all_sem.at[step])

        def compute(step, row):
            keep(step, row).start()
            rows = pl.ds(pl.multiple_of(row * piece, piece), piece)
            value = plain_dot(land[row], w[...], NT).astype(jnp.bfloat16)
            for head in range(heads):
                heads_ref[head, rows, :] = value[:, head * HD : (head + 1) * HD]

        wait_all(loads)
        gather.each(compute, gather.forward)
        for step in range(size):
            keep(step, gather.row_at(step)).wait()
        gather.finish()

    return pl.pallas_call(
        kernel,
        out_shape=[bf(heads, GLEN, HD), bf(size, piece, D)],
        in_specs=[ANY, ANY],
        out_specs=[VMEM, ANY],
        scratch_shapes=gather_scratch(size, piece)
        + [
            pltpu.VMEM((width, D), jnp.bfloat16),
            pltpu.SemaphoreType.DMA((cols,)),
            pltpu.SemaphoreType.DMA((size,)),
        ],
        compiler_params=comm_params(6),
        cost_estimate=SHORT,
        name="branch_back",
    )(low, w_all)


def stream_back(size, grads, w_all, x, grad_middle, gain, blocks_out):
    piece = x.shape[0]
    cols, _, depth, width = w_all.shape

    def kernel(
        g_hbm, w_ref, x_hbm, middle_hbm, gain_ref, blocks_ref, out_ref, gain_sum, target_ref,
        stage, land, total, send, receive, w, w_sem, g_ref, x_ref, middle_ref, g_sem, late_sem, *rest,
    ):
        loads = fetches([(w_ref.at[c], w.at[:, pl.ds(c * depth, depth), :]) for c in range(cols)], w_sem)
        greet(row_and_col_peers(size, cols))
        outward = Outward(size, cols, blocks_ref, rest[0], target_ref, *rest[1:])
        outward.start()
        scatter = Scatter(size, stage, land, total, send, receive)

        def g_load(step):
            rows = pl.ds(pl.multiple_of(scatter.row_at(step) * piece, piece), piece)
            return pltpu.make_async_copy(g_hbm.at[:, rows], g_ref.at[:, rows], g_sem.at[step])

        for step in range(size):
            g_load(step).start()
        late = fetches([(x_hbm, x_ref), (middle_hbm, middle_ref)], late_sem)
        wait_all(loads)
        gain_sum[...] = jnp.zeros_like(gain_sum)

        def partial(step, row, store):
            g_load(step).wait()

            @span_loop
            def _(t, half, columns, depth_rows):
                rows = pl.ds(pl.multiple_of(row * piece, piece), piece)
                value = plain_dot(g_ref[0, rows, :], w[0, depth_rows, :], NT)
                for j in (1, 2):
                    value += plain_dot(g_ref[j, rows, :], w[j, depth_rows, :], NT)
                store(half, columns, value)

        scatter.run_short(partial, outward.forward, greeted=True)

        def finish(rows):
            stream = [x_ref[rows, columns].astype(jnp.float32) for columns in (LEFT, RIGHT)]
            base = [middle_ref[rows, columns] for columns in (LEFT, RIGHT)]
            inverse = lax.rsqrt(row_mean(stream[0] * stream[0], stream[1] * stream[1]) + EPSILON)

            def store(columns, value):
                blocked_store(out_ref, rows, depth, columns, value.astype(jnp.bfloat16))

            norm_back(rows, total, stream, inverse, gain_ref, base, store, gain_sum)

        wait_all(late)
        strip_loop(piece, finish)
        outward.finish()

    return pl.pallas_call(
        kernel,
        out_shape=[bf(cols, piece, depth), fl(1, D), bf(cols // size, size, piece, depth)],
        in_specs=[ANY, ANY, ANY, ANY, VMEM, ANY],
        out_specs=[VMEM, VMEM, ANY],
        scratch_shapes=scatter_scratch(size, piece, 1)
        + [pltpu.VMEM((3, D, width), jnp.bfloat16), dma(cols)]
        + [
            pltpu.VMEM((3, GLEN, width), jnp.bfloat16), pltpu.VMEM((piece, D), jnp.bfloat16),
            pltpu.VMEM((piece, D), jnp.float32), dma(size), dma(2),
        ]
        + Outward.scratch(size, cols, piece, depth),
        compiler_params=comm_params(7),
        cost_estimate=SHORT,
        name="stream_back",
    )(grads, w_all, x, grad_middle, gain, blocks_out)


def row_and_col_peers(size, cols):
    row, col = here()
    return [(lax.rem(row + d, size), col) for d in range(1, size)] + [
        (row, lax.rem(col + e, cols)) for e in range(1, cols)
    ]


class Inward:
    def __init__(self, size, cols, source, middle, land, first_send, first_receive, send, receive, own):
        self.size, self.cols, self.groups = size, cols, cols // size
        self.source, self.middle, self.land = source, middle, land
        self.first_send, self.first_receive = first_send, first_receive
        self.send, self.receive, self.own = send, receive, own
        self.row, self.col = here()

    @staticmethod
    def scratch(size, cols, piece, depth):
        return [
            pltpu.VMEM((size, cols // size, piece, depth), jnp.bfloat16),
            pltpu.VMEM((cols, piece, depth), jnp.bfloat16),
            dma(size - 1), dma(size - 1), dma(cols), dma(cols), dma(2),
        ]

    def start(self):
        row, col = self.row, self.col
        self.first = []
        for d in range(1, self.size):
            peer = lax.rem(row + d, self.size)
            self.first.append(
                remote(
                    self.source.at[:, peer], self.middle.at[row],
                    self.first_send.at[d - 1], self.first_receive.at[d - 1], (peer, col),
                )
            )
            self.first[-1].start()
        self.keep = pltpu.make_async_copy(self.source.at[:, row], self.middle.at[row], self.own.at[0])
        self.keep.start()

    def forward(self):
        row, col = self.row, self.col
        for d in range(self.size):
            origin = lax.rem(row + self.size - d, self.size)
            if d == 0:
                self.keep.wait()
            else:
                self.first[d - 1].wait_recv()
            for i in range(self.groups):
                group = origin * self.groups + i

                @pl.when(group != col)
                def _():
                    remote(
                        self.middle.at[origin, i], self.land.at[col],
                        self.send.at[group], self.receive.at[col], (row, group),
                    ).start()

                @pl.when(group == col)
                def _():
                    pltpu.make_async_copy(self.middle.at[origin, i], self.land.at[col], self.own.at[1]).start()

    def finish(self):
        row, col = self.row, self.col
        pltpu.make_async_copy(self.middle.at[0, 0], self.land.at[col], self.own.at[1]).wait()
        for e in range(1, self.cols):
            peer = lax.rem(col + e, self.cols)
            remote(
                self.middle.at[0, 0], self.land.at[peer], self.send.at[peer], self.receive.at[peer], (row, peer)
            ).wait()
        for copy in self.first:
            copy.wait_send()


class Outward:
    def __init__(self, size, cols, source, middle, target, first_send, first_receive, send, receive, own):
        self.size, self.cols, self.groups = size, cols, cols // size
        self.source, self.middle, self.target = source, middle, target
        self.first_send, self.first_receive = first_send, first_receive
        self.send, self.receive, self.own = send, receive, own
        self.row, self.col = here()

    @staticmethod
    def scratch(size, cols, piece, depth):
        return [
            pltpu.VMEM((cols, piece, depth), jnp.bfloat16),
            dma(cols - 1), dma(cols - 1), dma(cols), dma(cols), dma(cols // size),
        ]

    def start(self):
        row, col = self.row, self.col
        self.first = []
        for e in range(1, self.cols):
            peer = lax.rem(col + e, self.cols)
            self.first.append(
                remote(
                    self.source.at[peer], self.middle.at[col],
                    self.first_send.at[e - 1], self.first_receive.at[e - 1], (row, peer),
                )
            )
            self.first[-1].start()

    def forward(self):
        row, col = self.row, self.col
        for e in range(self.cols):
            group = lax.rem(col + self.cols - e, self.cols)
            if e:
                self.first[e - 1].wait_recv()
            block = self.middle.at[group] if e else self.source.at[col]
            home, i = group // self.groups, lax.rem(group, self.groups)

            @pl.when(home != row)
            def _():
                remote(
                    block, self.target.at[i, row],
                    self.send.at[group], self.receive.at[i * self.size + row], (home, col),
                ).start()

            @pl.when(home == row)
            def _():
                pltpu.make_async_copy(block, self.target.at[i, row], self.own.at[i]).start()

    def finish(self):
        row, col = self.row, self.col
        for i in range(self.groups):
            pltpu.make_async_copy(self.middle.at[0], self.target.at[i, row], self.own.at[i]).wait()
            for d in range(1, self.size):
                peer = lax.rem(row + d, self.size)
                remote(
                    self.middle.at[0], self.target.at[i, peer],
                    self.send.at[peer * self.groups + i], self.receive.at[i * self.size + peer], (peer, col),
                ).wait()
        for copy in self.first:
            copy.wait_send()


def by_pieces(block, size):
    return block.reshape(block.shape[0] // GLEN, size, GLEN // size, block.shape[1])


def enter(size, cols, stream_in, cotangent, gains):
    pieces = by_pieces(stream_in, size)
    piece, depth = pieces.shape[2:]
    scratch = Inward.scratch(size, cols, piece, depth)

    def kernel(
        x_ref, cot_ref, gains_ref, tokens_ref, normed_ref, gain_in_ref, gain_mid_ref, cot_tokens_ref, all_cot_ref,
        gains_land, gains_send, gains_receive, gather_send, gather_receive, gather_own, *rest,
    ):
        greet(row_and_col_peers(size, cols))
        exchange = Inward(size, cols, x_ref, *rest[: len(scratch)])
        second = Inward(size, cols, cot_ref, *rest[len(scratch) :])
        gather = Gather(size, cot_tokens_ref, all_cot_ref, gather_send, gather_receive, gather_own)
        second.start()
        exchange.start()
        row, col = here()
        copies = []
        for e in range(1, cols):
            peer = lax.rem(col + e, cols)
            copies.append(
                remote(gains_ref, gains_land.at[col], gains_send.at[e - 1], gains_receive.at[e - 1], (row, peer))
            )
            copies[-1].start()
        gains_land[col] = gains_ref[...]
        second.forward()
        exchange.forward()
        second.finish()

        def assemble(rows):
            for c in range(cols):
                cot_tokens_ref[rows, c * depth : (c + 1) * depth] = second.land[c, rows, :]

        strip_loop(piece, assemble)
        gather.start(greeted=True, hold=False)
        gather.forward()
        for copy in copies:
            copy.wait()
        for c in range(cols):
            gain_in_ref[:, c * depth : (c + 1) * depth] = gains_land[c, 0:1, :]
            gain_mid_ref[:, c * depth : (c + 1) * depth] = gains_land[c, 1:2, :]
        exchange.finish()
        land = exchange.land

        def norm(rows):
            total = jnp.zeros((STRIP, 1), jnp.float32)
            for c in range(cols):
                part = land[c, rows, :]
                tokens_ref[rows, c * depth : (c + 1) * depth] = part
                part = part.astype(jnp.float32)
                total += jnp.sum(part * part, axis=1, keepdims=True)
            inverse = lax.rsqrt(total / D + EPSILON)
            for c in range(cols):
                columns = slice(c * depth, (c + 1) * depth)
                normed_ref[rows, columns] = (
                    land[c, rows, :].astype(jnp.float32) * inverse * gain_in_ref[:, columns]
                ).astype(jnp.bfloat16)

        strip_loop(piece, norm)
        for step in range(size - 1):
            gather.wait(step)
        gather.keep.wait()
        gather.finish()

    return pl.pallas_call(
        kernel,
        out_shape=[bf(piece, D), bf(piece, D), fl(1, D), fl(1, D), bf(piece, D), bf(size, piece, D)],
        in_specs=[ANY, ANY, VMEM],
        out_specs=[VMEM] * 5 + [ANY],
        scratch_shapes=[pltpu.VMEM((cols, 8, depth), jnp.float32), dma(cols - 1), dma(cols - 1)]
        + [dma(Gather.semaphores(size)), dma(Gather.semaphores(size)), pltpu.SemaphoreType.DMA]
        + scratch * 2,
        compiler_params=comm_params(8),
        cost_estimate=SHORT,
        name="enter",
    )(pieces, by_pieces(cotangent, size), jnp.pad(gains, ((0, 6), (0, 0))))


def leave(size, cols, blocks_grad, stats, sums):
    _, piece, depth = blocks_grad.shape
    groups = cols // size

    def kernel(
        grad_ref, stats_ref, sums_ref, grad_target, stats_target, sums_target,
        stats_row, stats_all, sums_col, sums_part, sums_row,
        a_send, a_receive, b_send, b_receive, c_send, c_receive, d_send, d_receive, *rest,
    ):
        row, col = here()
        greet(row_and_col_peers(size, cols))
        grad = Outward(size, cols, grad_ref, rest[0], grad_target, *rest[1:])
        home, slot = col // groups, lax.rem(col, groups)
        col_peers = [lax.rem(col + e, cols) for e in range(1, cols)]
        row_peers = [lax.rem(row + d, size) for d in range(1, size)]

        def sums_first(peer):
            return remote(sums_ref.at[peer], sums_col.at[col], c_send.at[peer], c_receive.at[col], (row, peer))

        for peer in col_peers:
            sums_first(peer).start()
        sums_col[col] = sums_ref[col]

        @pl.when(home != row)
        def _():
            remote(stats_ref, stats_row.at[row], a_send, a_receive.at[row], (home, col)).start()

        @pl.when(home == row)
        def _():
            stats_row[row] = stats_ref[...]

        grad.start()
        for peer in col_peers:
            remote(sums_ref.at[peer], sums_col.at[peer], c_send.at[peer], c_receive.at[peer], (row, peer)).wait()
        total = sums_col[0]
        for c in range(1, cols):
            total += sums_col[c]
        sums_part[...] = total
        sums_row[row] = total
        for peer in row_peers:
            remote(sums_part, sums_row.at[row], d_send.at[peer], d_receive.at[row], (peer, col)).start()

        @pl.when(home == row)
        def _():
            for peer in row_peers:
                remote(stats_ref, stats_row.at[peer], a_send, a_receive.at[peer], (peer, col)).wait_recv()
            for e, peer in enumerate(col_peers):
                remote(stats_row, stats_all.at[slot], b_send.at[e], b_receive.at[slot], (row, peer)).start()
            stats_all[slot] = stats_row[...]

        grad.forward()
        for peer in row_peers:
            remote(sums_part, sums_row.at[peer], d_send.at[peer], d_receive.at[peer], (peer, col)).wait()
        whole = sums_row[0]
        for r in range(1, size):
            whole += sums_row[r]
        line = lax.broadcasted_iota(jnp.int32, (8, depth), 0)
        sums_target[...] = jnp.where(line < 2, whole, total)

        @pl.when(home == row)
        def _():
            for e, peer in enumerate(col_peers):
                remote(stats_row, stats_all.at[slot], b_send.at[e], b_receive.at[slot], (row, peer)).wait_send()

        @pl.when(home != row)
        def _():
            remote(stats_ref, stats_row.at[row], a_send, a_receive.at[row], (home, col)).wait_send()

        for i in range(groups):
            group = row * groups + i

            @pl.when(group != col)
            def _():
                remote(stats_row, stats_all.at[i], b_send.at[0], b_receive.at[i], (row, group)).wait_recv()

        stats_target[...] = stats_all[...]
        grad.finish()

    return pl.pallas_call(
        kernel,
        out_shape=[
            bf(groups, size, piece, depth),
            fl(groups, size, 8, piece), fl(8, depth),
        ],
        in_specs=[VMEM] * 3,
        out_specs=[ANY, VMEM, VMEM],
        scratch_shapes=[
            pltpu.VMEM((size, 8, piece), jnp.float32),
            pltpu.VMEM((groups, size, 8, piece), jnp.float32),
            pltpu.VMEM((cols, 8, depth), jnp.float32),
            pltpu.VMEM((8, depth), jnp.float32),
            pltpu.VMEM((size, 8, depth), jnp.float32),
            pltpu.SemaphoreType.DMA, dma(size), dma(cols - 1), dma(groups), dma(cols), dma(cols), dma(size), dma(size),
        ]
        + Outward.scratch(size, cols, piece, depth),
        compiler_params=comm_params(10),
        cost_estimate=SHORT,
        name="leave",
    )(blocks_grad, stats, sums)


def over_col(partial, axis):
    return lax.psum_scatter(partial.astype(jnp.bfloat16), "col", scatter_dimension=axis, tiled=True)


def flat(pieces):
    return pieces.reshape(GLEN, D)


def local(
    stream_in,
    w_qkv,
    w_out,
    w_gate_up,
    w_down,
    gain_attn,
    gain_ffn,
    gate_logit,
    memory,
    memory_norm,
    offsets,
    lengths,
    cotangent,
):
    head_here = memory.shape[1]
    size = lax.axis_size("row")
    cols = lax.axis_size("col")
    all_qkv = lax.all_gather(w_qkv, "col", axis=0, tiled=False)
    units = w_down.shape[0] // 2
    packs = [
        jnp.concatenate([w_gate_up[:, :, part], w_down[part].T[None]], axis=0)
        for part in (slice(0, units), slice(units, None))
    ]
    all_packs = [lax.all_gather(pack, "col", axis=0, tiled=False) for pack in packs]
    gate_value = jax.nn.sigmoid(gate_logit)
    group = (memory[0], memory_norm[0], offsets[0], lengths[0], gate_value)
    stream, normed_in, gain_in, gain_mid, cot, all_cot = enter(
        size, cols, stream_in, cotangent, jnp.stack([gain_attn, gain_ffn])
    )
    heads_all, all_in, all_out = project_heads(size, normed_in, all_qkv, w_out)
    attn, dot_part, memory_part, logsum, memory_new, norm_new = attend(heads_all, *group)
    middle, normed_ffn, stat_branch = branch_out(size, attn, all_out, stream, gain_mid)
    hidden_first, grads_first, all_ffn = feed_forward(size, normed_ffn, all_packs[0], all_cot, True)
    part_first = weight_grads(flat(all_ffn), grads_first, flat(all_cot), hidden_first)
    part_first, all_ffn = lax.optimization_barrier((part_first, all_ffn))
    scattered_first = over_col(part_first, 1)
    hidden_second, grads_second = feed_forward(size, all_ffn, all_packs[1], all_cot, False)
    grad_middle, low_branch, part_gain_ffn, part_second = middle_back(
        size, (grads_first, grads_second), all_packs, middle, cot, gain_mid, all_ffn, all_cot, hidden_second
    )
    scattered_second = over_col(part_second, 1)
    grad_heads, all_branch = branch_back(size, low_branch, all_out)
    grads_qkv, gate_sums, blocks_out, stat_ffn = attend_back(
        size, heads_all, grad_heads, dot_part, memory_part, logsum, *group,
        (hidden_first, hidden_second), all_packs, middle,
    )
    part_attn = weight_grads(flat(all_in), grads_qkv, flat(all_branch), attn)
    grads_qkv, part_attn, scattered_first = lax.optimization_barrier((grads_qkv, part_attn, scattered_first))
    scattered_attn = over_col(part_attn, 1)
    blocks_grad, part_gain_attn, stream_out = stream_back(
        size, grads_qkv, all_qkv, stream, grad_middle, gain_in, blocks_out
    )
    grad_gate_up = jnp.concatenate([scattered_first[:2], scattered_second[:2]], axis=2).astype(jnp.float32)
    grad_down = jnp.concatenate([scattered_first[2], scattered_second[2]], axis=1).T.astype(jnp.float32)
    blocks_grad, grad_gate_up, grad_down = lax.optimization_barrier((blocks_grad, grad_gate_up, grad_down))
    grad_qkv, grad_out = scattered_attn[:3].astype(jnp.float32), scattered_attn[3].T.astype(jnp.float32)
    logit_part = gate_value * (1.0 - gate_value) * jnp.sum(gate_sums, axis=(1, 2))
    features_here = gain_attn.shape[0]
    sums = jnp.concatenate(
        [
            part_gain_attn.reshape(cols, 1, features_here),
            part_gain_ffn.reshape(cols, 1, features_here),
            jnp.broadcast_to(
                jnp.pad(logit_part, (0, features_here - head_here))[None, None], (cols, 6, features_here)
            ),
        ],
        axis=1,
    )
    stats = jnp.sqrt(jnp.concatenate([stat_branch[:, :2], stat_ffn[:, :2]], axis=1).T)
    stream_grad, stats_all, sums = leave(
        size, cols, blocks_grad, jnp.pad(stats, ((0, 4), (0, 0))), sums
    )
    stream_out = stream_out.reshape(stream_in.shape)
    stream_grad = stream_grad.reshape(stream_in.shape).astype(jnp.float32)
    rms_table = stats_all[:, :, :4].transpose(2, 0, 1, 3).reshape(4, stream_in.shape[0])
    grad_gain_attn, grad_gain_ffn, grad_gate_logit = sums[0], sums[1], sums[2, :head_here]
    return (
        stream_out,
        stream_grad,
        grad_qkv,
        grad_out,
        grad_gate_up,
        grad_down,
        grad_gain_attn,
        grad_gain_ffn,
        grad_gate_logit,
        memory_new[None],
        norm_new.reshape(1, head_here, HD),
        rms_table,
    )


def solution(mesh):
    return jax.shard_map(
        local,
        mesh=mesh,
        in_specs=(
            P("row", "col"),
            P(None, "col", "row"),
            P("row", "col"),
            P(None, "col", "row"),
            P("row", "col"),
            P("col"),
            P("col"),
            P("row"),
            P("col", "row", None, None),
            P("col", "row", None),
            P("col", None),
            P("col", None),
            P("row", "col"),
        ),
        out_specs=(
            P("row", "col"),
            P("row", "col"),
            P(None, "col", "row"),
            P("row", "col"),
            P(None, "col", "row"),
            P("row", "col"),
            P("col"),
            P("col"),
            P("row"),
            P("col", "row", None, None),
            P("col", "row", None),
            P(None, "row"),
        ),
        check_vma=False,
    )
```

```python
import functools

import jax
import jax.numpy as jnp
from jax import lax
from jax.experimental import pallas as pl
from jax.experimental.pallas import tpu as pltpu
from jax.sharding import PartitionSpec as P

D = 2048
HD = 128
PROMPT = 1024
CONT = 4
CLEN = 128
GLEN = 1536


EPSILON = 1e-06
MASKED_LOGIT = -1e30
BIG_VMEM = 60 * 1024 * 1024
SHORT = pl.CostEstimate(flops=1000, bytes_accessed=1000, transcendentals=0)


def feature_map(values):
    return jnp.where(values > 0, values + 1.0, jnp.exp(jnp.minimum(values, 0.0)))


def feature_slope(values):
    return jnp.where(values > 0, 1.0, jnp.exp(jnp.minimum(values, 0.0)))


def split_two(value):
    high = value.astype(jnp.bfloat16)
    return high, (value - high.astype(jnp.float32)).astype(jnp.bfloat16)


def wide_dot(left, right, dims):
    left_high, left_low = split_two(left)
    right_high, right_low = split_two(right)

    def one(a, b):
        return lax.dot_general(a, b, (dims, ((), ())), preferred_element_type=jnp.float32)

    return one(left_high, right_high) + one(left_high, right_low) + one(left_low, right_high)


def narrow_dot(left, right, dims):
    right_high, right_low = split_two(right)

    def one(b):
        return lax.dot_general(left, b, (dims, ((), ())), preferred_element_type=jnp.float32)

    return one(right_high) + one(right_low)


def plain_dot(left, right, dims):
    return lax.dot_general(left, right, (dims, ((), ())), preferred_element_type=jnp.float32)


NN = ((1,), (0,))
NT = ((1,), (1,))
TN = ((0,), (0,))
QT = 256
PROMPT_TILES = PROMPT // QT
TILES = GLEN // QT


def tile_rows(tile):
    return pl.ds(pl.multiple_of(tile * QT, QT), QT) if not isinstance(tile, int) else slice(tile * QT, (tile + 1) * QT)


def tile_scores(tile, q, k_ref, offsets_ref, lengths_ref):
    scale = HD ** (-0.5)
    row = lax.broadcasted_iota(jnp.int32, (QT, QT), 0)
    column = lax.broadcasted_iota(jnp.int32, (QT, QT), 1)
    own = plain_dot(q, k_ref[tile_rows(tile)], NT) * scale
    if isinstance(tile, int) and tile < PROMPT_TILES:
        seen = tile * QT
        own = jnp.where(row >= column, own, MASKED_LOGIT)
        ahead = plain_dot(q, k_ref[:seen], NT) * scale if seen else None
        return ahead, own, seen
    first = (tile - PROMPT_TILES) * (QT // CLEN)
    upper = lax.broadcasted_iota(jnp.int32, (QT, 1), 0) >= CLEN
    limit = jnp.where(upper, offsets_ref[first + 1], offsets_ref[first])
    live = jnp.where(upper, lengths_ref[first + 1] + CLEN, lengths_ref[first])
    same = (row >= CLEN) == (column >= CLEN)
    own = jnp.where((row >= column) & same & (column < live), own, MASKED_LOGIT)
    ahead = plain_dot(q, k_ref[:PROMPT], NT) * scale
    position = lax.broadcasted_iota(jnp.int32, (QT, PROMPT), 1)
    return jnp.where(position < limit, ahead, MASKED_LOGIT), own, PROMPT


def each_tile(body):
    for tile in range(PROMPT_TILES):
        body(tile)
    pl.loop(PROMPT_TILES, TILES)(body)


def attend_kernel(
    offsets_ref, lengths_ref, gate_ref, qkv_ref, memory_ref, norm_ref,
    attn_ref, dot_ref, part_ref, logsum_ref, memory_new_ref, norm_new_ref,
):
    head = pl.program_id(0)
    gate = gate_ref[head]
    q_ref, k_ref, v_ref = qkv_ref.at[0, 0], qkv_ref.at[1, 0], qkv_ref.at[2, 0]
    memory_one = memory_ref[0]
    norm_one = norm_ref[0]
    for tile in range(TILES):
        rows = slice(tile * QT, (tile + 1) * QT)
        q = q_ref[rows]
        ahead, own, seen = tile_scores(tile, q, k_ref, offsets_ref, lengths_ref)
        peak = jnp.max(own, axis=1, keepdims=True)
        if ahead is not None:
            peak = jnp.maximum(peak, jnp.max(ahead, axis=1, keepdims=True))
        own = jnp.exp(own - peak)
        total = jnp.sum(own, axis=1, keepdims=True)
        dot_part = plain_dot(own.astype(jnp.bfloat16), v_ref[rows], NN)
        if ahead is not None:
            ahead = jnp.exp(ahead - peak)
            total += jnp.sum(ahead, axis=1, keepdims=True)
            dot_part += plain_dot(ahead.astype(jnp.bfloat16), v_ref[:seen], NN)
        dot_part = dot_part / total
        lifted = feature_map(q.astype(jnp.float32))
        memory_part = wide_dot(lifted, memory_one, NN) / jnp.sum(
            lifted * norm_one, axis=1, keepdims=True
        )
        attn_ref[rows, :] = (gate * memory_part + (1.0 - gate) * dot_part).astype(jnp.bfloat16)
        dot_ref[0, rows, :] = dot_part
        part_ref[0, rows, :] = memory_part
        logsum_ref[0, rows, :] = peak + jnp.log(total)
    lifted_keys = feature_map(k_ref[:PROMPT].astype(jnp.float32))
    high, low = split_two(lifted_keys)
    v = v_ref[:PROMPT]
    memory_new_ref[0] = memory_one + (plain_dot(high, v, TN) + plain_dot(low, v, TN)) / PROMPT
    norm_new_ref[0] = norm_one + jnp.mean(lifted_keys, axis=0, keepdims=True)


def head_block(shape, lead=0):
    zeros = (0,) * (len(shape) - 1 - lead)
    return pl.BlockSpec(shape, lambda h: (0,) * lead + (h,) + zeros)


SMEM_SPEC = pl.BlockSpec(memory_space=pltpu.SMEM)


def attend(heads_all, memory_one, norm_one, offsets, lengths, gate_value):
    heads = heads_all.shape[1]
    f32 = jnp.float32
    row_block = head_block((1, GLEN, HD))
    column = pl.BlockSpec((GLEN, HD), lambda h: (0, h))
    return pl.pallas_call(
        attend_kernel,
        grid=(heads,),
        in_specs=[
            SMEM_SPEC, SMEM_SPEC, SMEM_SPEC,
            head_block((3, 1, GLEN, HD), 1), head_block((1, HD, HD)), head_block((1, 1, HD)),
        ],
        out_specs=[
            column, row_block, row_block, head_block((1, GLEN, 1)),
            head_block((1, HD, HD)), head_block((1, 1, HD)),
        ],
        out_shape=[
            jax.ShapeDtypeStruct((GLEN, heads * HD), jnp.bfloat16),
            jax.ShapeDtypeStruct((heads, GLEN, HD), f32),
            jax.ShapeDtypeStruct((heads, GLEN, HD), f32),
            jax.ShapeDtypeStruct((heads, GLEN, 1), f32),
            jax.ShapeDtypeStruct((heads, HD, HD), f32),
            jax.ShapeDtypeStruct((heads, 1, HD), f32),
        ],
        compiler_params=pltpu.CompilerParams(vmem_limit_bytes=BIG_VMEM),
        cost_estimate=SHORT,
        name="attend",
    )(offsets, lengths, gate_value, heads_all, memory_one, norm_one[:, None, :])


def attend_back_kernel(
    size, cols, depth, wide,
    offsets_ref, lengths_ref, gate_ref, qkv_ref, grad_ref, dot_ref, part_ref, logsum_ref,
    memory_ref, norm_ref, middle_hbm, hidden_a, hidden_b, pack_a, pack_b,
    out_ref, gate_out_ref, blocks_ref, stat_ref,
    key_sum, value_sum, query_sum, stage, land, total, send, receive, h, w, h_sem, w_sem, middle_ref, middle_sem,
):
    head = pl.program_id(0)
    piece = GLEN // size
    scatter = Scatter(size, stage, land, total, send, receive)

    def h_load(i, step):
        rows = pl.ds(pl.multiple_of(scatter.row_at(step) * piece, piece), piece)
        return pltpu.make_async_copy((hidden_a, hidden_b)[i].at[rows], h.at[i, rows], h_sem.at[i, step])

    def w_load(i, c):
        return pltpu.make_async_copy(
            (pack_a, pack_b)[i].at[c, 2], w.at[i, pl.ds(pl.multiple_of(c * depth, depth), depth), :], w_sem.at[i, c]
        )

    def partial(step, at, store):
        for i in range(2):
            h_load(i, step).wait()

        @span_loop
        def _(t, half, columns, depth_rows):
            @pl.when(step == 0)
            def _():
                for k in range(SPAN // depth):
                    for i in range(2):
                        w_load(i, t * (SPAN // depth) + k).wait()

            rows = pl.ds(pl.multiple_of(at * piece, piece), piece)
            store(
                half, columns,
                plain_dot(h[0, rows, :], w[0, depth_rows, :], NT) + plain_dot(h[1, rows, :], w[1, depth_rows, :], NT),
            )

    middle_load = pltpu.make_async_copy(middle_hbm, middle_ref, middle_sem)

    @pl.when(head == 0)
    def _():
        for i in range(2):
            h_load(i, 0).start()
        for c in range(cols):
            for i in range(2):
                w_load(i, c).start()
        for step in range(1, size):
            for i in range(2):
                h_load(i, step).start()
        middle_load.start()
        scatter.begin(partial)

    @pl.when(head == pl.num_programs(0) // 2)
    def _():
        scatter.middle()

    gate = gate_ref[head]
    keep = 1.0 - gate
    scale = HD ** (-0.5)
    q_ref, k_ref, v_ref = qkv_ref.at[0, 0], qkv_ref.at[1, 0], qkv_ref.at[2, 0]
    memory_one = memory_ref[0]
    norm_one = norm_ref[0]
    gate_out_ref[0] = jnp.zeros((1, HD), jnp.float32)
    key_sum[...] = jnp.zeros_like(key_sum)
    value_sum[...] = jnp.zeros_like(value_sum)

    @pl.loop(0, TILES)
    def _(tile):
        rows = tile_rows(tile)
        grad = grad_ref[0, rows, :]
        grad_float = grad.astype(jnp.float32)
        memory_part = part_ref[0, rows, :]
        gate_out_ref[0] += jnp.sum(grad_float * (memory_part - dot_ref[0, rows, :]), axis=0, keepdims=True)
        q_float = q_ref[rows].astype(jnp.float32)
        lifted = feature_map(q_float)
        inverse = gate / jnp.sum(lifted * norm_one, axis=1, keepdims=True)
        against_memory = jnp.sum(grad_float * memory_part, axis=1, keepdims=True)
        grad_lifted = inverse * (narrow_dot(grad, memory_one, NT) - against_memory * norm_one)
        query_sum[rows, :] = grad_lifted * feature_slope(q_float)

    def one(tile):
        rows = tile_rows(tile)
        q = q_ref[rows]
        grad = grad_ref[0, rows, :]
        grad_float = grad.astype(jnp.float32)
        against_dot = jnp.sum(grad_float * dot_ref[0, rows, :], axis=1, keepdims=True)
        logsum = logsum_ref[0, rows, :]
        ahead, own, seen = tile_scores(tile, q, k_ref, offsets_ref, lengths_ref)
        own = jnp.exp(own - logsum)
        value_sum[rows, :] += plain_dot(own.astype(jnp.bfloat16), grad, TN)
        own = (keep * own * (plain_dot(grad, v_ref[rows], NT) - against_dot)).astype(jnp.bfloat16)
        key_sum[rows, :] += plain_dot(own, q, TN)
        grad_q = plain_dot(own, k_ref[rows], NN)
        if ahead is not None:
            ahead = jnp.exp(ahead - logsum)
            value_sum[:seen, :] += plain_dot(ahead.astype(jnp.bfloat16), grad, TN)
            ahead = (keep * ahead * (plain_dot(grad, v_ref[:seen], NT) - against_dot)).astype(
                jnp.bfloat16
            )
            key_sum[:seen, :] += plain_dot(ahead, q, TN)
            grad_q += plain_dot(ahead, k_ref[:seen], NN)
        out_ref[0, rows, :] = (grad_q * scale + query_sum[rows, :]).astype(jnp.bfloat16)

    each_tile(one)
    out_ref[1, :, :] = (key_sum[...] * scale).astype(jnp.bfloat16)
    out_ref[2, :, :] = (value_sum[...] * keep).astype(jnp.bfloat16)

    def finish(rows):
        ffn = [total[half, rows, :] for half in range(2)]
        result = [middle_ref[rows, columns] + ffn[half] for half, columns in enumerate((LEFT, RIGHT))]
        for half, columns in enumerate((LEFT, RIGHT)):
            blocked_store(blocks_ref, rows, depth, columns, result[half].astype(jnp.bfloat16))
        stat_ref[rows, :] = lanes(
            row_mean(ffn[0] * ffn[0], ffn[1] * ffn[1]),
            row_mean(result[0] * result[0], result[1] * result[1]),
        )

    @pl.when(head == pl.num_programs(0) - 1)
    def _():
        scatter.own(partial)
        scatter.end()
        middle_load.wait()
        strip_loop(piece, finish)


def whole_block(shape):
    return pl.BlockSpec(shape, lambda h: (0,) * len(shape), pipeline_mode=pl.Buffered(1))


def attend_back(
    size, heads_all, grad_heads, dot_part, memory_part, logsum, memory_one, norm_one, offsets, lengths, gate_value,
    hiddens, packs, middle,
):
    heads = heads_all.shape[1]
    piece = middle.shape[0]
    cols, _, depth, wide = packs[0].shape
    row_block = head_block((1, GLEN, HD))
    return pl.pallas_call(
        functools.partial(attend_back_kernel, size, cols, depth, wide),
        grid=(heads,),
        in_specs=[
            SMEM_SPEC, SMEM_SPEC, SMEM_SPEC,
            head_block((3, 1, GLEN, HD), 1), row_block, row_block, row_block,
            head_block((1, GLEN, 1)), head_block((1, HD, HD)), head_block((1, 1, HD)),
            ANY, ANY, ANY, ANY, ANY,
        ],
        out_specs=[
            pl.BlockSpec((3, GLEN, HD), lambda h: (0, 0, h)),
            head_block((1, 1, HD)),
            whole_block((cols, piece, depth)), whole_block((piece, HD)),
        ],
        out_shape=[bf(3, GLEN, heads * HD), fl(heads, 1, HD), bf(cols, piece, depth), fl(piece, HD)],
        scratch_shapes=[pltpu.VMEM((GLEN, HD), jnp.float32)] * 3
        + scatter_scratch(size, piece)
        + [
            pltpu.VMEM((2, GLEN, wide), jnp.bfloat16),
            pltpu.VMEM((2, D, wide), jnp.bfloat16),
            dma(2, size), dma(2, cols), pltpu.VMEM((piece, D), jnp.float32), pltpu.SemaphoreType.DMA,
        ],
        compiler_params=comm_params(5),
        cost_estimate=SHORT,
        name="attend_back",
    )(
        offsets, lengths, gate_value, heads_all, grad_heads, dot_part, memory_part, logsum,
        memory_one, norm_one[:, None, :], middle, *hiddens, *packs,
    )


ANY = pl.BlockSpec(memory_space=pl.ANY)
VMEM = pl.BlockSpec(memory_space=pltpu.VMEM)
MESH_ID = pl.DeviceIdType.MESH
HALF = D // 2
AG_CUTS = 8


def remote(source, target, send, receive, device):
    return pltpu.make_async_remote_copy(
        src_ref=source, dst_ref=target, send_sem=send, recv_sem=receive,
        device_id=device, device_id_type=MESH_ID,
    )


def dma(*shape):
    return pltpu.SemaphoreType.DMA(shape)


def here():
    return lax.axis_index("row"), lax.axis_index("col")


def greet(peers):
    barrier = pltpu.get_barrier_semaphore()
    for peer in peers:
        pl.semaphore_signal(barrier, inc=1, device_id=peer, device_id_type=MESH_ID)
    pl.semaphore_wait(barrier, len(peers))


def square(row):
    along_x = (row // 2) * 2 + (1 - lax.rem(row, 2))
    along_y = lax.rem(row + 2, 4)
    across = (along_y // 2) * 2 + (1 - lax.rem(along_y, 2))
    return along_x, along_y, across


class Gather:
    def __init__(self, size, source, land, send, receive, own):
        self.size = size
        row, col = self.row, self.col = here()
        piece = source.shape[0]
        self.keep = pltpu.make_async_copy(source, land.at[row], own)
        if size != 4:
            self.peers = [(lax.rem(row + d, size), col) for d in range(1, size)]
            self.order = [lax.rem(row + size - d, size) for d in range(1, size)]
            self.copies = [
                remote(source, land.at[row], send.at[i], receive.at[i], peer) for i, peer in enumerate(self.peers)
            ]
            return
        self.order = rx, ry, rd = square(row)
        px, py = self.peers = [(rx, col), (ry, col)]
        height = piece // AG_CUTS
        cuts = [pl.ds(cut * height, height) for cut in range(AG_CUTS)]

        def out(cut, base, peer):
            return remote(
                source.at[cuts[cut]], land.at[row, cuts[cut]], send.at[base + cut], receive.at[base + cut], peer
            )

        def onward(cut, owner, peer):
            place = land.at[owner, cuts[cut]]
            return remote(place, place, send.at[2 * AG_CUTS + cut], receive.at[2 * AG_CUTS + cut], peer)

        middle = AG_CUTS // 2
        self.to_x = [out(cut, 0, px) for cut in range(AG_CUTS)]
        self.to_y = [out(cut, AG_CUTS, py) for cut in range(AG_CUTS)]
        self.onward = [onward(cut, rx, py) for cut in range(middle)] + [
            onward(cut, ry, px) for cut in range(middle, AG_CUTS)
        ]

    @staticmethod
    def semaphores(size):
        return 3 * AG_CUTS if size == 4 else size - 1

    def start(self, greeted=False, hold=True):
        if not greeted:
            greet(self.peers)
        if self.size != 4:
            for copy in self.copies:
                copy.start()
        else:
            for step in range(AG_CUTS):
                self.to_x[step].start()
                self.to_y[(step + AG_CUTS // 2) % AG_CUTS].start()
        self.keep.start()
        if hold:
            self.keep.wait()

    def forward(self):
        if self.size != 4:
            return
        for step in range(AG_CUTS // 2):
            later = step + AG_CUTS // 2
            self.to_x[step].wait_recv()
            self.onward[step].start()
            self.to_y[later].wait_recv()
            self.onward[later].start()

    def wait(self, step):
        middle = AG_CUTS // 2
        if self.size != 4:
            waits = [self.copies[step]]
        else:
            waits = (self.to_x[middle:], self.to_y[:middle], self.onward)[step]
        for copy in waits:
            copy.wait_recv()
        return self.order[step]

    def row_at(self, step):
        if self.size != 4:
            return lax.rem(self.row + self.size - step, self.size)
        along_x = lax.rem(lax.rem(self.row, 2) + lax.rem(step, 2), 2)
        return 2 * lax.rem(self.row // 2 + step // 2, 2) + along_x

    def each(self, body, between):
        @pl.loop(0, self.size)
        def _(step):
            for k in range(1, self.size):

                @pl.when(step == k)
                def _():
                    if k == 1:
                        between()
                    self.wait(k - 1)

            body(step, self.row_at(step))

    def finish(self):
        for copy in self.copies if self.size != 4 else [*self.to_x, *self.to_y, *self.onward]:
            copy.wait_send()


class CoreGather:
    def __init__(self, cols, source, target, far_send, far_receive, near_send, near_receive, own):
        row, col = here()
        pair = (col // 2) * 2 + 1 - lax.rem(col, 2)
        chips = cols // 2
        self.greets = [(row, lax.rem(col + 2 * e, cols)) for e in range(1, chips)] + [(row, pair)]
        self.far = [
            remote(source, target.at[col], far_send.at[e], far_receive.at[e], peer)
            for e, peer in enumerate(self.greets[:-1])
        ]
        self.near = [remote(source, target.at[col], near_send.at[0], near_receive.at[0], (row, pair))]
        for e in range(1, chips):
            place = target.at[lax.rem(col + cols - 2 * e, cols)]
            self.near.append(remote(place, place, near_send.at[e], near_receive.at[e], (row, pair)))
        self.keep = pltpu.make_async_copy(source, target.at[col], own)

    @staticmethod
    def scratch(cols):
        far, near = cols // 2 - 1, cols // 2
        return [dma(far), dma(far), dma(near), dma(near), pltpu.SemaphoreType.DMA]

    def start(self):
        for copy in [*self.far, self.near[0], self.keep]:
            copy.start()

    def forward(self):
        for e, copy in enumerate(self.far):
            copy.wait_recv()
            self.near[e + 1].start()

    def finish(self):
        for copy in self.near:
            copy.wait()
        for copy in self.far:
            copy.wait_send()
        self.keep.wait()


class Scatter:
    def __init__(self, size, stage, land, total, send, receive):
        self.size, self.stage, self.land, self.total = size, stage, land, total
        self.send, self.receive = send, receive
        self.row, self.col = here()
        self.plan()

    @staticmethod
    def semaphores(size):
        return 6 if size == 4 else size - 1

    @staticmethod
    def stage_shape(size, piece):
        return (3 if size == 4 else size - 1, 2, piece, HALF)

    @staticmethod
    def land_shape(size, piece):
        return (6, piece, HALF) if size == 4 else (size - 1, 2, piece, HALF)

    def plan(self):
        row, col, stage = self.row, self.col, self.stage

        def copy(index, source, peer):
            return remote(source, self.land.at[index], self.send.at[index], self.receive.at[index], peer)

        if self.size != 4:
            others = [lax.rem(row + d, self.size) for d in range(1, self.size)]
            self.peers = [(peer, col) for peer in others]
            self.order = [*others, row]
            self.copies = [copy(slot, stage.at[slot], peer) for slot, peer in enumerate(self.peers)]
            self.after = [[slot] for slot in range(self.size - 1)]
            return
        rx, ry, rd = square(row)
        px, py = self.peers = [(rx, col), (ry, col)]
        self.order = [rd, rx, ry, row]
        self.copies = [
            copy(0, stage.at[0, 0], px), copy(1, stage.at[0, 1], py), copy(2, stage.at[1, 0], px),
            copy(3, stage.at[2, 1], py), copy(4, stage.at[2, 0], py), copy(5, stage.at[1, 1], px),
        ]
        self.after = [[0, 1], [2], [3]]

    def begin(self, partial, greeted=False):
        if not greeted:
            greet(self.peers)

        @pl.loop(0, self.size - 1)
        def _(step):
            def store(half, columns, value):
                self.stage[step, half, :, columns] = value.astype(jnp.bfloat16)

            partial(step, self.row_at(step), store)
            for k, indices in enumerate(self.after):

                @pl.when(step == k)
                def _():
                    for index in indices:
                        self.copies[index].start()

    def row_at(self, step):
        if self.size != 4:
            return lax.rem(self.row + 1 + step, self.size)
        along_x = lax.rem(lax.rem(self.row, 2) + 3 - step // 2, 2)
        return 2 * lax.rem(self.row // 2 + 3 - lax.rem(step, 2), 2) + along_x

    def middle(self):
        if self.size != 4:
            return
        self.copies[0].wait_recv()
        self.add_stage(2, 0, self.land.at[0])
        self.copies[4].start()
        self.copies[1].wait_recv()
        self.add_stage(1, 1, self.land.at[1])
        self.copies[5].start()

    def own(self, partial):
        def store(half, columns, value):
            self.total[half, :, columns] = value

        partial(self.size - 1, self.order[-1], store)

    def end(self):
        if self.size != 4:
            for slot, copy in enumerate(self.copies):
                copy.wait_recv()
                self.add_total(0, self.land.at[slot, 0])
                self.add_total(1, self.land.at[slot, 1])
        else:
            for index, half in ((2, 0), (3, 1), (4, 0), (5, 1)):
                self.copies[index].wait_recv()
                self.add_total(half, self.land.at[index])
        for copy in self.copies:
            copy.wait_send()

    def run(self, partial, late=None, greeted=False):
        self.begin(partial, greeted)
        self.middle()
        self.own(partial)
        if late is not None:
            late()
        self.end()

    def run_short(self, partial, late=None, greeted=False):
        if not greeted:
            greet(self.peers)

        @pl.loop(0, self.size)
        def _(step):
            @pl.when(step == self.size - 1)
            def _():
                self.middle()

            def store(half, columns, value):
                self.total[half, :, columns] = value
                self.stage[step, half, :, columns] = value.astype(jnp.bfloat16)

            partial(step, self.row_at(step), store)
            for k, indices in enumerate(self.after):

                @pl.when(step == k)
                def _():
                    for index in indices:
                        self.copies[index].start()

        if late is not None:
            late()
        self.end()

    def add_stage(self, slot, half, landed):
        @pl.loop(0, landed.shape[0] // STRIP)
        def _(i):
            rows = pl.ds(pl.multiple_of(i * STRIP, STRIP), STRIP)
            value = self.stage[slot, half, rows, :].astype(jnp.float32) + landed[rows, :].astype(jnp.float32)
            self.stage[slot, half, rows, :] = value.astype(jnp.bfloat16)

    def add_total(self, half, landed):
        @pl.loop(0, landed.shape[0] // STRIP)
        def _(i):
            rows = pl.ds(pl.multiple_of(i * STRIP, STRIP), STRIP)
            self.total[half, rows, :] += landed[rows, :].astype(jnp.float32)


STRIP = 32


def scatter_scratch(size, piece, spare=0):
    count = Scatter.semaphores(size)
    slots, *shape = Scatter.stage_shape(size, piece)
    return [
        pltpu.VMEM((slots + spare, *shape), jnp.bfloat16),
        pltpu.VMEM(Scatter.land_shape(size, piece), jnp.bfloat16),
        pltpu.VMEM((2, piece, HALF), jnp.float32),
        pltpu.SemaphoreType.DMA((count,)),
        pltpu.SemaphoreType.DMA((count,)),
    ]


def gather_scratch(size, piece):
    count = Gather.semaphores(size)
    return [
        pltpu.VMEM((size, piece, D), jnp.bfloat16),
        pltpu.SemaphoreType.DMA((count,)),
        pltpu.SemaphoreType.DMA((count,)),
        pltpu.SemaphoreType.DMA,
    ]


def fetches(pairs, semaphores):
    copies = [pltpu.make_async_copy(a, b, semaphores.at[i]) for i, (a, b) in enumerate(pairs)]
    for copy in copies:
        copy.start()
    return copies


def wait_all(copies):
    for copy in copies:
        copy.wait()


def tiles_of(width, tile):
    def run(body):
        @pl.loop(0, width // tile)
        def _(t):
            body(t, pl.ds(pl.multiple_of(t * tile, tile), tile))

    return run


SPAN = 512


def span_loop(body):
    inside = HALF // SPAN

    @pl.loop(0, D // SPAN)
    def _(t):
        body(
            t, t // inside,
            pl.ds(pl.multiple_of(lax.rem(t, inside) * SPAN, SPAN), SPAN),
            pl.ds(pl.multiple_of(t * SPAN, SPAN), SPAN),
        )


def comm_params(identity):
    return pltpu.CompilerParams(
        collective_id=identity, has_side_effects=True, vmem_limit_bytes=BIG_VMEM
    )


def bf(*shape):
    return jax.ShapeDtypeStruct(shape, jnp.bfloat16)


def fl(*shape):
    return jax.ShapeDtypeStruct(shape, jnp.float32)


def project_heads(size, normed, w_all, w_out):
    piece = normed.shape[0]
    cols, _, depth, width = w_all.shape
    heads = width // HD

    def kernel(
        x_ref, w_ref, out_ref, heads_ref, all_ref, all_out_ref,
        land, send, receive, own, w, w_sem, all_sem, *rest,
    ):
        loads = fetches([(w_ref.at[c], w.at[:, pl.ds(c * depth, depth), :]) for c in range(cols)], w_sem)
        gather = Gather(size, x_ref, land, send, receive, own)
        beside = CoreGather(cols, out_ref, all_out_ref, *rest)
        greet([*gather.peers, *beside.greets])
        gather.start(greeted=True)
        beside.start()

        def keep(step, row):
            return pltpu.make_async_copy(land.at[row], all_ref.at[row], all_sem.at[step])

        def compute(step, row):
            keep(step, row).start()
            rows = pl.ds(pl.multiple_of(row * piece, piece), piece)

            @pl.loop(0, 3)
            def _(j):
                value = jnp.dot(land[row], w[j], preferred_element_type=jnp.float32).astype(jnp.bfloat16)
                for head in range(heads):
                    heads_ref[j, head, rows, :] = value[:, head * HD : (head + 1) * HD]

        wait_all(loads)
        gather.each(compute, gather.forward)
        beside.forward()
        beside.finish()
        for step in range(size):
            keep(step, gather.row_at(step)).wait()
        gather.finish()

    return pl.pallas_call(
        kernel,
        out_shape=[bf(3, heads, GLEN, HD), bf(size, piece, D), bf(cols, *w_out.shape)],
        in_specs=[ANY, ANY, ANY],
        out_specs=[VMEM, ANY, ANY],
        scratch_shapes=gather_scratch(size, piece)
        + [
            pltpu.VMEM((3, D, width), jnp.bfloat16),
            pltpu.SemaphoreType.DMA((cols,)),
            pltpu.SemaphoreType.DMA((size,)),
        ]
        + CoreGather.scratch(cols),
        compiler_params=comm_params(1),
        cost_estimate=SHORT,
        name="project_heads",
    )(normed, w_all, w_out)


def strip_loop(piece, body):
    @pl.loop(0, piece // STRIP)
    def _(i):
        body(pl.ds(pl.multiple_of(i * STRIP, STRIP), STRIP))


def row_mean(first, second):
    return (jnp.sum(first, axis=1, keepdims=True) + jnp.sum(second, axis=1, keepdims=True)) / D


def lanes(first, second):
    lane = lax.broadcasted_iota(jnp.int32, (STRIP, HD), 1)
    return jnp.where(lane == 0, first, jnp.where(lane == 1, second, 0.0))


LEFT, RIGHT = slice(0, HALF), slice(HALF, D)


def branch_out(size, attn, w_all, x, gain):
    piece = GLEN // size
    cols, width, depth = w_all.shape

    def kernel(
        attn_ref, w_ref, x_hbm, gain_ref, middle_ref, normed_ref, stat_ref,
        stage, land, total, send, receive, w, w_sem, x_ref, x_sem,
    ):
        loads = fetches([(w_ref.at[c], w.at[:, pl.ds(c * depth, depth)]) for c in range(cols)], w_sem)
        x_load = fetches([(x_hbm, x_ref)], x_sem)
        scatter = Scatter(size, stage, land, total, send, receive)
        wait_all(loads)

        def partial(step, row, store):
            rows = pl.ds(pl.multiple_of(row * piece, piece), piece)
            left = attn_ref[rows, :]

            @span_loop
            def _(t, half, columns, depth_rows):
                store(half, columns, plain_dot(left, w[:, depth_rows], NN))

        scatter.run_short(partial)

        def finish(rows):
            branch = (total[0, rows, :], total[1, rows, :])
            middle = (
                x_ref[rows, LEFT].astype(jnp.float32) + branch[0],
                x_ref[rows, RIGHT].astype(jnp.float32) + branch[1],
            )
            mean = row_mean(middle[0] * middle[0], middle[1] * middle[1])
            inverse = lax.rsqrt(mean + EPSILON)
            for part, columns in zip(middle, (LEFT, RIGHT)):
                middle_ref[rows, columns] = part
                normed_ref[rows, columns] = (part * inverse * gain_ref[:, columns]).astype(jnp.bfloat16)
            stat_ref[rows, :] = lanes(row_mean(branch[0] * branch[0], branch[1] * branch[1]), mean)

        wait_all(x_load)
        strip_loop(piece, finish)

    return pl.pallas_call(
        kernel,
        out_shape=[fl(piece, D), bf(piece, D), fl(piece, HD)],
        in_specs=[VMEM, ANY, ANY, VMEM],
        out_specs=[VMEM, VMEM, VMEM],
        scratch_shapes=scatter_scratch(size, piece, 1)
        + [pltpu.VMEM((width, D), jnp.bfloat16), dma(cols), pltpu.VMEM((piece, D), jnp.bfloat16), dma(1)],
        compiler_params=comm_params(2),
        cost_estimate=SHORT,
        name="branch_out",
    )(attn, w_all, x, gain)


def feed_forward(size, tokens, pack, cot, first):
    piece = GLEN // size
    cols, _, depth, wide = pack.shape
    tile = min(wide, 512)
    count = wide // tile

    def kernel(x_ref, pack_ref, cot_ref, hidden_ref, grad_ref, *rest):
        if first:
            all_ref, land, send, receive, own, all_sem, *rest = rest
        else:
            land, own, *rest = rest
        w, cot_all, back, stage, w_sem, cot_sem, out_sem = rest
        if first:
            gather = Gather(size, x_ref, land, send, receive, own)
            gather.start()
            order = [gather.row, *gather.order]
        else:
            order = list(range(size))
        w_loads = fetches(
            [(pack_ref.at[c, j], w.at[j, pl.ds(c * depth, depth), :]) for j in (2, 0, 1) for c in range(cols)], w_sem
        )
        cot_loads = fetches([(cot_ref.at[row], cot_all.at[row]) for row in order], cot_sem)
        if not first:
            x_loads = fetches([(x_ref.at[row], land.at[row]) for row in order], own)

        def backward(row):
            @tiles_of(wide, tile)
            def _(t, columns):
                back[row, :, columns] = plain_dot(cot_all[row], w[2, :, columns], NN).astype(jnp.bfloat16)

        def moves(row, slot, columns):
            rows = pl.ds(pl.multiple_of(row * piece, piece), piece)
            return [
                pltpu.make_async_copy(stage.at[slot, 0], hidden_ref.at[rows, columns], out_sem.at[slot, 0]),
                pltpu.make_async_copy(stage.at[slot, 1], grad_ref.at[0, rows, columns], out_sem.at[slot, 1]),
                pltpu.make_async_copy(stage.at[slot, 2], grad_ref.at[1, rows, columns], out_sem.at[slot, 2]),
            ]

        def compute(row):
            if first:
                store = pltpu.make_async_copy(land.at[row], all_ref.at[row], all_sem)
                store.start()

            @pl.loop(0, count)
            def _(t):
                columns = pl.ds(pl.multiple_of(t * tile, tile), tile)
                slot = lax.rem(t, 2)
                x = land[row]
                gate_pre = jnp.dot(x, w[0, :, columns], preferred_element_type=jnp.float32)
                up_pre = jnp.dot(x, w[1, :, columns], preferred_element_type=jnp.float32)
                sigmoid = jax.nn.sigmoid(gate_pre)
                silu = gate_pre * sigmoid
                grad_hidden = back[row, :, columns].astype(jnp.float32)

                @pl.when(t >= 2)
                def _():
                    wait_all(moves(row, slot, columns))

                stage[slot, 0] = (silu * up_pre).astype(jnp.bfloat16)
                stage[slot, 1] = (grad_hidden * up_pre * (sigmoid + silu * (1.0 - sigmoid))).astype(jnp.bfloat16)
                stage[slot, 2] = (grad_hidden * silu).astype(jnp.bfloat16)
                for move in moves(row, slot, columns):
                    move.start()

            for slot in range(min(2, count)):
                wait_all(moves(row, slot, pl.ds(slot * tile, tile)))
            if first:
                store.wait()

        wait_all(w_loads[:cols])
        if first:
            cot_loads[0].wait()

            @pl.loop(0, size)
            def _(d):
                @pl.when(d == 1)
                def _():
                    gather.forward()
                    wait_all(cot_loads[1:])

                backward(lax.rem(gather.row + d, size))

            wait_all(w_loads[cols:])
            gather.each(lambda step, row: compute(row), lambda: None)
            gather.finish()
            return

        @pl.loop(0, size)
        def _(row):
            pltpu.make_async_copy(cot_ref.at[row], cot_all.at[row], cot_sem.at[row]).wait()
            backward(row)

        wait_all(w_loads[cols:])

        @pl.loop(0, size)
        def _(row):
            pltpu.make_async_copy(x_ref.at[row], land.at[row], own.at[row]).wait()
            compute(row)

    out_shape = [bf(GLEN, wide), bf(2, GLEN, wide)]
    if first:
        out_shape.append(bf(size, piece, D))
        scratch = gather_scratch(size, piece) + [pltpu.SemaphoreType.DMA]
    else:
        scratch = [pltpu.VMEM((size, piece, D), jnp.bfloat16), dma(size)]
    return pl.pallas_call(
        kernel,
        out_shape=out_shape,
        in_specs=[ANY] * 3,
        out_specs=[ANY] * len(out_shape),
        scratch_shapes=scratch
        + [
            pltpu.VMEM((3, D, wide), jnp.bfloat16),
            pltpu.VMEM((size, piece, D), jnp.bfloat16),
            pltpu.VMEM((size, piece, wide), jnp.bfloat16),
            pltpu.VMEM((2, 3, piece, tile), jnp.bfloat16),
            dma(3 * cols), dma(size), dma(2, 3),
        ],
        compiler_params=comm_params(3) if first else pltpu.CompilerParams(vmem_limit_bytes=BIG_VMEM),
        cost_estimate=SHORT,
        name="feed_first" if first else "feed_second",
    )(tokens, pack, cot)


def weight_grads_kernel(x_ref, y_ref, g_ref, h_ref, out_ref):
    count = g_ref.shape[0]
    for j in range(count):
        out_ref[j] = plain_dot(x_ref[...], g_ref[j], TN).astype(jnp.bfloat16)
    out_ref[count] = plain_dot(y_ref[...], h_ref[...], TN).astype(jnp.bfloat16)


def weight_grads(x, grads, y, hidden):
    count, _, wide = grads.shape
    tile = 256
    block = pl.BlockSpec((GLEN, tile), lambda i: (0, i))
    return pl.pallas_call(
        weight_grads_kernel,
        grid=(D // tile,),
        in_specs=[
            block, block,
            pl.BlockSpec((count, GLEN, wide), lambda i: (0, 0, 0), pipeline_mode=pl.Buffered(1)),
            pl.BlockSpec((GLEN, wide), lambda i: (0, 0), pipeline_mode=pl.Buffered(1)),
        ],
        out_specs=pl.BlockSpec((count + 1, tile, wide), lambda i: (0, i, 0)),
        out_shape=bf(count + 1, D, wide),
        compiler_params=pltpu.CompilerParams(vmem_limit_bytes=BIG_VMEM),
        cost_estimate=SHORT,
        name="weight_grads",
    )(x, y, grads, hidden)


def norm_back(rows, total, stream, inverse, gain_ref, base, store, gain_sum):
    u = [total[half, rows, :] * gain_ref[:, columns] for half, columns in enumerate((LEFT, RIGHT))]
    inner = row_mean(u[0] * stream[0], u[1] * stream[1]) * inverse * inverse * inverse
    for half, columns in enumerate((LEFT, RIGHT)):
        store(columns, base[half] + inverse * u[half] - stream[half] * inner)
        gain_sum[:, columns] += jnp.sum(total[half, rows, :] * stream[half] * inverse, axis=0, keepdims=True)


def middle_back(size, grads, packs, middle, cot, gain, tokens, all_cot, hidden):
    piece = middle.shape[0]
    cols, _, depth, wide = packs[0].shape
    block = 256

    def kernel(
        first_ref, second_ref, pack_a, pack_b, middle_hbm, cot_hbm, gain_ref, x_ref, y_ref, hidden_ref,
        grad_ref, low_ref, gain_sum, part_ref,
        stage, land, total, send, receive, w, g_first, g_second, h, x, part,
        w_sem, first_sem, second_sem, h_sem, x_sem, part_sem, middle_ref, cot_ref, late_sem,
    ):
        pack_refs = (pack_a, pack_b)
        scatter = Scatter(size, stage, land, total, send, receive)

        def piece_rows(at):
            return pl.ds(pl.multiple_of(at * piece, piece), piece)

        def first_load(step):
            slot = lax.rem(step, 2)
            return pltpu.make_async_copy(
                first_ref.at[:, piece_rows(scatter.row_at(step))], g_first.at[slot], first_sem.at[slot]
            )

        def second_load(step):
            rows = piece_rows(scatter.row_at(step))
            return pltpu.make_async_copy(second_ref.at[:, rows], g_second.at[:, rows], second_sem.at[step])

        def w_load(i, c):
            return pltpu.make_async_copy(
                pack_refs[i].at[c, pl.ds(0, 2)], w.at[i, :, pl.ds(pl.multiple_of(c * depth, depth), depth), :], w_sem.at[i, c]
            )

        first_load(0).start()
        second_load(0).start()
        for c in range(cols):
            for i in range(2):
                w_load(i, c).start()
        first_load(1).start()
        for step in range(1, size):
            second_load(step).start()
        h_load = pltpu.make_async_copy(hidden_ref, h, h_sem)
        h_load.start()
        late = fetches([(middle_hbm, middle_ref), (cot_hbm, cot_ref)], late_sem)
        gain_sum[...] = jnp.zeros_like(gain_sum)

        def partial(step, at, store):
            first_load(step).wait()
            second_load(step).wait()

            @span_loop
            def _(t, half, columns, depth_rows):
                @pl.when(step == 0)
                def _():
                    for k in range(SPAN // depth):
                        for i in range(2):
                            w_load(i, t * (SPAN // depth) + k).wait()

                rows = piece_rows(at)
                value = 0.0
                for j in range(2):
                    value += plain_dot(g_first[lax.rem(step, 2), j], w[0, j, depth_rows, :], NT)
                    value += plain_dot(g_second[j, rows, :], w[1, j, depth_rows, :], NT)
                store(half, columns, value)

            @pl.when(step + 2 < size)
            def _():
                first_load(step + 2).start()

        def x_loads(i, slot):
            columns = pl.ds(pl.multiple_of(i * block, block), block)
            return [
                pltpu.make_async_copy(source.at[:, :, columns], x.at[slot, k], x_sem.at[slot, k])
                for k, source in enumerate((x_ref, y_ref))
            ]

        def part_move(i, slot):
            columns = pl.ds(pl.multiple_of(i * block, block), block)
            return pltpu.make_async_copy(part.at[slot], part_ref.at[:, columns, :], part_sem.at[slot])

        def weights():
            count = D // block
            for load in x_loads(0, 0):
                load.start()
            h_load.wait()

            @pl.loop(0, count)
            def _(i):
                slot = lax.rem(i, 2)

                @pl.when(i + 1 < count)
                def _():
                    for load in x_loads(i + 1, 1 - slot):
                        load.start()

                wait_all(x_loads(i, slot))

                @pl.when(i >= 2)
                def _():
                    part_move(i, slot).wait()


                @pl.loop(0, 2)
                def _(j):
                    part[slot, j] = plain_dot(x[slot, 0].reshape(GLEN, block), g_second[j], TN).astype(jnp.bfloat16)

                part[slot, 2] = plain_dot(x[slot, 1].reshape(GLEN, block), h[...], TN).astype(jnp.bfloat16)
                part_move(i, slot).start()

            for slot in range(2):
                part_move(slot, slot).wait()

        scatter.run_short(partial, weights)

        def finish(rows):
            stream = [middle_ref[rows, columns] for columns in (LEFT, RIGHT)]
            base = [cot_ref[rows, columns].astype(jnp.float32) for columns in (LEFT, RIGHT)]
            inverse = lax.rsqrt(row_mean(stream[0] * stream[0], stream[1] * stream[1]) + EPSILON)

            def store(columns, value):
                grad_ref[rows, columns] = value
                low_ref[rows, columns] = value.astype(jnp.bfloat16)

            norm_back(rows, total, stream, inverse, gain_ref, base, store, gain_sum)

        wait_all(late)
        strip_loop(piece, finish)

    return pl.pallas_call(
        kernel,
        out_shape=[fl(piece, D), bf(piece, D), fl(1, D), bf(3, D, wide)],
        in_specs=[ANY] * 6 + [VMEM] + [ANY] * 3,
        out_specs=[VMEM, VMEM, VMEM, ANY],
        scratch_shapes=scatter_scratch(size, piece, 1)
        + [
            pltpu.VMEM((2, 2, D, wide), jnp.bfloat16),
            pltpu.VMEM((2, 2, piece, wide), jnp.bfloat16),
            pltpu.VMEM((2, GLEN, wide), jnp.bfloat16),
            pltpu.VMEM((GLEN, wide), jnp.bfloat16),
            pltpu.VMEM((2, 2, size, piece, block), jnp.bfloat16),
            pltpu.VMEM((2, 3, block, wide), jnp.bfloat16),
            dma(2, cols), dma(2), dma(size), pltpu.SemaphoreType.DMA, dma(2, 2), dma(2),
            pltpu.VMEM((piece, D), jnp.float32), pltpu.VMEM((piece, D), jnp.bfloat16), dma(2),
        ],
        compiler_params=comm_params(4),
        cost_estimate=SHORT,
        name="middle_back",
    )(*grads, *packs, middle, cot, gain, tokens, all_cot, hidden)


def blocked_store(ref, rows, depth, columns, value):
    for i in range(value.shape[1] // depth):
        ref[columns.start // depth + i, rows, :] = value[:, i * depth : (i + 1) * depth]


def branch_back(size, low, w_all):
    piece = low.shape[0]
    cols, width, depth = w_all.shape
    heads = width // HD

    def kernel(x_ref, w_ref, heads_ref, all_ref, land, send, receive, own, w, w_sem, all_sem):
        loads = fetches([(w_ref.at[c], w.at[:, pl.ds(c * depth, depth)]) for c in range(cols)], w_sem)
        gather = Gather(size, x_ref, land, send, receive, own)
        gather.start()

        def keep(step, row):
            return pltpu.make_async_copy(land.at[row], all_ref.at[row], all_sem.at[step])

        def compute(step, row):
            keep(step, row).start()
            rows = pl.ds(pl.multiple_of(row * piece, piece), piece)
            value = plain_dot(land[row], w[...], NT).astype(jnp.bfloat16)
            for head in range(heads):
                heads_ref[head, rows, :] = value[:, head * HD : (head + 1) * HD]

        wait_all(loads)
        gather.each(compute, gather.forward)
        for step in range(size):
            keep(step, gather.row_at(step)).wait()
        gather.finish()

    return pl.pallas_call(
        kernel,
        out_shape=[bf(heads, GLEN, HD), bf(size, piece, D)],
        in_specs=[ANY, ANY],
        out_specs=[VMEM, ANY],
        scratch_shapes=gather_scratch(size, piece)
        + [
            pltpu.VMEM((width, D), jnp.bfloat16),
            pltpu.SemaphoreType.DMA((cols,)),
            pltpu.SemaphoreType.DMA((size,)),
        ],
        compiler_params=comm_params(6),
        cost_estimate=SHORT,
        name="branch_back",
    )(low, w_all)


def stream_back(size, grads, w_all, x, grad_middle, gain, blocks_out):
    piece = x.shape[0]
    cols, _, depth, width = w_all.shape

    def kernel(
        g_hbm, w_ref, x_hbm, middle_hbm, gain_ref, blocks_ref, out_ref, gain_sum, target_ref,
        stage, land, total, send, receive, w, w_sem, g_ref, x_ref, middle_ref, g_sem, late_sem, *rest,
    ):
        loads = fetches([(w_ref.at[c], w.at[:, pl.ds(c * depth, depth), :]) for c in range(cols)], w_sem)
        greet(row_and_col_peers(size, cols))
        outward = Outward(size, cols, blocks_ref, rest[0], target_ref, *rest[1:])
        outward.start()
        scatter = Scatter(size, stage, land, total, send, receive)

        def g_load(step):
            rows = pl.ds(pl.multiple_of(scatter.row_at(step) * piece, piece), piece)
            return pltpu.make_async_copy(g_hbm.at[:, rows], g_ref.at[:, rows], g_sem.at[step])

        for step in range(size):
            g_load(step).start()
        late = fetches([(x_hbm, x_ref), (middle_hbm, middle_ref)], late_sem)
        wait_all(loads)
        gain_sum[...] = jnp.zeros_like(gain_sum)

        def partial(step, row, store):
            g_load(step).wait()

            @span_loop
            def _(t, half, columns, depth_rows):
                rows = pl.ds(pl.multiple_of(row * piece, piece), piece)
                value = plain_dot(g_ref[0, rows, :], w[0, depth_rows, :], NT)
                for j in (1, 2):
                    value += plain_dot(g_ref[j, rows, :], w[j, depth_rows, :], NT)
                store(half, columns, value)

        scatter.run_short(partial, outward.forward, greeted=True)

        def finish(rows):
            stream = [x_ref[rows, columns].astype(jnp.float32) for columns in (LEFT, RIGHT)]
            base = [middle_ref[rows, columns] for columns in (LEFT, RIGHT)]
            inverse = lax.rsqrt(row_mean(stream[0] * stream[0], stream[1] * stream[1]) + EPSILON)

            def store(columns, value):
                blocked_store(out_ref, rows, depth, columns, value.astype(jnp.bfloat16))

            norm_back(rows, total, stream, inverse, gain_ref, base, store, gain_sum)

        wait_all(late)
        strip_loop(piece, finish)
        outward.finish()

    return pl.pallas_call(
        kernel,
        out_shape=[bf(cols, piece, depth), fl(1, D), bf(cols // size, size, piece, depth)],
        in_specs=[ANY, ANY, ANY, ANY, VMEM, ANY],
        out_specs=[VMEM, VMEM, ANY],
        scratch_shapes=scatter_scratch(size, piece, 1)
        + [pltpu.VMEM((3, D, width), jnp.bfloat16), dma(cols)]
        + [
            pltpu.VMEM((3, GLEN, width), jnp.bfloat16), pltpu.VMEM((piece, D), jnp.bfloat16),
            pltpu.VMEM((piece, D), jnp.float32), dma(size), dma(2),
        ]
        + Outward.scratch(size, cols, piece, depth),
        compiler_params=comm_params(7),
        cost_estimate=SHORT,
        name="stream_back",
    )(grads, w_all, x, grad_middle, gain, blocks_out)


def row_and_col_peers(size, cols):
    row, col = here()
    return [(lax.rem(row + d, size), col) for d in range(1, size)] + [
        (row, lax.rem(col + e, cols)) for e in range(1, cols)
    ]


class Inward:
    def __init__(self, size, cols, source, middle, land, first_send, first_receive, send, receive, own):
        self.size, self.cols, self.groups = size, cols, cols // size
        self.source, self.middle, self.land = source, middle, land
        self.first_send, self.first_receive = first_send, first_receive
        self.send, self.receive, self.own = send, receive, own
        self.row, self.col = here()

    @staticmethod
    def scratch(size, cols, piece, depth):
        return [
            pltpu.VMEM((size, cols // size, piece, depth), jnp.bfloat16),
            pltpu.VMEM((cols, piece, depth), jnp.bfloat16),
            dma(size - 1), dma(size - 1), dma(cols), dma(cols), dma(2),
        ]

    def start(self):
        row, col = self.row, self.col
        self.first = []
        for d in range(1, self.size):
            peer = lax.rem(row + d, self.size)
            self.first.append(
                remote(
                    self.source.at[:, peer], self.middle.at[row],
                    self.first_send.at[d - 1], self.first_receive.at[d - 1], (peer, col),
                )
            )
            self.first[-1].start()
        self.keep = pltpu.make_async_copy(self.source.at[:, row], self.middle.at[row], self.own.at[0])
        self.keep.start()

    def forward(self):
        row, col = self.row, self.col
        for d in range(self.size):
            origin = lax.rem(row + self.size - d, self.size)
            if d == 0:
                self.keep.wait()
            else:
                self.first[d - 1].wait_recv()
            for i in range(self.groups):
                group = origin * self.groups + i

                @pl.when(group != col)
                def _():
                    remote(
                        self.middle.at[origin, i], self.land.at[col],
                        self.send.at[group], self.receive.at[col], (row, group),
                    ).start()

                @pl.when(group == col)
                def _():
                    pltpu.make_async_copy(self.middle.at[origin, i], self.land.at[col], self.own.at[1]).start()

    def finish(self):
        row, col = self.row, self.col
        pltpu.make_async_copy(self.middle.at[0, 0], self.land.at[col], self.own.at[1]).wait()
        for e in range(1, self.cols):
            peer = lax.rem(col + e, self.cols)
            remote(
                self.middle.at[0, 0], self.land.at[peer], self.send.at[peer], self.receive.at[peer], (row, peer)
            ).wait()
        for copy in self.first:
            copy.wait_send()


class Outward:
    def __init__(self, size, cols, source, middle, target, first_send, first_receive, send, receive, own):
        self.size, self.cols, self.groups = size, cols, cols // size
        self.source, self.middle, self.target = source, middle, target
        self.first_send, self.first_receive = first_send, first_receive
        self.send, self.receive, self.own = send, receive, own
        self.row, self.col = here()

    @staticmethod
    def scratch(size, cols, piece, depth):
        return [
            pltpu.VMEM((cols, piece, depth), jnp.bfloat16),
            dma(cols - 1), dma(cols - 1), dma(cols), dma(cols), dma(cols // size),
        ]

    def start(self):
        row, col = self.row, self.col
        self.first = []
        for e in range(1, self.cols):
            peer = lax.rem(col + e, self.cols)
            self.first.append(
                remote(
                    self.source.at[peer], self.middle.at[col],
                    self.first_send.at[e - 1], self.first_receive.at[e - 1], (row, peer),
                )
            )
            self.first[-1].start()

    def forward(self):
        row, col = self.row, self.col
        for e in range(self.cols):
            group = lax.rem(col + self.cols - e, self.cols)
            if e:
                self.first[e - 1].wait_recv()
            block = self.middle.at[group] if e else self.source.at[col]
            home, i = group // self.groups, lax.rem(group, self.groups)

            @pl.when(home != row)
            def _():
                remote(
                    block, self.target.at[i, row],
                    self.send.at[group], self.receive.at[i * self.size + row], (home, col),
                ).start()

            @pl.when(home == row)
            def _():
                pltpu.make_async_copy(block, self.target.at[i, row], self.own.at[i]).start()

    def finish(self):
        row, col = self.row, self.col
        for i in range(self.groups):
            pltpu.make_async_copy(self.middle.at[0], self.target.at[i, row], self.own.at[i]).wait()
            for d in range(1, self.size):
                peer = lax.rem(row + d, self.size)
                remote(
                    self.middle.at[0], self.target.at[i, peer],
                    self.send.at[peer * self.groups + i], self.receive.at[i * self.size + peer], (peer, col),
                ).wait()
        for copy in self.first:
            copy.wait_send()


def by_pieces(block, size):
    return block.reshape(block.shape[0] // GLEN, size, GLEN // size, block.shape[1])


def enter(size, cols, stream_in, cotangent, gains):
    pieces = by_pieces(stream_in, size)
    piece, depth = pieces.shape[2:]
    scratch = Inward.scratch(size, cols, piece, depth)

    def kernel(
        x_ref, cot_ref, gains_ref, tokens_ref, normed_ref, gain_in_ref, gain_mid_ref, cot_tokens_ref, all_cot_ref,
        gains_land, gains_send, gains_receive, gather_send, gather_receive, gather_own, *rest,
    ):
        greet(row_and_col_peers(size, cols))
        exchange = Inward(size, cols, x_ref, *rest[: len(scratch)])
        second = Inward(size, cols, cot_ref, *rest[len(scratch) :])
        gather = Gather(size, cot_tokens_ref, all_cot_ref, gather_send, gather_receive, gather_own)
        second.start()
        exchange.start()
        row, col = here()
        copies = []
        for e in range(1, cols):
            peer = lax.rem(col + e, cols)
            copies.append(
                remote(gains_ref, gains_land.at[col], gains_send.at[e - 1], gains_receive.at[e - 1], (row, peer))
            )
            copies[-1].start()
        gains_land[col] = gains_ref[...]
        second.forward()
        exchange.forward()
        second.finish()

        def assemble(rows):
            for c in range(cols):
                cot_tokens_ref[rows, c * depth : (c + 1) * depth] = second.land[c, rows, :]

        strip_loop(piece, assemble)
        gather.start(greeted=True, hold=False)
        gather.forward()
        for copy in copies:
            copy.wait()
        for c in range(cols):
            gain_in_ref[:, c * depth : (c + 1) * depth] = gains_land[c, 0:1, :]
            gain_mid_ref[:, c * depth : (c + 1) * depth] = gains_land[c, 1:2, :]
        exchange.finish()
        land = exchange.land

        def norm(rows):
            total = jnp.zeros((STRIP, 1), jnp.float32)
            for c in range(cols):
                part = land[c, rows, :]
                tokens_ref[rows, c * depth : (c + 1) * depth] = part
                part = part.astype(jnp.float32)
                total += jnp.sum(part * part, axis=1, keepdims=True)
            inverse = lax.rsqrt(total / D + EPSILON)
            for c in range(cols):
                columns = slice(c * depth, (c + 1) * depth)
                normed_ref[rows, columns] = (
                    land[c, rows, :].astype(jnp.float32) * inverse * gain_in_ref[:, columns]
                ).astype(jnp.bfloat16)

        strip_loop(piece, norm)
        for step in range(size - 1):
            gather.wait(step)
        gather.keep.wait()
        gather.finish()

    return pl.pallas_call(
        kernel,
        out_shape=[bf(piece, D), bf(piece, D), fl(1, D), fl(1, D), bf(piece, D), bf(size, piece, D)],
        in_specs=[ANY, ANY, VMEM],
        out_specs=[VMEM] * 5 + [ANY],
        scratch_shapes=[pltpu.VMEM((cols, 8, depth), jnp.float32), dma(cols - 1), dma(cols - 1)]
        + [dma(Gather.semaphores(size)), dma(Gather.semaphores(size)), pltpu.SemaphoreType.DMA]
        + scratch * 2,
        compiler_params=comm_params(8),
        cost_estimate=SHORT,
        name="enter",
    )(pieces, by_pieces(cotangent, size), jnp.pad(gains, ((0, 6), (0, 0))))


def leave(size, cols, blocks_grad, stats, sums):
    _, piece, depth = blocks_grad.shape
    groups = cols // size

    def kernel(
        grad_ref, stats_ref, sums_ref, grad_target, stats_target, sums_target,
        stats_row, stats_all, sums_col, sums_part, sums_row,
        a_send, a_receive, b_send, b_receive, c_send, c_receive, d_send, d_receive, *rest,
    ):
        row, col = here()
        greet(row_and_col_peers(size, cols))
        grad = Outward(size, cols, grad_ref, rest[0], grad_target, *rest[1:])
        home, slot = col // groups, lax.rem(col, groups)
        col_peers = [lax.rem(col + e, cols) for e in range(1, cols)]
        row_peers = [lax.rem(row + d, size) for d in range(1, size)]

        def sums_first(peer):
            return remote(sums_ref.at[peer], sums_col.at[col], c_send.at[peer], c_receive.at[col], (row, peer))

        for peer in col_peers:
            sums_first(peer).start()
        sums_col[col] = sums_ref[col]

        @pl.when(home != row)
        def _():
            remote(stats_ref, stats_row.at[row], a_send, a_receive.at[row], (home, col)).start()

        @pl.when(home == row)
        def _():
            stats_row[row] = stats_ref[...]

        grad.start()
        for peer in col_peers:
            remote(sums_ref.at[peer], sums_col.at[peer], c_send.at[peer], c_receive.at[peer], (row, peer)).wait()
        total = sums_col[0]
        for c in range(1, cols):
            total += sums_col[c]
        sums_part[...] = total
        sums_row[row] = total
        for peer in row_peers:
            remote(sums_part, sums_row.at[row], d_send.at[peer], d_receive.at[row], (peer, col)).start()

        @pl.when(home == row)
        def _():
            for peer in row_peers:
                remote(stats_ref, stats_row.at[peer], a_send, a_receive.at[peer], (peer, col)).wait_recv()
            for e, peer in enumerate(col_peers):
                remote(stats_row, stats_all.at[slot], b_send.at[e], b_receive.at[slot], (row, peer)).start()
            stats_all[slot] = stats_row[...]

        grad.forward()
        for peer in row_peers:
            remote(sums_part, sums_row.at[peer], d_send.at[peer], d_receive.at[peer], (peer, col)).wait()
        whole = sums_row[0]
        for r in range(1, size):
            whole += sums_row[r]
        line = lax.broadcasted_iota(jnp.int32, (8, depth), 0)
        sums_target[...] = jnp.where(line < 2, whole, total)

        @pl.when(home == row)
        def _():
            for e, peer in enumerate(col_peers):
                remote(stats_row, stats_all.at[slot], b_send.at[e], b_receive.at[slot], (row, peer)).wait_send()

        @pl.when(home != row)
        def _():
            remote(stats_ref, stats_row.at[row], a_send, a_receive.at[row], (home, col)).wait_send()

        for i in range(groups):
            group = row * groups + i

            @pl.when(group != col)
            def _():
                remote(stats_row, stats_all.at[i], b_send.at[0], b_receive.at[i], (row, group)).wait_recv()

        stats_target[...] = stats_all[...]
        grad.finish()

    return pl.pallas_call(
        kernel,
        out_shape=[
            bf(groups, size, piece, depth),
            fl(groups, size, 8, piece), fl(8, depth),
        ],
        in_specs=[VMEM] * 3,
        out_specs=[ANY, VMEM, VMEM],
        scratch_shapes=[
            pltpu.VMEM((size, 8, piece), jnp.float32),
            pltpu.VMEM((groups, size, 8, piece), jnp.float32),
            pltpu.VMEM((cols, 8, depth), jnp.float32),
            pltpu.VMEM((8, depth), jnp.float32),
            pltpu.VMEM((size, 8, depth), jnp.float32),
            pltpu.SemaphoreType.DMA, dma(size), dma(cols - 1), dma(groups), dma(cols), dma(cols), dma(size), dma(size),
        ]
        + Outward.scratch(size, cols, piece, depth),
        compiler_params=comm_params(10),
        cost_estimate=SHORT,
        name="leave",
    )(blocks_grad, stats, sums)


def over_col(partial, axis):
    return lax.psum_scatter(partial.astype(jnp.bfloat16), "col", scatter_dimension=axis, tiled=True)


def flat(pieces):
    return pieces.reshape(GLEN, D)


def local(
    stream_in,
    w_qkv,
    w_out,
    w_gate_up,
    w_down,
    gain_attn,
    gain_ffn,
    gate_logit,
    memory,
    memory_norm,
    offsets,
    lengths,
    cotangent,
):
    head_here = memory.shape[1]
    size = lax.axis_size("row")
    cols = lax.axis_size("col")
    all_qkv = lax.all_gather(w_qkv, "col", axis=0, tiled=False)
    units = w_down.shape[0] // 2
    packs = [
        jnp.concatenate([w_gate_up[:, :, part], w_down[part].T[None]], axis=0)
        for part in (slice(0, units), slice(units, None))
    ]
    all_packs = [lax.all_gather(pack, "col", axis=0, tiled=False) for pack in packs]
    gate_value = jax.nn.sigmoid(gate_logit)
    group = (memory[0], memory_norm[0], offsets[0], lengths[0], gate_value)
    stream, normed_in, gain_in, gain_mid, cot, all_cot = enter(
        size, cols, stream_in, cotangent, jnp.stack([gain_attn, gain_ffn])
    )
    heads_all, all_in, all_out = project_heads(size, normed_in, all_qkv, w_out)
    attn, dot_part, memory_part, logsum, memory_new, norm_new = attend(heads_all, *group)
    middle, normed_ffn, stat_branch = branch_out(size, attn, all_out, stream, gain_mid)
    hidden_first, grads_first, all_ffn = feed_forward(size, normed_ffn, all_packs[0], all_cot, True)
    part_first = weight_grads(flat(all_ffn), grads_first, flat(all_cot), hidden_first)
    part_first, all_ffn = lax.optimization_barrier((part_first, all_ffn))
    scattered_first = over_col(part_first, 1)
    hidden_second, grads_second = feed_forward(size, all_ffn, all_packs[1], all_cot, False)
    grad_middle, low_branch, part_gain_ffn, part_second = middle_back(
        size, (grads_first, grads_second), all_packs, middle, cot, gain_mid, all_ffn, all_cot, hidden_second
    )
    scattered_second = over_col(part_second, 1)
    grad_heads, all_branch = branch_back(size, low_branch, all_out)
    grads_qkv, gate_sums, blocks_out, stat_ffn = attend_back(
        size, heads_all, grad_heads, dot_part, memory_part, logsum, *group,
        (hidden_first, hidden_second), all_packs, middle,
    )
    part_attn = weight_grads(flat(all_in), grads_qkv, flat(all_branch), attn)
    grads_qkv, part_attn, scattered_first = lax.optimization_barrier((grads_qkv, part_attn, scattered_first))
    scattered_attn = over_col(part_attn, 1)
    blocks_grad, part_gain_attn, stream_out = stream_back(
        size, grads_qkv, all_qkv, stream, grad_middle, gain_in, blocks_out
    )
    grad_gate_up = jnp.concatenate([scattered_first[:2], scattered_second[:2]], axis=2).astype(jnp.float32)
    grad_down = jnp.concatenate([scattered_first[2], scattered_second[2]], axis=1).T.astype(jnp.float32)
    blocks_grad, grad_gate_up, grad_down = lax.optimization_barrier((blocks_grad, grad_gate_up, grad_down))
    grad_qkv, grad_out = scattered_attn[:3].astype(jnp.float32), scattered_attn[3].T.astype(jnp.float32)
    logit_part = gate_value * (1.0 - gate_value) * jnp.sum(gate_sums, axis=(1, 2))
    features_here = gain_attn.shape[0]
    sums = jnp.concatenate(
        [
            part_gain_attn.reshape(cols, 1, features_here),
            part_gain_ffn.reshape(cols, 1, features_here),
            jnp.broadcast_to(
                jnp.pad(logit_part, (0, features_here - head_here))[None, None], (cols, 6, features_here)
            ),
        ],
        axis=1,
    )
    stats = jnp.sqrt(jnp.concatenate([stat_branch[:, :2], stat_ffn[:, :2]], axis=1).T)
    stream_grad, stats_all, sums = leave(
        size, cols, blocks_grad, jnp.pad(stats, ((0, 4), (0, 0))), sums
    )
    stream_out = stream_out.reshape(stream_in.shape)
    stream_grad = stream_grad.reshape(stream_in.shape).astype(jnp.float32)
    rms_table = stats_all[:, :, :4].transpose(2, 0, 1, 3).reshape(4, stream_in.shape[0])
    grad_gain_attn, grad_gain_ffn, grad_gate_logit = sums[0], sums[1], sums[2, :head_here]
    return (
        stream_out,
        stream_grad,
        grad_qkv,
        grad_out,
        grad_gate_up,
        grad_down,
        grad_gain_attn,
        grad_gain_ffn,
        grad_gate_logit,
        memory_new[None],
        norm_new.reshape(1, head_here, HD),
        rms_table,
    )


def solution(mesh):
    return jax.shard_map(
        local,
        mesh=mesh,
        in_specs=(
            P("row", "col"),
            P(None, "col", "row"),
            P("row", "col"),
            P(None, "col", "row"),
            P("row", "col"),
            P("col"),
            P("col"),
            P("row"),
            P("col", "row", None, None),
            P("col", "row", None),
            P("col", None),
            P("col", None),
            P("row", "col"),
        ),
        out_specs=(
            P("row", "col"),
            P("row", "col"),
            P(None, "col", "row"),
            P("row", "col"),
            P(None, "col", "row"),
            P("row", "col"),
            P("col"),
            P("col"),
            P("row"),
            P("col", "row", None, None),
            P("col", "row", None),
            P(None, "row"),
        ),
        check_vma=False,
    )
```
